32 devices in a mesh: gauss: 16 (over z, x, core), tile: 2 (over y).
Axes of the slice: x: 2, y: 2, z: 4, core: 2. Of those that a mesh axis runs over, the one named last changes fastest.
Arguments:
- splats: float32 [9, 32768], P(None, ('gauss', 'tile')), may hold values from -8 to 260, as said below
- sh_coeffs: float32 [48, 32768], P(None, ('gauss', 'tile')), may hold values from -2 to 2
- send_list: int32 [32768], P(('gauss', 'tile')), may hold values from 0 to 1023, as said below
- block_slots: int32 [16, 96, 128], P('gauss', 'tile'), may hold values from 0 to 1023, as said below
- block_tiles: int32 [16, 96], P('gauss', 'tile'), may hold values from 0 to 8, as said below
- target: float32 [3, 256, 256], P(None, 'gauss', 'tile'), may hold values from 0 to 1
Outputs:
- rendered: float32 [3, 256, 256], P(None, 'gauss', 'tile')
- grad_splats: float32 [9, 32768], P(None, ('gauss', 'tile'))
- grad_sh: float32 [48, 32768], P(None, ('gauss', 'tile'))
The draws below stay inside these ranges and needn't reach their ends.
Inputs may be any that keep to these rules, and one draw needn't show every extreme that they name: `send_list`: each device's 1024 entries are a permutation of 0 to 1023. `block_tiles`: each device's 48 entries never fall; each of its tiles 0 to 7 has at least one block; the value 8 marks an unused slot; in every draw some device uses all 48 slots. `block_slots`: entries index the device's received Gaussians. `splats`: conics are positive definite; view directions have unit length; opacity logits (row 5) lie between -8 and -2.
All inputs are finite; a program needn't handle non-finite values.
Results may differ from the reference program's by a relative error of at most 0.0003.
Values sent between devices are 32-bit elements; how exact they have to be, the bound alone decides.
A program may use at most 64 MiB of HBM per device.

```python
import math
import jax
import jax.numpy as jnp
from jax import lax

TILE_SIDE = 16
BLOCK_LEN = 128
SH_COEFFS = 48
TILES_DEV = 8
BLOCK_SLOTS = 48
SEND_CAP = 64
ROW_BANDS = 16
COL_BANDS = 2
OWN_SLOTS = 1024
GAUSSIANS = 32768
IMAGE_H = 256
IMAGE_W = 256


def owner_orders(key):
    devices_total = ROW_BANDS * COL_BANDS
    subkeys = jax.random.split(jax.random.fold_in(key, 11), devices_total)
    return jax.vmap(lambda single: jax.random.permutation(single, OWN_SLOTS))(subkeys).astype(jnp.int32)


def draw_send_list(key, part):
    return owner_orders(key).reshape(-1)


def draw_splats(key, part):
    orders = owner_orders(key)
    devices_total = ROW_BANDS * COL_BANDS
    position = jnp.arange(OWN_SLOTS)
    dest_band = position // SEND_CAP
    dest_tile = position % SEND_CAP % TILES_DEV
    col_band = jnp.arange(devices_total) % COL_BANDS
    subkeys = jax.random.split(jax.random.fold_in(key, 23), 8)
    grid_shape = (devices_total, OWN_SLOTS)
    scale_low, scale_high, logit_low, logit_high = (1.5, 5.0, -7.0, -2.0)
    offset_x = jax.random.uniform(subkeys[0], grid_shape, jnp.float32, -4.0, TILE_SIDE + 4.0)
    offset_y = jax.random.uniform(subkeys[1], grid_shape, jnp.float32, -4.0, TILE_SIDE + 4.0)
    place_x = (TILE_SIDE * (TILES_DEV * col_band[:, None] + dest_tile[None, :])).astype(jnp.float32) + offset_x
    place_y = (TILE_SIDE * dest_band[None, :] + 0 * col_band[:, None]).astype(jnp.float32) + offset_y
    scale_first = jnp.exp(jax.random.uniform(subkeys[2], grid_shape, jnp.float32, math.log(scale_low), math.log(scale_high)))
    scale_second = jnp.exp(jax.random.uniform(subkeys[3], grid_shape, jnp.float32, math.log(scale_low), math.log(scale_high)))
    angles = jax.random.uniform(subkeys[4], grid_shape, jnp.float32, -math.pi, math.pi)
    inverse_first = 1.0 / (scale_first * scale_first)
    inverse_second = 1.0 / (scale_second * scale_second)
    cosine = jnp.cos(angles)
    sine = jnp.sin(angles)
    conic_a = cosine * cosine * inverse_first + sine * sine * inverse_second
    conic_c = sine * sine * inverse_first + cosine * cosine * inverse_second
    conic_b = cosine * sine * (inverse_first - inverse_second)
    logits = jax.random.uniform(subkeys[5], grid_shape, jnp.float32, logit_low, logit_high)
    along_z = jax.random.uniform(subkeys[6], grid_shape, jnp.float32, 0.6, 1.0)
    azimuth = jax.random.uniform(subkeys[7], grid_shape, jnp.float32, -math.pi, math.pi)
    radial = jnp.sqrt(1.0 - along_z * along_z)
    values = jnp.stack([place_x, place_y, conic_a, conic_b, conic_c, logits, radial * jnp.cos(azimuth), radial * jnp.sin(azimuth), along_z])
    placed = jnp.zeros((9, devices_total, OWN_SLOTS), jnp.float32).at[:, jnp.arange(devices_total)[:, None], orders].set(values)
    return placed.reshape(9, devices_total * OWN_SLOTS)


def tile_layout(key):
    devices_total = ROW_BANDS * COL_BANDS
    subkeys = jax.random.split(jax.random.fold_in(key, 37), 4)
    base_live = jax.random.randint(subkeys[0], (devices_total,), TILES_DEV, 3 * TILES_DEV + 1)
    heavy = jax.random.randint(subkeys[1], (devices_total,), 0, 8) == 0
    forced = jax.random.randint(subkeys[2], (), 0, devices_total)
    live = jnp.where(heavy | (jnp.arange(devices_total) == forced), BLOCK_SLOTS, base_live)
    slot_pos = jnp.arange(BLOCK_SLOTS)
    extra = jax.random.randint(subkeys[3], (devices_total, BLOCK_SLOTS), 0, TILES_DEV)
    tiles_drawn = jnp.where(slot_pos[None, :] < TILES_DEV, slot_pos[None, :], extra)
    tiles_drawn = jnp.where(slot_pos[None, :] < live[:, None], tiles_drawn, TILES_DEV)
    return jnp.sort(tiles_drawn, axis=1).astype(jnp.int32)


def draw_block_tiles(key, part):
    return tile_layout(key).reshape(ROW_BANDS, COL_BANDS * BLOCK_SLOTS)


def draw_block_slots(key, part):
    devices_total = ROW_BANDS * COL_BANDS
    tiles_drawn = tile_layout(key)
    subkeys = jax.random.split(jax.random.fold_in(key, 41), 3)
    grid_shape = (devices_total, BLOCK_SLOTS, BLOCK_LEN)
    nearby = jnp.clip(tiles_drawn[:, :, None] + jax.random.randint(subkeys[0], grid_shape, -1, 2), 0, TILES_DEV - 1)
    source = jax.random.randint(subkeys[1], grid_shape, 0, ROW_BANDS)
    column = jax.random.randint(subkeys[2], grid_shape, 0, SEND_CAP // TILES_DEV)
    chosen = source * SEND_CAP + column * TILES_DEV + nearby
    return chosen.reshape(ROW_BANDS, COL_BANDS * BLOCK_SLOTS, BLOCK_LEN).astype(jnp.int32)


def block_levels(stream_key, dims, cuts, least, largest):
    def one(axis_at, parts):
        steps = jax.random.uniform(jax.random.fold_in(jax.random.fold_in(stream_key, 6), axis_at), (parts,), jnp.float32, least / len(cuts), largest / len(cuts))
        return jnp.repeat(jnp.exp(steps), dims[axis_at] // parts).reshape((-1,) + (1,) * (len(dims) - axis_at - 1))

    level = one(*cuts[0])
    for cut in cuts[1:]:
        level = level * one(*cut)
    return level


def scatter_about(own_key, shape, scale, limit, pieces=(), dtype=jnp.bfloat16):
    array = scale * jax.random.normal(own_key, shape, jnp.float32)
    if pieces:
        array = array * block_levels(own_key, shape, pieces, -0.22, 0.18)
    return jnp.clip(array, -limit, limit).astype(dtype)


def setup_inputs(seed: int = 0) -> dict:
    key_list = jax.random.split(jax.random.key(seed), 7)
    splats = draw_splats(jax.random.fold_in(key_list[6], 71), 0)
    sh_coeffs = scatter_about(key_list[1], (SH_COEFFS, GAUSSIANS), 0.35, 2.0, ((1, 32),), jnp.float32)
    send_list = draw_send_list(jax.random.fold_in(key_list[6], 71), 0)
    block_slots = draw_block_slots(jax.random.fold_in(key_list[6], 71), 0)
    block_tiles = draw_block_tiles(jax.random.fold_in(key_list[6], 71), 0)
    target = jnp.clip(1.0 * jax.random.uniform(key_list[5], (3, IMAGE_H, IMAGE_W), jnp.float32) ** block_levels(key_list[5], (3, IMAGE_H, IMAGE_W), ((1, 16), (2, 2)), -0.2, 0.2), 0.0, 1.0)
    return dict(splats=splats, sh_coeffs=sh_coeffs, send_list=send_list, block_slots=block_slots, block_tiles=block_tiles, target=target)


HIGHEST = lax.Precision.HIGHEST
BASE_ZERO = 0.28209479177387814
BASE_ONE = 0.4886025119029199
BASE_TWO = (1.0925484305920792, -1.0925484305920792, 0.31539156525252005, -1.0925484305920792, 0.5462742152960396)
BASE_THREE = (-0.5900435899266435, 2.890611442640554, -0.4570457994644658, 0.3731763325901154, -0.4570457994644658, 1.445305721320277, -0.5900435899266435)
CONST_ONE = 0.0001
CONST_TWO = 0.0009

def harmonics(direction):
    coord_x, coord_y, coord_z = (direction[0], direction[1], direction[2])
    square_x, square_y, square_z = (coord_x * coord_x, coord_y * coord_y, coord_z * coord_z)
    rows_list = [jnp.full_like(coord_x, BASE_ZERO), -BASE_ONE * coord_y, BASE_ONE * coord_z, -BASE_ONE * coord_x, BASE_TWO[0] * coord_x * coord_y, BASE_TWO[1] * coord_y * coord_z, BASE_TWO[2] * (2.0 * square_z - square_x - square_y), BASE_TWO[3] * coord_x * coord_z, BASE_TWO[4] * (square_x - square_y), BASE_THREE[0] * coord_y * (3.0 * square_x - square_y), BASE_THREE[1] * coord_x * coord_y * coord_z, BASE_THREE[2] * coord_y * (4.0 * square_z - square_x - square_y), BASE_THREE[3] * coord_z * (2.0 * square_z - 3.0 * square_x - 3.0 * square_y), BASE_THREE[4] * coord_x * (4.0 * square_z - square_x - square_y), BASE_THREE[5] * coord_z * (square_x - square_y), BASE_THREE[6] * coord_x * (square_x - 3.0 * square_y)]
    return jnp.stack(rows_list)

def shade(direction, coeffs):
    basis = harmonics(direction)
    return 0.5 + lax.optimization_barrier(jnp.sum(coeffs.reshape(3, 16, -1) * basis[None], axis=1))

def composite(records):
    members = records.shape[1]
    pixels = jnp.arange(TILE_SIDE * TILE_SIDE)
    pixel_u = (pixels % TILE_SIDE).astype(jnp.float32)
    pixel_v = (pixels // TILE_SIDE).astype(jnp.float32)
    delta_x = pixel_u[None, :] - records[0][:, None]
    delta_y = pixel_v[None, :] - records[1][:, None]
    exponent = -0.5 * (records[2][:, None] * delta_x * delta_x + records[4][:, None] * delta_y * delta_y) - records[3][:, None] * delta_x * delta_y
    alphas = jax.nn.sigmoid(records[5])[:, None] * jnp.exp(exponent)
    logged = jnp.log1p(-alphas)
    positions = jnp.arange(members)
    earlier_mask = (positions[None, :] < positions[:, None]).astype(jnp.float32)
    before = jnp.dot(earlier_mask, logged, precision=HIGHEST, preferred_element_type=jnp.float32)
    weight = alphas * jnp.exp(before)
    colour = jnp.dot(records[6:9], weight, precision=HIGHEST, preferred_element_type=jnp.float32)
    return jnp.concatenate([colour, lax.optimization_barrier(jnp.sum(logged, axis=0, keepdims=True))], axis=0)

def combine(results, tile_ids):
    positions = jnp.arange(results.shape[0])
    earlier = ((tile_ids[:, None] == tile_ids[None, :]) & (positions[None, :] < positions[:, None])).astype(jnp.float32)
    prefix = jnp.dot(earlier, results[:, 3], precision=HIGHEST, preferred_element_type=jnp.float32)
    member = (jnp.arange(TILES_DEV)[:, None] == tile_ids[None, :]).astype(jnp.float32)
    shaded = jnp.exp(prefix)[:, None, :] * results[:, 0:3]
    return jnp.einsum('kb,bcp->kcp', member, shaded, precision=HIGHEST)

def to_image(tiles_img):
    return tiles_img.reshape(TILES_DEV, 3, TILE_SIDE, TILE_SIDE).transpose(1, 2, 0, 3).reshape(3, TILE_SIDE, TILES_DEV * TILE_SIDE)

def window():
    tap_offsets = jnp.arange(11).astype(jnp.float32) - 5.0
    profile = jnp.exp(-tap_offsets * tap_offsets / 4.5)
    return profile / jnp.sum(profile)

def blur(padded, rows_out, cols_out):
    weights = window()
    across = weights[0] * padded[..., :, 0:cols_out]
    for offset in range(1, 11):
        across = across + weights[offset] * padded[..., :, offset:offset + cols_out]
    result = weights[0] * across[..., 0:rows_out, :]
    for offset in range(1, 11):
        result = result + weights[offset] * across[..., offset:offset + rows_out, :]
    return result

def similarity(mu_x, mu_y, sq_x, sq_y, cross_xy):
    mean_xy = mu_x * mu_y
    numerator = (2.0 * mean_xy + CONST_ONE) * (2.0 * (cross_xy - mean_xy) + CONST_TWO)
    denominator = (mu_x * mu_x + mu_y * mu_y + CONST_ONE) * (sq_x - mu_x * mu_x + sq_y - mu_y * mu_y + CONST_TWO)
    return numerator / denominator

def render(splats, sh_coeffs, send_list, block_slots, block_tiles):
    colour = shade(splats[6:9], sh_coeffs)
    records = jnp.concatenate([splats[0:6], colour], axis=0)
    slot_ids = jnp.arange(OWN_SLOTS).astype(jnp.int32)

    @jax.checkpoint
    def one_device(device):
        row_band = device // COL_BANDS
        col_band = device % COL_BANDS
        owner_ids = slot_ids // SEND_CAP * COL_BANDS + col_band
        chosen = owner_ids * OWN_SLOTS + send_list[owner_ids * OWN_SLOTS + row_band * SEND_CAP + slot_ids % SEND_CAP]
        received = records[:, chosen]
        tile_ids = lax.dynamic_slice_in_dim(block_tiles[row_band], (col_band * BLOCK_SLOTS).astype(jnp.int32), BLOCK_SLOTS, 0)
        slot_rows = lax.dynamic_slice_in_dim(block_slots[row_band], (col_band * BLOCK_SLOTS).astype(jnp.int32), BLOCK_SLOTS, 0)
        gathered = received[:, slot_rows.reshape(-1)].reshape(9, BLOCK_SLOTS, BLOCK_LEN)
        anchor_x = (TILE_SIDE * (TILES_DEV * col_band + jnp.minimum(tile_ids, TILES_DEV - 1))).astype(jnp.float32)
        anchor_y = (TILE_SIDE * row_band).astype(jnp.float32)
        shifted = jnp.concatenate([gathered[0:1] - anchor_x[None, :, None], gathered[1:2] - anchor_y, gathered[2:9]], axis=0)
        per_block = jnp.moveaxis(shifted, 1, 0)
        results = jax.vmap(composite)(per_block)
        return to_image(combine(results, tile_ids))
    pictures = lax.map(one_device, jnp.arange(ROW_BANDS * COL_BANDS).astype(jnp.int32))
    pictures = pictures.reshape(ROW_BANDS, COL_BANDS, 3, TILE_SIDE, TILES_DEV * TILE_SIDE)
    return pictures.transpose(2, 0, 3, 1, 4).reshape(3, IMAGE_H, IMAGE_W)

def loss_of(rendered, target):
    stacked = jnp.stack([rendered, target, rendered * rendered, target * target, rendered * target])
    padded = jnp.pad(stacked, ((0, 0), (0, 0), (5, 5), (5, 5)))
    moments = blur(padded, IMAGE_H, IMAGE_W)
    ssim = similarity(moments[0], moments[1], moments[2], moments[3], moments[4])
    residue = rendered - target
    return jnp.sum(0.8 * residue * residue) + jnp.sum(0.2 * (1.0 - ssim))

def reference(splats, sh_coeffs, send_list, block_slots, block_tiles, target):

    def objective(splat_rows, coeff_rows):
        rendered = render(splat_rows, coeff_rows, send_list, block_slots, block_tiles)
        return (loss_of(rendered, target), rendered)
    loss_value, pullback, rendered = jax.vjp(objective, splats, sh_coeffs, has_aux=True)
    grad_splats, grad_sh = pullback(jnp.ones_like(loss_value))
    return (rendered, grad_splats, grad_sh)
```

```python
import functools
import math

import jax
import jax.numpy as jnp
from jax import lax
from jax.experimental import pallas as pl
from jax.experimental.pallas import tpu as pltpu
from jax.sharding import PartitionSpec as P

TILE_SIDE = 16
TILES_DEV = 8


HIGHEST = lax.Precision.HIGHEST
BASE_ZERO = 0.28209479177387814
BASE_ONE = 0.4886025119029199
BASE_TWO = (
    1.0925484305920792,
    -1.0925484305920792,
    0.31539156525252005,
    -1.0925484305920792,
    0.5462742152960396,
)
BASE_THREE = (
    -0.5900435899266435,
    2.890611442640554,
    -0.4570457994644658,
    0.3731763325901154,
    -0.4570457994644658,
    1.445305721320277,
    -0.5900435899266435,
)
CONST_ONE = 0.0001
CONST_TWO = 0.0009


def harmonics(direction):
    coord_x, coord_y, coord_z = (direction[0], direction[1], direction[2])
    square_x, square_y, square_z = (coord_x * coord_x, coord_y * coord_y, coord_z * coord_z)
    rows_list = [
        jnp.full_like(coord_x, BASE_ZERO),
        -BASE_ONE * coord_y,
        BASE_ONE * coord_z,
        -BASE_ONE * coord_x,
        BASE_TWO[0] * coord_x * coord_y,
        BASE_TWO[1] * coord_y * coord_z,
        BASE_TWO[2] * (2.0 * square_z - square_x - square_y),
        BASE_TWO[3] * coord_x * coord_z,
        BASE_TWO[4] * (square_x - square_y),
        BASE_THREE[0] * coord_y * (3.0 * square_x - square_y),
        BASE_THREE[1] * coord_x * coord_y * coord_z,
        BASE_THREE[2] * coord_y * (4.0 * square_z - square_x - square_y),
        BASE_THREE[3] * coord_z * (2.0 * square_z - 3.0 * square_x - 3.0 * square_y),
        BASE_THREE[4] * coord_x * (4.0 * square_z - square_x - square_y),
        BASE_THREE[5] * coord_z * (square_x - square_y),
        BASE_THREE[6] * coord_x * (square_x - 3.0 * square_y),
    ]
    return jnp.stack(rows_list)


def shade(direction, coeffs):
    basis = harmonics(direction)
    return 0.5 + jnp.sum(coeffs.reshape(3, 16, -1) * basis[None], axis=1)


SEGMENTS = 8
STEPS = 16
BLOCK = SEGMENTS * STEPS
HALF = 128
CENTRE = 7.5


LOG2E = 1.4426950408889634
FIELDS = 9
COEF_ROWS = 48
GRAD_ROWS = 24
ACROSS = (((1,), (1,)), ((), ()))
DOWN = (((0,), (0,)), ((), ()))


def pick(table, index):
    return jnp.take_along_axis(table, index, axis=1, mode="promise_in_bounds")


def coarse(value):
    return value.astype(jnp.bfloat16).astype(jnp.float32)


def halves(value):
    high = value.astype(jnp.bfloat16)
    low = (value - high.astype(jnp.float32)).astype(jnp.bfloat16)
    return high, low


def pixel_basis():
    rows = lax.broadcasted_iota(jnp.int32, (8, 2 * HALF), 0)
    pixels = lax.broadcasted_iota(jnp.int32, (8, 2 * HALF), 1)
    along = (pixels % TILE_SIDE).astype(jnp.float32) - CENTRE
    down = (pixels // TILE_SIDE).astype(jnp.float32) - CENTRE
    basis = jnp.zeros((8, 2 * HALF), jnp.float32)
    terms = (along * along, along * down, down * down, along, down, jnp.ones_like(along))
    for at, term in enumerate(terms):
        basis = jnp.where(rows == at, term, basis)
    return basis


def spread_order(slots):
    lanes = lax.broadcasted_iota(jnp.int32, slots.shape, 1)
    return pick(slots, (lanes % SEGMENTS) * STEPS + lanes // SEGMENTS)


def tiles_of(tile_ref, first):
    at = lax.broadcasted_iota(jnp.int32, (SEGMENTS, BLOCK), 0)
    tiles = jnp.zeros((SEGMENTS, BLOCK), jnp.int32)
    for k in range(SEGMENTS):
        tiles = jnp.where(at == k, tile_ref[first + k], tiles)
    return tiles


def live_slots(tile_ref):
    live = jnp.int32(0)
    for slot in range(tile_ref.shape[0]):
        live = live + (tile_ref[slot] < TILES_DEV).astype(jnp.int32)
    return live


def forward_kernel(
    tile_ref, recv_ref, slots_ref, picture_ref, rec_ref, coef_ref, saved_ref,
    work_ref, image_ref, basis_ref,
):
    live = live_slots(tile_ref)
    chunks = recv_ref.shape[1] // BLOCK
    origin_x = (lax.axis_index("tile") * (TILE_SIDE * TILES_DEV)).astype(jnp.float32) + CENTRE
    origin_y = (lax.axis_index("gauss") * TILE_SIDE).astype(jnp.float32) + CENTRE
    work_ref[...] = jnp.zeros_like(work_ref)
    basis = pixel_basis()
    basis_ref[...] = jnp.concatenate([basis] * 3 + [jnp.zeros_like(basis)] * 3, axis=0).astype(
        jnp.bfloat16
    )

    def collect(group, carry):
        first = group * SEGMENTS
        slots = spread_order(slots_ref[pl.ds(pl.multiple_of(first, SEGMENTS), SEGMENTS), :])
        fine = slots % BLOCK
        chunk_at = slots // BLOCK
        found = [None] * FIELDS
        for chunk in range(chunks):
            hit = chunk_at == chunk
            for f in range(FIELDS):
                row = recv_ref[f : f + 1, chunk * BLOCK : (chunk + 1) * BLOCK]
                got = pick(jnp.broadcast_to(row, (SEGMENTS, BLOCK)), fine)
                found[f] = got if chunk == 0 else jnp.where(hit, got, found[f])
        tiles = tiles_of(tile_ref, first)
        base_x = (TILE_SIDE * jnp.minimum(tiles, TILES_DEV - 1)).astype(jnp.float32) + origin_x
        at_x = found[0] - base_x
        at_y = found[1] - origin_y
        con_a = -0.5 * found[2]
        con_b = -found[3]
        con_c = -0.5 * found[4]
        shut = 1.0 + jnp.exp(-found[5])
        for k, value in enumerate((at_x, at_y, con_a, con_b, con_c, 1.0 - 1.0 / shut)):
            rec_ref[k, pl.ds(pl.multiple_of(first, SEGMENTS), SEGMENTS), :] = value
        part_x = con_a * at_x
        part_y = con_c * at_y
        cross = con_b * at_y
        level = at_x * (part_x + cross) + at_y * part_y
        terms = (
            LOG2E * con_a,
            LOG2E * con_b,
            LOG2E * con_c,
            -LOG2E * (2.0 * part_x + cross),
            -LOG2E * (2.0 * part_y + con_b * at_x),
            LOG2E * (level - jnp.log(shut)),
        )

        def put(row, value):
            work_ref[pl.ds(first * COEF_ROWS + row, SEGMENTS, stride=COEF_ROWS), :] = value

        for k, term in enumerate(terms):
            high = coarse(term)
            rest = term - high
            middle = coarse(rest)
            put(k, high)
            put(8 + k, middle)
            put(16 + k, rest - middle)
        for c in range(3):
            high = coarse(found[6 + c])
            put(24 + c, high)
            put(32 + c, found[6 + c] - high)
            put(40 + c, high)
        return carry

    lax.fori_loop(0, (live + SEGMENTS - 1) // SEGMENTS, collect, 0)
    seg_at = lax.broadcasted_iota(jnp.int32, (SEGMENTS, HALF), 0)
    own_seg = seg_at == lax.broadcasted_iota(jnp.int32, (SEGMENTS, HALF), 1) % SEGMENTS

    def draw_local(slot):
        coefs = work_ref[pl.ds(pl.multiple_of(slot * COEF_ROWS, COEF_ROWS), COEF_ROWS), :].astype(
            jnp.bfloat16
        )
        coef_ref[slot] = coefs
        power = lax.dot_general(coefs, basis_ref[...], DOWN, preferred_element_type=jnp.float32)
        through = [jnp.ones((SEGMENTS, HALF), jnp.float32) for side in range(2)]
        weights = [[], []]
        for step in range(STEPS):
            for side in range(2):
                alpha = jnp.exp2(
                    power[step * SEGMENTS : (step + 1) * SEGMENTS, side * HALF : (side + 1) * HALF]
                )
                weight = alpha * through[side]
                through[side] = through[side] - weight
                weights[side].append(weight)
        weight = jnp.concatenate([jnp.concatenate(w, axis=0) for w in weights], axis=1)
        tints = []
        for part in (24, 32):
            for c in range(3):
                row = work_ref[pl.ds(slot * COEF_ROWS + part + c, 1), :]
                tints.append(jnp.where(own_seg, jnp.broadcast_to(row, (SEGMENTS, HALF)), 0.0))
        tint = jnp.concatenate(tints, axis=0).astype(jnp.bfloat16)
        sums = jnp.dot(
            jnp.concatenate([tint, tint], axis=1),
            jnp.concatenate(halves(weight), axis=0),
            preferred_element_type=jnp.float32,
        )
        return through, sums[0:24] + sums[24:48]

    def draw_join(slot, carry, through, sums):
        tile = tile_ref[slot]
        fresh = (slot == 0) | (tile != tile_ref[jnp.maximum(slot - 1, 0)])
        after = []
        for side in range(2):
            start = jnp.where(fresh, 1.0, carry[side])
            running = through[side]
            for shift in (1, 2, 4):
                running = jnp.where(
                    seg_at >= shift, running * pltpu.roll(running, shift, 0), running
                )
            before = jnp.where(seg_at == 0, 1.0, pltpu.roll(running, 1, 0)) * start
            after.append(start * running[SEGMENTS - 1 : SEGMENTS])
            lanes = slice(side * HALF, (side + 1) * HALF)
            saved_ref[slot, 0, :, lanes] = before
            saved_ref[slot, 1, :, lanes] = through[side]
            for c in range(3):
                part = sums[c * SEGMENTS : (c + 1) * SEGMENTS, lanes]
                saved_ref[slot, 2 + c, :, lanes] = part
                shade_sum = jnp.sum(before * part, axis=0, keepdims=True)
                held = jnp.where(fresh, 0.0, image_ref[tile, c : c + 1, lanes])
                image_ref[tile, c : c + 1, lanes] = held + shade_sum
        return tuple(after)

    def draw(pair, carry):
        locals_two = [draw_local(2 * pair + k) for k in range(2)]
        for k in range(2):
            carry = draw_join(2 * pair + k, carry, *locals_two[k])
        return carry

    ones = jnp.ones((1, HALF), jnp.float32)
    lax.fori_loop(0, (live + 1) // 2, draw, (ones, ones))
    lane_tile = lax.broadcasted_iota(jnp.int32, (SEGMENTS, HALF), 1) // TILE_SIDE
    for side in range(2):
        lanes = slice(side * HALF, (side + 1) * HALF)
        for c in range(3):
            shown = jnp.zeros((SEGMENTS, HALF), jnp.float32)
            for tile in range(TILES_DEV):
                row = jnp.broadcast_to(image_ref[tile, c : c + 1, lanes], (SEGMENTS, HALF))
                moved = pltpu.roll(row, TILE_SIDE * tile, 1) if tile else row
                for bit in (1, 2, 4):
                    moved = jnp.where(
                        (seg_at & bit) > 0, pltpu.roll(moved, HALF - TILE_SIDE * bit, 1), moved
                    )
                shown = jnp.where(lane_tile == tile, moved, shown)
            picture_ref[c, side * SEGMENTS : (side + 1) * SEGMENTS, :] = shown


def backward_kernel(
    tile_ref, rec_ref, coef_ref, saved_ref, grad_ref, slots_ref, out_ref,
    rhs_ref, mom_ref, back_ref, where_ref, acc_ref,
):
    live = live_slots(tile_ref)
    chunks = out_ref.shape[1]
    slots_total = coef_ref.shape[0]
    acc_ref[...] = jnp.zeros_like(acc_ref)
    basis = pixel_basis()
    blank = jnp.zeros_like(basis)
    basis16 = jnp.concatenate([basis, blank], axis=0).astype(jnp.bfloat16)
    for tile in range(TILES_DEV):
        grads = grad_ref[tile]
        high = coarse(grads)
        rhs_ref[tile, :, 0 : 2 * HALF] = jnp.concatenate([basis] * 3 + [blank] * 3, axis=0).astype(
            jnp.bfloat16
        )
        rhs_ref[tile, :, 2 * HALF : 4 * HALF] = jnp.concatenate(
            [blank] * 3 + [high, high, grads - high], axis=0
        ).astype(jnp.bfloat16)
    seg_at = lax.broadcasted_iota(jnp.int32, (SEGMENTS, HALF), 0)

    def pull_scan(slot, carry):
        tile = tile_ref[slot]
        final = (slot >= live - 1) | (tile != tile_ref[jnp.minimum(slot + 1, slots_total - 1)])
        grads = grad_ref[jnp.minimum(tile, TILES_DEV - 1)]
        after = []
        behind = []
        for side in range(2):
            lanes = slice(side * HALF, (side + 1) * HALF)
            start = jnp.where(final, 0.0, carry[side])
            total = grads[0:1, lanes] * saved_ref[slot, 2, :, lanes]
            for c in (1, 2):
                total = total + grads[c : c + 1, lanes] * saved_ref[slot, 2 + c, :, lanes]
            factor = saved_ref[slot, 1, :, lanes]
            for shift in (1, 2, 4):
                inside = seg_at < SEGMENTS - shift
                total = jnp.where(
                    inside, total + factor * pltpu.roll(total, SEGMENTS - shift, 0), total
                )
                factor = jnp.where(
                    inside, factor * pltpu.roll(factor, SEGMENTS - shift, 0), factor
                )
            entering = total + factor * start
            after.append(entering[0:1])
            behind.append(
                jnp.where(seg_at < SEGMENTS - 1, pltpu.roll(entering, SEGMENTS - 1, 0), start)
            )
        return tuple(after), behind

    def pull_one(slot, behind):
        tile = jnp.minimum(tile_ref[slot], TILES_DEV - 1)
        both = lax.dot_general(
            coef_ref[slot], rhs_ref[tile], DOWN, preferred_element_type=jnp.float32
        )
        weights = []
        forces = []
        for side in range(2):
            lanes = slice(side * HALF, (side + 1) * HALF)
            through = saved_ref[slot, 0, :, lanes]
            alphas = []
            shares = []
            for step in range(STEPS):
                alpha = jnp.exp2(both[step * SEGMENTS : (step + 1) * SEGMENTS, lanes])
                weight = alpha * through
                through = through - weight
                alphas.append(alpha)
                shares.append(weight)
            pulls = [None] * STEPS
            later = behind[side]
            for step in reversed(range(STEPS)):
                lit = both[
                    step * SEGMENTS : (step + 1) * SEGMENTS,
                    (2 + side) * HALF : (3 + side) * HALF,
                ]
                gap = lit - later
                later = later + alphas[step] * gap
                pulls[step] = shares[step] * gap
            weights.append(jnp.concatenate(shares, axis=0))
            forces.append(jnp.concatenate(pulls, axis=0))
        found = lax.dot_general(
            basis16,
            jnp.concatenate(halves(jnp.concatenate(forces, axis=1)), axis=0),
            ACROSS,
            preferred_element_type=jnp.float32,
        )
        painted = lax.dot_general(
            jnp.concatenate(halves(grad_ref[tile]), axis=0),
            jnp.concatenate(halves(jnp.concatenate(weights, axis=1)), axis=0),
            ACROSS,
            preferred_element_type=jnp.float32,
        )
        painted = painted[0:8] + painted[8:16]
        mom_ref[slot, 0:8, :] = found[0:8, :BLOCK] + found[0:8, BLOCK:]
        mom_ref[slot, 8:16, :] = painted[:, :BLOCK] + painted[:, BLOCK:]

    def pull(turn, carry):
        pair = (live + 1) // 2 - 1 - turn
        behinds = []
        for k in (1, 0):
            carry, behind = pull_scan(2 * pair + k, carry)
            behinds.append(behind)
        for k in (1, 0):
            pull_one(2 * pair + k, behinds[1 - k])
        return carry

    zeros = jnp.zeros((1, HALF), jnp.float32)
    lax.fori_loop(0, (live + 1) // 2, pull, (zeros, zeros))
    lane_rows = lax.broadcasted_iota(jnp.int32, (BLOCK, 4 * BLOCK), 0)
    chunk_rows = lax.broadcasted_iota(jnp.int32, (chunks, BLOCK), 0)

    def settle(group, carry):
        first = pl.multiple_of(group * SEGMENTS, SEGMENTS)
        tiles = tiles_of(tile_ref, first)
        used = tiles < TILES_DEV
        rows = pl.ds(first, SEGMENTS)

        m_xx, m_xy, m_yy, m_x, m_y, m_0 = [
            mom_ref[rows, k, :] for k in range(6)
        ]
        at_x, at_y, con_a, con_b, con_c, shut_s = [rec_ref[k, rows, :] for k in range(6)]
        h_x = m_x - at_x * m_0
        h_y = m_y - at_y * m_0
        h_xx = m_xx - 2.0 * at_x * m_x + at_x * at_x * m_0
        h_xy = m_xy - at_x * m_y - at_y * m_x + at_x * at_y * m_0
        h_yy = m_yy - 2.0 * at_y * m_y + at_y * at_y * m_0
        results = [
            -2.0 * con_a * h_x - con_b * h_y,
            -2.0 * con_c * h_y - con_b * h_x,
            -0.5 * h_xx,
            -h_xy,
            -0.5 * h_yy,
            shut_s * m_0,
        ] + [mom_ref[rows, 8 + c, :] for c in range(3)]
        for f, value in enumerate(results):
            kept = jnp.where(used, value, 0.0)
            high = coarse(kept)
            back_ref[rows, f, :] = high
            back_ref[rows, 12 + f, :] = kept - high
        slots = spread_order(slots_ref[rows, :])
        where_ref[0, rows, :] = slots % BLOCK
        where_ref[1, rows, :] = slots // BLOCK
        for quad in range(0, SEGMENTS, 4):
            stacked = []
            for k in range(quad, quad + 4):
                hit = chunk_rows == where_ref[1, pl.ds(first + k, 1), :]
                stacked.append(
                    jnp.concatenate(
                        [
                            jnp.where(hit, back_ref[first + k, part + f : part + f + 1, :], 0.0)
                            for part in (0, 12)
                            for f in range(FIELDS)
                        ],
                        axis=0,
                    ).astype(jnp.bfloat16)
                )
            fine = jnp.concatenate(
                [where_ref[0, pl.ds(first + k, 1), :] for k in range(quad, quad + 4)], axis=1
            )
            select = jnp.where(lane_rows == fine, 1.0, 0.0).astype(jnp.bfloat16)
            acc_ref[...] += lax.dot_general(
                jnp.concatenate(stacked, axis=1), select, ACROSS, preferred_element_type=jnp.float32
            )
        return carry

    lax.fori_loop(0, (live + SEGMENTS - 1) // SEGMENTS, settle, 0)
    total = FIELDS * chunks
    for f in range(FIELDS):
        out_ref[f] = (
            acc_ref[f * chunks : (f + 1) * chunks, :]
            + acc_ref[total + f * chunks : total + (f + 1) * chunks, :]
        )


def smem():
    return pl.BlockSpec(memory_space=pltpu.SMEM)


def vmem():
    return pl.BlockSpec(memory_space=pltpu.VMEM)


def draw_tiles(tile_ids, received, slots):
    slots_total = slots.shape[0]
    side = TILE_SIDE * TILE_SIDE
    return pl.pallas_call(
        forward_kernel,
        out_shape=(
            jax.ShapeDtypeStruct((3, TILE_SIDE, TILES_DEV * TILE_SIDE), jnp.float32),
            jax.ShapeDtypeStruct((6, slots_total, BLOCK), jnp.float32),
            jax.ShapeDtypeStruct((slots_total, COEF_ROWS, BLOCK), jnp.bfloat16),
            jax.ShapeDtypeStruct((slots_total, 5, SEGMENTS, side), jnp.float32),
        ),
        in_specs=[smem(), vmem(), vmem()],
        out_specs=(vmem(), vmem(), vmem(), vmem()),
        scratch_shapes=[
            pltpu.VMEM((slots_total * COEF_ROWS, BLOCK), jnp.float32),
            pltpu.VMEM((TILES_DEV + 1, 8, side), jnp.float32),
            pltpu.VMEM((COEF_ROWS, side), jnp.bfloat16),
        ],
        compiler_params=pltpu.CompilerParams(vmem_limit_bytes=48 * 1024 * 1024),
        name="draw_tiles",
    )(tile_ids, received, slots)


def pull_tiles(tile_ids, recs, coefs, saved, grads, slots, own):
    slots_total = coefs.shape[0]
    side = TILE_SIDE * TILE_SIDE
    chunks = own // BLOCK
    return pl.pallas_call(
        backward_kernel,
        out_shape=jax.ShapeDtypeStruct((FIELDS, chunks, BLOCK), jnp.float32),
        in_specs=[smem(), vmem(), vmem(), vmem(), vmem(), vmem()],
        out_specs=vmem(),
        scratch_shapes=[
            pltpu.VMEM((TILES_DEV, COEF_ROWS, 2 * side), jnp.bfloat16),
            pltpu.VMEM((slots_total, 16, BLOCK), jnp.float32),
            pltpu.VMEM((slots_total, GRAD_ROWS, BLOCK), jnp.float32),
            pltpu.VMEM((2, slots_total, BLOCK), jnp.int32),
            pltpu.VMEM((2 * FIELDS * chunks, BLOCK), jnp.float32),
        ],
        compiler_params=pltpu.CompilerParams(vmem_limit_bytes=48 * 1024 * 1024),
        name="pull_tiles",
    )(tile_ids, recs, coefs, saved, grads, slots)


WAYS = [(down, right) for down in (-1, 0, 1) for right in (-1, 0, 1) if (down, right) != (0, 0)]
NORM = sum(math.exp(-m * m / 4.5) for m in range(-5, 6))


def halo_kernel(bands, cols_total, shown_ref, target_ref, out_ref, send_sem, recv_sem):
    band = lax.axis_index("gauss")
    column = lax.axis_index("tile")
    rows, cols = shown_ref.shape[1:]
    out_ref[...] = jnp.zeros_like(out_ref)
    barrier = pltpu.get_barrier_semaphore()

    def exists(way):
        there_band = band + way[0]
        there_col = column + way[1]
        return (
            (there_band >= 0) & (there_band < bands) & (there_col >= 0) & (there_col < cols_total)
        )

    def copies(at):
        down, right = WAYS[at]
        landing = len(WAYS) - 1 - at
        return [
            pltpu.make_async_remote_copy(
                src_ref=source,
                dst_ref=out_ref.at[
                    pl.ds(3 * kind, 3), pl.ds(rows * (1 - down), rows), pl.ds(cols * (1 - right), cols)
                ],
                send_sem=send_sem.at[kind, at],
                recv_sem=recv_sem.at[kind, landing],
                device_id=(band + down, column + right),
                device_id_type=pl.DeviceIdType.MESH,
            )
            for kind, source in enumerate((shown_ref, target_ref))
        ]

    for at, way in enumerate(WAYS):

        @pl.when(exists(way))
        def _(way=way):
            pl.semaphore_signal(
                barrier,
                inc=1,
                device_id=(band + way[0], column + way[1]),
                device_id_type=pl.DeviceIdType.MESH,
            )

    peers = sum(exists(way).astype(jnp.int32) for way in WAYS)
    pl.semaphore_wait(barrier, peers)

    for at, way in enumerate(WAYS):

        @pl.when(exists(way))
        def _(at=at):
            for copy in copies(at):
                copy.start()

    out_ref[0:3, rows : 2 * rows, cols : 2 * cols] = shown_ref[...]
    out_ref[3:6, rows : 2 * rows, cols : 2 * cols] = target_ref[...]
    for at, way in enumerate(WAYS):

        @pl.when(exists(way))
        def _(at=at):
            for copy in copies(at):
                copy.wait_send()
            for kind, source in enumerate((shown_ref, target_ref)):
                pltpu.make_async_remote_copy(
                    src_ref=source,
                    dst_ref=out_ref.at[
                        pl.ds(3 * kind, 3),
                        pl.ds(rows * (1 + WAYS[at][0]), rows),
                        pl.ds(cols * (1 + WAYS[at][1]), cols),
                    ],
                    send_sem=send_sem.at[kind, at],
                    recv_sem=recv_sem.at[kind, at],
                    device_id=(band + WAYS[at][0], column + WAYS[at][1]),
                    device_id_type=pl.DeviceIdType.MESH,
                ).wait_recv()


def exchange(rendered, target):
    channels, rows, cols = rendered.shape
    return pl.pallas_call(
        functools.partial(halo_kernel, lax.axis_size("gauss"), lax.axis_size("tile")),
        out_shape=jax.ShapeDtypeStruct((2 * channels, 3 * rows, 3 * cols), jnp.float32),
        in_specs=[vmem(), vmem()],
        out_specs=vmem(),
        scratch_shapes=[
            pltpu.SemaphoreType.DMA((2, len(WAYS))),
            pltpu.SemaphoreType.DMA((2, len(WAYS))),
        ],
        compiler_params=pltpu.CompilerParams(collective_id=0, has_side_effects=True),
        name="halo",
    )(rendered, target)


def banded(shape, offset):
    gap = (
        lax.broadcasted_iota(jnp.int32, shape, 0) - lax.broadcasted_iota(jnp.int32, shape, 1) + offset
    ).astype(jnp.float32)
    return jnp.where(jnp.abs(gap) < 5.5, jnp.exp(gap * gap / -4.5) * (1.0 / NORM), 0.0)


def exact_dot(left, right):
    return jnp.dot(left, right, precision=HIGHEST, preferred_element_type=jnp.float32)


def ssim_kernel(place_ref, wide_ref, out_ref, stack_ref):
    tall, wide = wide_ref.shape[1:]
    rows, cols = tall // 3, wide // 3
    row_from, rows_mid = rows // 2, 2 * rows
    col_from, cols_mid = cols // 2, 2 * cols
    for c in range(3):
        pic = wide_ref[c]
        aim = wide_ref[3 + c]
        for kind, plane in enumerate((pic, aim, pic * pic + aim * aim, pic * aim)):
            at = 3 * kind + c
            stack_ref[at * tall : (at + 1) * tall, :] = plane
    across = exact_dot(stack_ref[...], banded((wide, cols_mid), -col_from))
    moments = exact_dot(
        banded((rows_mid, tall), row_from),
        jnp.concatenate([across[at * tall : (at + 1) * tall] for at in range(12)], axis=1),
    )
    row_at = place_ref[0] + row_from - rows + lax.broadcasted_iota(jnp.int32, (rows_mid, cols_mid), 0)
    col_at = place_ref[1] + col_from - cols + lax.broadcasted_iota(jnp.int32, (rows_mid, cols_mid), 1)
    inside = (row_at >= 0) & (row_at < place_ref[2]) & (col_at >= 0) & (col_at < place_ref[3])
    slopes = [None] * 9
    for c in range(3):
        mu_x, mu_y, squares, cross = [
            moments[:, (3 * kind + c) * cols_mid : (3 * kind + c + 1) * cols_mid] for kind in range(4)
        ]
        mean_xy = mu_x * mu_y
        mean_sq = mu_x * mu_x + mu_y * mu_y
        top_1 = 2.0 * mean_xy + CONST_ONE
        top_2 = 2.0 * (cross - mean_xy) + CONST_TWO
        low_1 = mean_sq + CONST_ONE
        low_2 = squares - mean_sq + CONST_TWO
        inverse = -0.2 / (low_1 * low_2)
        value = top_1 * top_2 * inverse
        value_1 = value * low_2 * inverse * -5.0
        value_2 = value * low_1 * inverse * -5.0
        slope_mean = 2.0 * mu_y * (top_2 - top_1) * inverse - 2.0 * mu_x * (value_1 - value_2)
        for kind, slope in enumerate((slope_mean, -value_2, 2.0 * top_1 * inverse)):
            slopes[3 * kind + c] = jnp.where(inside, slope, 0.0)
    down = exact_dot(
        banded((rows, rows_mid), rows - row_from), jnp.concatenate(slopes, axis=1)
    )
    spread = exact_dot(
        jnp.concatenate([down[:, at * cols_mid : (at + 1) * cols_mid] for at in range(9)], axis=0),
        banded((cols_mid, cols), col_from - cols),
    )
    lane_row = lax.broadcasted_iota(jnp.int32, (SEGMENTS, HALF), 1) // TILE_SIDE
    seg_at = lax.broadcasted_iota(jnp.int32, (SEGMENTS, HALF), 0)
    out_ref[...] = jnp.zeros_like(out_ref)
    for c in range(3):
        pic = wide_ref[c, rows : 2 * rows, cols : 2 * cols]
        aim = wide_ref[3 + c, rows : 2 * rows, cols : 2 * cols]
        parts = [spread[(3 * kind + c) * rows : (3 * kind + c + 1) * rows] for kind in range(3)]
        total = parts[0] + 2.0 * pic * parts[1] + aim * parts[2] + 1.6 * (pic - aim)
        for side in range(2):
            part = total[side * SEGMENTS : (side + 1) * SEGMENTS]
            skewed = pltpu.roll(part, 0, 1, stride=TILE_SIDE, stride_axis=0)
            for tile in range(TILES_DEV):
                moved = pltpu.roll(skewed, HALF - TILE_SIDE * tile, 1) if tile else skewed
                kept = jnp.where(lane_row == seg_at, moved, 0.0)
                out_ref[tile, c : c + 1, side * HALF : (side + 1) * HALF] = jnp.sum(
                    kept, axis=0, keepdims=True
                )


def ssim_pull(place, wide):
    return pl.pallas_call(
        ssim_kernel,
        out_shape=jax.ShapeDtypeStruct((TILES_DEV, 8, TILE_SIDE * TILE_SIDE), jnp.float32),
        in_specs=[smem(), vmem()],
        out_specs=vmem(),
        scratch_shapes=[pltpu.VMEM((12 * wide.shape[1], wide.shape[2]), jnp.float32)],
        name="ssim_pull",
    )(place, wide)


def body(splats, sh_coeffs, send_list, block_slots, block_tiles, target):
    row_band = lax.axis_index("gauss")
    col_band = lax.axis_index("tile")
    owners = lax.axis_size("gauss")
    peers = lax.axis_size("tile")
    own_records = jnp.concatenate([splats[0:6], shade(splats[6:9], sh_coeffs)], axis=0)
    received = lax.all_to_all(
        own_records[:, send_list], "gauss", split_axis=1, concat_axis=1, tiled=True
    )
    tile_ids = block_tiles[0]
    slot_rows = block_slots[0]
    slots_total = slot_rows.shape[0]
    rendered, recs, coefs, saved = draw_tiles(tile_ids, received, slot_rows)
    rows_here, cols_here = rendered.shape[1:]
    place = jnp.stack(
        [row_band * rows_here, col_band * cols_here, rows_here * owners, cols_here * peers]
    ).astype(jnp.int32)
    tile_grad = ssim_pull(place, exchange(rendered, target))
    table_grad = pull_tiles(
        tile_ids, recs, coefs, saved, tile_grad, slot_rows, received.shape[1]
    ).reshape(received.shape)
    back_records = lax.all_to_all(table_grad, "gauss", split_axis=1, concat_axis=1, tiled=True)
    own_grad = jnp.zeros_like(own_records).at[:, send_list].set(back_records)
    unused_colour, shade_pull = jax.vjp(shade, splats[6:9], sh_coeffs)
    dir_grad, grad_sh = shade_pull(own_grad[6:9])
    grad_splats = jnp.concatenate([own_grad[0:6], dir_grad], axis=0)
    return (rendered, grad_splats, grad_sh)


def solution(mesh):
    in_specs = (
        P(None, ("gauss", "tile")),
        P(None, ("gauss", "tile")),
        P(("gauss", "tile")),
        P("gauss", "tile", None),
        P("gauss", "tile"),
        P(None, "gauss", "tile"),
    )
    out_specs = (P(None, "gauss", "tile"), P(None, ("gauss", "tile")), P(None, ("gauss", "tile")))
    return jax.shard_map(body, mesh=mesh, in_specs=in_specs, out_specs=out_specs, check_vma=False)
```

```python
import functools
import math

import jax
import jax.numpy as jnp
from jax import lax
from jax.experimental import pallas as pl
from jax.experimental.pallas import tpu as pltpu
from jax.sharding import PartitionSpec as P

TILE_SIDE = 16
TILES_DEV = 8


HIGHEST = lax.Precision.HIGHEST
BASE_ZERO = 0.28209479177387814
BASE_ONE = 0.4886025119029199
BASE_TWO = (
    1.0925484305920792,
    -1.0925484305920792,
    0.31539156525252005,
    -1.0925484305920792,
    0.5462742152960396,
)
BASE_THREE = (
    -0.5900435899266435,
    2.890611442640554,
    -0.4570457994644658,
    0.3731763325901154,
    -0.4570457994644658,
    1.445305721320277,
    -0.5900435899266435,
)
CONST_ONE = 0.0001
CONST_TWO = 0.0009


SEGMENTS = 8
STEPS = 16
BLOCK = SEGMENTS * STEPS
HALF = 128
CENTRE = 7.5


LOG2E = 1.4426950408889634
FIELDS = 9
COEF_ROWS = 48
GROUP = 8
GRAD_ROWS = 24
ACROSS = (((1,), (1,)), ((), ()))
DOWN = (((0,), (0,)), ((), ()))


def pick(table, index):
    return jnp.take_along_axis(table, index, axis=1, mode="promise_in_bounds")


def coarse(value):
    return value.astype(jnp.bfloat16).astype(jnp.float32)


def halves(value):
    high = value.astype(jnp.bfloat16)
    low = (value - high.astype(jnp.float32)).astype(jnp.bfloat16)
    return high, low


def pixel_basis():
    rows = lax.broadcasted_iota(jnp.int32, (8, 2 * HALF), 0)
    pixels = lax.broadcasted_iota(jnp.int32, (8, 2 * HALF), 1)
    along = (pixels % TILE_SIDE).astype(jnp.float32) - CENTRE
    down = (pixels // TILE_SIDE).astype(jnp.float32) - CENTRE
    basis = jnp.zeros((8, 2 * HALF), jnp.float32)
    terms = (along * along, along * down, down * down, along, down, jnp.ones_like(along))
    for at, term in enumerate(terms):
        basis = jnp.where(rows == at, term, basis)
    return basis


def spread_order(slots):
    lanes = lax.broadcasted_iota(jnp.int32, slots.shape, 1)
    return pick(slots, (lanes % SEGMENTS) * STEPS + lanes // SEGMENTS)


def tiles_of(tile_ref, first):
    at = lax.broadcasted_iota(jnp.int32, (SEGMENTS, BLOCK), 0)
    tiles = jnp.zeros((SEGMENTS, BLOCK), jnp.int32)
    for k in range(SEGMENTS):
        tiles = jnp.where(at == k, tile_ref[first + k], tiles)
    return tiles


def live_slots(tile_ref):
    live = jnp.int32(0)
    for slot in range(tile_ref.shape[0]):
        live = live + (tile_ref[slot] < TILES_DEV).astype(jnp.int32)
    return live


def forward_kernel(
    tile_ref, recv_ref, slots_ref, picture_ref, rec_ref, coef_ref, saved_ref,
    work_ref, image_ref, basis_ref,
):
    live = live_slots(tile_ref)
    chunks = recv_ref.shape[1] // BLOCK
    origin_x = (lax.axis_index("tile") * (TILE_SIDE * TILES_DEV)).astype(jnp.float32) + CENTRE
    origin_y = (lax.axis_index("gauss") * TILE_SIDE).astype(jnp.float32) + CENTRE
    work_ref[...] = jnp.zeros_like(work_ref)
    basis = pixel_basis()
    basis_ref[...] = jnp.concatenate([basis] * 3 + [jnp.zeros_like(basis)] * 3, axis=0).astype(
        jnp.bfloat16
    )

    def collect(group, carry):
        first = group * SEGMENTS
        slots = spread_order(slots_ref[pl.ds(pl.multiple_of(first, SEGMENTS), SEGMENTS), :])
        fine = slots % BLOCK
        chunk_at = slots // BLOCK
        found = [None] * FIELDS
        for chunk in range(chunks):
            hit = chunk_at == chunk
            for f in range(FIELDS):
                row = recv_ref[f : f + 1, chunk * BLOCK : (chunk + 1) * BLOCK]
                got = pick(jnp.broadcast_to(row, (SEGMENTS, BLOCK)), fine)
                found[f] = got if chunk == 0 else jnp.where(hit, got, found[f])
        tiles = tiles_of(tile_ref, first)
        base_x = (TILE_SIDE * jnp.minimum(tiles, TILES_DEV - 1)).astype(jnp.float32) + origin_x
        at_x = found[0] - base_x
        at_y = found[1] - origin_y
        con_a = -0.5 * found[2]
        con_b = -found[3]
        con_c = -0.5 * found[4]
        shut = 1.0 + jnp.exp(-found[5])
        for k, value in enumerate((at_x, at_y, con_a, con_b, con_c, 1.0 - 1.0 / shut)):
            rec_ref[k, pl.ds(pl.multiple_of(first, SEGMENTS), SEGMENTS), :] = value
        part_x = con_a * at_x
        part_y = con_c * at_y
        cross = con_b * at_y
        level = at_x * (part_x + cross) + at_y * part_y
        terms = (
            LOG2E * con_a,
            LOG2E * con_b,
            LOG2E * con_c,
            -LOG2E * (2.0 * part_x + cross),
            -LOG2E * (2.0 * part_y + con_b * at_x),
            LOG2E * (level - jnp.log(shut)),
        )

        def put(row, value):
            work_ref[pl.ds(first * COEF_ROWS + row, SEGMENTS, stride=COEF_ROWS), :] = value

        for k, term in enumerate(terms):
            high = coarse(term)
            rest = term - high
            middle = coarse(rest)
            put(k, high)
            put(8 + k, middle)
            put(16 + k, rest - middle)
        for c in range(3):
            high = coarse(found[6 + c])
            put(24 + c, high)
            put(32 + c, found[6 + c] - high)
            put(40 + c, high)
        return carry

    lax.fori_loop(0, (live + SEGMENTS - 1) // SEGMENTS, collect, 0)
    seg_at = lax.broadcasted_iota(jnp.int32, (SEGMENTS, HALF), 0)
    own_seg = seg_at == lax.broadcasted_iota(jnp.int32, (SEGMENTS, HALF), 1) % SEGMENTS

    def draw_local(slot):
        coefs = work_ref[pl.ds(pl.multiple_of(slot * COEF_ROWS, COEF_ROWS), COEF_ROWS), :].astype(
            jnp.bfloat16
        )
        coef_ref[slot] = coefs
        power = lax.dot_general(coefs, basis_ref[...], DOWN, preferred_element_type=jnp.float32)
        through = [jnp.ones((SEGMENTS, HALF), jnp.float32) for side in range(2)]
        weights = [[], []]
        for step in range(STEPS):
            for side in range(2):
                alpha = jnp.exp2(
                    power[step * SEGMENTS : (step + 1) * SEGMENTS, side * HALF : (side + 1) * HALF]
                )
                weight = alpha * through[side]
                through[side] = through[side] - weight
                weights[side].append(weight)
        weight = jnp.concatenate([jnp.concatenate(w, axis=0) for w in weights], axis=1)
        tints = []
        for part in (24, 32):
            for c in range(3):
                row = work_ref[pl.ds(slot * COEF_ROWS + part + c, 1), :]
                tints.append(jnp.where(own_seg, jnp.broadcast_to(row, (SEGMENTS, HALF)), 0.0))
        tint = jnp.concatenate(tints, axis=0).astype(jnp.bfloat16)
        sums = jnp.dot(
            jnp.concatenate([tint, tint], axis=1),
            jnp.concatenate(halves(weight), axis=0),
            preferred_element_type=jnp.float32,
        )
        return through, sums[0:24] + sums[24:48]

    def draw_join(slot, carry, through, sums):
        tile = tile_ref[slot]
        fresh = (slot == 0) | (tile != tile_ref[jnp.maximum(slot - 1, 0)])
        after = []
        for side in range(2):
            start = jnp.where(fresh, 1.0, carry[side])
            running = through[side]
            for shift in (1, 2, 4):
                running = jnp.where(
                    seg_at >= shift, running * pltpu.roll(running, shift, 0), running
                )
            before = jnp.where(seg_at == 0, 1.0, pltpu.roll(running, 1, 0)) * start
            after.append(start * running[SEGMENTS - 1 : SEGMENTS])
            lanes = slice(side * HALF, (side + 1) * HALF)
            saved_ref[slot, 0, :, lanes] = before
            saved_ref[slot, 1, :, lanes] = through[side]
            for c in range(3):
                part = sums[c * SEGMENTS : (c + 1) * SEGMENTS, lanes]
                saved_ref[slot, 2 + c, :, lanes] = part
                shade_sum = jnp.sum(before * part, axis=0, keepdims=True)
                held = jnp.where(fresh, 0.0, image_ref[tile, c : c + 1, lanes])
                image_ref[tile, c : c + 1, lanes] = held + shade_sum
        return tuple(after)

    def draw(pair, carry):
        locals_two = [draw_local(GROUP * pair + k) for k in range(GROUP)]
        for k in range(GROUP):
            carry = draw_join(GROUP * pair + k, carry, *locals_two[k])
        return carry

    ones = jnp.ones((1, HALF), jnp.float32)
    lax.fori_loop(0, (live + GROUP - 1) // GROUP, draw, (ones, ones))
    lane_tile = lax.broadcasted_iota(jnp.int32, (SEGMENTS, HALF), 1) // TILE_SIDE
    for side in range(2):
        lanes = slice(side * HALF, (side + 1) * HALF)
        for c in range(3):
            shown = jnp.zeros((SEGMENTS, HALF), jnp.float32)
            for tile in range(TILES_DEV):
                row = jnp.broadcast_to(image_ref[tile, c : c + 1, lanes], (SEGMENTS, HALF))
                moved = pltpu.roll(row, TILE_SIDE * tile, 1) if tile else row
                for bit in (1, 2, 4):
                    moved = jnp.where(
                        (seg_at & bit) > 0, pltpu.roll(moved, HALF - TILE_SIDE * bit, 1), moved
                    )
                shown = jnp.where(lane_tile == tile, moved, shown)
            picture_ref[c, side * SEGMENTS : (side + 1) * SEGMENTS, :] = shown


def backward_kernel(
    tile_ref, rec_ref, coef_ref, saved_ref, grad_ref, slots_ref, out_ref,
    rhs_ref, mom_ref, back_ref, where_ref, acc_ref,
):
    live = live_slots(tile_ref)
    chunks = out_ref.shape[1] // BLOCK
    slots_total = coef_ref.shape[0]
    acc_ref[...] = jnp.zeros_like(acc_ref)
    basis = pixel_basis()
    blank = jnp.zeros_like(basis)
    basis16 = jnp.concatenate([basis, blank], axis=0).astype(jnp.bfloat16)
    for tile in range(TILES_DEV):
        grads = grad_ref[tile]
        high = coarse(grads)
        rhs_ref[tile, :, 0 : 2 * HALF] = jnp.concatenate([basis] * 3 + [blank] * 3, axis=0).astype(
            jnp.bfloat16
        )
        rhs_ref[tile, :, 2 * HALF : 4 * HALF] = jnp.concatenate(
            [blank] * 3 + [high, high, grads - high], axis=0
        ).astype(jnp.bfloat16)
    seg_at = lax.broadcasted_iota(jnp.int32, (SEGMENTS, HALF), 0)

    def pull_scan(slot, carry):
        tile = tile_ref[slot]
        final = (slot >= live - 1) | (tile != tile_ref[jnp.minimum(slot + 1, slots_total - 1)])
        grads = grad_ref[jnp.minimum(tile, TILES_DEV - 1)]
        after = []
        behind = []
        for side in range(2):
            lanes = slice(side * HALF, (side + 1) * HALF)
            start = jnp.where(final, 0.0, carry[side])
            total = grads[0:1, lanes] * saved_ref[slot, 2, :, lanes]
            for c in (1, 2):
                total = total + grads[c : c + 1, lanes] * saved_ref[slot, 2 + c, :, lanes]
            factor = saved_ref[slot, 1, :, lanes]
            for shift in (1, 2, 4):
                inside = seg_at < SEGMENTS - shift
                total = jnp.where(
                    inside, total + factor * pltpu.roll(total, SEGMENTS - shift, 0), total
                )
                factor = jnp.where(
                    inside, factor * pltpu.roll(factor, SEGMENTS - shift, 0), factor
                )
            entering = total + factor * start
            after.append(entering[0:1])
            behind.append(
                jnp.where(seg_at < SEGMENTS - 1, pltpu.roll(entering, SEGMENTS - 1, 0), start)
            )
        return tuple(after), behind

    def pull_one(slot, behind):
        tile = jnp.minimum(tile_ref[slot], TILES_DEV - 1)
        both = lax.dot_general(
            coef_ref[slot], rhs_ref[tile], DOWN, preferred_element_type=jnp.float32
        )
        weights = []
        forces = []
        for side in range(2):
            lanes = slice(side * HALF, (side + 1) * HALF)
            through = saved_ref[slot, 0, :, lanes]
            alphas = []
            shares = []
            for step in range(STEPS):
                alpha = jnp.exp2(both[step * SEGMENTS : (step + 1) * SEGMENTS, lanes])
                weight = alpha * through
                through = through - weight
                alphas.append(alpha)
                shares.append(weight)
            pulls = [None] * STEPS
            later = behind[side]
            for step in reversed(range(STEPS)):
                lit = both[
                    step * SEGMENTS : (step + 1) * SEGMENTS,
                    (2 + side) * HALF : (3 + side) * HALF,
                ]
                gap = lit - later
                later = later + alphas[step] * gap
                pulls[step] = shares[step] * gap
            weights.append(jnp.concatenate(shares, axis=0))
            forces.append(jnp.concatenate(pulls, axis=0))
        found = lax.dot_general(
            basis16,
            jnp.concatenate(halves(jnp.concatenate(forces, axis=1)), axis=0),
            ACROSS,
            preferred_element_type=jnp.float32,
        )
        painted = lax.dot_general(
            jnp.concatenate(halves(grad_ref[tile]), axis=0),
            jnp.concatenate(halves(jnp.concatenate(weights, axis=1)), axis=0),
            ACROSS,
            preferred_element_type=jnp.float32,
        )
        painted = painted[0:8] + painted[8:16]
        mom_ref[slot, 0:8, :] = found[0:8, :BLOCK] + found[0:8, BLOCK:]
        mom_ref[slot, 8:16, :] = painted[:, :BLOCK] + painted[:, BLOCK:]

    def pull(turn, carry):
        group = (live + GROUP - 1) // GROUP - 1 - turn
        behinds = [None] * GROUP
        for k in reversed(range(GROUP)):
            carry, behinds[k] = pull_scan(GROUP * group + k, carry)
        for k in range(GROUP):
            pull_one(GROUP * group + k, behinds[k])
        return carry

    zeros = jnp.zeros((1, HALF), jnp.float32)
    lax.fori_loop(0, (live + GROUP - 1) // GROUP, pull, (zeros, zeros))
    lane_rows = lax.broadcasted_iota(jnp.int32, (BLOCK, 4 * BLOCK), 0)
    chunk_rows = lax.broadcasted_iota(jnp.int32, (chunks, BLOCK), 0)

    def settle(group, carry):
        first = pl.multiple_of(group * SEGMENTS, SEGMENTS)
        tiles = tiles_of(tile_ref, first)
        used = tiles < TILES_DEV
        rows = pl.ds(first, SEGMENTS)

        m_xx, m_xy, m_yy, m_x, m_y, m_0 = [
            mom_ref[rows, k, :] for k in range(6)
        ]
        at_x, at_y, con_a, con_b, con_c, shut_s = [rec_ref[k, rows, :] for k in range(6)]
        h_x = m_x - at_x * m_0
        h_y = m_y - at_y * m_0
        h_xx = m_xx - 2.0 * at_x * m_x + at_x * at_x * m_0
        h_xy = m_xy - at_x * m_y - at_y * m_x + at_x * at_y * m_0
        h_yy = m_yy - 2.0 * at_y * m_y + at_y * at_y * m_0
        results = [
            -2.0 * con_a * h_x - con_b * h_y,
            -2.0 * con_c * h_y - con_b * h_x,
            -0.5 * h_xx,
            -h_xy,
            -0.5 * h_yy,
            shut_s * m_0,
        ] + [mom_ref[rows, 8 + c, :] for c in range(3)]
        for f, value in enumerate(results):
            kept = jnp.where(used, value, 0.0)
            high = coarse(kept)
            back_ref[rows, f, :] = high
            back_ref[rows, 12 + f, :] = kept - high
        slots = spread_order(slots_ref[rows, :])
        where_ref[0, rows, :] = slots % BLOCK
        where_ref[1, rows, :] = slots // BLOCK
        for quad in range(0, SEGMENTS, 4):
            stacked = []
            for k in range(quad, quad + 4):
                hit = chunk_rows == where_ref[1, pl.ds(first + k, 1), :]
                stacked.append(
                    jnp.concatenate(
                        [
                            jnp.where(hit, back_ref[first + k, part + f : part + f + 1, :], 0.0)
                            for part in (0, 12)
                            for f in range(FIELDS)
                        ],
                        axis=0,
                    ).astype(jnp.bfloat16)
                )
            fine = jnp.concatenate(
                [where_ref[0, pl.ds(first + k, 1), :] for k in range(quad, quad + 4)], axis=1
            )
            select = jnp.where(lane_rows == fine, 1.0, 0.0).astype(jnp.bfloat16)
            acc_ref[...] += lax.dot_general(
                jnp.concatenate(stacked, axis=1), select, ACROSS, preferred_element_type=jnp.float32
            )
        return carry

    lax.fori_loop(0, (live + SEGMENTS - 1) // SEGMENTS, settle, 0)
    total = FIELDS * chunks
    for chunk in range(chunks):
        lanes = slice(chunk * BLOCK, (chunk + 1) * BLOCK)
        out_ref[0:8, lanes] = (
            acc_ref[pl.ds(chunk, 8, stride=chunks), :]
            + acc_ref[pl.ds(total + chunk, 8, stride=chunks), :]
        )
        at = 8 * chunks + chunk
        out_ref[8:9, lanes] = acc_ref[at : at + 1, :] + acc_ref[total + at : total + at + 1, :]


def smem():
    return pl.BlockSpec(memory_space=pltpu.SMEM)


def vmem():
    return pl.BlockSpec(memory_space=pltpu.VMEM)


def draw_tiles(tile_ids, received, slots):
    slots_total = slots.shape[0]
    side = TILE_SIDE * TILE_SIDE
    return pl.pallas_call(
        forward_kernel,
        out_shape=(
            jax.ShapeDtypeStruct((3, TILE_SIDE, TILES_DEV * TILE_SIDE), jnp.float32),
            jax.ShapeDtypeStruct((6, slots_total, BLOCK), jnp.float32),
            jax.ShapeDtypeStruct((slots_total, COEF_ROWS, BLOCK), jnp.bfloat16),
            jax.ShapeDtypeStruct((slots_total, 5, SEGMENTS, side), jnp.float32),
        ),
        in_specs=[smem(), vmem(), vmem()],
        out_specs=(vmem(), vmem(), vmem(), vmem()),
        scratch_shapes=[
            pltpu.VMEM((slots_total * COEF_ROWS, BLOCK), jnp.float32),
            pltpu.VMEM((TILES_DEV + 1, 8, side), jnp.float32),
            pltpu.VMEM((COEF_ROWS, side), jnp.bfloat16),
        ],
        compiler_params=pltpu.CompilerParams(vmem_limit_bytes=48 * 1024 * 1024),
        name="draw_tiles",
    )(tile_ids, received, slots)


def pull_tiles(tile_ids, recs, coefs, saved, grads, slots, own):
    slots_total = coefs.shape[0]
    side = TILE_SIDE * TILE_SIDE
    chunks = own // BLOCK
    return pl.pallas_call(
        backward_kernel,
        out_shape=jax.ShapeDtypeStruct((FIELDS, own), jnp.float32),
        in_specs=[smem(), vmem(), vmem(), vmem(), vmem(), vmem()],
        out_specs=vmem(),
        scratch_shapes=[
            pltpu.VMEM((TILES_DEV, COEF_ROWS, 2 * side), jnp.bfloat16),
            pltpu.VMEM((slots_total, 16, BLOCK), jnp.float32),
            pltpu.VMEM((slots_total, GRAD_ROWS, BLOCK), jnp.float32),
            pltpu.VMEM((2, slots_total, BLOCK), jnp.int32),
            pltpu.VMEM((2 * FIELDS * chunks, BLOCK), jnp.float32),
        ],
        compiler_params=pltpu.CompilerParams(vmem_limit_bytes=48 * 1024 * 1024),
        name="pull_tiles",
    )(tile_ids, recs, coefs, saved, grads, slots)


WAYS = [(down, right) for down in (-1, 0, 1) for right in (-1, 0, 1) if (down, right) != (0, 0)]
NORM = sum(math.exp(-m * m / 4.5) for m in range(-5, 6))


def halo_kernel(bands, cols_total, shown_ref, target_ref, out_ref, send_sem, recv_sem):
    band = lax.axis_index("gauss")
    column = lax.axis_index("tile")
    rows, cols = shown_ref.shape[1:]
    out_ref[...] = jnp.zeros_like(out_ref)
    barrier = pltpu.get_barrier_semaphore()

    def exists(way):
        there_band = band + way[0]
        there_col = column + way[1]
        return (
            (there_band >= 0) & (there_band < bands) & (there_col >= 0) & (there_col < cols_total)
        )

    def copies(at):
        down, right = WAYS[at]
        landing = len(WAYS) - 1 - at
        return [
            pltpu.make_async_remote_copy(
                src_ref=source,
                dst_ref=out_ref.at[
                    pl.ds(3 * kind, 3), pl.ds(rows * (1 - down), rows), pl.ds(cols * (1 - right), cols)
                ],
                send_sem=send_sem.at[kind, at],
                recv_sem=recv_sem.at[kind, landing],
                device_id=(band + down, column + right),
                device_id_type=pl.DeviceIdType.MESH,
            )
            for kind, source in enumerate((shown_ref, target_ref))
        ]

    for at, way in enumerate(WAYS):

        @pl.when(exists(way))
        def _(way=way):
            pl.semaphore_signal(
                barrier,
                inc=1,
                device_id=(band + way[0], column + way[1]),
                device_id_type=pl.DeviceIdType.MESH,
            )

    peers = sum(exists(way).astype(jnp.int32) for way in WAYS)
    pl.semaphore_wait(barrier, peers)

    for at, way in enumerate(WAYS):

        @pl.when(exists(way))
        def _(at=at):
            for copy in copies(at):
                copy.start()

    out_ref[0:3, rows : 2 * rows, cols : 2 * cols] = shown_ref[...]
    out_ref[3:6, rows : 2 * rows, cols : 2 * cols] = target_ref[...]
    for at, way in enumerate(WAYS):

        @pl.when(exists(way))
        def _(at=at):
            for copy in copies(at):
                copy.wait_send()
            for kind, source in enumerate((shown_ref, target_ref)):
                pltpu.make_async_remote_copy(
                    src_ref=source,
                    dst_ref=out_ref.at[
                        pl.ds(3 * kind, 3),
                        pl.ds(rows * (1 + WAYS[at][0]), rows),
                        pl.ds(cols * (1 + WAYS[at][1]), cols),
                    ],
                    send_sem=send_sem.at[kind, at],
                    recv_sem=recv_sem.at[kind, at],
                    device_id=(band + WAYS[at][0], column + WAYS[at][1]),
                    device_id_type=pl.DeviceIdType.MESH,
                ).wait_recv()


def exchange(rendered, target):
    channels, rows, cols = rendered.shape
    return pl.pallas_call(
        functools.partial(halo_kernel, lax.axis_size("gauss"), lax.axis_size("tile")),
        out_shape=jax.ShapeDtypeStruct((2 * channels, 3 * rows, 3 * cols), jnp.float32),
        in_specs=[vmem(), vmem()],
        out_specs=vmem(),
        scratch_shapes=[
            pltpu.SemaphoreType.DMA((2, len(WAYS))),
            pltpu.SemaphoreType.DMA((2, len(WAYS))),
        ],
        compiler_params=pltpu.CompilerParams(collective_id=0, has_side_effects=True),
        name="halo",
    )(rendered, target)


def banded(shape, offset):
    gap = (
        lax.broadcasted_iota(jnp.int32, shape, 0) - lax.broadcasted_iota(jnp.int32, shape, 1) + offset
    ).astype(jnp.float32)
    return jnp.where(jnp.abs(gap) < 5.5, jnp.exp(gap * gap / -4.5) * (1.0 / NORM), 0.0)


def exact_dot(left, right):
    return jnp.dot(left, right, precision=HIGHEST, preferred_element_type=jnp.float32)


def ssim_kernel(place_ref, wide_ref, out_ref, stack_ref):
    tall, wide = wide_ref.shape[1:]
    rows, cols = tall // 3, wide // 3
    row_from, rows_mid = rows // 2, 2 * rows
    col_from, cols_mid = cols // 2, 2 * cols
    for c in range(3):
        pic = wide_ref[c]
        aim = wide_ref[3 + c]
        for kind, plane in enumerate((pic, aim, pic * pic + aim * aim, pic * aim)):
            at = 3 * kind + c
            stack_ref[at * tall : (at + 1) * tall, :] = plane
    across = exact_dot(stack_ref[...], banded((wide, cols_mid), -col_from))
    moments = exact_dot(
        banded((rows_mid, tall), row_from),
        jnp.concatenate([across[at * tall : (at + 1) * tall] for at in range(12)], axis=1),
    )
    row_at = place_ref[0] + row_from - rows + lax.broadcasted_iota(jnp.int32, (rows_mid, cols_mid), 0)
    col_at = place_ref[1] + col_from - cols + lax.broadcasted_iota(jnp.int32, (rows_mid, cols_mid), 1)
    inside = (row_at >= 0) & (row_at < place_ref[2]) & (col_at >= 0) & (col_at < place_ref[3])
    slopes = [None] * 9
    for c in range(3):
        mu_x, mu_y, squares, cross = [
            moments[:, (3 * kind + c) * cols_mid : (3 * kind + c + 1) * cols_mid] for kind in range(4)
        ]
        mean_xy = mu_x * mu_y
        mean_sq = mu_x * mu_x + mu_y * mu_y
        top_1 = 2.0 * mean_xy + CONST_ONE
        top_2 = 2.0 * (cross - mean_xy) + CONST_TWO
        low_1 = mean_sq + CONST_ONE
        low_2 = squares - mean_sq + CONST_TWO
        inverse = -0.2 / (low_1 * low_2)
        value = top_1 * top_2 * inverse
        value_1 = value * low_2 * inverse * -5.0
        value_2 = value * low_1 * inverse * -5.0
        slope_mean = 2.0 * mu_y * (top_2 - top_1) * inverse - 2.0 * mu_x * (value_1 - value_2)
        for kind, slope in enumerate((slope_mean, -value_2, 2.0 * top_1 * inverse)):
            slopes[3 * kind + c] = jnp.where(inside, slope, 0.0)
    down = exact_dot(
        banded((rows, rows_mid), rows - row_from), jnp.concatenate(slopes, axis=1)
    )
    spread = exact_dot(
        jnp.concatenate([down[:, at * cols_mid : (at + 1) * cols_mid] for at in range(9)], axis=0),
        banded((cols_mid, cols), col_from - cols),
    )
    lane_row = lax.broadcasted_iota(jnp.int32, (SEGMENTS, HALF), 1) // TILE_SIDE
    seg_at = lax.broadcasted_iota(jnp.int32, (SEGMENTS, HALF), 0)
    out_ref[...] = jnp.zeros_like(out_ref)
    for c in range(3):
        pic = wide_ref[c, rows : 2 * rows, cols : 2 * cols]
        aim = wide_ref[3 + c, rows : 2 * rows, cols : 2 * cols]
        parts = [spread[(3 * kind + c) * rows : (3 * kind + c + 1) * rows] for kind in range(3)]
        total = parts[0] + 2.0 * pic * parts[1] + aim * parts[2] + 1.6 * (pic - aim)
        for side in range(2):
            part = total[side * SEGMENTS : (side + 1) * SEGMENTS]
            skewed = pltpu.roll(part, 0, 1, stride=TILE_SIDE, stride_axis=0)
            for tile in range(TILES_DEV):
                moved = pltpu.roll(skewed, HALF - TILE_SIDE * tile, 1) if tile else skewed
                kept = jnp.where(lane_row == seg_at, moved, 0.0)
                out_ref[tile, c : c + 1, side * HALF : (side + 1) * HALF] = jnp.sum(
                    kept, axis=0, keepdims=True
                )


def ssim_pull(place, wide):
    return pl.pallas_call(
        ssim_kernel,
        out_shape=jax.ShapeDtypeStruct((TILES_DEV, 8, TILE_SIDE * TILE_SIDE), jnp.float32),
        in_specs=[smem(), vmem()],
        out_specs=vmem(),
        scratch_shapes=[pltpu.VMEM((12 * wide.shape[1], wide.shape[2]), jnp.float32)],
        name="ssim_pull",
    )(place, wide)


MESH = pl.DeviceIdType.MESH
PACKED = 8


def basis_rows(x, y, z):
    xx, yy, zz = x * x, y * y, z * z
    return [
        jnp.full_like(x, BASE_ZERO),
        -BASE_ONE * y,
        BASE_ONE * z,
        -BASE_ONE * x,
        BASE_TWO[0] * x * y,
        BASE_TWO[1] * y * z,
        BASE_TWO[2] * (2.0 * zz - xx - yy),
        BASE_TWO[3] * x * z,
        BASE_TWO[4] * (xx - yy),
        BASE_THREE[0] * y * (3.0 * xx - yy),
        BASE_THREE[1] * x * y * z,
        BASE_THREE[2] * y * (4.0 * zz - xx - yy),
        BASE_THREE[3] * z * (2.0 * zz - 3.0 * xx - 3.0 * yy),
        BASE_THREE[4] * x * (4.0 * zz - xx - yy),
        BASE_THREE[5] * z * (xx - yy),
        BASE_THREE[6] * x * (xx - 3.0 * yy),
    ]


def slope_rows(x, y, z):
    xx, yy, zz = x * x, y * y, z * z
    xy, yz, xz = x * y, y * z, x * z
    none = jnp.zeros_like(x)
    one = jnp.ones_like(x)
    two, three = BASE_TWO, BASE_THREE
    along_x = [
        none, none, none, -BASE_ONE * one,
        two[0] * y, none, -2.0 * two[2] * x, two[3] * z, 2.0 * two[4] * x,
        6.0 * three[0] * xy, three[1] * yz, -2.0 * three[2] * xy, -6.0 * three[3] * xz,
        three[4] * (4.0 * zz - 3.0 * xx - yy), 2.0 * three[5] * xz, three[6] * (3.0 * xx - 3.0 * yy),
    ]
    along_y = [
        none, -BASE_ONE * one, none, none,
        two[0] * x, two[1] * z, -2.0 * two[2] * y, none, -2.0 * two[4] * y,
        three[0] * (3.0 * xx - 3.0 * yy), three[1] * xz, three[2] * (4.0 * zz - xx - 3.0 * yy),
        -6.0 * three[3] * yz, -2.0 * three[4] * xy, -2.0 * three[5] * yz, -6.0 * three[6] * xy,
    ]
    along_z = [
        none, none, BASE_ONE * one, none,
        none, two[1] * y, 4.0 * two[2] * z, two[3] * x, none,
        none, three[1] * xy, 8.0 * three[2] * yz, three[3] * (6.0 * zz - 3.0 * xx - 3.0 * yy),
        8.0 * three[4] * xz, three[5] * (xx - yy), none,
    ]
    return along_x, along_y, along_z


def lane_of():
    return lax.broadcasted_iota(jnp.int32, (8, BLOCK), 1)


def row_of():
    return lax.broadcasted_iota(jnp.int32, (8, BLOCK), 0)


def gather_rows(table, chunks, index):
    index = jnp.broadcast_to(index, (8, BLOCK))
    fine = index % BLOCK
    chunk_at = index // BLOCK
    first = pick(table(0, 0), fine)
    last = pick(table(1, 0), fine)
    for chunk in range(1, chunks):
        hit = chunk_at == chunk
        first = jnp.where(hit, pick(table(0, chunk), fine), first)
        last = jnp.where(hit, pick(table(1, chunk), fine), last)
    return first, last


def pack_two(first, last):
    left = lane_of() < BLOCK // 2
    swapped = pltpu.roll(first, BLOCK // 2, 1)
    one = jnp.where(left, first, pltpu.roll(swapped, 4, 0))
    two = jnp.where(left, swapped, pltpu.roll(first, 4, 0))
    tail = row_of() >= 4
    ninth = jnp.broadcast_to(last[0:1], (8, BLOCK))
    return jnp.where(tail, ninth, one), jnp.where(tail, pltpu.roll(ninth, BLOCK // 2, 1), two)


def unpack_two(one, two):
    left = lane_of() < BLOCK // 2
    upper = jnp.where(left, one, pltpu.roll(two, BLOCK // 2, 1))
    lower = jnp.where(left, pltpu.roll(one, BLOCK // 2, 1), two)
    return jnp.where(row_of() < 4, upper, pltpu.roll(lower, 4, 0)), upper[4:5]


def greet(owners):
    barrier = pltpu.get_barrier_semaphore()
    band = lax.axis_index("gauss")
    column = lax.axis_index("tile")
    for gap in range(1, owners):
        pl.semaphore_signal(
            barrier,
            inc=1,
            device_id=(lax.rem(band + gap, owners), column),
            device_id_type=MESH,
        )
    return barrier


def parcel(owners, gap, out_ref, in_ref, send_sem, recv_sem):
    band = lax.axis_index("gauss")
    there = lax.rem(band + gap, owners)
    return pltpu.make_async_remote_copy(
        src_ref=out_ref.at[there],
        dst_ref=in_ref.at[band],
        send_sem=send_sem.at[gap],
        recv_sem=recv_sem.at[gap],
        device_id=(there, lax.axis_index("tile")),
        device_id_type=MESH,
    )


def post(owners, barrier, out_ref, in_ref, send_sem, recv_sem):
    band = lax.axis_index("gauss")
    pl.semaphore_wait(barrier, owners - 1)
    for gap in range(1, owners):
        parcel(owners, gap, out_ref, in_ref, send_sem, recv_sem).start()
    in_ref[band] = out_ref[band]


def take_in(owners, out_ref, in_ref, send_sem, recv_sem):
    for gap in range(1, owners):
        parcel(owners, gap, out_ref, in_ref, send_sem, recv_sem).wait()


def deliver_kernel(
    owners, splats_ref, sh_ref, send_ref, recv_ref, home_ref,
    table_ref, out_ref, in_ref, send_sem, recv_sem,
):
    barrier = greet(owners)
    own = splats_ref.shape[1]
    chunks = own // BLOCK
    basis = jnp.concatenate(
        basis_rows(splats_ref[6:7, :], splats_ref[7:8, :], splats_ref[8:9, :]), axis=0
    )
    colours = [
        0.5 + jnp.sum(sh_ref[16 * c : 16 * (c + 1), :] * basis, axis=0, keepdims=True)
        for c in range(3)
    ]
    table_ref[0:6, :] = splats_ref[0:6, :]
    table_ref[6:9, :] = jnp.concatenate(colours, axis=0)
    table_ref[9:16, :] = jnp.zeros((7, own), jnp.float32)

    def table(part, chunk):
        return table_ref[8 * part : 8 * (part + 1), chunk * BLOCK : (chunk + 1) * BLOCK]

    for chunk in range(chunks):
        one, two = pack_two(*gather_rows(table, chunks, send_ref[chunk : chunk + 1, :]))
        out_ref[2 * chunk] = one
        out_ref[2 * chunk + 1] = two
    post(owners, barrier, out_ref, in_ref, send_sem, recv_sem)
    chunk_rows = lax.broadcasted_iota(jnp.int32, (chunks, BLOCK), 0)
    lanes = lax.broadcasted_iota(jnp.int32, (chunks, BLOCK), 1).astype(jnp.float32)
    lane_rows = lax.broadcasted_iota(jnp.int32, (BLOCK, BLOCK), 0)
    home = jnp.zeros((2 * chunks, BLOCK), jnp.float32)
    for chunk in range(chunks):
        index = send_ref[chunk : chunk + 1, :]
        hit = chunk_rows == index // BLOCK
        source = jnp.concatenate(
            [jnp.where(hit, float(chunk), 0.0), jnp.where(hit, lanes, 0.0)], axis=0
        ).astype(jnp.bfloat16)
        select = jnp.where(lane_rows == index % BLOCK, 1.0, 0.0).astype(jnp.bfloat16)
        home = home + lax.dot_general(source, select, ACROSS, preferred_element_type=jnp.float32)
    home_ref[...] = (home[:chunks] * float(BLOCK) + home[chunks:]).astype(jnp.int32)
    take_in(owners, out_ref, in_ref, send_sem, recv_sem)
    for chunk in range(chunks):
        first, ninth = unpack_two(in_ref[2 * chunk], in_ref[2 * chunk + 1])
        recv_ref[0:8, chunk * BLOCK : (chunk + 1) * BLOCK] = first
        recv_ref[8:9, chunk * BLOCK : (chunk + 1) * BLOCK] = ninth


def parcels(owners):
    return [
        pltpu.VMEM((owners, PACKED, BLOCK), jnp.float32),
        pltpu.VMEM((owners, PACKED, BLOCK), jnp.float32),
        pltpu.SemaphoreType.DMA((owners,)),
        pltpu.SemaphoreType.DMA((owners,)),
    ]


def deliver(splats, sh_coeffs, send_list):
    own = splats.shape[1]
    owners = lax.axis_size("gauss")
    return pl.pallas_call(
        functools.partial(deliver_kernel, owners),
        out_shape=(
            jax.ShapeDtypeStruct((FIELDS, own), jnp.float32),
            jax.ShapeDtypeStruct((own // BLOCK, BLOCK), jnp.int32),
        ),
        in_specs=[vmem(), vmem(), vmem()],
        out_specs=(vmem(), vmem()),
        scratch_shapes=[pltpu.VMEM((16, own), jnp.float32)] + parcels(owners),
        compiler_params=pltpu.CompilerParams(collective_id=1, has_side_effects=True),
        name="deliver",
    )(splats, sh_coeffs, send_list.reshape(own // BLOCK, BLOCK))


def home_kernel(
    owners, pulled_ref, home_ref, splats_ref, sh_ref, splat_grad_ref, sh_grad_ref,
    table_ref, slope_ref, out_ref, in_ref, send_sem, recv_sem,
):
    barrier = greet(owners)
    own = splats_ref.shape[1]
    chunks = own // BLOCK
    for chunk in range(chunks):
        lanes = slice(chunk * BLOCK, (chunk + 1) * BLOCK)
        one, two = pack_two(pulled_ref[0:8, lanes], pulled_ref[8:9, lanes])
        out_ref[2 * chunk] = one
        out_ref[2 * chunk + 1] = two
    post(owners, barrier, out_ref, in_ref, send_sem, recv_sem)
    facing = [splats_ref[6 + d : 7 + d, :] for d in range(3)]
    slope_ref[0:16, :] = jnp.concatenate(basis_rows(*facing), axis=0)
    for d, rows in enumerate(slope_rows(*facing)):
        slope_ref[16 * (d + 1) : 16 * (d + 2), :] = jnp.concatenate(rows, axis=0)
    take_in(owners, out_ref, in_ref, send_sem, recv_sem)
    for chunk in range(chunks):
        first, ninth = unpack_two(in_ref[2 * chunk], in_ref[2 * chunk + 1])
        table_ref[0:8, chunk * BLOCK : (chunk + 1) * BLOCK] = first
        table_ref[8:16, chunk * BLOCK : (chunk + 1) * BLOCK] = jnp.broadcast_to(ninth, (8, BLOCK))

    def table(part, chunk):
        return table_ref[8 * part : 8 * (part + 1), chunk * BLOCK : (chunk + 1) * BLOCK]

    for chunk in range(chunks):
        lanes = slice(chunk * BLOCK, (chunk + 1) * BLOCK)
        first, last = gather_rows(table, chunks, home_ref[chunk : chunk + 1, :])
        splat_grad_ref[0:6, lanes] = first[0:6]
        tints = (first[6:7], first[7:8], last[0:1])
        basis = slope_ref[0:16, lanes]
        mixed = jnp.zeros((16, BLOCK), jnp.float32)
        for c in range(3):
            tint = jnp.broadcast_to(tints[c], (16, BLOCK))
            sh_grad_ref[16 * c : 16 * (c + 1), lanes] = tint * basis
            mixed = mixed + tint * sh_ref[16 * c : 16 * (c + 1), lanes]
        splat_grad_ref[6:9, lanes] = jnp.concatenate(
            [
                jnp.sum(mixed * slope_ref[16 * d : 16 * (d + 1), lanes], axis=0, keepdims=True)
                for d in (1, 2, 3)
            ],
            axis=0,
        )


def bring_home(pulled, home, splats, sh_coeffs):
    own = splats.shape[1]
    owners = lax.axis_size("gauss")
    return pl.pallas_call(
        functools.partial(home_kernel, owners),
        out_shape=(
            jax.ShapeDtypeStruct(splats.shape, jnp.float32),
            jax.ShapeDtypeStruct(sh_coeffs.shape, jnp.float32),
        ),
        in_specs=[vmem()] * 4,
        out_specs=(vmem(), vmem()),
        scratch_shapes=[
            pltpu.VMEM((16, own), jnp.float32),
            pltpu.VMEM((64, own), jnp.float32),
        ]
        + parcels(owners),
        compiler_params=pltpu.CompilerParams(collective_id=2, has_side_effects=True),
        name="bring_home",
    )(pulled, home, splats, sh_coeffs)


def body(splats, sh_coeffs, send_list, block_slots, block_tiles, target):
    row_band = lax.axis_index("gauss")
    col_band = lax.axis_index("tile")
    received, home = deliver(splats, sh_coeffs, send_list)
    tile_ids = block_tiles[0]
    slot_rows = block_slots[0]
    rendered, recs, coefs, saved = draw_tiles(tile_ids, received, slot_rows)
    rows_here, cols_here = rendered.shape[1:]
    place = jnp.stack(
        [
            row_band * rows_here,
            col_band * cols_here,
            rows_here * lax.axis_size("gauss"),
            cols_here * lax.axis_size("tile"),
        ]
    ).astype(jnp.int32)
    tile_grad = ssim_pull(place, exchange(rendered, target))
    pulled = pull_tiles(tile_ids, recs, coefs, saved, tile_grad, slot_rows, received.shape[1])
    grad_splats, grad_sh = bring_home(pulled, home, splats, sh_coeffs)
    return (rendered, grad_splats, grad_sh)


def solution(mesh):
    in_specs = (
        P(None, ("gauss", "tile")),
        P(None, ("gauss", "tile")),
        P(("gauss", "tile")),
        P("gauss", "tile", None),
        P("gauss", "tile"),
        P(None, "gauss", "tile"),
    )
    out_specs = (P(None, "gauss", "tile"), P(None, ("gauss", "tile")), P(None, ("gauss", "tile")))
    return jax.shard_map(body, mesh=mesh, in_specs=in_specs, out_specs=out_specs, check_vma=False)
```

```python
import functools
import math

import jax
import jax.numpy as jnp
from jax import lax
from jax.experimental import pallas as pl
from jax.experimental.pallas import tpu as pltpu
from jax.sharding import PartitionSpec as P

TILE_SIDE = 16
TILES_DEV = 8


BASE_ZERO = 0.28209479177387814
BASE_ONE = 0.4886025119029199
BASE_TWO = (
    1.0925484305920792,
    -1.0925484305920792,
    0.31539156525252005,
    -1.0925484305920792,
    0.5462742152960396,
)
BASE_THREE = (
    -0.5900435899266435,
    2.890611442640554,
    -0.4570457994644658,
    0.3731763325901154,
    -0.4570457994644658,
    1.445305721320277,
    -0.5900435899266435,
)
CONST_ONE = 0.0001
CONST_TWO = 0.0009


SEGMENTS = 8
STEPS = 16
BLOCK = SEGMENTS * STEPS
HALF = 128
CENTRE = 7.5
MESH = pl.DeviceIdType.MESH
VMEM_ROOM = 60 * 1024 * 1024


LOG2E = 1.4426950408889634
FIELDS = 9
COEF_ROWS = 48
GROUP = 8
GRAD_ROWS = 24
ACROSS = (((1,), (1,)), ((), ()))
DOWN = (((0,), (0,)), ((), ()))


def pick(table, index):
    return jnp.take_along_axis(table, index, axis=1, mode="promise_in_bounds")


def coarse(value):
    return value.astype(jnp.bfloat16).astype(jnp.float32)


def halves(value):
    high = value.astype(jnp.bfloat16)
    low = (value - high.astype(jnp.float32)).astype(jnp.bfloat16)
    return high, low


def pixel_basis():
    rows = lax.broadcasted_iota(jnp.int32, (8, 2 * HALF), 0)
    pixels = lax.broadcasted_iota(jnp.int32, (8, 2 * HALF), 1)
    along = (pixels % TILE_SIDE).astype(jnp.float32) - CENTRE
    down = (pixels // TILE_SIDE).astype(jnp.float32) - CENTRE
    basis = jnp.zeros((8, 2 * HALF), jnp.float32)
    terms = (along * along, along * down, down * down, along, down, jnp.ones_like(along))
    for at, term in enumerate(terms):
        basis = jnp.where(rows == at, term, basis)
    return basis


def spread_order(slots):
    lanes = lax.broadcasted_iota(jnp.int32, slots.shape, 1)
    return pick(slots, (lanes % SEGMENTS) * STEPS + lanes // SEGMENTS)


def tiles_of(tile_ref, first):
    at = lax.broadcasted_iota(jnp.int32, (SEGMENTS, BLOCK), 0)
    tiles = jnp.zeros((SEGMENTS, BLOCK), jnp.int32)
    for k in range(SEGMENTS):
        tiles = jnp.where(at == k, tile_ref[first + k], tiles)
    return tiles


def live_slots(tile_ref):
    live = jnp.int32(0)
    for slot in range(tile_ref.shape[0]):
        live = live + (tile_ref[slot] < TILES_DEV).astype(jnp.int32)
    return live


def forward_kernel(
    tile_ref, recv_ref, slots_ref, picture_ref, rec_ref, coef_ref, saved_ref,
    work_ref, image_ref, basis_ref,
):
    live = live_slots(tile_ref)
    chunks = recv_ref.shape[1] // BLOCK
    origin_x = (lax.axis_index("tile") * (TILE_SIDE * TILES_DEV)).astype(jnp.float32) + CENTRE
    origin_y = (lax.axis_index("gauss") * TILE_SIDE).astype(jnp.float32) + CENTRE
    work_ref[...] = jnp.zeros_like(work_ref)
    basis = pixel_basis()
    basis_ref[...] = jnp.concatenate([basis] * 3 + [jnp.zeros_like(basis)] * 3, axis=0).astype(
        jnp.bfloat16
    )

    def collect(group, carry):
        first = group * SEGMENTS
        slots = spread_order(slots_ref[pl.ds(pl.multiple_of(first, SEGMENTS), SEGMENTS), :])
        fine = slots % BLOCK
        chunk_at = slots // BLOCK
        found = [None] * FIELDS
        for chunk in range(chunks):
            hit = chunk_at == chunk
            for f in range(FIELDS):
                row = recv_ref[f : f + 1, chunk * BLOCK : (chunk + 1) * BLOCK]
                got = pick(jnp.broadcast_to(row, (SEGMENTS, BLOCK)), fine)
                found[f] = got if chunk == 0 else jnp.where(hit, got, found[f])
        tiles = tiles_of(tile_ref, first)
        base_x = (TILE_SIDE * jnp.minimum(tiles, TILES_DEV - 1)).astype(jnp.float32) + origin_x
        at_x = found[0] - base_x
        at_y = found[1] - origin_y
        con_a = -0.5 * found[2]
        con_b = -found[3]
        con_c = -0.5 * found[4]
        shut = 1.0 + jnp.exp(-found[5])
        for k, value in enumerate((at_x, at_y, con_a, con_b, con_c, 1.0 - 1.0 / shut)):
            rec_ref[k, pl.ds(pl.multiple_of(first, SEGMENTS), SEGMENTS), :] = value
        part_x = con_a * at_x
        part_y = con_c * at_y
        cross = con_b * at_y
        level = at_x * (part_x + cross) + at_y * part_y
        terms = (
            LOG2E * con_a,
            LOG2E * con_b,
            LOG2E * con_c,
            -LOG2E * (2.0 * part_x + cross),
            -LOG2E * (2.0 * part_y + con_b * at_x),
            LOG2E * (level - jnp.log(shut)),
        )

        def put(row, value):
            work_ref[pl.ds(first * COEF_ROWS + row, SEGMENTS, stride=COEF_ROWS), :] = value

        for k, term in enumerate(terms):
            high = coarse(term)
            rest = term - high
            middle = coarse(rest)
            put(k, high)
            put(8 + k, middle)
            put(16 + k, rest - middle)
        for c in range(3):
            high = coarse(found[6 + c])
            put(24 + c, high)
            put(32 + c, found[6 + c] - high)
            put(40 + c, high)
        return carry

    lax.fori_loop(0, (live + SEGMENTS - 1) // SEGMENTS, collect, 0)
    seg_at = lax.broadcasted_iota(jnp.int32, (SEGMENTS, HALF), 0)
    own_seg = seg_at == lax.broadcasted_iota(jnp.int32, (SEGMENTS, HALF), 1) % SEGMENTS

    def draw_local(slot):
        coefs = work_ref[pl.ds(pl.multiple_of(slot * COEF_ROWS, COEF_ROWS), COEF_ROWS), :].astype(
            jnp.bfloat16
        )
        coef_ref[slot] = coefs
        power = lax.dot_general(coefs, basis_ref[...], DOWN, preferred_element_type=jnp.float32)
        through = [jnp.ones((SEGMENTS, HALF), jnp.float32) for side in range(2)]
        weights = [[], []]
        for step in range(STEPS):
            for side in range(2):
                alpha = jnp.exp2(
                    power[step * SEGMENTS : (step + 1) * SEGMENTS, side * HALF : (side + 1) * HALF]
                )
                weight = alpha * through[side]
                through[side] = through[side] - weight
                weights[side].append(weight)
        weight = jnp.concatenate([jnp.concatenate(w, axis=0) for w in weights], axis=1)
        tints = []
        for part in (24, 32):
            for c in range(3):
                row = work_ref[pl.ds(slot * COEF_ROWS + part + c, 1), :]
                tints.append(jnp.where(own_seg, jnp.broadcast_to(row, (SEGMENTS, HALF)), 0.0))
        tint = jnp.concatenate(tints, axis=0).astype(jnp.bfloat16)
        sums = jnp.dot(
            jnp.concatenate([tint, tint], axis=1),
            jnp.concatenate(halves(weight), axis=0),
            preferred_element_type=jnp.float32,
        )
        return through, sums[0:24] + sums[24:48]

    def draw_join(slot, carry, through, sums):
        tile = tile_ref[slot]
        fresh = (slot == 0) | (tile != tile_ref[jnp.maximum(slot - 1, 0)])
        after = []
        for side in range(2):
            start = jnp.where(fresh, 1.0, carry[side])
            running = through[side]
            for shift in (1, 2, 4):
                running = jnp.where(
                    seg_at >= shift, running * pltpu.roll(running, shift, 0), running
                )
            before = jnp.where(seg_at == 0, 1.0, pltpu.roll(running, 1, 0)) * start
            after.append(start * running[SEGMENTS - 1 : SEGMENTS])
            lanes = slice(side * HALF, (side + 1) * HALF)
            saved_ref[slot, 0, :, lanes] = before
            saved_ref[slot, 1, :, lanes] = through[side]
            for c in range(3):
                part = sums[c * SEGMENTS : (c + 1) * SEGMENTS, lanes]
                saved_ref[slot, 2 + c, :, lanes] = part
                shade_sum = jnp.sum(before * part, axis=0, keepdims=True)
                held = jnp.where(fresh, 0.0, image_ref[tile, c : c + 1, lanes])
                image_ref[tile, c : c + 1, lanes] = held + shade_sum
        return tuple(after)

    def draw(pair, carry):
        locals_two = [draw_local(GROUP * pair + k) for k in range(GROUP)]
        for k in range(GROUP):
            carry = draw_join(GROUP * pair + k, carry, *locals_two[k])
        return carry

    ones = jnp.ones((1, HALF), jnp.float32)
    lax.fori_loop(0, (live + GROUP - 1) // GROUP, draw, (ones, ones))
    lane_tile = lax.broadcasted_iota(jnp.int32, (SEGMENTS, HALF), 1) // TILE_SIDE
    for side in range(2):
        lanes = slice(side * HALF, (side + 1) * HALF)
        for c in range(3):
            shown = jnp.zeros((SEGMENTS, HALF), jnp.float32)
            for tile in range(TILES_DEV):
                row = jnp.broadcast_to(image_ref[tile, c : c + 1, lanes], (SEGMENTS, HALF))
                moved = pltpu.roll(row, TILE_SIDE * tile, 1) if tile else row
                for bit in (1, 2, 4):
                    moved = jnp.where(
                        (seg_at & bit) > 0, pltpu.roll(moved, HALF - TILE_SIDE * bit, 1), moved
                    )
                shown = jnp.where(lane_tile == tile, moved, shown)
            picture_ref[c, side * SEGMENTS : (side + 1) * SEGMENTS, :] = shown


def backward_kernel(
    tile_ref, rec_ref, coef_ref, saved_ref, grad_ref, slots_ref, out_ref,
    rhs_ref, mom_ref, back_ref, where_ref, acc_ref,
):
    live = live_slots(tile_ref)
    chunks = out_ref.shape[1] // BLOCK
    slots_total = coef_ref.shape[0]
    acc_ref[...] = jnp.zeros_like(acc_ref)
    basis = pixel_basis()
    blank = jnp.zeros_like(basis)
    basis16 = jnp.concatenate([basis, blank], axis=0).astype(jnp.bfloat16)
    for tile in range(TILES_DEV):
        grads = grad_ref[tile]
        high = coarse(grads)
        rhs_ref[tile, :, 0 : 2 * HALF] = jnp.concatenate([basis] * 3 + [blank] * 3, axis=0).astype(
            jnp.bfloat16
        )
        rhs_ref[tile, :, 2 * HALF : 4 * HALF] = jnp.concatenate(
            [blank] * 3 + [high, high, grads - high], axis=0
        ).astype(jnp.bfloat16)
    seg_at = lax.broadcasted_iota(jnp.int32, (SEGMENTS, HALF), 0)

    def pull_scan(slot, carry):
        tile = tile_ref[slot]
        final = (slot >= live - 1) | (tile != tile_ref[jnp.minimum(slot + 1, slots_total - 1)])
        grads = grad_ref[jnp.minimum(tile, TILES_DEV - 1)]
        after = []
        behind = []
        for side in range(2):
            lanes = slice(side * HALF, (side + 1) * HALF)
            start = jnp.where(final, 0.0, carry[side])
            total = grads[0:1, lanes] * saved_ref[slot, 2, :, lanes]
            for c in (1, 2):
                total = total + grads[c : c + 1, lanes] * saved_ref[slot, 2 + c, :, lanes]
            factor = saved_ref[slot, 1, :, lanes]
            for shift in (1, 2, 4):
                inside = seg_at < SEGMENTS - shift
                total = jnp.where(
                    inside, total + factor * pltpu.roll(total, SEGMENTS - shift, 0), total
                )
                factor = jnp.where(
                    inside, factor * pltpu.roll(factor, SEGMENTS - shift, 0), factor
                )
            entering = total + factor * start
            after.append(entering[0:1])
            behind.append(
                jnp.where(seg_at < SEGMENTS - 1, pltpu.roll(entering, SEGMENTS - 1, 0), start)
            )
        return tuple(after), behind

    def pull_one(slot, behind):
        tile = jnp.minimum(tile_ref[slot], TILES_DEV - 1)
        both = lax.dot_general(
            coef_ref[slot], rhs_ref[tile], DOWN, preferred_element_type=jnp.float32
        )
        weights = []
        forces = []
        for side in range(2):
            lanes = slice(side * HALF, (side + 1) * HALF)
            through = saved_ref[slot, 0, :, lanes]
            alphas = []
            shares = []
            for step in range(STEPS):
                alpha = jnp.exp2(both[step * SEGMENTS : (step + 1) * SEGMENTS, lanes])
                weight = alpha * through
                through = through - weight
                alphas.append(alpha)
                shares.append(weight)
            pulls = [None] * STEPS
            later = behind[side]
            for step in reversed(range(STEPS)):
                lit = both[
                    step * SEGMENTS : (step + 1) * SEGMENTS,
                    (2 + side) * HALF : (3 + side) * HALF,
                ]
                gap = lit - later
                later = later + alphas[step] * gap
                pulls[step] = shares[step] * gap
            weights.append(jnp.concatenate(shares, axis=0))
            forces.append(jnp.concatenate(pulls, axis=0))
        found = lax.dot_general(
            basis16,
            jnp.concatenate(halves(jnp.concatenate(forces, axis=1)), axis=0),
            ACROSS,
            preferred_element_type=jnp.float32,
        )
        painted = lax.dot_general(
            jnp.concatenate(halves(grad_ref[tile]), axis=0),
            jnp.concatenate(halves(jnp.concatenate(weights, axis=1)), axis=0),
            ACROSS,
            preferred_element_type=jnp.float32,
        )
        painted = painted[0:8] + painted[8:16]
        mom_ref[slot, 0:8, :] = found[0:8, :BLOCK] + found[0:8, BLOCK:]
        mom_ref[slot, 8:16, :] = painted[:, :BLOCK] + painted[:, BLOCK:]

    def pull(turn, carry):
        group = (live + GROUP - 1) // GROUP - 1 - turn
        behinds = [None] * GROUP
        for k in reversed(range(GROUP)):
            carry, behinds[k] = pull_scan(GROUP * group + k, carry)
        for k in range(GROUP):
            pull_one(GROUP * group + k, behinds[k])
        return carry

    zeros = jnp.zeros((1, HALF), jnp.float32)
    lax.fori_loop(0, (live + GROUP - 1) // GROUP, pull, (zeros, zeros))
    lane_rows = lax.broadcasted_iota(jnp.int32, (BLOCK, 4 * BLOCK), 0)
    chunk_rows = lax.broadcasted_iota(jnp.int32, (chunks, BLOCK), 0)

    def settle(group, carry):
        first = pl.multiple_of(group * SEGMENTS, SEGMENTS)
        tiles = tiles_of(tile_ref, first)
        used = tiles < TILES_DEV
        rows = pl.ds(first, SEGMENTS)

        m_xx, m_xy, m_yy, m_x, m_y, m_0 = [
            mom_ref[rows, k, :] for k in range(6)
        ]
        at_x, at_y, con_a, con_b, con_c, shut_s = [rec_ref[k, rows, :] for k in range(6)]
        h_x = m_x - at_x * m_0
        h_y = m_y - at_y * m_0
        h_xx = m_xx - 2.0 * at_x * m_x + at_x * at_x * m_0
        h_xy = m_xy - at_x * m_y - at_y * m_x + at_x * at_y * m_0
        h_yy = m_yy - 2.0 * at_y * m_y + at_y * at_y * m_0
        results = [
            -2.0 * con_a * h_x - con_b * h_y,
            -2.0 * con_c * h_y - con_b * h_x,
            -0.5 * h_xx,
            -h_xy,
            -0.5 * h_yy,
            shut_s * m_0,
        ] + [mom_ref[rows, 8 + c, :] for c in range(3)]
        for f, value in enumerate(results):
            kept = jnp.where(used, value, 0.0)
            high = coarse(kept)
            back_ref[rows, f, :] = high
            back_ref[rows, 12 + f, :] = kept - high
        slots = spread_order(slots_ref[rows, :])
        where_ref[0, rows, :] = slots % BLOCK
        where_ref[1, rows, :] = slots // BLOCK
        for quad in range(0, SEGMENTS, 4):
            stacked = []
            for k in range(quad, quad + 4):
                hit = chunk_rows == where_ref[1, pl.ds(first + k, 1), :]
                stacked.append(
                    jnp.concatenate(
                        [
                            jnp.where(hit, back_ref[first + k, part + f : part + f + 1, :], 0.0)
                            for part in (0, 12)
                            for f in range(FIELDS)
                        ],
                        axis=0,
                    ).astype(jnp.bfloat16)
                )
            fine = jnp.concatenate(
                [where_ref[0, pl.ds(first + k, 1), :] for k in range(quad, quad + 4)], axis=1
            )
            select = jnp.where(lane_rows == fine, 1.0, 0.0).astype(jnp.bfloat16)
            acc_ref[...] += lax.dot_general(
                jnp.concatenate(stacked, axis=1), select, ACROSS, preferred_element_type=jnp.float32
            )
        return carry

    lax.fori_loop(0, (live + SEGMENTS - 1) // SEGMENTS, settle, 0)
    total = FIELDS * chunks
    for chunk in range(chunks):
        lanes = slice(chunk * BLOCK, (chunk + 1) * BLOCK)
        out_ref[0:8, lanes] = (
            acc_ref[pl.ds(chunk, 8, stride=chunks), :]
            + acc_ref[pl.ds(total + chunk, 8, stride=chunks), :]
        )
        at = 8 * chunks + chunk
        out_ref[8:9, lanes] = acc_ref[at : at + 1, :] + acc_ref[total + at : total + at + 1, :]


def smem():
    return pl.BlockSpec(memory_space=pltpu.SMEM)


def vmem():
    return pl.BlockSpec(memory_space=pltpu.VMEM)


def draw_tiles(tile_ids, received, slots):
    slots_total = slots.shape[0]
    side = TILE_SIDE * TILE_SIDE
    return pl.pallas_call(
        forward_kernel,
        out_shape=(
            jax.ShapeDtypeStruct((3, TILE_SIDE, TILES_DEV * TILE_SIDE), jnp.float32),
            jax.ShapeDtypeStruct((6, slots_total, BLOCK), jnp.float32),
            jax.ShapeDtypeStruct((slots_total, COEF_ROWS, BLOCK), jnp.bfloat16),
            jax.ShapeDtypeStruct((slots_total, 5, SEGMENTS, side), jnp.float32),
        ),
        in_specs=[smem(), vmem(), vmem()],
        out_specs=(vmem(), vmem(), vmem(), vmem()),
        scratch_shapes=[
            pltpu.VMEM((slots_total * COEF_ROWS, BLOCK), jnp.float32),
            pltpu.VMEM((TILES_DEV + 1, 8, side), jnp.float32),
            pltpu.VMEM((COEF_ROWS, side), jnp.bfloat16),
        ],
        compiler_params=pltpu.CompilerParams(vmem_limit_bytes=VMEM_ROOM),
        name="draw_tiles",
    )(tile_ids, received, slots)


def pull_tiles(tile_ids, recs, coefs, saved, grads, slots, own):
    slots_total = coefs.shape[0]
    side = TILE_SIDE * TILE_SIDE
    chunks = own // BLOCK
    return pl.pallas_call(
        backward_kernel,
        out_shape=jax.ShapeDtypeStruct((FIELDS, own), jnp.float32),
        in_specs=[smem(), vmem(), vmem(), vmem(), vmem(), vmem()],
        out_specs=vmem(),
        scratch_shapes=[
            pltpu.VMEM((TILES_DEV, COEF_ROWS, 2 * side), jnp.bfloat16),
            pltpu.VMEM((slots_total, 16, BLOCK), jnp.float32),
            pltpu.VMEM((slots_total, GRAD_ROWS, BLOCK), jnp.float32),
            pltpu.VMEM((2, slots_total, BLOCK), jnp.int32),
            pltpu.VMEM((2 * FIELDS * chunks, BLOCK), jnp.float32),
        ],
        compiler_params=pltpu.CompilerParams(vmem_limit_bytes=VMEM_ROOM),
        name="pull_tiles",
    )(tile_ids, recs, coefs, saved, grads, slots)


WAYS = [(down, right) for down in (-1, 0, 1) for right in (-1, 0, 1) if (down, right) != (0, 0)]
NORM = sum(math.exp(-m * m / 4.5) for m in range(-5, 6))
EXT_ROWS = 40
MID_ROWS = 32


def neighbour(bands, columns, way):
    there_band = lax.axis_index("gauss") + way[0]
    there_col = lax.axis_index("tile") + way[1]
    exists = (there_band >= 0) & (there_band < bands) & (there_col >= 0) & (there_col < columns)
    return exists, (there_band, there_col)


def greet_round(bands, columns):
    barrier = pltpu.get_barrier_semaphore()
    peers = jnp.int32(0)
    for way in WAYS:
        exists, there = neighbour(bands, columns, way)
        peers = peers + exists.astype(jnp.int32)

        @pl.when(exists)
        def _(there=there):
            pl.semaphore_signal(barrier, inc=1, device_id=there, device_id_type=MESH)

    return barrier, peers


def border_copies(bands, columns, plane_ref, edge_ref, tall_ref, side_ref, send_sem, recv_sem):
    found = []
    for at, way in enumerate(WAYS):
        exists, there = neighbour(bands, columns, way)
        landing = len(WAYS) - 1 - at
        source = plane_ref if way[1] == 0 else edge_ref
        target = tall_ref.at[landing] if way[1] == 0 else side_ref.at[landing]
        found.append(
            (
                exists,
                pltpu.make_async_remote_copy(
                    src_ref=source,
                    dst_ref=target,
                    send_sem=send_sem.at[at],
                    recv_sem=recv_sem.at[landing],
                    device_id=there,
                    device_id_type=MESH,
                ),
                pltpu.make_async_remote_copy(
                    src_ref=source,
                    dst_ref=tall_ref.at[at] if way[1] == 0 else side_ref.at[at],
                    send_sem=send_sem.at[at],
                    recv_sem=recv_sem.at[at],
                    device_id=there,
                    device_id_type=MESH,
                ),
            )
        )
    return found


def border_start(copies):
    for exists, out, back in copies:

        @pl.when(exists)
        def _(out=out):
            out.start()


def border_wait(copies):
    for exists, out, back in copies:

        @pl.when(exists)
        def _(out=out, back=back):
            out.wait_send()
            back.wait_recv()


def pack_edges(plane_ref, edge_ref):
    lanes = lax.broadcasted_iota(jnp.int32, edge_ref.shape, 1)
    packed = jnp.zeros(edge_ref.shape, jnp.float32)
    for c in range(3):
        plane = plane_ref[c]
        near = pltpu.roll(plane, 32 * c, 1) if c else plane
        far = pltpu.roll(plane, 32 * c + 32, 1)
        packed = jnp.where(
            lanes // 32 == c, jnp.where(lanes % 32 < 16, near, far), packed
        )
    edge_ref[...] = packed


def stretch(above, own, below):
    turn = lax.broadcasted_iota(jnp.int32, (8, own.shape[1]), 0) >= 6
    mixed = jnp.where(turn, above[0:8], below[8:16])
    return jnp.concatenate([own, above[8:16], below[0:8], mixed], axis=0)


def extend(plane_ref, tall_ref, side_ref):
    east = lax.broadcasted_iota(jnp.int32, side_ref.shape[1:], 1) % 32 < 16
    borders = [
        jnp.where(east, side_ref[WAYS.index((down, 1))], side_ref[WAYS.index((down, -1))])
        for down in (-1, 0, 1)
    ]
    border = stretch(*borders)
    planes = []
    for c in range(3):
        main = stretch(
            tall_ref[WAYS.index((-1, 0)), c], plane_ref[c], tall_ref[WAYS.index((1, 0)), c]
        )
        turned = pltpu.roll(border, HALF - 32 * c, 1) if c else border
        planes.append(jnp.concatenate([main, turned], axis=1))
    return planes


def window_weight(gap):
    gap = gap.astype(jnp.float32)
    return jnp.where(jnp.abs(gap) < 5.5, jnp.exp(gap * gap / -4.5) * (1.0 / NORM), 0.0)


def split_rows(value):
    first = coarse(value)
    rest = value - first
    second = coarse(rest)
    return first, second, rest - second


def six_data(value, axis):
    first, second, third = split_rows(value)
    return jnp.concatenate([first, second, third, first, second, first], axis=axis).astype(
        jnp.bfloat16
    )


def six_weights(value, axis):
    first, second, third = split_rows(value)
    return jnp.concatenate([first, first, first, second, second, third], axis=axis).astype(
        jnp.bfloat16
    )


def ext_row(at):
    return jnp.where(at < 16, at, jnp.where(at < 24, at - 24, jnp.where(at < 38, at - 8, at - 48)))


def ext_col(at):
    return jnp.where(at < 144, at, jnp.where(at < 160, at - 160, 10000))


def mid_col(at):
    return jnp.where(at < 192, at, at - 256)


def iota(shape, axis):
    return lax.broadcasted_iota(jnp.int32, shape, axis)


def fdot(left, right):
    return jnp.dot(left, right, preferred_element_type=jnp.float32)


def contrast_kernel(
    bands, columns, shown_ref, aim_ref, out_ref,
    edge_ref, tall_ref, side_ref, wide_ref, back_ref, send_sem, recv_sem,
):
    band = lax.axis_index("gauss")
    column = lax.axis_index("tile")
    rows, cols = shown_ref.shape[1:]
    tall_ref[...] = jnp.zeros_like(tall_ref)
    side_ref[...] = jnp.zeros_like(side_ref)
    barrier, peers = greet_round(bands, columns)
    pack_edges(shown_ref, edge_ref)
    copies = border_copies(
        bands, columns, shown_ref, edge_ref, tall_ref, side_ref, send_sem, recv_sem
    )
    pl.semaphore_wait(barrier, peers)
    border_start(copies)
    wide = 2 * cols
    for half in range(2):
        lanes = slice(half * cols, (half + 1) * cols)
        shape = (wide, cols)
        across = window_weight(mid_col(iota(shape, 1) + half * cols) - ext_col(iota(shape, 0)))
        wide_ref[:, lanes] = six_weights(across, 0)
    back = window_weight(mid_col(iota((wide, cols), 0)) - iota((wide, cols), 1))
    back_ref[...] = six_weights(back, 0)
    shape = (MID_ROWS, EXT_ROWS)
    down = window_weight(iota(shape, 0) - 5 - ext_row(iota(shape, 1)))
    down = six_weights(down, 1)
    shape = (rows, MID_ROWS)
    up = six_weights(window_weight(iota(shape, 0) - iota(shape, 1) + 5), 1)
    border_wait(copies)
    pics = extend(shown_ref, tall_ref, side_ref)
    strips = []
    for kind in range(4):
        for c in range(3):
            pic, aim = pics[c], aim_ref[c]
            plane = (pic, aim, pic * pic + aim * aim, pic * aim)[kind] if kind > 1 else (
                pic if kind == 0 else aim
            )
            strips.append(fdot(down, six_data(plane, 0)))
    moments = fdot(six_data(jnp.concatenate(strips, axis=0), 1), wide_ref[...])
    shape = (MID_ROWS, wide)
    row_at = band * rows + iota(shape, 0) - 5
    col_at = column * cols + mid_col(iota(shape, 1))
    inside = (row_at >= 0) & (row_at < bands * rows) & (col_at >= 0) & (col_at < columns * cols)
    strips = [None] * 9
    for c in range(3):
        mu_x, mu_y, squares, cross = [
            moments[(3 * kind + c) * MID_ROWS : (3 * kind + c + 1) * MID_ROWS] for kind in range(4)
        ]
        mean_xy = mu_x * mu_y
        mean_sq = mu_x * mu_x + mu_y * mu_y
        top_1 = 2.0 * mean_xy + CONST_ONE
        top_2 = 2.0 * (cross - mean_xy) + CONST_TWO
        low_1 = mean_sq + CONST_ONE
        low_2 = squares - mean_sq + CONST_TWO
        inverse = -0.2 / (low_1 * low_2)
        value = top_1 * top_2 * inverse
        value_1 = value * low_2 * inverse * -5.0
        value_2 = value * low_1 * inverse * -5.0
        slope_mean = 2.0 * mu_y * (top_2 - top_1) * inverse - 2.0 * mu_x * (value_1 - value_2)
        for kind, slope in enumerate((slope_mean, -value_2, 2.0 * top_1 * inverse)):
            strips[3 * kind + c] = fdot(up, six_data(jnp.where(inside, slope, 0.0), 0))
    spread = fdot(six_data(jnp.concatenate(strips, axis=0), 1), back_ref[...])
    lane_row = iota((SEGMENTS, HALF), 1) // TILE_SIDE
    seg_at = iota((SEGMENTS, HALF), 0)
    out_ref[...] = jnp.zeros_like(out_ref)
    for c in range(3):
        pic = shown_ref[c]
        aim = aim_ref[c, 0:rows, 0:cols]
        parts = [spread[(3 * kind + c) * rows : (3 * kind + c + 1) * rows] for kind in range(3)]
        total = parts[0] + 2.0 * pic * parts[1] + aim * parts[2] + 1.6 * (pic - aim)
        for side in range(2):
            part = total[side * SEGMENTS : (side + 1) * SEGMENTS]
            skewed = pltpu.roll(part, 0, 1, stride=TILE_SIDE, stride_axis=0)
            for tile in range(TILES_DEV):
                moved = pltpu.roll(skewed, HALF - TILE_SIDE * tile, 1) if tile else skewed
                kept = jnp.where(lane_row == seg_at, moved, 0.0)
                out_ref[tile, c : c + 1, side * HALF : (side + 1) * HALF] = jnp.sum(
                    kept, axis=0, keepdims=True
                )


def border_scratch(rows, cols):
    ways = len(WAYS)
    return [
        pltpu.VMEM((rows, cols), jnp.float32),
        pltpu.VMEM((ways, 3, rows, cols), jnp.float32),
        pltpu.VMEM((ways, rows, cols), jnp.float32),
    ]


def contrast(rendered, aim):
    rows, cols = rendered.shape[1:]
    ways = len(WAYS)
    return pl.pallas_call(
        functools.partial(contrast_kernel, lax.axis_size("gauss"), lax.axis_size("tile")),
        out_shape=jax.ShapeDtypeStruct((TILES_DEV, 8, TILE_SIDE * TILE_SIDE), jnp.float32),
        in_specs=[vmem(), vmem()],
        out_specs=vmem(),
        scratch_shapes=border_scratch(rows, cols)
        + [
            pltpu.VMEM((12 * cols, 2 * cols), jnp.bfloat16),
            pltpu.VMEM((12 * cols, cols), jnp.bfloat16),
            pltpu.SemaphoreType.DMA((ways,)),
            pltpu.SemaphoreType.DMA((ways,)),
        ],
        compiler_params=pltpu.CompilerParams(
            collective_id=0, has_side_effects=True, vmem_limit_bytes=VMEM_ROOM
        ),
        name="contrast",
    )(rendered, aim)


PACKED = 8


def basis_rows(x, y, z):
    xx, yy, zz = x * x, y * y, z * z
    return [
        jnp.full_like(x, BASE_ZERO),
        -BASE_ONE * y,
        BASE_ONE * z,
        -BASE_ONE * x,
        BASE_TWO[0] * x * y,
        BASE_TWO[1] * y * z,
        BASE_TWO[2] * (2.0 * zz - xx - yy),
        BASE_TWO[3] * x * z,
        BASE_TWO[4] * (xx - yy),
        BASE_THREE[0] * y * (3.0 * xx - yy),
        BASE_THREE[1] * x * y * z,
        BASE_THREE[2] * y * (4.0 * zz - xx - yy),
        BASE_THREE[3] * z * (2.0 * zz - 3.0 * xx - 3.0 * yy),
        BASE_THREE[4] * x * (4.0 * zz - xx - yy),
        BASE_THREE[5] * z * (xx - yy),
        BASE_THREE[6] * x * (xx - 3.0 * yy),
    ]


def slope_rows(x, y, z):
    xx, yy, zz = x * x, y * y, z * z
    xy, yz, xz = x * y, y * z, x * z
    none = jnp.zeros_like(x)
    one = jnp.ones_like(x)
    two, three = BASE_TWO, BASE_THREE
    along_x = [
        none, none, none, -BASE_ONE * one,
        two[0] * y, none, -2.0 * two[2] * x, two[3] * z, 2.0 * two[4] * x,
        6.0 * three[0] * xy, three[1] * yz, -2.0 * three[2] * xy, -6.0 * three[3] * xz,
        three[4] * (4.0 * zz - 3.0 * xx - yy), 2.0 * three[5] * xz, three[6] * (3.0 * xx - 3.0 * yy),
    ]
    along_y = [
        none, -BASE_ONE * one, none, none,
        two[0] * x, two[1] * z, -2.0 * two[2] * y, none, -2.0 * two[4] * y,
        three[0] * (3.0 * xx - 3.0 * yy), three[1] * xz, three[2] * (4.0 * zz - xx - 3.0 * yy),
        -6.0 * three[3] * yz, -2.0 * three[4] * xy, -2.0 * three[5] * yz, -6.0 * three[6] * xy,
    ]
    along_z = [
        none, none, BASE_ONE * one, none,
        none, two[1] * y, 4.0 * two[2] * z, two[3] * x, none,
        none, three[1] * xy, 8.0 * three[2] * yz, three[3] * (6.0 * zz - 3.0 * xx - 3.0 * yy),
        8.0 * three[4] * xz, three[5] * (xx - yy), none,
    ]
    return along_x, along_y, along_z


def lane_of():
    return lax.broadcasted_iota(jnp.int32, (8, BLOCK), 1)


def row_of():
    return lax.broadcasted_iota(jnp.int32, (8, BLOCK), 0)


def gather_rows(table_ref, ninth_ref, chunks, index):
    index = jnp.broadcast_to(index, (8, BLOCK))
    fine = index % BLOCK
    chunk_at = index // BLOCK
    first = None
    ninth = jnp.zeros((8, BLOCK), jnp.float32)
    for chunk in range(chunks):
        got = pick(table_ref[0:8, chunk * BLOCK : (chunk + 1) * BLOCK], fine)
        first = got if chunk == 0 else jnp.where(chunk_at == chunk, got, first)
    for base in range(0, chunks, 8):
        got = pick(ninth_ref[base : base + 8, :], fine)
        ninth = ninth + jnp.where(chunk_at == row_of() + base, got, 0.0)
    return first, jnp.sum(ninth, axis=0, keepdims=True)


def pack_two(first, last):
    left = lane_of() < BLOCK // 2
    swapped = pltpu.roll(first, BLOCK // 2, 1)
    one = jnp.where(left, first, pltpu.roll(swapped, 4, 0))
    two = jnp.where(left, swapped, pltpu.roll(first, 4, 0))
    tail = row_of() >= 4
    ninth = jnp.broadcast_to(last, (8, BLOCK))
    return jnp.where(tail, ninth, one), jnp.where(tail, pltpu.roll(ninth, BLOCK // 2, 1), two)


def unpack_two(one, two):
    left = lane_of() < BLOCK // 2
    upper = jnp.where(left, one, pltpu.roll(two, BLOCK // 2, 1))
    lower = jnp.where(left, pltpu.roll(one, BLOCK // 2, 1), two)
    return jnp.where(row_of() < 4, upper, pltpu.roll(lower, 4, 0)), upper[4:5]


def ring(gap, owners):
    there = lax.axis_index("gauss") + gap
    return jnp.where(there >= owners, there - owners, there)


def greet(owners):
    barrier = pltpu.get_barrier_semaphore()
    column = lax.axis_index("tile")
    for gap in range(1, owners):
        pl.semaphore_signal(
            barrier, inc=1, device_id=(ring(gap, owners), column), device_id_type=MESH
        )
    return barrier


def parcel(owners, gap, out_ref, in_ref, send_sem, recv_sem):
    band = lax.axis_index("gauss")
    there = ring(gap, owners)
    return pltpu.make_async_remote_copy(
        src_ref=out_ref.at[there],
        dst_ref=in_ref.at[band],
        send_sem=send_sem.at[gap],
        recv_sem=recv_sem.at[gap],
        device_id=(there, lax.axis_index("tile")),
        device_id_type=MESH,
    )


def post(owners, out_ref, in_ref, send_sem, recv_sem):
    band = lax.axis_index("gauss")
    for gap in range(1, owners):
        parcel(owners, gap, out_ref, in_ref, send_sem, recv_sem).start()
    in_ref[band] = out_ref[band]


def take_in(owners, out_ref, in_ref, send_sem, recv_sem):
    for gap in range(1, owners):
        parcel(owners, gap, out_ref, in_ref, send_sem, recv_sem).wait()


def deliver_kernel(
    owners, columns, splats_ref, sh_ref, send_ref, target_ref, recv_ref, home_ref, aim_ref,
    table_ref, ninth_ref, edge_ref, tall_ref, side_ref, border_send, border_recv,
    out_ref, in_ref, send_sem, recv_sem,
):
    tall_ref[...] = jnp.zeros_like(tall_ref)
    side_ref[...] = jnp.zeros_like(side_ref)
    barrier = greet(owners)
    around, peers = greet_round(owners, columns)
    own = splats_ref.shape[1]
    chunks = own // BLOCK
    basis = jnp.concatenate(
        basis_rows(splats_ref[6:7, :], splats_ref[7:8, :], splats_ref[8:9, :]), axis=0
    )
    colours = [
        0.5 + jnp.sum(sh_ref[16 * c : 16 * (c + 1), :] * basis, axis=0, keepdims=True)
        for c in range(3)
    ]
    table_ref[0:6, :] = splats_ref[0:6, :]
    table_ref[6:8, :] = jnp.concatenate(colours[0:2], axis=0)
    for chunk in range(chunks):
        ninth_ref[chunk : chunk + 1, :] = colours[2][:, chunk * BLOCK : (chunk + 1) * BLOCK]
    for chunk in range(chunks):
        one, two = pack_two(
            *gather_rows(table_ref, ninth_ref, chunks, send_ref[chunk : chunk + 1, :])
        )
        out_ref[2 * chunk] = one
        out_ref[2 * chunk + 1] = two
    pack_edges(target_ref, edge_ref)
    pl.semaphore_wait(barrier, owners - 1 + peers)
    post(owners, out_ref, in_ref, send_sem, recv_sem)
    copies = border_copies(
        owners, columns, target_ref, edge_ref, tall_ref, side_ref, border_send, border_recv
    )
    border_start(copies)
    chunk_rows = lax.broadcasted_iota(jnp.int32, (chunks, BLOCK), 0)
    lanes = lax.broadcasted_iota(jnp.int32, (chunks, BLOCK), 1).astype(jnp.float32)
    lane_rows = lax.broadcasted_iota(jnp.int32, (BLOCK, BLOCK), 0)
    home = jnp.zeros((2 * chunks, BLOCK), jnp.float32)
    for chunk in range(chunks):
        index = send_ref[chunk : chunk + 1, :]
        hit = chunk_rows == index // BLOCK
        source = jnp.concatenate(
            [jnp.where(hit, float(chunk), 0.0), jnp.where(hit, lanes, 0.0)], axis=0
        ).astype(jnp.bfloat16)
        select = jnp.where(lane_rows == index % BLOCK, 1.0, 0.0).astype(jnp.bfloat16)
        home = home + lax.dot_general(source, select, ACROSS, preferred_element_type=jnp.float32)
    home_ref[...] = (home[:chunks] * float(BLOCK) + home[chunks:]).astype(jnp.int32)
    border_wait(copies)
    for c, plane in enumerate(extend(target_ref, tall_ref, side_ref)):
        aim_ref[c] = plane
    take_in(owners, out_ref, in_ref, send_sem, recv_sem)
    for chunk in range(chunks):
        first, ninth = unpack_two(in_ref[2 * chunk], in_ref[2 * chunk + 1])
        recv_ref[0:8, chunk * BLOCK : (chunk + 1) * BLOCK] = first
        recv_ref[8:9, chunk * BLOCK : (chunk + 1) * BLOCK] = ninth


def parcels(owners):
    return [
        pltpu.VMEM((owners, PACKED, BLOCK), jnp.float32),
        pltpu.VMEM((owners, PACKED, BLOCK), jnp.float32),
        pltpu.SemaphoreType.DMA((owners,)),
        pltpu.SemaphoreType.DMA((owners,)),
    ]


def deliver(splats, sh_coeffs, send_list, target):
    own = splats.shape[1]
    owners = lax.axis_size("gauss")
    rows, cols = target.shape[1:]
    ways = len(WAYS)
    return pl.pallas_call(
        functools.partial(deliver_kernel, owners, lax.axis_size("tile")),
        out_shape=(
            jax.ShapeDtypeStruct((FIELDS, own), jnp.float32),
            jax.ShapeDtypeStruct((own // BLOCK, BLOCK), jnp.int32),
            jax.ShapeDtypeStruct((3, EXT_ROWS, 2 * cols), jnp.float32),
        ),
        in_specs=[vmem()] * 4,
        out_specs=(vmem(), vmem(), vmem()),
        scratch_shapes=[
            pltpu.VMEM((8, own), jnp.float32),
            pltpu.VMEM((own // BLOCK, BLOCK), jnp.float32),
        ]
        + border_scratch(rows, cols)
        + [pltpu.SemaphoreType.DMA((ways,)), pltpu.SemaphoreType.DMA((ways,))]
        + parcels(owners),
        compiler_params=pltpu.CompilerParams(
            collective_id=1, has_side_effects=True, vmem_limit_bytes=VMEM_ROOM
        ),
        name="deliver",
    )(splats, sh_coeffs, send_list.reshape(own // BLOCK, BLOCK), target)


def home_kernel(owners, pulled_ref, splats_ref, in_ref, slope_ref, out_ref, send_sem, recv_sem):
    barrier = greet(owners)
    chunks = pulled_ref.shape[1] // BLOCK
    for chunk in range(chunks):
        lanes = slice(chunk * BLOCK, (chunk + 1) * BLOCK)
        one, two = pack_two(pulled_ref[0:8, lanes], pulled_ref[8:9, lanes])
        out_ref[2 * chunk] = one
        out_ref[2 * chunk + 1] = two
    pl.semaphore_wait(barrier, owners - 1)
    post(owners, out_ref, in_ref, send_sem, recv_sem)
    facing = [splats_ref[6 + d : 7 + d, :] for d in range(3)]
    slope_ref[0:16, :] = jnp.concatenate(basis_rows(*facing), axis=0)
    for d, rows in enumerate(slope_rows(*facing)):
        slope_ref[16 * (d + 1) : 16 * (d + 2), :] = jnp.concatenate(rows, axis=0)
    take_in(owners, out_ref, in_ref, send_sem, recv_sem)


def bring_home(pulled, splats):
    own = splats.shape[1]
    owners = lax.axis_size("gauss")
    landing, *rest = parcels(owners)[1:]
    return pl.pallas_call(
        functools.partial(home_kernel, owners),
        out_shape=(
            jax.ShapeDtypeStruct((owners, PACKED, BLOCK), jnp.float32),
            jax.ShapeDtypeStruct((64, own), jnp.float32),
        ),
        in_specs=[vmem()] * 2,
        out_specs=(vmem(), vmem()),
        scratch_shapes=[landing] + rest,
        compiler_params=pltpu.CompilerParams(
            collective_id=2, has_side_effects=True, vmem_limit_bytes=VMEM_ROOM
        ),
        name="bring_home",
    )(pulled, splats)


def settle_kernel(
    in_ref, slope_ref, home_ref, sh_ref, splat_grad_ref, sh_grad_ref, table_ref, ninth_ref
):
    chunks = sh_ref.shape[1] // BLOCK
    for chunk in range(chunks):
        first, ninth = unpack_two(in_ref[2 * chunk], in_ref[2 * chunk + 1])
        table_ref[:, chunk * BLOCK : (chunk + 1) * BLOCK] = first
        ninth_ref[chunk : chunk + 1, :] = ninth
    for chunk in range(chunks):
        lanes = slice(chunk * BLOCK, (chunk + 1) * BLOCK)
        first, last = gather_rows(table_ref, ninth_ref, chunks, home_ref[chunk : chunk + 1, :])
        splat_grad_ref[0:6, lanes] = first[0:6]
        tints = (first[6:7], first[7:8], last)
        basis = slope_ref[0:16, lanes]
        mixed = jnp.zeros((16, BLOCK), jnp.float32)
        for c in range(3):
            tint = jnp.broadcast_to(tints[c], (16, BLOCK))
            sh_grad_ref[16 * c : 16 * (c + 1), lanes] = tint * basis
            mixed = mixed + tint * sh_ref[16 * c : 16 * (c + 1), lanes]
        splat_grad_ref[6:9, lanes] = jnp.concatenate(
            [
                jnp.sum(mixed * slope_ref[16 * d : 16 * (d + 1), lanes], axis=0, keepdims=True)
                for d in (1, 2, 3)
            ],
            axis=0,
        )


def settle(landed, slopes, home, splats, sh_coeffs):
    own = splats.shape[1]
    return pl.pallas_call(
        settle_kernel,
        out_shape=(
            jax.ShapeDtypeStruct(splats.shape, jnp.float32),
            jax.ShapeDtypeStruct(sh_coeffs.shape, jnp.float32),
        ),
        in_specs=[vmem()] * 4,
        out_specs=(vmem(), vmem()),
        scratch_shapes=[
            pltpu.VMEM((8, own), jnp.float32),
            pltpu.VMEM((own // BLOCK, BLOCK), jnp.float32),
        ],
        compiler_params=pltpu.CompilerParams(vmem_limit_bytes=VMEM_ROOM),
        name="settle",
    )(landed, slopes, home, sh_coeffs)


def body(splats, sh_coeffs, send_list, block_slots, block_tiles, target):
    received, home, aim = deliver(splats, sh_coeffs, send_list, target)
    tile_ids = block_tiles[0]
    slot_rows = block_slots[0]
    rendered, recs, coefs, saved = draw_tiles(tile_ids, received, slot_rows)
    tile_grad = contrast(rendered, aim)
    pulled = pull_tiles(tile_ids, recs, coefs, saved, tile_grad, slot_rows, received.shape[1])
    landed, slopes = bring_home(pulled, splats)
    grad_splats, grad_sh = settle(landed, slopes, home, splats, sh_coeffs)
    return (rendered, grad_splats, grad_sh)


def solution(mesh):
    in_specs = (
        P(None, ("gauss", "tile")),
        P(None, ("gauss", "tile")),
        P(("gauss", "tile")),
        P("gauss", "tile", None),
        P("gauss", "tile"),
        P(None, "gauss", "tile"),
    )
    out_specs = (P(None, "gauss", "tile"), P(None, ("gauss", "tile")), P(None, ("gauss", "tile")))
    return jax.shard_map(body, mesh=mesh, in_specs=in_specs, out_specs=out_specs, check_vma=False)
```

```python
import functools
import math

import jax
import jax.numpy as jnp
from jax import lax
from jax.experimental import pallas as pl
from jax.experimental.pallas import tpu as pltpu
from jax.sharding import PartitionSpec as P

TILE_SIDE = 16
TILES_DEV = 8


BASE_ZERO = 0.28209479177387814
BASE_ONE = 0.4886025119029199
BASE_TWO = (
    1.0925484305920792,
    -1.0925484305920792,
    0.31539156525252005,
    -1.0925484305920792,
    0.5462742152960396,
)
BASE_THREE = (
    -0.5900435899266435,
    2.890611442640554,
    -0.4570457994644658,
    0.3731763325901154,
    -0.4570457994644658,
    1.445305721320277,
    -0.5900435899266435,
)
CONST_ONE = 0.0001
CONST_TWO = 0.0009


SEGMENTS = 8
STEPS = 16
BLOCK = SEGMENTS * STEPS
HALF = 128
CENTRE = 7.5
MESH = pl.DeviceIdType.MESH
VMEM_ROOM = 60 * 1024 * 1024


LOG2E = 1.4426950408889634
FIELDS = 9
COEF_ROWS = 48
GROUP = 8
WIDTH = 2
GRAD_ROWS = 24
ACROSS = (((1,), (1,)), ((), ()))
DOWN = (((0,), (0,)), ((), ()))


def pick(table, index):
    return jnp.take_along_axis(table, index, axis=1, mode="promise_in_bounds")


def coarse(value):
    return value.astype(jnp.bfloat16).astype(jnp.float32)


def halves(value):
    high = value.astype(jnp.bfloat16)
    low = (value - high.astype(jnp.float32)).astype(jnp.bfloat16)
    return high, low


def pixel_basis():
    rows = lax.broadcasted_iota(jnp.int32, (8, 2 * HALF), 0)
    pixels = lax.broadcasted_iota(jnp.int32, (8, 2 * HALF), 1)
    along = (pixels % TILE_SIDE).astype(jnp.float32) - CENTRE
    down = (pixels // TILE_SIDE).astype(jnp.float32) - CENTRE
    basis = jnp.zeros((8, 2 * HALF), jnp.float32)
    terms = (along * along, along * down, down * down, along, down, jnp.ones_like(along))
    for at, term in enumerate(terms):
        basis = jnp.where(rows == at, term, basis)
    return basis


def spread_order(slots):
    lanes = lax.broadcasted_iota(jnp.int32, slots.shape, 1)
    return pick(slots, (lanes % SEGMENTS) * STEPS + lanes // SEGMENTS)


def tiles_of(tile_ref, first):
    at = lax.broadcasted_iota(jnp.int32, (SEGMENTS, BLOCK), 0)
    tiles = jnp.zeros((SEGMENTS, BLOCK), jnp.int32)
    for k in range(SEGMENTS):
        tiles = jnp.where(at == k, tile_ref[first + k], tiles)
    return tiles


def live_slots(tile_ref):
    live = jnp.int32(0)
    for slot in range(tile_ref.shape[0]):
        live = live + (tile_ref[slot] < TILES_DEV).astype(jnp.int32)
    return live


def forward_kernel(
    tile_ref, recv_ref, slots_ref, picture_ref, rec_ref, coef_ref, saved_ref,
    work_ref, image_ref, basis_ref,
):
    live = live_slots(tile_ref)
    chunks = recv_ref.shape[1] // BLOCK
    origin_x = (lax.axis_index("tile") * (TILE_SIDE * TILES_DEV)).astype(jnp.float32) + CENTRE
    origin_y = (lax.axis_index("gauss") * TILE_SIDE).astype(jnp.float32) + CENTRE
    work_ref[...] = jnp.zeros_like(work_ref)
    basis = pixel_basis()
    basis_ref[...] = jnp.concatenate([basis] * 3 + [jnp.zeros_like(basis)] * 3, axis=0).astype(
        jnp.bfloat16
    )

    def collect(group, carry):
        first = group * SEGMENTS
        slots = spread_order(slots_ref[pl.ds(pl.multiple_of(first, SEGMENTS), SEGMENTS), :])
        fine = slots % BLOCK
        chunk_at = slots // BLOCK
        found = [None] * FIELDS
        for chunk in range(chunks):
            hit = chunk_at == chunk
            for f in range(FIELDS):
                row = recv_ref[f : f + 1, chunk * BLOCK : (chunk + 1) * BLOCK]
                got = pick(jnp.broadcast_to(row, (SEGMENTS, BLOCK)), fine)
                found[f] = got if chunk == 0 else jnp.where(hit, got, found[f])
        tiles = tiles_of(tile_ref, first)
        base_x = (TILE_SIDE * jnp.minimum(tiles, TILES_DEV - 1)).astype(jnp.float32) + origin_x
        at_x = found[0] - base_x
        at_y = found[1] - origin_y
        con_a = -0.5 * found[2]
        con_b = -found[3]
        con_c = -0.5 * found[4]
        shut = 1.0 + jnp.exp(-found[5])
        for k, value in enumerate((at_x, at_y, con_a, con_b, con_c, 1.0 - 1.0 / shut)):
            rec_ref[k, pl.ds(pl.multiple_of(first, SEGMENTS), SEGMENTS), :] = value
        part_x = con_a * at_x
        part_y = con_c * at_y
        cross = con_b * at_y
        level = at_x * (part_x + cross) + at_y * part_y
        terms = (
            LOG2E * con_a,
            LOG2E * con_b,
            LOG2E * con_c,
            -LOG2E * (2.0 * part_x + cross),
            -LOG2E * (2.0 * part_y + con_b * at_x),
            LOG2E * (level - jnp.log(shut)),
        )

        def put(row, value):
            work_ref[pl.ds(first * COEF_ROWS + row, SEGMENTS, stride=COEF_ROWS), :] = value

        for k, term in enumerate(terms):
            high = coarse(term)
            rest = term - high
            middle = coarse(rest)
            put(k, high)
            put(8 + k, middle)
            put(16 + k, rest - middle)
        for c in range(3):
            high = coarse(found[6 + c])
            put(24 + c, high)
            put(32 + c, found[6 + c] - high)
            put(40 + c, high)
        return carry

    lax.fori_loop(0, (live + SEGMENTS - 1) // SEGMENTS, collect, 0)
    seg_at = lax.broadcasted_iota(jnp.int32, (SEGMENTS, HALF), 0)
    own_seg = seg_at == lax.broadcasted_iota(jnp.int32, (SEGMENTS, HALF), 1) % SEGMENTS

    def draw_local(slot):
        coefs = work_ref[pl.ds(pl.multiple_of(slot * COEF_ROWS, COEF_ROWS), COEF_ROWS), :].astype(
            jnp.bfloat16
        )
        coef_ref[slot] = coefs
        power = lax.dot_general(coefs, basis_ref[...], DOWN, preferred_element_type=jnp.float32)
        through = [jnp.ones((SEGMENTS, HALF), jnp.float32) for side in range(2)]
        weights = [[], []]
        for step in range(STEPS):
            for side in range(2):
                alpha = jnp.exp2(
                    power[step * SEGMENTS : (step + 1) * SEGMENTS, side * HALF : (side + 1) * HALF]
                )
                weight = alpha * through[side]
                through[side] = through[side] - weight
                weights[side].append(weight)
        weight = jnp.concatenate([jnp.concatenate(w, axis=0) for w in weights], axis=1)
        tints = []
        for part in (24, 32):
            for c in range(3):
                row = work_ref[pl.ds(slot * COEF_ROWS + part + c, 1), :]
                tints.append(jnp.where(own_seg, jnp.broadcast_to(row, (SEGMENTS, HALF)), 0.0))
        tint = jnp.concatenate(tints, axis=0).astype(jnp.bfloat16)
        sums = jnp.dot(
            jnp.concatenate([tint, tint], axis=1),
            jnp.concatenate(halves(weight), axis=0),
            preferred_element_type=jnp.float32,
        )
        return through, sums[0:24] + sums[24:48]

    def draw_join(slot, carry, through, sums):
        tile = tile_ref[slot]
        fresh = (slot == 0) | (tile != tile_ref[jnp.maximum(slot - 1, 0)])
        after = []
        for side in range(2):
            start = jnp.where(fresh, 1.0, carry[side])
            running = through[side]
            for shift in (1, 2, 4):
                running = jnp.where(
                    seg_at >= shift, running * pltpu.roll(running, shift, 0), running
                )
            before = jnp.where(seg_at == 0, 1.0, pltpu.roll(running, 1, 0)) * start
            after.append(start * running[SEGMENTS - 1 : SEGMENTS])
            lanes = slice(side * HALF, (side + 1) * HALF)
            saved_ref[slot, 0, :, lanes] = before
            saved_ref[slot, 1, :, lanes] = through[side]
            for c in range(3):
                part = sums[c * SEGMENTS : (c + 1) * SEGMENTS, lanes]
                saved_ref[slot, 2 + c, :, lanes] = part
                shade_sum = jnp.sum(before * part, axis=0, keepdims=True)
                held = jnp.where(fresh, 0.0, image_ref[tile, c : c + 1, lanes])
                image_ref[tile, c : c + 1, lanes] = held + shade_sum
        return tuple(after)

    def draw(pair, carry):
        locals_two = [draw_local(GROUP * pair + k) for k in range(GROUP)]
        for k in range(GROUP):
            carry = draw_join(GROUP * pair + k, carry, *locals_two[k])
        return carry

    ones = jnp.ones((1, HALF), jnp.float32)
    lax.fori_loop(0, (live + GROUP - 1) // GROUP, draw, (ones, ones))
    lane_tile = lax.broadcasted_iota(jnp.int32, (SEGMENTS, HALF), 1) // TILE_SIDE
    for side in range(2):
        lanes = slice(side * HALF, (side + 1) * HALF)
        for c in range(3):
            shown = jnp.zeros((SEGMENTS, HALF), jnp.float32)
            for tile in range(TILES_DEV):
                row = jnp.broadcast_to(image_ref[tile, c : c + 1, lanes], (SEGMENTS, HALF))
                moved = pltpu.roll(row, TILE_SIDE * tile, 1) if tile else row
                for bit in (1, 2, 4):
                    moved = jnp.where(
                        (seg_at & bit) > 0, pltpu.roll(moved, HALF - TILE_SIDE * bit, 1), moved
                    )
                shown = jnp.where(lane_tile == tile, moved, shown)
            picture_ref[c, side * SEGMENTS : (side + 1) * SEGMENTS, :] = shown


def backward_kernel(
    tile_ref, rec_ref, coef_ref, saved_ref, grad_ref, slots_ref, out_ref,
    rhs_ref, mom_ref, back_ref, where_ref, acc_ref,
    alpha_ref, lit_ref, share_ref, heavy_ref, force_ref, behind_ref,
):
    live = live_slots(tile_ref)
    chunks = out_ref.shape[1] // BLOCK
    slots_total = coef_ref.shape[0]
    acc_ref[...] = jnp.zeros_like(acc_ref)
    basis = pixel_basis()
    blank = jnp.zeros_like(basis)
    basis16 = jnp.concatenate([basis, blank], axis=0).astype(jnp.bfloat16)
    for tile in range(TILES_DEV):
        grads = grad_ref[tile]
        high = coarse(grads)
        rhs_ref[tile, :, 0 : 2 * HALF] = jnp.concatenate([basis] * 3 + [blank] * 3, axis=0).astype(
            jnp.bfloat16
        )
        rhs_ref[tile, :, 2 * HALF : 4 * HALF] = jnp.concatenate(
            [blank] * 3 + [high, high, grads - high], axis=0
        ).astype(jnp.bfloat16)
    seg_at = lax.broadcasted_iota(jnp.int32, (SEGMENTS, HALF), 0)

    def prepare(slot, carry, buf):
        tile = tile_ref[slot]
        final = (slot >= live - 1) | (tile != tile_ref[jnp.minimum(slot + 1, slots_total - 1)])
        shown = jnp.minimum(tile, TILES_DEV - 1)
        grads = grad_ref[shown]
        after = []
        for side in range(2):
            lanes = slice(side * HALF, (side + 1) * HALF)
            start = jnp.where(final, 0.0, carry[side])
            total = grads[0:1, lanes] * saved_ref[slot, 2, :, lanes]
            for c in (1, 2):
                total = total + grads[c : c + 1, lanes] * saved_ref[slot, 2 + c, :, lanes]
            factor = saved_ref[slot, 1, :, lanes]
            for shift in (1, 2, 4):
                inside = seg_at < SEGMENTS - shift
                total = jnp.where(
                    inside, total + factor * pltpu.roll(total, SEGMENTS - shift, 0), total
                )
                factor = jnp.where(
                    inside, factor * pltpu.roll(factor, SEGMENTS - shift, 0), factor
                )
            entering = total + factor * start
            after.append(entering[0:1])
            behind_ref[buf, :, lanes] = jnp.where(
                seg_at < SEGMENTS - 1, pltpu.roll(entering, SEGMENTS - 1, 0), start
            )
        both = lax.dot_general(
            coef_ref[slot], rhs_ref[shown], DOWN, preferred_element_type=jnp.float32
        )
        alpha_ref[buf] = jnp.exp2(both[:, : 2 * HALF])
        lit_ref[buf] = both[:, 2 * HALF :]
        return tuple(after)

    def halve(target_ref, buf, step, lanes, pair):
        value = jnp.concatenate(pair, axis=0)
        high, low = halves(value)
        rows = 2 * SEGMENTS * step
        target_ref[buf, rows : rows + 2 * SEGMENTS, lanes] = high
        target_ref[buf, BLOCK + rows : BLOCK + rows + 2 * SEGMENTS, lanes] = low

    def trace(slots, bufs):
        chains = [(k, side) for k in range(len(slots)) for side in range(2)]
        lanes = [slice(side * HALF, (side + 1) * HALF) for side in range(2)]
        through = {
            (k, side): saved_ref[slots[k], 0, :, lanes[side]] for k, side in chains
        }
        for step in range(STEPS // 2):
            for k, side in chains:
                pair = []
                for at in (2 * step, 2 * step + 1):
                    rows = slice(at * SEGMENTS, (at + 1) * SEGMENTS)
                    weight = alpha_ref[bufs[k], rows, lanes[side]] * through[k, side]
                    through[k, side] = through[k, side] - weight
                    share_ref[bufs[k], rows, lanes[side]] = weight
                    pair.append(weight)
                halve(heavy_ref, bufs[k], step, lanes[side], pair)
        later = {(k, side): behind_ref[bufs[k], :, lanes[side]] for k, side in chains}
        for step in reversed(range(STEPS // 2)):
            for k, side in chains:
                pair = []
                for at in (2 * step + 1, 2 * step):
                    rows = slice(at * SEGMENTS, (at + 1) * SEGMENTS)
                    gap = lit_ref[bufs[k], rows, lanes[side]] - later[k, side]
                    later[k, side] = later[k, side] + alpha_ref[bufs[k], rows, lanes[side]] * gap
                    pair.append(share_ref[bufs[k], rows, lanes[side]] * gap)
                halve(force_ref, bufs[k], step, lanes[side], pair[::-1])

    def reduce(slot, place, buf):
        shown = jnp.minimum(tile_ref[slot], TILES_DEV - 1)
        found = lax.dot_general(
            basis16, force_ref[buf], ACROSS, preferred_element_type=jnp.float32
        )
        painted = lax.dot_general(
            jnp.concatenate(halves(grad_ref[shown]), axis=0),
            heavy_ref[buf],
            ACROSS,
            preferred_element_type=jnp.float32,
        )
        painted = painted[0:8] + painted[8:16]
        mom_ref[place, 0:8, :] = found[0:8, :BLOCK] + found[0:8, BLOCK:]
        mom_ref[place, 8:16, :] = painted[:, :BLOCK] + painted[:, BLOCK:]

    runs = (live + WIDTH - 1) // WIDTH

    def slot_of(run, k):
        return jnp.clip(runs - 1 - run, 0, slots_total // WIDTH - 1) * WIDTH + k

    def ready(run, carry, half):
        for k in reversed(range(WIDTH)):
            carry = prepare(slot_of(run, k), carry, half * WIDTH + k)
        return carry

    def pull(turn, carry):
        for part in range(4):
            half = part % 2
            run = 4 * turn + part
            for k in range(WIDTH):
                slot = slot_of(run - 1, k)
                late = (run == 0) | (run > runs)
                reduce(slot, jnp.where(late, slots_total, slot), (1 - half) * WIDTH + k)
            carry = ready(run + 1, carry, 1 - half)
            trace(
                [slot_of(run, k) for k in range(WIDTH)],
                [half * WIDTH + k for k in range(WIDTH)],
            )
        return carry

    zeros = jnp.zeros((1, HALF), jnp.float32)
    carry = ready(0, (zeros, zeros), 0)
    lax.fori_loop(0, (runs + 4) // 4, pull, carry)
    lane_rows = lax.broadcasted_iota(jnp.int32, (BLOCK, 4 * BLOCK), 0)
    chunk_rows = lax.broadcasted_iota(jnp.int32, (chunks, BLOCK), 0)

    def settle(group, carry):
        first = pl.multiple_of(group * SEGMENTS, SEGMENTS)
        tiles = tiles_of(tile_ref, first)
        used = tiles < TILES_DEV
        rows = pl.ds(first, SEGMENTS)

        m_xx, m_xy, m_yy, m_x, m_y, m_0 = [
            mom_ref[rows, k, :] for k in range(6)
        ]
        at_x, at_y, con_a, con_b, con_c, shut_s = [rec_ref[k, rows, :] for k in range(6)]
        h_x = m_x - at_x * m_0
        h_y = m_y - at_y * m_0
        h_xx = m_xx - 2.0 * at_x * m_x + at_x * at_x * m_0
        h_xy = m_xy - at_x * m_y - at_y * m_x + at_x * at_y * m_0
        h_yy = m_yy - 2.0 * at_y * m_y + at_y * at_y * m_0
        results = [
            -2.0 * con_a * h_x - con_b * h_y,
            -2.0 * con_c * h_y - con_b * h_x,
            -0.5 * h_xx,
            -h_xy,
            -0.5 * h_yy,
            shut_s * m_0,
        ] + [mom_ref[rows, 8 + c, :] for c in range(3)]
        for f, value in enumerate(results):
            kept = jnp.where(used, value, 0.0)
            high = coarse(kept)
            back_ref[rows, f, :] = high
            back_ref[rows, 12 + f, :] = kept - high
        slots = spread_order(slots_ref[rows, :])
        where_ref[0, rows, :] = slots % BLOCK
        where_ref[1, rows, :] = slots // BLOCK
        for quad in range(0, SEGMENTS, 4):
            stacked = []
            for k in range(quad, quad + 4):
                hit = chunk_rows == where_ref[1, pl.ds(first + k, 1), :]
                stacked.append(
                    jnp.concatenate(
                        [
                            jnp.where(hit, back_ref[first + k, part + f : part + f + 1, :], 0.0)
                            for part in (0, 12)
                            for f in range(FIELDS)
                        ],
                        axis=0,
                    ).astype(jnp.bfloat16)
                )
            fine = jnp.concatenate(
                [where_ref[0, pl.ds(first + k, 1), :] for k in range(quad, quad + 4)], axis=1
            )
            select = jnp.where(lane_rows == fine, 1.0, 0.0).astype(jnp.bfloat16)
            acc_ref[...] += lax.dot_general(
                jnp.concatenate(stacked, axis=1), select, ACROSS, preferred_element_type=jnp.float32
            )
        return carry

    lax.fori_loop(0, (live + SEGMENTS - 1) // SEGMENTS, settle, 0)
    total = FIELDS * chunks
    for chunk in range(chunks):
        lanes = slice(chunk * BLOCK, (chunk + 1) * BLOCK)
        out_ref[0:8, lanes] = (
            acc_ref[pl.ds(chunk, 8, stride=chunks), :]
            + acc_ref[pl.ds(total + chunk, 8, stride=chunks), :]
        )
        at = 8 * chunks + chunk
        out_ref[8:9, lanes] = acc_ref[at : at + 1, :] + acc_ref[total + at : total + at + 1, :]


def smem():
    return pl.BlockSpec(memory_space=pltpu.SMEM)


def vmem():
    return pl.BlockSpec(memory_space=pltpu.VMEM)


def draw_tiles(tile_ids, received, slots):
    slots_total = slots.shape[0]
    side = TILE_SIDE * TILE_SIDE
    return pl.pallas_call(
        forward_kernel,
        out_shape=(
            jax.ShapeDtypeStruct((3, TILE_SIDE, TILES_DEV * TILE_SIDE), jnp.float32),
            jax.ShapeDtypeStruct((6, slots_total, BLOCK), jnp.float32),
            jax.ShapeDtypeStruct((slots_total, COEF_ROWS, BLOCK), jnp.bfloat16),
            jax.ShapeDtypeStruct((slots_total, 5, SEGMENTS, side), jnp.float32),
        ),
        in_specs=[smem(), vmem(), vmem()],
        out_specs=(vmem(), vmem(), vmem(), vmem()),
        scratch_shapes=[
            pltpu.VMEM((slots_total * COEF_ROWS, BLOCK), jnp.float32),
            pltpu.VMEM((TILES_DEV + 1, 8, side), jnp.float32),
            pltpu.VMEM((COEF_ROWS, side), jnp.bfloat16),
        ],
        compiler_params=pltpu.CompilerParams(vmem_limit_bytes=VMEM_ROOM),
        name="draw_tiles",
    )(tile_ids, received, slots)


def pull_tiles(tile_ids, recs, coefs, saved, grads, slots, own):
    slots_total = coefs.shape[0]
    side = TILE_SIDE * TILE_SIDE
    chunks = own // BLOCK
    return pl.pallas_call(
        backward_kernel,
        out_shape=jax.ShapeDtypeStruct((FIELDS, own), jnp.float32),
        in_specs=[smem(), vmem(), vmem(), vmem(), vmem(), vmem()],
        out_specs=vmem(),
        scratch_shapes=[
            pltpu.VMEM((TILES_DEV, COEF_ROWS, 2 * side), jnp.bfloat16),
            pltpu.VMEM((slots_total + 1, 16, BLOCK), jnp.float32),
            pltpu.VMEM((slots_total, GRAD_ROWS, BLOCK), jnp.float32),
            pltpu.VMEM((2, slots_total, BLOCK), jnp.int32),
            pltpu.VMEM((2 * FIELDS * chunks, BLOCK), jnp.float32),
            pltpu.VMEM((2 * WIDTH, BLOCK, side), jnp.float32),
            pltpu.VMEM((2 * WIDTH, BLOCK, side), jnp.float32),
            pltpu.VMEM((2 * WIDTH, BLOCK, side), jnp.float32),
            pltpu.VMEM((2 * WIDTH, 2 * BLOCK, side), jnp.bfloat16),
            pltpu.VMEM((2 * WIDTH, 2 * BLOCK, side), jnp.bfloat16),
            pltpu.VMEM((2 * WIDTH, SEGMENTS, side), jnp.float32),
        ],
        compiler_params=pltpu.CompilerParams(vmem_limit_bytes=VMEM_ROOM),
        name="pull_tiles",
    )(tile_ids, recs, coefs, saved, grads, slots)


WAYS = [(down, right) for down in (-1, 0, 1) for right in (-1, 0, 1) if (down, right) != (0, 0)]
NORM = sum(math.exp(-m * m / 4.5) for m in range(-5, 6))
EXT_ROWS = 40
MID_ROWS = 32


def neighbour(bands, columns, way):
    there_band = lax.axis_index("gauss") + way[0]
    there_col = lax.axis_index("tile") + way[1]
    exists = (there_band >= 0) & (there_band < bands) & (there_col >= 0) & (there_col < columns)
    return exists, (there_band, there_col)


def greet_round(bands, columns):
    barrier = pltpu.get_barrier_semaphore()
    peers = jnp.int32(0)
    for way in WAYS:
        exists, there = neighbour(bands, columns, way)
        peers = peers + exists.astype(jnp.int32)

        @pl.when(exists)
        def _(there=there):
            pl.semaphore_signal(barrier, inc=1, device_id=there, device_id_type=MESH)

    return barrier, peers


def border_copies(bands, columns, plane_ref, edge_ref, tall_ref, side_ref, send_sem, recv_sem):
    found = []
    for at, way in enumerate(WAYS):
        exists, there = neighbour(bands, columns, way)
        landing = len(WAYS) - 1 - at
        source = plane_ref if way[1] == 0 else edge_ref
        target = tall_ref.at[landing] if way[1] == 0 else side_ref.at[landing]
        found.append(
            (
                exists,
                pltpu.make_async_remote_copy(
                    src_ref=source,
                    dst_ref=target,
                    send_sem=send_sem.at[at],
                    recv_sem=recv_sem.at[landing],
                    device_id=there,
                    device_id_type=MESH,
                ),
                pltpu.make_async_remote_copy(
                    src_ref=source,
                    dst_ref=tall_ref.at[at] if way[1] == 0 else side_ref.at[at],
                    send_sem=send_sem.at[at],
                    recv_sem=recv_sem.at[at],
                    device_id=there,
                    device_id_type=MESH,
                ),
            )
        )
    return found


def border_start(copies):
    for exists, out, back in copies:

        @pl.when(exists)
        def _(out=out):
            out.start()


def border_wait(copies):
    for exists, out, back in copies:

        @pl.when(exists)
        def _(out=out, back=back):
            out.wait_send()
            back.wait_recv()


def pack_edges(plane_ref, edge_ref):
    lanes = lax.broadcasted_iota(jnp.int32, edge_ref.shape, 1)
    packed = jnp.zeros(edge_ref.shape, jnp.float32)
    for c in range(3):
        plane = plane_ref[c]
        near = pltpu.roll(plane, 32 * c, 1) if c else plane
        far = pltpu.roll(plane, 32 * c + 32, 1)
        packed = jnp.where(
            lanes // 32 == c, jnp.where(lanes % 32 < 16, near, far), packed
        )
    edge_ref[...] = packed


def stretch(above, own, below):
    turn = lax.broadcasted_iota(jnp.int32, (8, own.shape[1]), 0) >= 6
    mixed = jnp.where(turn, above[0:8], below[8:16])
    return jnp.concatenate([own, above[8:16], below[0:8], mixed], axis=0)


def extend(plane_ref, tall_ref, side_ref):
    east = lax.broadcasted_iota(jnp.int32, side_ref.shape[1:], 1) % 32 < 16
    borders = [
        jnp.where(east, side_ref[WAYS.index((down, 1))], side_ref[WAYS.index((down, -1))])
        for down in (-1, 0, 1)
    ]
    border = stretch(*borders)
    planes = []
    for c in range(3):
        main = stretch(
            tall_ref[WAYS.index((-1, 0)), c], plane_ref[c], tall_ref[WAYS.index((1, 0)), c]
        )
        turned = pltpu.roll(border, HALF - 32 * c, 1) if c else border
        planes.append(jnp.concatenate([main, turned], axis=1))
    return planes


def window_weight(gap):
    gap = gap.astype(jnp.float32)
    return jnp.where(jnp.abs(gap) < 5.5, jnp.exp(gap * gap / -4.5) * (1.0 / NORM), 0.0)


def split_rows(value):
    first = coarse(value)
    rest = value - first
    second = coarse(rest)
    return first, second, rest - second


def six_data(value, axis):
    first, second, third = split_rows(value)
    return jnp.concatenate([first, second, third, first, second, first], axis=axis).astype(
        jnp.bfloat16
    )


def six_weights(value, axis):
    first, second, third = split_rows(value)
    return jnp.concatenate([first, first, first, second, second, third], axis=axis).astype(
        jnp.bfloat16
    )


def ext_row(at):
    return jnp.where(at < 16, at, jnp.where(at < 24, at - 24, jnp.where(at < 38, at - 8, at - 48)))


def ext_col(at):
    return jnp.where(at < 144, at, jnp.where(at < 160, at - 160, 10000))


def mid_col(at):
    return jnp.where(at < 192, at, at - 256)


def iota(shape, axis):
    return lax.broadcasted_iota(jnp.int32, shape, axis)


def fdot(left, right):
    return jnp.dot(left, right, preferred_element_type=jnp.float32)


def contrast_kernel(
    bands, columns, shown_ref, aim_ref, out_ref,
    edge_ref, tall_ref, side_ref, wide_ref, back_ref, send_sem, recv_sem,
):
    band = lax.axis_index("gauss")
    column = lax.axis_index("tile")
    rows, cols = shown_ref.shape[1:]
    tall_ref[...] = jnp.zeros_like(tall_ref)
    side_ref[...] = jnp.zeros_like(side_ref)
    barrier, peers = greet_round(bands, columns)
    pack_edges(shown_ref, edge_ref)
    copies = border_copies(
        bands, columns, shown_ref, edge_ref, tall_ref, side_ref, send_sem, recv_sem
    )
    pl.semaphore_wait(barrier, peers)
    border_start(copies)
    wide = 2 * cols
    for half in range(2):
        lanes = slice(half * cols, (half + 1) * cols)
        shape = (wide, cols)
        across = window_weight(mid_col(iota(shape, 1) + half * cols) - ext_col(iota(shape, 0)))
        wide_ref[:, lanes] = six_weights(across, 0)
    back = window_weight(mid_col(iota((wide, cols), 0)) - iota((wide, cols), 1))
    back_ref[...] = six_weights(back, 0)
    shape = (MID_ROWS, EXT_ROWS)
    down = window_weight(iota(shape, 0) - 5 - ext_row(iota(shape, 1)))
    down = six_weights(down, 1)
    shape = (rows, MID_ROWS)
    up = six_weights(window_weight(iota(shape, 0) - iota(shape, 1) + 5), 1)
    border_wait(copies)
    pics = extend(shown_ref, tall_ref, side_ref)
    strips = []
    for kind in range(4):
        for c in range(3):
            pic, aim = pics[c], aim_ref[c]
            plane = (pic, aim, pic * pic + aim * aim, pic * aim)[kind] if kind > 1 else (
                pic if kind == 0 else aim
            )
            strips.append(fdot(down, six_data(plane, 0)))
    moments = fdot(six_data(jnp.concatenate(strips, axis=0), 1), wide_ref[...])
    shape = (MID_ROWS, wide)
    row_at = band * rows + iota(shape, 0) - 5
    col_at = column * cols + mid_col(iota(shape, 1))
    inside = (row_at >= 0) & (row_at < bands * rows) & (col_at >= 0) & (col_at < columns * cols)
    strips = [None] * 9
    for c in range(3):
        mu_x, mu_y, squares, cross = [
            moments[(3 * kind + c) * MID_ROWS : (3 * kind + c + 1) * MID_ROWS] for kind in range(4)
        ]
        mean_xy = mu_x * mu_y
        mean_sq = mu_x * mu_x + mu_y * mu_y
        top_1 = 2.0 * mean_xy + CONST_ONE
        top_2 = 2.0 * (cross - mean_xy) + CONST_TWO
        low_1 = mean_sq + CONST_ONE
        low_2 = squares - mean_sq + CONST_TWO
        inverse = -0.2 / (low_1 * low_2)
        value = top_1 * top_2 * inverse
        value_1 = value * low_2 * inverse * -5.0
        value_2 = value * low_1 * inverse * -5.0
        slope_mean = 2.0 * mu_y * (top_2 - top_1) * inverse - 2.0 * mu_x * (value_1 - value_2)
        for kind, slope in enumerate((slope_mean, -value_2, 2.0 * top_1 * inverse)):
            strips[3 * kind + c] = fdot(up, six_data(jnp.where(inside, slope, 0.0), 0))
    spread = fdot(six_data(jnp.concatenate(strips, axis=0), 1), back_ref[...])
    lane_row = iota((SEGMENTS, HALF), 1) // TILE_SIDE
    seg_at = iota((SEGMENTS, HALF), 0)
    out_ref[...] = jnp.zeros_like(out_ref)
    for c in range(3):
        pic = shown_ref[c]
        aim = aim_ref[c, 0:rows, 0:cols]
        parts = [spread[(3 * kind + c) * rows : (3 * kind + c + 1) * rows] for kind in range(3)]
        total = parts[0] + 2.0 * pic * parts[1] + aim * parts[2] + 1.6 * (pic - aim)
        for side in range(2):
            part = total[side * SEGMENTS : (side + 1) * SEGMENTS]
            skewed = pltpu.roll(part, 0, 1, stride=TILE_SIDE, stride_axis=0)
            for tile in range(TILES_DEV):
                moved = pltpu.roll(skewed, HALF - TILE_SIDE * tile, 1) if tile else skewed
                kept = jnp.where(lane_row == seg_at, moved, 0.0)
                out_ref[tile, c : c + 1, side * HALF : (side + 1) * HALF] = jnp.sum(
                    kept, axis=0, keepdims=True
                )


def border_scratch(rows, cols):
    ways = len(WAYS)
    return [
        pltpu.VMEM((rows, cols), jnp.float32),
        pltpu.VMEM((ways, 3, rows, cols), jnp.float32),
        pltpu.VMEM((ways, rows, cols), jnp.float32),
    ]


def contrast(rendered, aim):
    rows, cols = rendered.shape[1:]
    ways = len(WAYS)
    return pl.pallas_call(
        functools.partial(contrast_kernel, lax.axis_size("gauss"), lax.axis_size("tile")),
        out_shape=jax.ShapeDtypeStruct((TILES_DEV, 8, TILE_SIDE * TILE_SIDE), jnp.float32),
        in_specs=[vmem(), vmem()],
        out_specs=vmem(),
        scratch_shapes=border_scratch(rows, cols)
        + [
            pltpu.VMEM((12 * cols, 2 * cols), jnp.bfloat16),
            pltpu.VMEM((12 * cols, cols), jnp.bfloat16),
            pltpu.SemaphoreType.DMA((ways,)),
            pltpu.SemaphoreType.DMA((ways,)),
        ],
        compiler_params=pltpu.CompilerParams(
            collective_id=0, has_side_effects=True, vmem_limit_bytes=VMEM_ROOM
        ),
        name="contrast",
    )(rendered, aim)


PACKED = 8


def basis_rows(x, y, z):
    xx, yy, zz = x * x, y * y, z * z
    return [
        jnp.full_like(x, BASE_ZERO),
        -BASE_ONE * y,
        BASE_ONE * z,
        -BASE_ONE * x,
        BASE_TWO[0] * x * y,
        BASE_TWO[1] * y * z,
        BASE_TWO[2] * (2.0 * zz - xx - yy),
        BASE_TWO[3] * x * z,
        BASE_TWO[4] * (xx - yy),
        BASE_THREE[0] * y * (3.0 * xx - yy),
        BASE_THREE[1] * x * y * z,
        BASE_THREE[2] * y * (4.0 * zz - xx - yy),
        BASE_THREE[3] * z * (2.0 * zz - 3.0 * xx - 3.0 * yy),
        BASE_THREE[4] * x * (4.0 * zz - xx - yy),
        BASE_THREE[5] * z * (xx - yy),
        BASE_THREE[6] * x * (xx - 3.0 * yy),
    ]


def slope_rows(x, y, z):
    xx, yy, zz = x * x, y * y, z * z
    xy, yz, xz = x * y, y * z, x * z
    none = jnp.zeros_like(x)
    one = jnp.ones_like(x)
    two, three = BASE_TWO, BASE_THREE
    along_x = [
        none, none, none, -BASE_ONE * one,
        two[0] * y, none, -2.0 * two[2] * x, two[3] * z, 2.0 * two[4] * x,
        6.0 * three[0] * xy, three[1] * yz, -2.0 * three[2] * xy, -6.0 * three[3] * xz,
        three[4] * (4.0 * zz - 3.0 * xx - yy), 2.0 * three[5] * xz, three[6] * (3.0 * xx - 3.0 * yy),
    ]
    along_y = [
        none, -BASE_ONE * one, none, none,
        two[0] * x, two[1] * z, -2.0 * two[2] * y, none, -2.0 * two[4] * y,
        three[0] * (3.0 * xx - 3.0 * yy), three[1] * xz, three[2] * (4.0 * zz - xx - 3.0 * yy),
        -6.0 * three[3] * yz, -2.0 * three[4] * xy, -2.0 * three[5] * yz, -6.0 * three[6] * xy,
    ]
    along_z = [
        none, none, BASE_ONE * one, none,
        none, two[1] * y, 4.0 * two[2] * z, two[3] * x, none,
        none, three[1] * xy, 8.0 * three[2] * yz, three[3] * (6.0 * zz - 3.0 * xx - 3.0 * yy),
        8.0 * three[4] * xz, three[5] * (xx - yy), none,
    ]
    return along_x, along_y, along_z


def lane_of():
    return lax.broadcasted_iota(jnp.int32, (8, BLOCK), 1)


def row_of():
    return lax.broadcasted_iota(jnp.int32, (8, BLOCK), 0)


def gather_rows(table_ref, ninth_ref, chunks, index):
    index = jnp.broadcast_to(index, (8, BLOCK))
    fine = index % BLOCK
    chunk_at = index // BLOCK
    first = None
    ninth = jnp.zeros((8, BLOCK), jnp.float32)
    for chunk in range(chunks):
        got = pick(table_ref[0:8, chunk * BLOCK : (chunk + 1) * BLOCK], fine)
        first = got if chunk == 0 else jnp.where(chunk_at == chunk, got, first)
    for base in range(0, chunks, 8):
        got = pick(ninth_ref[base : base + 8, :], fine)
        ninth = ninth + jnp.where(chunk_at == row_of() + base, got, 0.0)
    return first, jnp.sum(ninth, axis=0, keepdims=True)


def pack_two(first, last):
    left = lane_of() < BLOCK // 2
    swapped = pltpu.roll(first, BLOCK // 2, 1)
    one = jnp.where(left, first, pltpu.roll(swapped, 4, 0))
    two = jnp.where(left, swapped, pltpu.roll(first, 4, 0))
    tail = row_of() >= 4
    ninth = jnp.broadcast_to(last, (8, BLOCK))
    return jnp.where(tail, ninth, one), jnp.where(tail, pltpu.roll(ninth, BLOCK // 2, 1), two)


def unpack_two(one, two):
    left = lane_of() < BLOCK // 2
    upper = jnp.where(left, one, pltpu.roll(two, BLOCK // 2, 1))
    lower = jnp.where(left, pltpu.roll(one, BLOCK // 2, 1), two)
    return jnp.where(row_of() < 4, upper, pltpu.roll(lower, 4, 0)), upper[4:5]


def ring(gap, owners):
    there = lax.axis_index("gauss") + gap
    return jnp.where(there >= owners, there - owners, there)


def greet(owners):
    barrier = pltpu.get_barrier_semaphore()
    column = lax.axis_index("tile")
    for gap in range(1, owners):
        pl.semaphore_signal(
            barrier, inc=1, device_id=(ring(gap, owners), column), device_id_type=MESH
        )
    return barrier


def parcel(owners, gap, out_ref, in_ref, send_sem, recv_sem):
    band = lax.axis_index("gauss")
    there = ring(gap, owners)
    return pltpu.make_async_remote_copy(
        src_ref=out_ref.at[there],
        dst_ref=in_ref.at[band],
        send_sem=send_sem.at[gap],
        recv_sem=recv_sem.at[gap],
        device_id=(there, lax.axis_index("tile")),
        device_id_type=MESH,
    )


def post(owners, out_ref, in_ref, send_sem, recv_sem):
    band = lax.axis_index("gauss")
    for gap in range(1, owners):
        parcel(owners, gap, out_ref, in_ref, send_sem, recv_sem).start()
    in_ref[band] = out_ref[band]


def take_in(owners, out_ref, in_ref, send_sem, recv_sem):
    for gap in range(1, owners):
        parcel(owners, gap, out_ref, in_ref, send_sem, recv_sem).wait()


def deliver_kernel(
    owners, columns, splats_ref, sh_ref, send_ref, target_ref, recv_ref, home_ref, aim_ref,
    table_ref, ninth_ref, edge_ref, tall_ref, side_ref, border_send, border_recv,
    out_ref, in_ref, send_sem, recv_sem,
):
    tall_ref[...] = jnp.zeros_like(tall_ref)
    side_ref[...] = jnp.zeros_like(side_ref)
    barrier = greet(owners)
    around, peers = greet_round(owners, columns)
    own = splats_ref.shape[1]
    chunks = own // BLOCK
    basis = jnp.concatenate(
        basis_rows(splats_ref[6:7, :], splats_ref[7:8, :], splats_ref[8:9, :]), axis=0
    )
    colours = [
        0.5 + jnp.sum(sh_ref[16 * c : 16 * (c + 1), :] * basis, axis=0, keepdims=True)
        for c in range(3)
    ]
    table_ref[0:6, :] = splats_ref[0:6, :]
    table_ref[6:8, :] = jnp.concatenate(colours[0:2], axis=0)
    for chunk in range(chunks):
        ninth_ref[chunk : chunk + 1, :] = colours[2][:, chunk * BLOCK : (chunk + 1) * BLOCK]
    for chunk in range(chunks):
        one, two = pack_two(
            *gather_rows(table_ref, ninth_ref, chunks, send_ref[chunk : chunk + 1, :])
        )
        out_ref[2 * chunk] = one
        out_ref[2 * chunk + 1] = two
    pack_edges(target_ref, edge_ref)
    pl.semaphore_wait(barrier, owners - 1 + peers)
    post(owners, out_ref, in_ref, send_sem, recv_sem)
    copies = border_copies(
        owners, columns, target_ref, edge_ref, tall_ref, side_ref, border_send, border_recv
    )
    border_start(copies)
    chunk_rows = lax.broadcasted_iota(jnp.int32, (chunks, BLOCK), 0)
    lanes = lax.broadcasted_iota(jnp.int32, (chunks, BLOCK), 1).astype(jnp.float32)
    lane_rows = lax.broadcasted_iota(jnp.int32, (BLOCK, BLOCK), 0)
    home = jnp.zeros((2 * chunks, BLOCK), jnp.float32)
    for chunk in range(chunks):
        index = send_ref[chunk : chunk + 1, :]
        hit = chunk_rows == index // BLOCK
        source = jnp.concatenate(
            [jnp.where(hit, float(chunk), 0.0), jnp.where(hit, lanes, 0.0)], axis=0
        ).astype(jnp.bfloat16)
        select = jnp.where(lane_rows == index % BLOCK, 1.0, 0.0).astype(jnp.bfloat16)
        home = home + lax.dot_general(source, select, ACROSS, preferred_element_type=jnp.float32)
    home_ref[...] = (home[:chunks] * float(BLOCK) + home[chunks:]).astype(jnp.int32)
    border_wait(copies)
    for c, plane in enumerate(extend(target_ref, tall_ref, side_ref)):
        aim_ref[c] = plane
    take_in(owners, out_ref, in_ref, send_sem, recv_sem)
    for chunk in range(chunks):
        first, ninth = unpack_two(in_ref[2 * chunk], in_ref[2 * chunk + 1])
        recv_ref[0:8, chunk * BLOCK : (chunk + 1) * BLOCK] = first
        recv_ref[8:9, chunk * BLOCK : (chunk + 1) * BLOCK] = ninth


def parcels(owners):
    return [
        pltpu.VMEM((owners, PACKED, BLOCK), jnp.float32),
        pltpu.VMEM((owners, PACKED, BLOCK), jnp.float32),
        pltpu.SemaphoreType.DMA((owners,)),
        pltpu.SemaphoreType.DMA((owners,)),
    ]


def deliver(splats, sh_coeffs, send_list, target):
    own = splats.shape[1]
    owners = lax.axis_size("gauss")
    rows, cols = target.shape[1:]
    ways = len(WAYS)
    return pl.pallas_call(
        functools.partial(deliver_kernel, owners, lax.axis_size("tile")),
        out_shape=(
            jax.ShapeDtypeStruct((FIELDS, own), jnp.float32),
            jax.ShapeDtypeStruct((own // BLOCK, BLOCK), jnp.int32),
            jax.ShapeDtypeStruct((3, EXT_ROWS, 2 * cols), jnp.float32),
        ),
        in_specs=[vmem()] * 4,
        out_specs=(vmem(), vmem(), vmem()),
        scratch_shapes=[
            pltpu.VMEM((8, own), jnp.float32),
            pltpu.VMEM((own // BLOCK, BLOCK), jnp.float32),
        ]
        + border_scratch(rows, cols)
        + [pltpu.SemaphoreType.DMA((ways,)), pltpu.SemaphoreType.DMA((ways,))]
        + parcels(owners),
        compiler_params=pltpu.CompilerParams(
            collective_id=1, has_side_effects=True, vmem_limit_bytes=VMEM_ROOM
        ),
        name="deliver",
    )(splats, sh_coeffs, send_list.reshape(own // BLOCK, BLOCK), target)


def home_kernel(owners, pulled_ref, splats_ref, in_ref, slope_ref, out_ref, send_sem, recv_sem):
    barrier = greet(owners)
    chunks = pulled_ref.shape[1] // BLOCK
    for chunk in range(chunks):
        lanes = slice(chunk * BLOCK, (chunk + 1) * BLOCK)
        one, two = pack_two(pulled_ref[0:8, lanes], pulled_ref[8:9, lanes])
        out_ref[2 * chunk] = one
        out_ref[2 * chunk + 1] = two
    pl.semaphore_wait(barrier, owners - 1)
    post(owners, out_ref, in_ref, send_sem, recv_sem)
    facing = [splats_ref[6 + d : 7 + d, :] for d in range(3)]
    slope_ref[0:16, :] = jnp.concatenate(basis_rows(*facing), axis=0)
    for d, rows in enumerate(slope_rows(*facing)):
        slope_ref[16 * (d + 1) : 16 * (d + 2), :] = jnp.concatenate(rows, axis=0)
    take_in(owners, out_ref, in_ref, send_sem, recv_sem)


def bring_home(pulled, splats):
    own = splats.shape[1]
    owners = lax.axis_size("gauss")
    landing, *rest = parcels(owners)[1:]
    return pl.pallas_call(
        functools.partial(home_kernel, owners),
        out_shape=(
            jax.ShapeDtypeStruct((owners, PACKED, BLOCK), jnp.float32),
            jax.ShapeDtypeStruct((64, own), jnp.float32),
        ),
        in_specs=[vmem()] * 2,
        out_specs=(vmem(), vmem()),
        scratch_shapes=[landing] + rest,
        compiler_params=pltpu.CompilerParams(
            collective_id=2, has_side_effects=True, vmem_limit_bytes=VMEM_ROOM
        ),
        name="bring_home",
    )(pulled, splats)


def settle_kernel(
    in_ref, slope_ref, home_ref, sh_ref, splat_grad_ref, sh_grad_ref, table_ref, ninth_ref
):
    chunks = sh_ref.shape[1] // BLOCK
    for chunk in range(chunks):
        first, ninth = unpack_two(in_ref[2 * chunk], in_ref[2 * chunk + 1])
        table_ref[:, chunk * BLOCK : (chunk + 1) * BLOCK] = first
        ninth_ref[chunk : chunk + 1, :] = ninth
    for chunk in range(chunks):
        lanes = slice(chunk * BLOCK, (chunk + 1) * BLOCK)
        first, last = gather_rows(table_ref, ninth_ref, chunks, home_ref[chunk : chunk + 1, :])
        splat_grad_ref[0:6, lanes] = first[0:6]
        tints = (first[6:7], first[7:8], last)
        basis = slope_ref[0:16, lanes]
        mixed = jnp.zeros((16, BLOCK), jnp.float32)
        for c in range(3):
            tint = jnp.broadcast_to(tints[c], (16, BLOCK))
            sh_grad_ref[16 * c : 16 * (c + 1), lanes] = tint * basis
            mixed = mixed + tint * sh_ref[16 * c : 16 * (c + 1), lanes]
        splat_grad_ref[6:9, lanes] = jnp.concatenate(
            [
                jnp.sum(mixed * slope_ref[16 * d : 16 * (d + 1), lanes], axis=0, keepdims=True)
                for d in (1, 2, 3)
            ],
            axis=0,
        )


def settle(landed, slopes, home, splats, sh_coeffs):
    own = splats.shape[1]
    return pl.pallas_call(
        settle_kernel,
        out_shape=(
            jax.ShapeDtypeStruct(splats.shape, jnp.float32),
            jax.ShapeDtypeStruct(sh_coeffs.shape, jnp.float32),
        ),
        in_specs=[vmem()] * 4,
        out_specs=(vmem(), vmem()),
        scratch_shapes=[
            pltpu.VMEM((8, own), jnp.float32),
            pltpu.VMEM((own // BLOCK, BLOCK), jnp.float32),
        ],
        compiler_params=pltpu.CompilerParams(vmem_limit_bytes=VMEM_ROOM),
        name="settle",
    )(landed, slopes, home, sh_coeffs)


def body(splats, sh_coeffs, send_list, block_slots, block_tiles, target):
    received, home, aim = deliver(splats, sh_coeffs, send_list, target)
    tile_ids = block_tiles[0]
    slot_rows = block_slots[0]
    rendered, recs, coefs, saved = draw_tiles(tile_ids, received, slot_rows)
    tile_grad = contrast(rendered, aim)
    pulled = pull_tiles(tile_ids, recs, coefs, saved, tile_grad, slot_rows, received.shape[1])
    landed, slopes = bring_home(pulled, splats)
    grad_splats, grad_sh = settle(landed, slopes, home, splats, sh_coeffs)
    return (rendered, grad_splats, grad_sh)


def solution(mesh):
    in_specs = (
        P(None, ("gauss", "tile")),
        P(None, ("gauss", "tile")),
        P(("gauss", "tile")),
        P("gauss", "tile", None),
        P("gauss", "tile"),
        P(None, "gauss", "tile"),
    )
    out_specs = (P(None, "gauss", "tile"), P(None, ("gauss", "tile")), P(None, ("gauss", "tile")))
    return jax.shard_map(body, mesh=mesh, in_specs=in_specs, out_specs=out_specs, check_vma=False)
```

```python
import functools
import math

import jax
import jax.numpy as jnp
from jax import lax
from jax.experimental import pallas as pl
from jax.experimental.pallas import tpu as pltpu
from jax.sharding import PartitionSpec as P

TILE_SIDE = 16
TILES_DEV = 8


BASE_ZERO = 0.28209479177387814
BASE_ONE = 0.4886025119029199
BASE_TWO = (
    1.0925484305920792,
    -1.0925484305920792,
    0.31539156525252005,
    -1.0925484305920792,
    0.5462742152960396,
)
BASE_THREE = (
    -0.5900435899266435,
    2.890611442640554,
    -0.4570457994644658,
    0.3731763325901154,
    -0.4570457994644658,
    1.445305721320277,
    -0.5900435899266435,
)
CONST_ONE = 0.0001
CONST_TWO = 0.0009


SEGMENTS = 8
STEPS = 16
BLOCK = SEGMENTS * STEPS
HALF = 128
CENTRE = 7.5
MESH = pl.DeviceIdType.MESH
VMEM_ROOM = 16 * 1024 * 1024


LOG2E = 1.4426950408889634
FIELDS = 9
COEF_ROWS = 48
GROUP = 8
WIDTH = 2
GRAD_ROWS = 24
ACROSS = (((1,), (1,)), ((), ()))
DOWN = (((0,), (0,)), ((), ()))


def pick(table, index):
    return jnp.take_along_axis(table, index, axis=1, mode="promise_in_bounds")


def coarse(value):
    return value.astype(jnp.bfloat16).astype(jnp.float32)


def halves(value):
    high = value.astype(jnp.bfloat16)
    low = (value - high.astype(jnp.float32)).astype(jnp.bfloat16)
    return high, low


def pixel_basis():
    rows = lax.broadcasted_iota(jnp.int32, (8, 2 * HALF), 0)
    pixels = lax.broadcasted_iota(jnp.int32, (8, 2 * HALF), 1)
    along = (pixels % TILE_SIDE).astype(jnp.float32) - CENTRE
    down = (pixels // TILE_SIDE).astype(jnp.float32) - CENTRE
    basis = jnp.zeros((8, 2 * HALF), jnp.float32)
    terms = (along * along, along * down, down * down, along, down, jnp.ones_like(along))
    for at, term in enumerate(terms):
        basis = jnp.where(rows == at, term, basis)
    return basis


def spread_order(slots):
    lanes = lax.broadcasted_iota(jnp.int32, slots.shape, 1)
    return pick(slots, (lanes % SEGMENTS) * STEPS + lanes // SEGMENTS)


def tiles_of(tile_ref, first):
    at = lax.broadcasted_iota(jnp.int32, (SEGMENTS, BLOCK), 0)
    tiles = jnp.zeros((SEGMENTS, BLOCK), jnp.int32)
    for k in range(SEGMENTS):
        tiles = jnp.where(at == k, tile_ref[first + k], tiles)
    return tiles


def live_slots(tile_ref):
    live = jnp.int32(0)
    for slot in range(tile_ref.shape[0]):
        live = live + (tile_ref[slot] < TILES_DEV).astype(jnp.int32)
    return live


def forward_kernel(
    tile_ref, recv_ref, slots_ref, picture_ref, rec_ref, coef_ref, saved_ref,
    work_ref, image_ref, basis_ref,
):
    live = live_slots(tile_ref)
    chunks = recv_ref.shape[1] // BLOCK
    origin_x = (lax.axis_index("tile") * (TILE_SIDE * TILES_DEV)).astype(jnp.float32) + CENTRE
    origin_y = (lax.axis_index("gauss") * TILE_SIDE).astype(jnp.float32) + CENTRE
    work_ref[...] = jnp.zeros_like(work_ref)
    basis = pixel_basis()
    basis_ref[...] = jnp.concatenate([basis] * 3 + [jnp.zeros_like(basis)] * 3, axis=0).astype(
        jnp.bfloat16
    )

    def collect(group, carry):
        first = group * SEGMENTS
        slots = slots_ref[pl.ds(pl.multiple_of(first, SEGMENTS), SEGMENTS), :]
        fine = slots % BLOCK
        chunk_at = slots // BLOCK
        found = [None] * FIELDS
        for chunk in range(chunks):
            hit = chunk_at == chunk
            for f in range(FIELDS):
                row = recv_ref[f : f + 1, chunk * BLOCK : (chunk + 1) * BLOCK]
                got = pick(jnp.broadcast_to(row, (SEGMENTS, BLOCK)), fine)
                found[f] = got if chunk == 0 else jnp.where(hit, got, found[f])
        tiles = tiles_of(tile_ref, first)
        base_x = (TILE_SIDE * jnp.minimum(tiles, TILES_DEV - 1)).astype(jnp.float32) + origin_x
        at_x = found[0] - base_x
        at_y = found[1] - origin_y
        con_a = -0.5 * found[2]
        con_b = -found[3]
        con_c = -0.5 * found[4]
        shut = 1.0 + jnp.exp(-found[5])
        for k, value in enumerate((at_x, at_y, con_a, con_b, con_c, 1.0 - 1.0 / shut)):
            rec_ref[k, pl.ds(pl.multiple_of(first, SEGMENTS), SEGMENTS), :] = value
        part_x = con_a * at_x
        part_y = con_c * at_y
        cross = con_b * at_y
        level = at_x * (part_x + cross) + at_y * part_y
        terms = (
            LOG2E * con_a,
            LOG2E * con_b,
            LOG2E * con_c,
            -LOG2E * (2.0 * part_x + cross),
            -LOG2E * (2.0 * part_y + con_b * at_x),
            LOG2E * (level - jnp.log(shut)),
        )

        def put(row, value):
            work_ref[pl.ds(first * COEF_ROWS + row, SEGMENTS, stride=COEF_ROWS), :] = value

        for k, term in enumerate(terms):
            high = coarse(term)
            rest = term - high
            middle = coarse(rest)
            put(k, high)
            put(8 + k, middle)
            put(16 + k, rest - middle)
        for c in range(3):
            high = coarse(found[6 + c])
            put(24 + c, high)
            put(32 + c, found[6 + c] - high)
            put(40 + c, high)
        return carry

    lax.fori_loop(0, (live + SEGMENTS - 1) // SEGMENTS, collect, 0)
    seg_at = lax.broadcasted_iota(jnp.int32, (SEGMENTS, HALF), 0)
    own_seg = seg_at == lax.broadcasted_iota(jnp.int32, (SEGMENTS, HALF), 1) % SEGMENTS

    def draw_local(slot):
        coefs = work_ref[pl.ds(pl.multiple_of(slot * COEF_ROWS, COEF_ROWS), COEF_ROWS), :].astype(
            jnp.bfloat16
        )
        coef_ref[slot] = coefs
        power = lax.dot_general(coefs, basis_ref[...], DOWN, preferred_element_type=jnp.float32)
        through = [jnp.ones((SEGMENTS, HALF), jnp.float32) for side in range(2)]
        weights = [[], []]
        for step in range(STEPS):
            for side in range(2):
                alpha = jnp.exp2(
                    power[step * SEGMENTS : (step + 1) * SEGMENTS, side * HALF : (side + 1) * HALF]
                )
                weight = alpha * through[side]
                through[side] = through[side] - weight
                weights[side].append(weight)
        weight = jnp.concatenate([jnp.concatenate(w, axis=0) for w in weights], axis=1)
        tints = []
        for part in (24, 32):
            for c in range(3):
                row = work_ref[pl.ds(slot * COEF_ROWS + part + c, 1), :]
                tints.append(jnp.where(own_seg, jnp.broadcast_to(row, (SEGMENTS, HALF)), 0.0))
        tint = jnp.concatenate(tints, axis=0).astype(jnp.bfloat16)
        sums = jnp.dot(
            jnp.concatenate([tint, tint], axis=1),
            jnp.concatenate(halves(weight), axis=0),
            preferred_element_type=jnp.float32,
        )
        return through, sums[0:24] + sums[24:48]

    def draw_join(slot, carry, through, sums):
        tile = tile_ref[slot]
        fresh = (slot == 0) | (tile != tile_ref[jnp.maximum(slot - 1, 0)])
        after = []
        for side in range(2):
            start = jnp.where(fresh, 1.0, carry[side])
            running = through[side]
            for shift in (1, 2, 4):
                running = jnp.where(
                    seg_at >= shift, running * pltpu.roll(running, shift, 0), running
                )
            before = jnp.where(seg_at == 0, 1.0, pltpu.roll(running, 1, 0)) * start
            after.append(start * running[SEGMENTS - 1 : SEGMENTS])
            lanes = slice(side * HALF, (side + 1) * HALF)
            saved_ref[slot, 0, :, lanes] = before
            saved_ref[slot, 1, :, lanes] = through[side]
            for c in range(3):
                part = sums[c * SEGMENTS : (c + 1) * SEGMENTS, lanes]
                saved_ref[slot, 2 + c, :, lanes] = part
                shade_sum = jnp.sum(before * part, axis=0, keepdims=True)
                held = jnp.where(fresh, 0.0, image_ref[tile, c : c + 1, lanes])
                image_ref[tile, c : c + 1, lanes] = held + shade_sum
        return tuple(after)

    def draw(pair, carry):
        locals_two = [draw_local(GROUP * pair + k) for k in range(GROUP)]
        for k in range(GROUP):
            carry = draw_join(GROUP * pair + k, carry, *locals_two[k])
        return carry

    ones = jnp.ones((1, HALF), jnp.float32)
    lax.fori_loop(0, (live + GROUP - 1) // GROUP, draw, (ones, ones))
    lane_tile = lax.broadcasted_iota(jnp.int32, (SEGMENTS, HALF), 1) // TILE_SIDE
    for side in range(2):
        lanes = slice(side * HALF, (side + 1) * HALF)
        for c in range(3):
            shown = jnp.zeros((SEGMENTS, HALF), jnp.float32)
            for tile in range(TILES_DEV):
                row = jnp.broadcast_to(image_ref[tile, c : c + 1, lanes], (SEGMENTS, HALF))
                moved = pltpu.roll(row, TILE_SIDE * tile, 1) if tile else row
                for bit in (1, 2, 4):
                    moved = jnp.where(
                        (seg_at & bit) > 0, pltpu.roll(moved, HALF - TILE_SIDE * bit, 1), moved
                    )
                shown = jnp.where(lane_tile == tile, moved, shown)
            picture_ref[c, side * SEGMENTS : (side + 1) * SEGMENTS, :] = shown


def backward_kernel(
    tile_ref, rec_ref, coef_ref, saved_ref, grad_ref, slots_ref, out_ref,
    rhs_ref, mom_ref, back_ref, where_ref, acc_ref,
    alpha_ref, lit_ref, share_ref, heavy_ref, force_ref, behind_ref,
):
    live = live_slots(tile_ref)
    chunks = out_ref.shape[1] // BLOCK
    slots_total = coef_ref.shape[0]
    acc_ref[...] = jnp.zeros_like(acc_ref)
    basis = pixel_basis()
    blank = jnp.zeros_like(basis)
    basis16 = jnp.concatenate([basis, blank], axis=0).astype(jnp.bfloat16)
    for tile in range(TILES_DEV):
        grads = grad_ref[tile]
        high = coarse(grads)
        rhs_ref[tile, :, 0 : 2 * HALF] = jnp.concatenate([basis] * 3 + [blank] * 3, axis=0).astype(
            jnp.bfloat16
        )
        rhs_ref[tile, :, 2 * HALF : 4 * HALF] = jnp.concatenate(
            [blank] * 3 + [high, high, grads - high], axis=0
        ).astype(jnp.bfloat16)
    seg_at = lax.broadcasted_iota(jnp.int32, (SEGMENTS, HALF), 0)

    def prepare(slot, carry, buf):
        tile = tile_ref[slot]
        final = (slot >= live - 1) | (tile != tile_ref[jnp.minimum(slot + 1, slots_total - 1)])
        shown = jnp.minimum(tile, TILES_DEV - 1)
        grads = grad_ref[shown]
        after = []
        for side in range(2):
            lanes = slice(side * HALF, (side + 1) * HALF)
            start = jnp.where(final, 0.0, carry[side])
            total = grads[0:1, lanes] * saved_ref[slot, 2, :, lanes]
            for c in (1, 2):
                total = total + grads[c : c + 1, lanes] * saved_ref[slot, 2 + c, :, lanes]
            factor = saved_ref[slot, 1, :, lanes]
            for shift in (1, 2, 4):
                inside = seg_at < SEGMENTS - shift
                total = jnp.where(
                    inside, total + factor * pltpu.roll(total, SEGMENTS - shift, 0), total
                )
                factor = jnp.where(
                    inside, factor * pltpu.roll(factor, SEGMENTS - shift, 0), factor
                )
            entering = total + factor * start
            after.append(entering[0:1])
            behind_ref[buf, :, lanes] = jnp.where(
                seg_at < SEGMENTS - 1, pltpu.roll(entering, SEGMENTS - 1, 0), start
            )
        both = lax.dot_general(
            coef_ref[slot], rhs_ref[shown], DOWN, preferred_element_type=jnp.float32
        )
        alpha_ref[buf] = jnp.exp2(both[:, : 2 * HALF])
        lit_ref[buf] = both[:, 2 * HALF :]
        return tuple(after)

    def halve(target_ref, buf, step, lanes, pair):
        value = jnp.concatenate(pair, axis=0)
        high, low = halves(value)
        rows = 2 * SEGMENTS * step
        target_ref[buf, rows : rows + 2 * SEGMENTS, lanes] = high
        target_ref[buf, BLOCK + rows : BLOCK + rows + 2 * SEGMENTS, lanes] = low

    def trace(slots, bufs):
        chains = [(k, side) for k in range(len(slots)) for side in range(2)]
        lanes = [slice(side * HALF, (side + 1) * HALF) for side in range(2)]
        through = {
            (k, side): saved_ref[slots[k], 0, :, lanes[side]] for k, side in chains
        }
        for step in range(STEPS // 2):
            for k, side in chains:
                pair = []
                for at in (2 * step, 2 * step + 1):
                    rows = slice(at * SEGMENTS, (at + 1) * SEGMENTS)
                    weight = alpha_ref[bufs[k], rows, lanes[side]] * through[k, side]
                    through[k, side] = through[k, side] - weight
                    share_ref[bufs[k], rows, lanes[side]] = weight
                    pair.append(weight)
                halve(heavy_ref, bufs[k], step, lanes[side], pair)
        later = {(k, side): behind_ref[bufs[k], :, lanes[side]] for k, side in chains}
        for step in reversed(range(STEPS // 2)):
            for k, side in chains:
                pair = []
                for at in (2 * step + 1, 2 * step):
                    rows = slice(at * SEGMENTS, (at + 1) * SEGMENTS)
                    gap = lit_ref[bufs[k], rows, lanes[side]] - later[k, side]
                    later[k, side] = later[k, side] + alpha_ref[bufs[k], rows, lanes[side]] * gap
                    pair.append(share_ref[bufs[k], rows, lanes[side]] * gap)
                halve(force_ref, bufs[k], step, lanes[side], pair[::-1])

    def reduce(slot, place, buf):
        shown = jnp.minimum(tile_ref[slot], TILES_DEV - 1)
        found = lax.dot_general(
            basis16, force_ref[buf], ACROSS, preferred_element_type=jnp.float32
        )
        painted = lax.dot_general(
            jnp.concatenate(halves(grad_ref[shown]), axis=0),
            heavy_ref[buf],
            ACROSS,
            preferred_element_type=jnp.float32,
        )
        painted = painted[0:8] + painted[8:16]
        mom_ref[place, 0:8, :] = found[0:8, :BLOCK] + found[0:8, BLOCK:]
        mom_ref[place, 8:16, :] = painted[:, :BLOCK] + painted[:, BLOCK:]

    runs = (live + WIDTH - 1) // WIDTH

    def slot_of(run, k):
        return jnp.clip(runs - 1 - run, 0, slots_total // WIDTH - 1) * WIDTH + k

    def ready(run, carry, half):
        for k in reversed(range(WIDTH)):
            carry = prepare(slot_of(run, k), carry, half * WIDTH + k)
        return carry

    def pull(turn, carry):
        for part in range(4):
            half = part % 2
            run = 4 * turn + part
            for k in range(WIDTH):
                slot = slot_of(run - 1, k)
                late = (run == 0) | (run > runs)
                reduce(slot, jnp.where(late, slots_total, slot), (1 - half) * WIDTH + k)
            carry = ready(run + 1, carry, 1 - half)
            trace(
                [slot_of(run, k) for k in range(WIDTH)],
                [half * WIDTH + k for k in range(WIDTH)],
            )
        return carry

    zeros = jnp.zeros((1, HALF), jnp.float32)
    carry = ready(0, (zeros, zeros), 0)
    lax.fori_loop(0, (runs + 4) // 4, pull, carry)
    lane_rows = lax.broadcasted_iota(jnp.int32, (BLOCK, 4 * BLOCK), 0)
    chunk_rows = lax.broadcasted_iota(jnp.int32, (chunks, BLOCK), 0)

    def settle(group, carry):
        first = pl.multiple_of(group * SEGMENTS, SEGMENTS)
        tiles = tiles_of(tile_ref, first)
        used = tiles < TILES_DEV
        rows = pl.ds(first, SEGMENTS)

        m_xx, m_xy, m_yy, m_x, m_y, m_0 = [
            mom_ref[rows, k, :] for k in range(6)
        ]
        at_x, at_y, con_a, con_b, con_c, shut_s = [rec_ref[k, rows, :] for k in range(6)]
        h_x = m_x - at_x * m_0
        h_y = m_y - at_y * m_0
        h_xx = m_xx - 2.0 * at_x * m_x + at_x * at_x * m_0
        h_xy = m_xy - at_x * m_y - at_y * m_x + at_x * at_y * m_0
        h_yy = m_yy - 2.0 * at_y * m_y + at_y * at_y * m_0
        results = [
            -2.0 * con_a * h_x - con_b * h_y,
            -2.0 * con_c * h_y - con_b * h_x,
            -0.5 * h_xx,
            -h_xy,
            -0.5 * h_yy,
            shut_s * m_0,
        ] + [mom_ref[rows, 8 + c, :] for c in range(3)]
        for f, value in enumerate(results):
            kept = jnp.where(used, value, 0.0)
            high = coarse(kept)
            back_ref[rows, f, :] = high
            back_ref[rows, 12 + f, :] = kept - high
        slots = slots_ref[rows, :]
        where_ref[0, rows, :] = slots % BLOCK
        where_ref[1, rows, :] = slots // BLOCK
        for quad in range(0, SEGMENTS, 4):
            stacked = []
            for k in range(quad, quad + 4):
                hit = chunk_rows == where_ref[1, pl.ds(first + k, 1), :]
                stacked.append(
                    jnp.concatenate(
                        [
                            jnp.where(hit, back_ref[first + k, part + f : part + f + 1, :], 0.0)
                            for part in (0, 12)
                            for f in range(FIELDS)
                        ],
                        axis=0,
                    ).astype(jnp.bfloat16)
                )
            fine = jnp.concatenate(
                [where_ref[0, pl.ds(first + k, 1), :] for k in range(quad, quad + 4)], axis=1
            )
            select = jnp.where(lane_rows == fine, 1.0, 0.0).astype(jnp.bfloat16)
            acc_ref[...] += lax.dot_general(
                jnp.concatenate(stacked, axis=1), select, ACROSS, preferred_element_type=jnp.float32
            )
        return carry

    lax.fori_loop(0, (live + SEGMENTS - 1) // SEGMENTS, settle, 0)
    total = FIELDS * chunks
    for chunk in range(chunks):
        lanes = slice(chunk * BLOCK, (chunk + 1) * BLOCK)
        out_ref[0:8, lanes] = (
            acc_ref[pl.ds(chunk, 8, stride=chunks), :]
            + acc_ref[pl.ds(total + chunk, 8, stride=chunks), :]
        )
        at = 8 * chunks + chunk
        out_ref[8:9, lanes] = acc_ref[at : at + 1, :] + acc_ref[total + at : total + at + 1, :]


def hbm():
    return pl.BlockSpec(memory_space=pltpu.HBM)


def smem():
    return pl.BlockSpec(memory_space=pltpu.SMEM)


def vmem():
    return pl.BlockSpec(memory_space=pltpu.VMEM)


def draw_tiles(tile_ids, received, slots):
    slots_total = slots.shape[0]
    side = TILE_SIDE * TILE_SIDE
    return pl.pallas_call(
        forward_kernel,
        out_shape=(
            jax.ShapeDtypeStruct((3, TILE_SIDE, TILES_DEV * TILE_SIDE), jnp.float32),
            jax.ShapeDtypeStruct((6, slots_total, BLOCK), jnp.float32),
            jax.ShapeDtypeStruct((slots_total, COEF_ROWS, BLOCK), jnp.bfloat16),
            jax.ShapeDtypeStruct((slots_total, 5, SEGMENTS, side), jnp.float32),
        ),
        in_specs=[smem(), vmem(), vmem()],
        out_specs=(vmem(), vmem(), vmem(), vmem()),
        scratch_shapes=[
            pltpu.VMEM((slots_total * COEF_ROWS, BLOCK), jnp.float32),
            pltpu.VMEM((TILES_DEV + 1, 8, side), jnp.float32),
            pltpu.VMEM((COEF_ROWS, side), jnp.bfloat16),
        ],
        compiler_params=pltpu.CompilerParams(vmem_limit_bytes=VMEM_ROOM),
        name="draw_tiles",
    )(tile_ids, received, slots)


def pull_tiles(tile_ids, recs, coefs, saved, grads, slots, own):
    slots_total = coefs.shape[0]
    side = TILE_SIDE * TILE_SIDE
    chunks = own // BLOCK
    return pl.pallas_call(
        backward_kernel,
        out_shape=jax.ShapeDtypeStruct((FIELDS, own), jnp.float32),
        in_specs=[smem(), vmem(), vmem(), vmem(), vmem(), vmem()],
        out_specs=vmem(),
        scratch_shapes=[
            pltpu.VMEM((TILES_DEV, COEF_ROWS, 2 * side), jnp.bfloat16),
            pltpu.VMEM((slots_total + 1, 16, BLOCK), jnp.float32),
            pltpu.VMEM((slots_total, GRAD_ROWS, BLOCK), jnp.float32),
            pltpu.VMEM((2, slots_total, BLOCK), jnp.int32),
            pltpu.VMEM((2 * FIELDS * chunks, BLOCK), jnp.float32),
            pltpu.VMEM((2 * WIDTH, BLOCK, side), jnp.float32),
            pltpu.VMEM((2 * WIDTH, BLOCK, side), jnp.float32),
            pltpu.VMEM((2 * WIDTH, BLOCK, side), jnp.float32),
            pltpu.VMEM((2 * WIDTH, 2 * BLOCK, side), jnp.bfloat16),
            pltpu.VMEM((2 * WIDTH, 2 * BLOCK, side), jnp.bfloat16),
            pltpu.VMEM((2 * WIDTH, SEGMENTS, side), jnp.float32),
        ],
        compiler_params=pltpu.CompilerParams(vmem_limit_bytes=VMEM_ROOM),
        name="pull_tiles",
    )(tile_ids, recs, coefs, saved, grads, slots)


WAYS = [(down, right) for down in (-1, 0, 1) for right in (-1, 0, 1) if (down, right) != (0, 0)]
NORM = sum(math.exp(-m * m / 4.5) for m in range(-5, 6))
EXT_ROWS = 40
MID_ROWS = 32


def neighbour(bands, columns, way):
    there_band = lax.axis_index("gauss") + way[0]
    there_col = lax.axis_index("tile") + way[1]
    exists = (there_band >= 0) & (there_band < bands) & (there_col >= 0) & (there_col < columns)
    return exists, (there_band, there_col)


def greet_round(bands, columns):
    barrier = pltpu.get_barrier_semaphore()
    peers = jnp.int32(0)
    for way in WAYS:
        exists, there = neighbour(bands, columns, way)
        peers = peers + exists.astype(jnp.int32)

        @pl.when(exists)
        def _(there=there):
            pl.semaphore_signal(barrier, inc=1, device_id=there, device_id_type=MESH)

    return barrier, peers


def border_copies(bands, columns, plane_ref, edge_ref, tall_ref, side_ref, send_sem, recv_sem):
    found = []
    for at, way in enumerate(WAYS):
        exists, there = neighbour(bands, columns, way)
        landing = len(WAYS) - 1 - at
        source = plane_ref if way[1] == 0 else edge_ref
        target = tall_ref.at[landing] if way[1] == 0 else side_ref.at[landing]
        found.append(
            (
                exists,
                pltpu.make_async_remote_copy(
                    src_ref=source,
                    dst_ref=target,
                    send_sem=send_sem.at[at],
                    recv_sem=recv_sem.at[landing],
                    device_id=there,
                    device_id_type=MESH,
                ),
                pltpu.make_async_remote_copy(
                    src_ref=source,
                    dst_ref=tall_ref.at[at] if way[1] == 0 else side_ref.at[at],
                    send_sem=send_sem.at[at],
                    recv_sem=recv_sem.at[at],
                    device_id=there,
                    device_id_type=MESH,
                ),
            )
        )
    return found


def border_start(copies):
    for exists, out, back in copies:

        @pl.when(exists)
        def _(out=out):
            out.start()


def border_wait(copies):
    for exists, out, back in copies:

        @pl.when(exists)
        def _(out=out, back=back):
            out.wait_send()
            back.wait_recv()


def pack_edges(plane_ref, edge_ref):
    lanes = lax.broadcasted_iota(jnp.int32, edge_ref.shape, 1)
    packed = jnp.zeros(edge_ref.shape, jnp.float32)
    for c in range(3):
        plane = plane_ref[c]
        near = pltpu.roll(plane, 32 * c, 1) if c else plane
        far = pltpu.roll(plane, 32 * c + 32, 1)
        packed = jnp.where(
            lanes // 32 == c, jnp.where(lanes % 32 < 16, near, far), packed
        )
    edge_ref[...] = packed


def stretch(above, own, below):
    turn = lax.broadcasted_iota(jnp.int32, (8, own.shape[1]), 0) >= 6
    mixed = jnp.where(turn, above[0:8], below[8:16])
    return jnp.concatenate([own, above[8:16], below[0:8], mixed], axis=0)


def extend(plane_ref, tall_ref, side_ref):
    east = lax.broadcasted_iota(jnp.int32, side_ref.shape[1:], 1) % 32 < 16
    borders = [
        jnp.where(east, side_ref[WAYS.index((down, 1))], side_ref[WAYS.index((down, -1))])
        for down in (-1, 0, 1)
    ]
    border = stretch(*borders)
    planes = []
    for c in range(3):
        main = stretch(
            tall_ref[WAYS.index((-1, 0)), c], plane_ref[c], tall_ref[WAYS.index((1, 0)), c]
        )
        turned = pltpu.roll(border, HALF - 32 * c, 1) if c else border
        planes.append(jnp.concatenate([main, turned], axis=1))
    return planes


def window_weight(gap):
    gap = gap.astype(jnp.float32)
    return jnp.where(jnp.abs(gap) < 5.5, jnp.exp(gap * gap / -4.5) * (1.0 / NORM), 0.0)


def split_rows(value):
    first = coarse(value)
    rest = value - first
    second = coarse(rest)
    return first, second, rest - second


def six_data(value, axis):
    first, second, third = split_rows(value)
    return jnp.concatenate([first, second, third, first, second, first], axis=axis).astype(
        jnp.bfloat16
    )


def six_weights(value, axis):
    first, second, third = split_rows(value)
    return jnp.concatenate([first, first, first, second, second, third], axis=axis).astype(
        jnp.bfloat16
    )


def ext_row(at):
    return jnp.where(at < 16, at, jnp.where(at < 24, at - 24, jnp.where(at < 38, at - 8, at - 48)))


def ext_col(at):
    return jnp.where(at < 144, at, jnp.where(at < 160, at - 160, 10000))


def mid_col(at):
    return jnp.where(at < 192, at, at - 256)


def iota(shape, axis):
    return lax.broadcasted_iota(jnp.int32, shape, axis)


def fdot(left, right):
    return jnp.dot(left, right, preferred_element_type=jnp.float32)


def contrast_kernel(
    bands, columns, shown_ref, aim_ref, out_ref,
    edge_ref, tall_ref, side_ref, wide_ref, back_ref, send_sem, recv_sem,
):
    band = lax.axis_index("gauss")
    column = lax.axis_index("tile")
    rows, cols = shown_ref.shape[1:]
    tall_ref[...] = jnp.zeros_like(tall_ref)
    side_ref[...] = jnp.zeros_like(side_ref)
    barrier, peers = greet_round(bands, columns)
    pack_edges(shown_ref, edge_ref)
    copies = border_copies(
        bands, columns, shown_ref, edge_ref, tall_ref, side_ref, send_sem, recv_sem
    )
    pl.semaphore_wait(barrier, peers)
    border_start(copies)
    wide = 2 * cols
    for half in range(2):
        lanes = slice(half * cols, (half + 1) * cols)
        shape = (wide, cols)
        across = window_weight(mid_col(iota(shape, 1) + half * cols) - ext_col(iota(shape, 0)))
        wide_ref[:, lanes] = six_weights(across, 0)
    back = window_weight(mid_col(iota((wide, cols), 0)) - iota((wide, cols), 1))
    back_ref[...] = six_weights(back, 0)
    shape = (MID_ROWS, EXT_ROWS)
    down = window_weight(iota(shape, 0) - 5 - ext_row(iota(shape, 1)))
    down = six_weights(down, 1)
    shape = (rows, MID_ROWS)
    up = six_weights(window_weight(iota(shape, 0) - iota(shape, 1) + 5), 1)
    border_wait(copies)
    pics = extend(shown_ref, tall_ref, side_ref)
    strips = []
    for kind in range(4):
        for c in range(3):
            pic, aim = pics[c], aim_ref[c]
            plane = (pic, aim, pic * pic + aim * aim, pic * aim)[kind] if kind > 1 else (
                pic if kind == 0 else aim
            )
            strips.append(fdot(down, six_data(plane, 0)))
    moments = fdot(six_data(jnp.concatenate(strips, axis=0), 1), wide_ref[...])
    shape = (MID_ROWS, wide)
    row_at = band * rows + iota(shape, 0) - 5
    col_at = column * cols + mid_col(iota(shape, 1))
    inside = (row_at >= 0) & (row_at < bands * rows) & (col_at >= 0) & (col_at < columns * cols)
    strips = [None] * 9
    for c in range(3):
        mu_x, mu_y, squares, cross = [
            moments[(3 * kind + c) * MID_ROWS : (3 * kind + c + 1) * MID_ROWS] for kind in range(4)
        ]
        mean_xy = mu_x * mu_y
        mean_sq = mu_x * mu_x + mu_y * mu_y
        top_1 = 2.0 * mean_xy + CONST_ONE
        top_2 = 2.0 * (cross - mean_xy) + CONST_TWO
        low_1 = mean_sq + CONST_ONE
        low_2 = squares - mean_sq + CONST_TWO
        inverse = -0.2 / (low_1 * low_2)
        value = top_1 * top_2 * inverse
        value_1 = value * low_2 * inverse * -5.0
        value_2 = value * low_1 * inverse * -5.0
        slope_mean = 2.0 * mu_y * (top_2 - top_1) * inverse - 2.0 * mu_x * (value_1 - value_2)
        for kind, slope in enumerate((slope_mean, -value_2, 2.0 * top_1 * inverse)):
            strips[3 * kind + c] = fdot(up, six_data(jnp.where(inside, slope, 0.0), 0))
    spread = fdot(six_data(jnp.concatenate(strips, axis=0), 1), back_ref[...])
    lane_row = iota((SEGMENTS, HALF), 1) // TILE_SIDE
    seg_at = iota((SEGMENTS, HALF), 0)
    out_ref[...] = jnp.zeros_like(out_ref)
    for c in range(3):
        pic = shown_ref[c]
        aim = aim_ref[c, 0:rows, 0:cols]
        parts = [spread[(3 * kind + c) * rows : (3 * kind + c + 1) * rows] for kind in range(3)]
        total = parts[0] + 2.0 * pic * parts[1] + aim * parts[2] + 1.6 * (pic - aim)
        for side in range(2):
            part = total[side * SEGMENTS : (side + 1) * SEGMENTS]
            skewed = pltpu.roll(part, 0, 1, stride=TILE_SIDE, stride_axis=0)
            for tile in range(TILES_DEV):
                moved = pltpu.roll(skewed, HALF - TILE_SIDE * tile, 1) if tile else skewed
                kept = jnp.where(lane_row == seg_at, moved, 0.0)
                out_ref[tile, c : c + 1, side * HALF : (side + 1) * HALF] = jnp.sum(
                    kept, axis=0, keepdims=True
                )


def border_scratch(rows, cols):
    ways = len(WAYS)
    return [
        pltpu.VMEM((rows, cols), jnp.float32),
        pltpu.VMEM((ways, 3, rows, cols), jnp.float32),
        pltpu.VMEM((ways, rows, cols), jnp.float32),
    ]


def contrast(rendered, aim):
    rows, cols = rendered.shape[1:]
    ways = len(WAYS)
    return pl.pallas_call(
        functools.partial(contrast_kernel, lax.axis_size("gauss"), lax.axis_size("tile")),
        out_shape=jax.ShapeDtypeStruct((TILES_DEV, 8, TILE_SIDE * TILE_SIDE), jnp.float32),
        in_specs=[vmem(), vmem()],
        out_specs=vmem(),
        scratch_shapes=border_scratch(rows, cols)
        + [
            pltpu.VMEM((12 * cols, 2 * cols), jnp.bfloat16),
            pltpu.VMEM((12 * cols, cols), jnp.bfloat16),
            pltpu.SemaphoreType.DMA((ways,)),
            pltpu.SemaphoreType.DMA((ways,)),
        ],
        compiler_params=pltpu.CompilerParams(
            collective_id=0, has_side_effects=True, vmem_limit_bytes=VMEM_ROOM
        ),
        name="contrast",
    )(rendered, aim)


PACKED = 8


def basis_rows(x, y, z):
    xx, yy, zz = x * x, y * y, z * z
    return [
        jnp.full_like(x, BASE_ZERO),
        -BASE_ONE * y,
        BASE_ONE * z,
        -BASE_ONE * x,
        BASE_TWO[0] * x * y,
        BASE_TWO[1] * y * z,
        BASE_TWO[2] * (2.0 * zz - xx - yy),
        BASE_TWO[3] * x * z,
        BASE_TWO[4] * (xx - yy),
        BASE_THREE[0] * y * (3.0 * xx - yy),
        BASE_THREE[1] * x * y * z,
        BASE_THREE[2] * y * (4.0 * zz - xx - yy),
        BASE_THREE[3] * z * (2.0 * zz - 3.0 * xx - 3.0 * yy),
        BASE_THREE[4] * x * (4.0 * zz - xx - yy),
        BASE_THREE[5] * z * (xx - yy),
        BASE_THREE[6] * x * (xx - 3.0 * yy),
    ]


def slope_rows(x, y, z):
    xx, yy, zz = x * x, y * y, z * z
    xy, yz, xz = x * y, y * z, x * z
    none = jnp.zeros_like(x)
    one = jnp.ones_like(x)
    two, three = BASE_TWO, BASE_THREE
    along_x = [
        none, none, none, -BASE_ONE * one,
        two[0] * y, none, -2.0 * two[2] * x, two[3] * z, 2.0 * two[4] * x,
        6.0 * three[0] * xy, three[1] * yz, -2.0 * three[2] * xy, -6.0 * three[3] * xz,
        three[4] * (4.0 * zz - 3.0 * xx - yy), 2.0 * three[5] * xz, three[6] * (3.0 * xx - 3.0 * yy),
    ]
    along_y = [
        none, -BASE_ONE * one, none, none,
        two[0] * x, two[1] * z, -2.0 * two[2] * y, none, -2.0 * two[4] * y,
        three[0] * (3.0 * xx - 3.0 * yy), three[1] * xz, three[2] * (4.0 * zz - xx - 3.0 * yy),
        -6.0 * three[3] * yz, -2.0 * three[4] * xy, -2.0 * three[5] * yz, -6.0 * three[6] * xy,
    ]
    along_z = [
        none, none, BASE_ONE * one, none,
        none, two[1] * y, 4.0 * two[2] * z, two[3] * x, none,
        none, three[1] * xy, 8.0 * three[2] * yz, three[3] * (6.0 * zz - 3.0 * xx - 3.0 * yy),
        8.0 * three[4] * xz, three[5] * (xx - yy), none,
    ]
    return along_x, along_y, along_z


def lane_of():
    return lax.broadcasted_iota(jnp.int32, (8, BLOCK), 1)


def row_of():
    return lax.broadcasted_iota(jnp.int32, (8, BLOCK), 0)


def gather_rows(table_ref, ninth_ref, chunks, index):
    index = jnp.broadcast_to(index, (8, BLOCK))
    fine = index % BLOCK
    chunk_at = index // BLOCK
    first = None
    ninth = jnp.zeros((8, BLOCK), jnp.float32)
    for chunk in range(chunks):
        got = pick(table_ref[0:8, chunk * BLOCK : (chunk + 1) * BLOCK], fine)
        first = got if chunk == 0 else jnp.where(chunk_at == chunk, got, first)
    for base in range(0, chunks, 8):
        got = pick(ninth_ref[base : base + 8, :], fine)
        ninth = ninth + jnp.where(chunk_at == row_of() + base, got, 0.0)
    return first, jnp.sum(ninth, axis=0, keepdims=True)


def pack_two(first, last):
    left = lane_of() < BLOCK // 2
    swapped = pltpu.roll(first, BLOCK // 2, 1)
    one = jnp.where(left, first, pltpu.roll(swapped, 4, 0))
    two = jnp.where(left, swapped, pltpu.roll(first, 4, 0))
    tail = row_of() >= 4
    ninth = jnp.broadcast_to(last, (8, BLOCK))
    return jnp.where(tail, ninth, one), jnp.where(tail, pltpu.roll(ninth, BLOCK // 2, 1), two)


def unpack_two(one, two):
    left = lane_of() < BLOCK // 2
    upper = jnp.where(left, one, pltpu.roll(two, BLOCK // 2, 1))
    lower = jnp.where(left, pltpu.roll(one, BLOCK // 2, 1), two)
    return jnp.where(row_of() < 4, upper, pltpu.roll(lower, 4, 0)), upper[4:5]


def ring(gap, owners):
    there = lax.axis_index("gauss") + gap
    return jnp.where(there >= owners, there - owners, there)


def greet(owners):
    barrier = pltpu.get_barrier_semaphore()
    column = lax.axis_index("tile")
    for gap in range(1, owners):
        pl.semaphore_signal(
            barrier, inc=1, device_id=(ring(gap, owners), column), device_id_type=MESH
        )
    return barrier


def parcel(owners, gap, out_ref, in_ref, send_sem, recv_sem):
    band = lax.axis_index("gauss")
    there = ring(gap, owners)
    return pltpu.make_async_remote_copy(
        src_ref=out_ref.at[there],
        dst_ref=in_ref.at[band],
        send_sem=send_sem.at[gap],
        recv_sem=recv_sem.at[gap],
        device_id=(there, lax.axis_index("tile")),
        device_id_type=MESH,
    )


def post(owners, out_ref, in_ref, send_sem, recv_sem):
    band = lax.axis_index("gauss")
    for gap in range(1, owners):
        parcel(owners, gap, out_ref, in_ref, send_sem, recv_sem).start()
    in_ref[band] = out_ref[band]


def take_in(owners, out_ref, in_ref, send_sem, recv_sem):
    for gap in range(1, owners):
        parcel(owners, gap, out_ref, in_ref, send_sem, recv_sem).wait()


def deliver_kernel(
    owners, columns, *refs,
):
    sources, refs = refs[:6], refs[6:]
    recv_ref, home_ref, aim_ref, order_ref, tile_ref = refs[:5]
    table_ref, ninth_ref, edge_ref, tall_ref, side_ref, border_send, border_recv = refs[5:12]
    splats_ref, sh_ref, send_ref, target_ref, slots_ref, load_sem = refs[12:18]
    out_ref, in_ref, send_sem, recv_sem = refs[18:]
    loads = [
        pltpu.make_async_copy(source, local, load_sem.at[at])
        for at, (source, local) in enumerate(
            zip(sources, (splats_ref, sh_ref, send_ref, target_ref, slots_ref, tile_ref))
        )
    ]
    for load in loads:
        load.start()
    tall_ref[...] = jnp.zeros_like(tall_ref)
    side_ref[...] = jnp.zeros_like(side_ref)
    barrier = greet(owners)
    around, peers = greet_round(owners, columns)
    for load in loads:
        load.wait()
    own = splats_ref.shape[1]
    chunks = own // BLOCK
    basis = jnp.concatenate(
        basis_rows(splats_ref[6:7, :], splats_ref[7:8, :], splats_ref[8:9, :]), axis=0
    )
    colours = [
        0.5 + jnp.sum(sh_ref[16 * c : 16 * (c + 1), :] * basis, axis=0, keepdims=True)
        for c in range(3)
    ]
    table_ref[0:6, :] = splats_ref[0:6, :]
    table_ref[6:8, :] = jnp.concatenate(colours[0:2], axis=0)
    for chunk in range(chunks):
        ninth_ref[chunk : chunk + 1, :] = colours[2][:, chunk * BLOCK : (chunk + 1) * BLOCK]
    for chunk in range(chunks):
        one, two = pack_two(
            *gather_rows(table_ref, ninth_ref, chunks, send_ref[chunk : chunk + 1, :])
        )
        out_ref[2 * chunk] = one
        out_ref[2 * chunk + 1] = two
    pack_edges(target_ref, edge_ref)
    pl.semaphore_wait(barrier, owners - 1 + peers)
    post(owners, out_ref, in_ref, send_sem, recv_sem)
    copies = border_copies(
        owners, columns, target_ref, edge_ref, tall_ref, side_ref, border_send, border_recv
    )
    border_start(copies)
    chunk_rows = lax.broadcasted_iota(jnp.int32, (chunks, BLOCK), 0)
    lanes = lax.broadcasted_iota(jnp.int32, (chunks, BLOCK), 1).astype(jnp.float32)
    lane_rows = lax.broadcasted_iota(jnp.int32, (BLOCK, BLOCK), 0)
    home = jnp.zeros((2 * chunks, BLOCK), jnp.float32)
    for chunk in range(chunks):
        index = send_ref[chunk : chunk + 1, :]
        hit = chunk_rows == index // BLOCK
        source = jnp.concatenate(
            [jnp.where(hit, float(chunk), 0.0), jnp.where(hit, lanes, 0.0)], axis=0
        ).astype(jnp.bfloat16)
        select = jnp.where(lane_rows == index % BLOCK, 1.0, 0.0).astype(jnp.bfloat16)
        home = home + lax.dot_general(source, select, ACROSS, preferred_element_type=jnp.float32)
    home_ref[...] = (home[:chunks] * float(BLOCK) + home[chunks:]).astype(jnp.int32)
    for first in range(0, slots_ref.shape[0], SEGMENTS):
        rows = slice(first, first + SEGMENTS)
        order_ref[rows, :] = spread_order(slots_ref[rows, :])
    border_wait(copies)
    for c, plane in enumerate(extend(target_ref, tall_ref, side_ref)):
        aim_ref[c] = plane
    take_in(owners, out_ref, in_ref, send_sem, recv_sem)
    for chunk in range(chunks):
        first, ninth = unpack_two(in_ref[2 * chunk], in_ref[2 * chunk + 1])
        recv_ref[0:8, chunk * BLOCK : (chunk + 1) * BLOCK] = first
        recv_ref[8:9, chunk * BLOCK : (chunk + 1) * BLOCK] = ninth


def parcels(owners):
    return [
        pltpu.VMEM((owners, PACKED, BLOCK), jnp.float32),
        pltpu.VMEM((owners, PACKED, BLOCK), jnp.float32),
        pltpu.SemaphoreType.DMA((owners,)),
        pltpu.SemaphoreType.DMA((owners,)),
    ]


def deliver(splats, sh_coeffs, send_list, target, slots, tile_ids):
    own = splats.shape[1]
    owners = lax.axis_size("gauss")
    rows, cols = target.shape[1:]
    ways = len(WAYS)
    return pl.pallas_call(
        functools.partial(deliver_kernel, owners, lax.axis_size("tile")),
        out_shape=(
            jax.ShapeDtypeStruct((FIELDS, own), jnp.float32),
            jax.ShapeDtypeStruct((own // BLOCK, BLOCK), jnp.int32),
            jax.ShapeDtypeStruct((3, EXT_ROWS, 2 * cols), jnp.float32),
            jax.ShapeDtypeStruct(slots.shape, jnp.int32),
            jax.ShapeDtypeStruct(tile_ids.shape, jnp.int32),
        ),
        in_specs=[hbm()] * 6,
        out_specs=(vmem(),) * 5,
        scratch_shapes=[
            pltpu.VMEM((8, own), jnp.float32),
            pltpu.VMEM((own // BLOCK, BLOCK), jnp.float32),
        ]
        + border_scratch(rows, cols)
        + [pltpu.SemaphoreType.DMA((ways,)), pltpu.SemaphoreType.DMA((ways,))]
        + [
            pltpu.VMEM(splats.shape, jnp.float32),
            pltpu.VMEM(sh_coeffs.shape, jnp.float32),
            pltpu.VMEM((own // BLOCK, BLOCK), jnp.int32),
            pltpu.VMEM(target.shape, jnp.float32),
            pltpu.VMEM(slots.shape, jnp.int32),
            pltpu.SemaphoreType.DMA((6,)),
        ]
        + parcels(owners),
        compiler_params=pltpu.CompilerParams(
            collective_id=1, has_side_effects=True, vmem_limit_bytes=VMEM_ROOM
        ),
        name="deliver",
    )(
        *[
            pltpu.with_memory_space_constraint(value, pltpu.HBM)
            for value in (
                splats, sh_coeffs, send_list.reshape(own // BLOCK, BLOCK), target, slots, tile_ids,
            )
        ]
    )


def home_kernel(owners, pulled_ref, splats_ref, in_ref, slope_ref, out_ref, send_sem, recv_sem):
    barrier = greet(owners)
    chunks = pulled_ref.shape[1] // BLOCK
    for chunk in range(chunks):
        lanes = slice(chunk * BLOCK, (chunk + 1) * BLOCK)
        one, two = pack_two(pulled_ref[0:8, lanes], pulled_ref[8:9, lanes])
        out_ref[2 * chunk] = one
        out_ref[2 * chunk + 1] = two
    pl.semaphore_wait(barrier, owners - 1)
    post(owners, out_ref, in_ref, send_sem, recv_sem)
    facing = [splats_ref[6 + d : 7 + d, :] for d in range(3)]
    slope_ref[0:16, :] = jnp.concatenate(basis_rows(*facing), axis=0)
    for d, rows in enumerate(slope_rows(*facing)):
        slope_ref[16 * (d + 1) : 16 * (d + 2), :] = jnp.concatenate(rows, axis=0)
    take_in(owners, out_ref, in_ref, send_sem, recv_sem)


def bring_home(pulled, splats):
    own = splats.shape[1]
    owners = lax.axis_size("gauss")
    landing, *rest = parcels(owners)[1:]
    return pl.pallas_call(
        functools.partial(home_kernel, owners),
        out_shape=(
            jax.ShapeDtypeStruct((owners, PACKED, BLOCK), jnp.float32),
            jax.ShapeDtypeStruct((64, own), jnp.float32),
        ),
        in_specs=[vmem()] * 2,
        out_specs=(vmem(), vmem()),
        scratch_shapes=[landing] + rest,
        compiler_params=pltpu.CompilerParams(
            collective_id=2, has_side_effects=True, vmem_limit_bytes=VMEM_ROOM
        ),
        name="bring_home",
    )(pulled, splats)


def settle_kernel(
    in_ref, slope_ref, home_ref, sh_ref, shown_ref, rendered_ref, splat_grad_ref, sh_grad_ref,
    table_ref, ninth_ref,
):
    rendered_ref[...] = shown_ref[...]
    chunks = sh_ref.shape[1] // BLOCK
    for chunk in range(chunks):
        first, ninth = unpack_two(in_ref[2 * chunk], in_ref[2 * chunk + 1])
        table_ref[:, chunk * BLOCK : (chunk + 1) * BLOCK] = first
        ninth_ref[chunk : chunk + 1, :] = ninth
    for chunk in range(chunks):
        lanes = slice(chunk * BLOCK, (chunk + 1) * BLOCK)
        first, last = gather_rows(table_ref, ninth_ref, chunks, home_ref[chunk : chunk + 1, :])
        splat_grad_ref[0:6, lanes] = first[0:6]
        tints = (first[6:7], first[7:8], last)
        basis = slope_ref[0:16, lanes]
        mixed = jnp.zeros((16, BLOCK), jnp.float32)
        for c in range(3):
            tint = jnp.broadcast_to(tints[c], (16, BLOCK))
            sh_grad_ref[16 * c : 16 * (c + 1), lanes] = tint * basis
            mixed = mixed + tint * sh_ref[16 * c : 16 * (c + 1), lanes]
        splat_grad_ref[6:9, lanes] = jnp.concatenate(
            [
                jnp.sum(mixed * slope_ref[16 * d : 16 * (d + 1), lanes], axis=0, keepdims=True)
                for d in (1, 2, 3)
            ],
            axis=0,
        )


def settle(landed, slopes, home, splats, sh_coeffs, shown):
    own = splats.shape[1]
    return pl.pallas_call(
        settle_kernel,
        out_shape=(
            jax.ShapeDtypeStruct(shown.shape, jnp.float32),
            jax.ShapeDtypeStruct(splats.shape, jnp.float32),
            jax.ShapeDtypeStruct(sh_coeffs.shape, jnp.float32),
        ),
        in_specs=[vmem()] * 5,
        out_specs=(vmem(), vmem(), vmem()),
        scratch_shapes=[
            pltpu.VMEM((8, own), jnp.float32),
            pltpu.VMEM((own // BLOCK, BLOCK), jnp.float32),
        ],
        compiler_params=pltpu.CompilerParams(vmem_limit_bytes=VMEM_ROOM),
        name="settle",
    )(landed, slopes, home, sh_coeffs, shown)


def body(splats, sh_coeffs, send_list, block_slots, block_tiles, target):
    received, home, aim, order, tile_ids = deliver(
        splats, sh_coeffs, send_list, target, block_slots[0], block_tiles
    )
    tile_ids = tile_ids[0]
    shown, recs, coefs, saved = draw_tiles(tile_ids, received, order)
    tile_grad = contrast(shown, aim)
    pulled = pull_tiles(tile_ids, recs, coefs, saved, tile_grad, order, received.shape[1])
    landed, slopes = bring_home(pulled, splats)
    return settle(landed, slopes, home, splats, sh_coeffs, shown)


def solution(mesh):
    in_specs = (
        P(None, ("gauss", "tile")),
        P(None, ("gauss", "tile")),
        P(("gauss", "tile")),
        P("gauss", "tile", None),
        P("gauss", "tile"),
        P(None, "gauss", "tile"),
    )
    out_specs = (P(None, "gauss", "tile"), P(None, ("gauss", "tile")), P(None, ("gauss", "tile")))
    return jax.shard_map(body, mesh=mesh, in_specs=in_specs, out_specs=out_specs, check_vma=False)
```

```python
import functools
import math

import jax
import jax.numpy as jnp
from jax import lax
from jax.experimental import pallas as pl
from jax.experimental.pallas import tpu as pltpu
from jax.sharding import PartitionSpec as P

TILE_SIDE = 16
TILES_DEV = 8


BASE_ZERO = 0.28209479177387814
BASE_ONE = 0.4886025119029199
BASE_TWO = (
    1.0925484305920792,
    -1.0925484305920792,
    0.31539156525252005,
    -1.0925484305920792,
    0.5462742152960396,
)
BASE_THREE = (
    -0.5900435899266435,
    2.890611442640554,
    -0.4570457994644658,
    0.3731763325901154,
    -0.4570457994644658,
    1.445305721320277,
    -0.5900435899266435,
)
CONST_ONE = 0.0001
CONST_TWO = 0.0009


SEGMENTS = 8
STEPS = 16
BLOCK = SEGMENTS * STEPS
HALF = 128
CENTRE = 7.5
MESH = pl.DeviceIdType.MESH
VMEM_ROOM = 16 * 1024 * 1024


LOG2E = 1.4426950408889634
FIELDS = 9
COEF_ROWS = 48
GROUP = 8
WIDTH = 2
PACKED = 8
GRAD_ROWS = 24
ACROSS = (((1,), (1,)), ((), ()))
DOWN = (((0,), (0,)), ((), ()))


def pick(table, index):
    return jnp.take_along_axis(table, index, axis=1, mode="promise_in_bounds")


def coarse(value):
    return value.astype(jnp.bfloat16).astype(jnp.float32)


def halves(value):
    high = value.astype(jnp.bfloat16)
    low = (value - high.astype(jnp.float32)).astype(jnp.bfloat16)
    return high, low


def pixel_basis():
    rows = lax.broadcasted_iota(jnp.int32, (8, 2 * HALF), 0)
    pixels = lax.broadcasted_iota(jnp.int32, (8, 2 * HALF), 1)
    along = (pixels % TILE_SIDE).astype(jnp.float32) - CENTRE
    down = (pixels // TILE_SIDE).astype(jnp.float32) - CENTRE
    basis = jnp.zeros((8, 2 * HALF), jnp.float32)
    terms = (along * along, along * down, down * down, along, down, jnp.ones_like(along))
    for at, term in enumerate(terms):
        basis = jnp.where(rows == at, term, basis)
    return basis


def spread_order(slots):
    lanes = lax.broadcasted_iota(jnp.int32, slots.shape, 1)
    return pick(slots, (lanes % SEGMENTS) * STEPS + lanes // SEGMENTS)


def tiles_of(tile_ref, first):
    at = lax.broadcasted_iota(jnp.int32, (SEGMENTS, BLOCK), 0)
    tiles = jnp.zeros((SEGMENTS, BLOCK), jnp.int32)
    for k in range(SEGMENTS):
        tiles = jnp.where(at == k, tile_ref[0, first + k], tiles)
    return tiles


def forward_part(
    tile_ref, last_ref, recv_ref, slots_ref, picture_ref, rec_ref, coef_ref, saved_ref,
    work_ref, image_ref, basis_ref,
):
    slots_total = slots_ref.shape[0]
    chunks = recv_ref.shape[1] // BLOCK
    origin_x = (lax.axis_index("tile") * (TILE_SIDE * TILES_DEV)).astype(jnp.float32) + CENTRE
    origin_y = (lax.axis_index("gauss") * TILE_SIDE).astype(jnp.float32) + CENTRE
    work_ref[...] = jnp.zeros_like(work_ref)
    basis = pixel_basis()
    basis_ref[...] = jnp.concatenate([basis] * 3 + [jnp.zeros_like(basis)] * 3, axis=0).astype(
        jnp.bfloat16
    )

    def collect(group, carry):
        first = group * SEGMENTS
        slots = slots_ref[pl.ds(pl.multiple_of(first, SEGMENTS), SEGMENTS), :]
        fine = slots % BLOCK
        chunk_at = slots // BLOCK
        found = [None] * FIELDS
        for chunk in range(chunks):
            hit = chunk_at == chunk
            for f in range(FIELDS):
                row = recv_ref[f : f + 1, chunk * BLOCK : (chunk + 1) * BLOCK]
                got = pick(jnp.broadcast_to(row, (SEGMENTS, BLOCK)), fine)
                found[f] = got if chunk == 0 else jnp.where(hit, got, found[f])
        tiles = tiles_of(tile_ref, first)
        base_x = (TILE_SIDE * jnp.minimum(tiles, TILES_DEV - 1)).astype(jnp.float32) + origin_x
        at_x = found[0] - base_x
        at_y = found[1] - origin_y
        con_a = -0.5 * found[2]
        con_b = -found[3]
        con_c = -0.5 * found[4]
        shut = 1.0 + jnp.exp(-found[5])
        for k, value in enumerate((at_x, at_y, con_a, con_b, con_c, 1.0 - 1.0 / shut)):
            rec_ref[k, pl.ds(pl.multiple_of(first, SEGMENTS), SEGMENTS), :] = value
        part_x = con_a * at_x
        part_y = con_c * at_y
        cross = con_b * at_y
        level = at_x * (part_x + cross) + at_y * part_y
        terms = (
            LOG2E * con_a,
            LOG2E * con_b,
            LOG2E * con_c,
            -LOG2E * (2.0 * part_x + cross),
            -LOG2E * (2.0 * part_y + con_b * at_x),
            LOG2E * (level - jnp.log(shut)),
        )

        def put(row, value):
            work_ref[pl.ds(first * COEF_ROWS + row, SEGMENTS, stride=COEF_ROWS), :] = value

        for k, term in enumerate(terms):
            high = coarse(term)
            rest = term - high
            middle = coarse(rest)
            put(k, high)
            put(8 + k, middle)
            put(16 + k, rest - middle)
        for c in range(3):
            high = coarse(found[6 + c])
            put(24 + c, high)
            put(32 + c, found[6 + c] - high)
            put(40 + c, high)
        return carry

    lax.fori_loop(0, slots_total // SEGMENTS, collect, 0)
    seg_at = lax.broadcasted_iota(jnp.int32, (SEGMENTS, HALF), 0)
    own_seg = seg_at == lax.broadcasted_iota(jnp.int32, (SEGMENTS, HALF), 1) % SEGMENTS

    def draw_local(slot):
        coefs = work_ref[pl.ds(pl.multiple_of(slot * COEF_ROWS, COEF_ROWS), COEF_ROWS), :].astype(
            jnp.bfloat16
        )
        coef_ref[slot] = coefs
        power = lax.dot_general(coefs, basis_ref[...], DOWN, preferred_element_type=jnp.float32)
        through = [jnp.ones((SEGMENTS, HALF), jnp.float32) for side in range(2)]
        weights = [[], []]
        for step in range(STEPS):
            for side in range(2):
                alpha = jnp.exp2(
                    power[step * SEGMENTS : (step + 1) * SEGMENTS, side * HALF : (side + 1) * HALF]
                )
                weight = alpha * through[side]
                through[side] = through[side] - weight
                weights[side].append(weight)
        weight = jnp.concatenate([jnp.concatenate(w, axis=0) for w in weights], axis=1)
        tints = []
        for part in (24, 32):
            for c in range(3):
                row = work_ref[pl.ds(slot * COEF_ROWS + part + c, 1), :]
                tints.append(jnp.where(own_seg, jnp.broadcast_to(row, (SEGMENTS, HALF)), 0.0))
        tint = jnp.concatenate(tints, axis=0).astype(jnp.bfloat16)
        sums = jnp.dot(
            jnp.concatenate([tint, tint], axis=1),
            jnp.concatenate(halves(weight), axis=0),
            preferred_element_type=jnp.float32,
        )
        return through, sums[0:24] + sums[24:48]

    def draw_join(slot, carry, through, sums):
        tile = tile_ref[0, slot]
        fresh = (slot == 0) | (tile != tile_ref[0, jnp.maximum(slot - 1, 0)])
        after = []
        for side in range(2):
            start = jnp.where(fresh, 1.0, carry[side][0])
            running = through[side]
            for shift in (1, 2, 4):
                running = jnp.where(
                    seg_at >= shift, running * pltpu.roll(running, shift, 0), running
                )
            before = jnp.where(seg_at == 0, 1.0, pltpu.roll(running, 1, 0)) * start
            kept = [start * running[SEGMENTS - 1 : SEGMENTS]]
            lanes = slice(side * HALF, (side + 1) * HALF)
            saved_ref[slot, 0, :, lanes] = before
            saved_ref[slot, 1, :, lanes] = through[side]
            for c in range(3):
                part = sums[c * SEGMENTS : (c + 1) * SEGMENTS, lanes]
                saved_ref[slot, 2 + c, :, lanes] = part
                shade_sum = jnp.sum(before * part, axis=0, keepdims=True)
                shade_sum = jnp.where(fresh, 0.0, carry[side][1 + c]) + shade_sum
                image_ref[slot, c : c + 1, lanes] = shade_sum
                kept.append(shade_sum)
            after.append(tuple(kept))
        return tuple(after)

    def draw(pair, carry):
        locals_two = [draw_local(GROUP * pair + k) for k in range(GROUP)]
        for k in range(GROUP):
            carry = draw_join(GROUP * pair + k, carry, *locals_two[k])
        return carry

    start = (jnp.ones((1, HALF), jnp.float32),) + (jnp.zeros((1, HALF), jnp.float32),) * 3
    lax.fori_loop(0, slots_total // GROUP, draw, (start, start))
    lane_tile = lax.broadcasted_iota(jnp.int32, (SEGMENTS, HALF), 1) // TILE_SIDE
    for side in range(2):
        lanes = slice(side * HALF, (side + 1) * HALF)
        for c in range(3):
            shown = jnp.zeros((SEGMENTS, HALF), jnp.float32)
            for tile in range(TILES_DEV):
                row = image_ref[last_ref[tile], c : c + 1, lanes]
                row = jnp.broadcast_to(row, (SEGMENTS, HALF))
                moved = pltpu.roll(row, TILE_SIDE * tile, 1) if tile else row
                for bit in (1, 2, 4):
                    moved = jnp.where(
                        (seg_at & bit) > 0, pltpu.roll(moved, HALF - TILE_SIDE * bit, 1), moved
                    )
                shown = jnp.where(lane_tile == tile, moved, shown)
            picture_ref[c, side * SEGMENTS : (side + 1) * SEGMENTS, :] = shown


def backward_part(
    tile_ref, rec_ref, coef_ref, saved_ref, grad_ref, slots_ref, out_ref,
    rhs_ref, mom_ref, back_ref, where_ref, acc_ref,
    alpha_ref, lit_ref, share_ref, heavy_ref, force_ref, behind_ref,
):
    chunks = out_ref.shape[1] // BLOCK
    slots_total = coef_ref.shape[0]
    acc_ref[...] = jnp.zeros_like(acc_ref)
    basis = pixel_basis()
    blank = jnp.zeros_like(basis)
    basis16 = jnp.concatenate([basis, blank], axis=0).astype(jnp.bfloat16)
    for tile in range(TILES_DEV):
        grads = grad_ref[tile]
        high = coarse(grads)
        rhs_ref[tile, :, 0 : 2 * HALF] = jnp.concatenate([basis] * 3 + [blank] * 3, axis=0).astype(
            jnp.bfloat16
        )
        rhs_ref[tile, :, 2 * HALF : 4 * HALF] = jnp.concatenate(
            [blank] * 3 + [high, high, grads - high], axis=0
        ).astype(jnp.bfloat16)
    seg_at = lax.broadcasted_iota(jnp.int32, (SEGMENTS, HALF), 0)

    def prepare(slot, carry, buf):
        tile = tile_ref[0, slot]
        later = tile_ref[0, jnp.minimum(slot + 1, slots_total - 1)]
        final = (slot == slots_total - 1) | (tile != later)
        shown = jnp.minimum(tile, TILES_DEV - 1)
        grads = grad_ref[shown]
        after = []
        for side in range(2):
            lanes = slice(side * HALF, (side + 1) * HALF)
            start = jnp.where(final, 0.0, carry[side])
            total = grads[0:1, lanes] * saved_ref[slot, 2, :, lanes]
            for c in (1, 2):
                total = total + grads[c : c + 1, lanes] * saved_ref[slot, 2 + c, :, lanes]
            factor = saved_ref[slot, 1, :, lanes]
            for shift in (1, 2, 4):
                inside = seg_at < SEGMENTS - shift
                total = jnp.where(
                    inside, total + factor * pltpu.roll(total, SEGMENTS - shift, 0), total
                )
                factor = jnp.where(
                    inside, factor * pltpu.roll(factor, SEGMENTS - shift, 0), factor
                )
            entering = total + factor * start
            after.append(entering[0:1])
            behind_ref[buf, :, lanes] = jnp.where(
                seg_at < SEGMENTS - 1, pltpu.roll(entering, SEGMENTS - 1, 0), start
            )
        both = lax.dot_general(
            coef_ref[slot], rhs_ref[shown], DOWN, preferred_element_type=jnp.float32
        )
        alpha_ref[buf] = jnp.exp2(both[:, : 2 * HALF])
        lit_ref[buf] = both[:, 2 * HALF :]
        return tuple(after)

    def halve(target_ref, buf, step, lanes, pair):
        value = jnp.concatenate(pair, axis=0)
        high, low = halves(value)
        rows = 2 * SEGMENTS * step
        target_ref[buf, rows : rows + 2 * SEGMENTS, lanes] = high
        target_ref[buf, BLOCK + rows : BLOCK + rows + 2 * SEGMENTS, lanes] = low

    def trace(slots, bufs):
        chains = [(k, side) for k in range(len(slots)) for side in range(2)]
        lanes = [slice(side * HALF, (side + 1) * HALF) for side in range(2)]
        through = {
            (k, side): saved_ref[slots[k], 0, :, lanes[side]] for k, side in chains
        }
        for step in range(STEPS // 2):
            for k, side in chains:
                pair = []
                for at in (2 * step, 2 * step + 1):
                    rows = slice(at * SEGMENTS, (at + 1) * SEGMENTS)
                    weight = alpha_ref[bufs[k], rows, lanes[side]] * through[k, side]
                    through[k, side] = through[k, side] - weight
                    share_ref[bufs[k], rows, lanes[side]] = weight
                    pair.append(weight)
                halve(heavy_ref, bufs[k], step, lanes[side], pair)
        later = {(k, side): behind_ref[bufs[k], :, lanes[side]] for k, side in chains}
        for step in reversed(range(STEPS // 2)):
            for k, side in chains:
                pair = []
                for at in (2 * step + 1, 2 * step):
                    rows = slice(at * SEGMENTS, (at + 1) * SEGMENTS)
                    gap = lit_ref[bufs[k], rows, lanes[side]] - later[k, side]
                    later[k, side] = later[k, side] + alpha_ref[bufs[k], rows, lanes[side]] * gap
                    pair.append(share_ref[bufs[k], rows, lanes[side]] * gap)
                halve(force_ref, bufs[k], step, lanes[side], pair[::-1])

    def reduce(slot, place, buf):
        shown = jnp.minimum(tile_ref[0, slot], TILES_DEV - 1)
        found = lax.dot_general(
            basis16, force_ref[buf], ACROSS, preferred_element_type=jnp.float32
        )
        painted = lax.dot_general(
            jnp.concatenate(halves(grad_ref[shown]), axis=0),
            heavy_ref[buf],
            ACROSS,
            preferred_element_type=jnp.float32,
        )
        painted = painted[0:8] + painted[8:16]
        mom_ref[place, 0:8, :] = found[0:8, :BLOCK] + found[0:8, BLOCK:]
        mom_ref[place, 8:16, :] = painted[:, :BLOCK] + painted[:, BLOCK:]

    runs = slots_total // WIDTH

    def slot_of(run, k):
        return jnp.clip(runs - 1 - run, 0, slots_total // WIDTH - 1) * WIDTH + k

    def ready(run, carry, half):
        for k in reversed(range(WIDTH)):
            carry = prepare(slot_of(run, k), carry, half * WIDTH + k)
        return carry

    def pull(turn, carry):
        for part in range(4):
            half = part % 2
            run = 4 * turn + part
            for k in range(WIDTH):
                slot = slot_of(run - 1, k)
                late = (run == 0) | (run > runs)
                reduce(slot, jnp.where(late, slots_total, slot), (1 - half) * WIDTH + k)
            carry = ready(run + 1, carry, 1 - half)
            trace(
                [slot_of(run, k) for k in range(WIDTH)],
                [half * WIDTH + k for k in range(WIDTH)],
            )
        return carry

    zeros = jnp.zeros((1, HALF), jnp.float32)
    carry = ready(0, (zeros, zeros), 0)
    lax.fori_loop(0, (runs + 4) // 4, pull, carry)
    lane_rows = lax.broadcasted_iota(jnp.int32, (BLOCK, 4 * BLOCK), 0)
    chunk_rows = lax.broadcasted_iota(jnp.int32, (chunks, BLOCK), 0)

    def settle(group, carry):
        first = pl.multiple_of(group * SEGMENTS, SEGMENTS)
        tiles = tiles_of(tile_ref, first)
        used = tiles < TILES_DEV
        rows = pl.ds(first, SEGMENTS)

        m_xx, m_xy, m_yy, m_x, m_y, m_0 = [
            mom_ref[rows, k, :] for k in range(6)
        ]
        at_x, at_y, con_a, con_b, con_c, shut_s = [rec_ref[k, rows, :] for k in range(6)]
        h_x = m_x - at_x * m_0
        h_y = m_y - at_y * m_0
        h_xx = m_xx - 2.0 * at_x * m_x + at_x * at_x * m_0
        h_xy = m_xy - at_x * m_y - at_y * m_x + at_x * at_y * m_0
        h_yy = m_yy - 2.0 * at_y * m_y + at_y * at_y * m_0
        results = [
            -2.0 * con_a * h_x - con_b * h_y,
            -2.0 * con_c * h_y - con_b * h_x,
            -0.5 * h_xx,
            -h_xy,
            -0.5 * h_yy,
            shut_s * m_0,
        ] + [mom_ref[rows, 8 + c, :] for c in range(3)]
        for f, value in enumerate(results):
            kept = jnp.where(used, value, 0.0)
            high = coarse(kept)
            back_ref[rows, f, :] = high
            back_ref[rows, 12 + f, :] = kept - high
        slots = slots_ref[rows, :]
        where_ref[0, rows, :] = slots % BLOCK
        where_ref[1, rows, :] = slots // BLOCK
        for quad in range(0, SEGMENTS, 4):
            stacked = []
            for k in range(quad, quad + 4):
                hit = chunk_rows == where_ref[1, pl.ds(first + k, 1), :]
                stacked.append(
                    jnp.concatenate(
                        [
                            jnp.where(hit, back_ref[first + k, part + f : part + f + 1, :], 0.0)
                            for part in (0, 12)
                            for f in range(FIELDS)
                        ],
                        axis=0,
                    ).astype(jnp.bfloat16)
                )
            fine = jnp.concatenate(
                [where_ref[0, pl.ds(first + k, 1), :] for k in range(quad, quad + 4)], axis=1
            )
            select = jnp.where(lane_rows == fine, 1.0, 0.0).astype(jnp.bfloat16)
            acc_ref[...] += lax.dot_general(
                jnp.concatenate(stacked, axis=1), select, ACROSS, preferred_element_type=jnp.float32
            )
        return carry

    lax.fori_loop(0, slots_total // SEGMENTS, settle, 0)
    total = FIELDS * chunks
    for chunk in range(chunks):
        lanes = slice(chunk * BLOCK, (chunk + 1) * BLOCK)
        out_ref[0:8, lanes] = (
            acc_ref[pl.ds(chunk, 8, stride=chunks), :]
            + acc_ref[pl.ds(total + chunk, 8, stride=chunks), :]
        )
        at = 8 * chunks + chunk
        out_ref[8:9, lanes] = acc_ref[at : at + 1, :] + acc_ref[total + at : total + at + 1, :]


def hbm():
    return pl.BlockSpec(memory_space=pltpu.HBM)


def smem():
    return pl.BlockSpec(memory_space=pltpu.SMEM)


def vmem():
    return pl.BlockSpec(memory_space=pltpu.VMEM)


WAYS = [(down, right) for down in (-1, 0, 1) for right in (-1, 0, 1) if (down, right) != (0, 0)]
NORM = sum(math.exp(-m * m / 4.5) for m in range(-5, 6))
EXT_ROWS = 40
MID_ROWS = 32


def neighbour(bands, columns, way):
    there_band = lax.axis_index("gauss") + way[0]
    there_col = lax.axis_index("tile") + way[1]
    exists = (there_band >= 0) & (there_band < bands) & (there_col >= 0) & (there_col < columns)
    return exists, (there_band, there_col)


def greet_round(barrier, bands, columns):
    peers = jnp.int32(0)
    for way in WAYS:
        exists, there = neighbour(bands, columns, way)
        peers = peers + exists.astype(jnp.int32)

        @pl.when(exists)
        def _(there=there):
            pl.semaphore_signal(barrier, inc=1, device_id=there, device_id_type=MESH)

    return peers


def border_copies(bands, columns, plane_ref, edge_ref, tall_ref, side_ref, send_sem, recv_sem):
    found = []
    for at, way in enumerate(WAYS):
        exists, there = neighbour(bands, columns, way)
        landing = len(WAYS) - 1 - at
        source = plane_ref if way[1] == 0 else edge_ref
        target = tall_ref.at[landing] if way[1] == 0 else side_ref.at[landing]
        found.append(
            (
                exists,
                pltpu.make_async_remote_copy(
                    src_ref=source,
                    dst_ref=target,
                    send_sem=send_sem.at[at],
                    recv_sem=recv_sem.at[landing],
                    device_id=there,
                    device_id_type=MESH,
                ),
                pltpu.make_async_remote_copy(
                    src_ref=source,
                    dst_ref=tall_ref.at[at] if way[1] == 0 else side_ref.at[at],
                    send_sem=send_sem.at[at],
                    recv_sem=recv_sem.at[at],
                    device_id=there,
                    device_id_type=MESH,
                ),
            )
        )
    return found


def border_start(copies):
    for exists, out, back in copies:

        @pl.when(exists)
        def _(out=out):
            out.start()


def border_wait(copies):
    for exists, out, back in copies:

        @pl.when(exists)
        def _(out=out, back=back):
            out.wait_send()
            back.wait_recv()


def pack_edges(plane_ref, edge_ref):
    lanes = lax.broadcasted_iota(jnp.int32, edge_ref.shape, 1)
    packed = jnp.zeros(edge_ref.shape, jnp.float32)
    for c in range(3):
        plane = plane_ref[c]
        near = pltpu.roll(plane, 32 * c, 1) if c else plane
        far = pltpu.roll(plane, 32 * c + 32, 1)
        packed = jnp.where(
            lanes // 32 == c, jnp.where(lanes % 32 < 16, near, far), packed
        )
    edge_ref[...] = packed


def stretch(above, own, below):
    turn = lax.broadcasted_iota(jnp.int32, (8, own.shape[1]), 0) >= 6
    mixed = jnp.where(turn, above[0:8], below[8:16])
    return jnp.concatenate([own, above[8:16], below[0:8], mixed], axis=0)


def extend(plane_ref, tall_ref, side_ref):
    east = lax.broadcasted_iota(jnp.int32, side_ref.shape[1:], 1) % 32 < 16
    borders = [
        jnp.where(east, side_ref[WAYS.index((down, 1))], side_ref[WAYS.index((down, -1))])
        for down in (-1, 0, 1)
    ]
    border = stretch(*borders)
    planes = []
    for c in range(3):
        main = stretch(
            tall_ref[WAYS.index((-1, 0)), c], plane_ref[c], tall_ref[WAYS.index((1, 0)), c]
        )
        turned = pltpu.roll(border, HALF - 32 * c, 1) if c else border
        planes.append(jnp.concatenate([main, turned], axis=1))
    return planes


def window_weight(gap):
    gap = gap.astype(jnp.float32)
    return jnp.where(jnp.abs(gap) < 5.5, jnp.exp(gap * gap / -4.5) * (1.0 / NORM), 0.0)


def split_rows(value):
    first = coarse(value)
    rest = value - first
    second = coarse(rest)
    return first, second, rest - second


def six_data(value, axis):
    first, second, third = split_rows(value)
    return jnp.concatenate([first, second, third, first, second, first], axis=axis).astype(
        jnp.bfloat16
    )


def six_weights(value, axis):
    first, second, third = split_rows(value)
    return jnp.concatenate([first, first, first, second, second, third], axis=axis).astype(
        jnp.bfloat16
    )


def ext_row(at):
    return jnp.where(at < 16, at, jnp.where(at < 24, at - 24, jnp.where(at < 38, at - 8, at - 48)))


def ext_col(at):
    return jnp.where(at < 144, at, jnp.where(at < 160, at - 160, 10000))


def mid_col(at):
    return jnp.where(at < 192, at, at - 256)


def iota(shape, axis):
    return lax.broadcasted_iota(jnp.int32, shape, axis)


def fdot(left, right):
    return jnp.dot(left, right, preferred_element_type=jnp.float32)


def contrast_part(
    bands, columns, shown_ref, aim_ref, out_ref,
    edge_ref, tall_ref, side_ref, wide_ref, back_ref, send_sem, recv_sem,
):
    band = lax.axis_index("gauss")
    column = lax.axis_index("tile")
    rows, cols = shown_ref.shape[1:]
    pack_edges(shown_ref, edge_ref)
    copies = border_copies(
        bands, columns, shown_ref, edge_ref, tall_ref, side_ref, send_sem, recv_sem
    )
    border_start(copies)
    wide = 2 * cols
    for half in range(2):
        lanes = slice(half * cols, (half + 1) * cols)
        shape = (wide, cols)
        across = window_weight(mid_col(iota(shape, 1) + half * cols) - ext_col(iota(shape, 0)))
        wide_ref[:, lanes] = six_weights(across, 0)
    back = window_weight(mid_col(iota((wide, cols), 0)) - iota((wide, cols), 1))
    back_ref[...] = six_weights(back, 0)
    shape = (MID_ROWS, EXT_ROWS)
    down = window_weight(iota(shape, 0) - 5 - ext_row(iota(shape, 1)))
    down = six_weights(down, 1)
    shape = (rows, MID_ROWS)
    up = six_weights(window_weight(iota(shape, 0) - iota(shape, 1) + 5), 1)
    border_wait(copies)
    pics = extend(shown_ref, tall_ref, side_ref)
    strips = []
    for kind in range(4):
        for c in range(3):
            pic, aim = pics[c], aim_ref[c]
            plane = (pic, aim, pic * pic + aim * aim, pic * aim)[kind] if kind > 1 else (
                pic if kind == 0 else aim
            )
            strips.append(fdot(down, six_data(plane, 0)))
    moments = fdot(six_data(jnp.concatenate(strips, axis=0), 1), wide_ref[...])
    shape = (MID_ROWS, wide)
    row_at = band * rows + iota(shape, 0) - 5
    col_at = column * cols + mid_col(iota(shape, 1))
    inside = (row_at >= 0) & (row_at < bands * rows) & (col_at >= 0) & (col_at < columns * cols)
    strips = [None] * 9
    for c in range(3):
        mu_x, mu_y, squares, cross = [
            moments[(3 * kind + c) * MID_ROWS : (3 * kind + c + 1) * MID_ROWS] for kind in range(4)
        ]
        mean_xy = mu_x * mu_y
        mean_sq = mu_x * mu_x + mu_y * mu_y
        top_1 = 2.0 * mean_xy + CONST_ONE
        top_2 = 2.0 * (cross - mean_xy) + CONST_TWO
        low_1 = mean_sq + CONST_ONE
        low_2 = squares - mean_sq + CONST_TWO
        inverse = -0.2 / (low_1 * low_2)
        value = top_1 * top_2 * inverse
        value_1 = value * low_2 * inverse * -5.0
        value_2 = value * low_1 * inverse * -5.0
        slope_mean = 2.0 * mu_y * (top_2 - top_1) * inverse - 2.0 * mu_x * (value_1 - value_2)
        for kind, slope in enumerate((slope_mean, -value_2, 2.0 * top_1 * inverse)):
            strips[3 * kind + c] = fdot(up, six_data(jnp.where(inside, slope, 0.0), 0))
    spread = fdot(six_data(jnp.concatenate(strips, axis=0), 1), back_ref[...])
    lane_row = iota((SEGMENTS, HALF), 1) // TILE_SIDE
    seg_at = iota((SEGMENTS, HALF), 0)
    out_ref[...] = jnp.zeros_like(out_ref)
    for c in range(3):
        pic = shown_ref[c]
        aim = aim_ref[c, 0:rows, 0:cols]
        parts = [spread[(3 * kind + c) * rows : (3 * kind + c + 1) * rows] for kind in range(3)]
        total = parts[0] + 2.0 * pic * parts[1] + aim * parts[2] + 1.6 * (pic - aim)
        for side in range(2):
            part = total[side * SEGMENTS : (side + 1) * SEGMENTS]
            skewed = pltpu.roll(part, 0, 1, stride=TILE_SIDE, stride_axis=0)
            for tile in range(TILES_DEV):
                moved = pltpu.roll(skewed, HALF - TILE_SIDE * tile, 1) if tile else skewed
                kept = jnp.where(lane_row == seg_at, moved, 0.0)
                out_ref[tile, c : c + 1, side * HALF : (side + 1) * HALF] = jnp.sum(
                    kept, axis=0, keepdims=True
                )


def border_scratch(rows, cols):
    ways = len(WAYS)
    return [
        pltpu.VMEM((rows, cols), jnp.float32),
        pltpu.VMEM((ways, 3, rows, cols), jnp.float32),
        pltpu.VMEM((ways, rows, cols), jnp.float32),
    ]


def basis_rows(x, y, z):
    xx, yy, zz = x * x, y * y, z * z
    return [
        jnp.full_like(x, BASE_ZERO),
        -BASE_ONE * y,
        BASE_ONE * z,
        -BASE_ONE * x,
        BASE_TWO[0] * x * y,
        BASE_TWO[1] * y * z,
        BASE_TWO[2] * (2.0 * zz - xx - yy),
        BASE_TWO[3] * x * z,
        BASE_TWO[4] * (xx - yy),
        BASE_THREE[0] * y * (3.0 * xx - yy),
        BASE_THREE[1] * x * y * z,
        BASE_THREE[2] * y * (4.0 * zz - xx - yy),
        BASE_THREE[3] * z * (2.0 * zz - 3.0 * xx - 3.0 * yy),
        BASE_THREE[4] * x * (4.0 * zz - xx - yy),
        BASE_THREE[5] * z * (xx - yy),
        BASE_THREE[6] * x * (xx - 3.0 * yy),
    ]


def slope_rows(x, y, z):
    xx, yy, zz = x * x, y * y, z * z
    xy, yz, xz = x * y, y * z, x * z
    none = jnp.zeros_like(x)
    one = jnp.ones_like(x)
    two, three = BASE_TWO, BASE_THREE
    along_x = [
        none, none, none, -BASE_ONE * one,
        two[0] * y, none, -2.0 * two[2] * x, two[3] * z, 2.0 * two[4] * x,
        6.0 * three[0] * xy, three[1] * yz, -2.0 * three[2] * xy, -6.0 * three[3] * xz,
        three[4] * (4.0 * zz - 3.0 * xx - yy), 2.0 * three[5] * xz, three[6] * (3.0 * xx - 3.0 * yy),
    ]
    along_y = [
        none, -BASE_ONE * one, none, none,
        two[0] * x, two[1] * z, -2.0 * two[2] * y, none, -2.0 * two[4] * y,
        three[0] * (3.0 * xx - 3.0 * yy), three[1] * xz, three[2] * (4.0 * zz - xx - 3.0 * yy),
        -6.0 * three[3] * yz, -2.0 * three[4] * xy, -2.0 * three[5] * yz, -6.0 * three[6] * xy,
    ]
    along_z = [
        none, none, BASE_ONE * one, none,
        none, two[1] * y, 4.0 * two[2] * z, two[3] * x, none,
        none, three[1] * xy, 8.0 * three[2] * yz, three[3] * (6.0 * zz - 3.0 * xx - 3.0 * yy),
        8.0 * three[4] * xz, three[5] * (xx - yy), none,
    ]
    return along_x, along_y, along_z


def lane_of():
    return lax.broadcasted_iota(jnp.int32, (8, BLOCK), 1)


def row_of():
    return lax.broadcasted_iota(jnp.int32, (8, BLOCK), 0)


def gather_rows(table_ref, ninth_ref, chunks, index):
    index = jnp.broadcast_to(index, (8, BLOCK))
    fine = index % BLOCK
    chunk_at = index // BLOCK
    first = None
    ninth = jnp.zeros((8, BLOCK), jnp.float32)
    for chunk in range(chunks):
        got = pick(table_ref[0:8, chunk * BLOCK : (chunk + 1) * BLOCK], fine)
        first = got if chunk == 0 else jnp.where(chunk_at == chunk, got, first)
    for base in range(0, chunks, 8):
        got = pick(ninth_ref[base : base + 8, :], fine)
        ninth = ninth + jnp.where(chunk_at == row_of() + base, got, 0.0)
    return first, jnp.sum(ninth, axis=0, keepdims=True)


def pack_two(first, last):
    left = lane_of() < BLOCK // 2
    swapped = pltpu.roll(first, BLOCK // 2, 1)
    one = jnp.where(left, first, pltpu.roll(swapped, 4, 0))
    two = jnp.where(left, swapped, pltpu.roll(first, 4, 0))
    tail = row_of() >= 4
    ninth = jnp.broadcast_to(last, (8, BLOCK))
    return jnp.where(tail, ninth, one), jnp.where(tail, pltpu.roll(ninth, BLOCK // 2, 1), two)


def unpack_two(one, two):
    left = lane_of() < BLOCK // 2
    upper = jnp.where(left, one, pltpu.roll(two, BLOCK // 2, 1))
    lower = jnp.where(left, pltpu.roll(one, BLOCK // 2, 1), two)
    return jnp.where(row_of() < 4, upper, pltpu.roll(lower, 4, 0)), upper[4:5]


def ring(gap, owners):
    there = lax.axis_index("gauss") + gap
    return jnp.where(there >= owners, there - owners, there)


def greet(owners):
    barrier = pltpu.get_barrier_semaphore()
    column = lax.axis_index("tile")
    for gap in range(1, owners):
        pl.semaphore_signal(
            barrier, inc=1, device_id=(ring(gap, owners), column), device_id_type=MESH
        )
    return barrier


def parcel(owners, gap, out_ref, in_ref, send_sem, recv_sem):
    band = lax.axis_index("gauss")
    there = ring(gap, owners)
    return pltpu.make_async_remote_copy(
        src_ref=out_ref.at[there],
        dst_ref=in_ref.at[band],
        send_sem=send_sem.at[gap],
        recv_sem=recv_sem.at[gap],
        device_id=(there, lax.axis_index("tile")),
        device_id_type=MESH,
    )


def post(owners, out_ref, in_ref, send_sem, recv_sem):
    band = lax.axis_index("gauss")
    for gap in range(1, owners):
        parcel(owners, gap, out_ref, in_ref, send_sem, recv_sem).start()
    in_ref[band] = out_ref[band]


def take_in(owners, out_ref, in_ref, send_sem, recv_sem):
    for gap in range(1, owners):
        parcel(owners, gap, out_ref, in_ref, send_sem, recv_sem).wait()


def count_tiles(tile_ref, last_ref):
    for tile in range(TILES_DEV):
        last = jnp.int32(-1)
        for slot in range(tile_ref.shape[1]):
            last = last + (tile_ref[0, slot] <= tile).astype(jnp.int32)
        last_ref[tile] = last


def deliver_part(
    owners, columns, loads, clear, recv_ref, home_ref, aim_ref, order_ref, slope_ref,
    tile_ref, last_ref, splats_ref, sh_ref, send_ref, target_ref, slots_ref,
    table_ref, ninth_ref, edge_ref, tall_ref, side_ref, border_send, border_recv,
    out_ref, in_ref, send_sem, recv_sem,
):
    for load in loads:
        load.start()
    for ref in clear:
        ref[...] = jnp.zeros_like(ref)
    barrier = greet(owners)
    peers = greet_round(barrier, owners, columns)
    for load in loads:
        load.wait()
    own = splats_ref.shape[1]
    chunks = own // BLOCK
    basis = jnp.concatenate(
        basis_rows(splats_ref[6:7, :], splats_ref[7:8, :], splats_ref[8:9, :]), axis=0
    )
    colours = [
        0.5 + jnp.sum(sh_ref[16 * c : 16 * (c + 1), :] * basis, axis=0, keepdims=True)
        for c in range(3)
    ]
    table_ref[0:6, :] = splats_ref[0:6, :]
    table_ref[6:8, :] = jnp.concatenate(colours[0:2], axis=0)
    for chunk in range(chunks):
        ninth_ref[chunk : chunk + 1, :] = colours[2][:, chunk * BLOCK : (chunk + 1) * BLOCK]
    for chunk in range(chunks):
        one, two = pack_two(
            *gather_rows(table_ref, ninth_ref, chunks, send_ref[chunk : chunk + 1, :])
        )
        out_ref[2 * chunk] = one
        out_ref[2 * chunk + 1] = two
    pack_edges(target_ref, edge_ref)
    pl.semaphore_wait(barrier, owners - 1 + peers)
    post(owners, out_ref, in_ref, send_sem, recv_sem)
    copies = border_copies(
        owners, columns, target_ref, edge_ref, tall_ref, side_ref, border_send, border_recv
    )
    border_start(copies)
    chunk_rows = lax.broadcasted_iota(jnp.int32, (chunks, BLOCK), 0)
    lanes = lax.broadcasted_iota(jnp.int32, (chunks, BLOCK), 1).astype(jnp.float32)
    lane_rows = lax.broadcasted_iota(jnp.int32, (BLOCK, BLOCK), 0)
    home = jnp.zeros((2 * chunks, BLOCK), jnp.float32)
    for chunk in range(chunks):
        index = send_ref[chunk : chunk + 1, :]
        hit = chunk_rows == index // BLOCK
        source = jnp.concatenate(
            [jnp.where(hit, float(chunk), 0.0), jnp.where(hit, lanes, 0.0)], axis=0
        ).astype(jnp.bfloat16)
        select = jnp.where(lane_rows == index % BLOCK, 1.0, 0.0).astype(jnp.bfloat16)
        home = home + lax.dot_general(source, select, ACROSS, preferred_element_type=jnp.float32)
    home_ref[...] = (home[:chunks] * float(BLOCK) + home[chunks:]).astype(jnp.int32)
    count_tiles(tile_ref, last_ref)
    facing = [splats_ref[6 + d : 7 + d, :] for d in range(3)]
    slope_ref[0:16, :] = basis
    for d, rows in enumerate(slope_rows(*facing)):
        slope_ref[16 * (d + 1) : 16 * (d + 2), :] = jnp.concatenate(rows, axis=0)
    for first in range(0, slots_ref.shape[0], SEGMENTS):
        rows = slice(first, first + SEGMENTS)
        order_ref[rows, :] = spread_order(slots_ref[rows, :])
    border_wait(copies)
    for c, plane in enumerate(extend(target_ref, tall_ref, side_ref)):
        aim_ref[c] = plane
    take_in(owners, out_ref, in_ref, send_sem, recv_sem)
    for chunk in range(chunks):
        first, ninth = unpack_two(in_ref[2 * chunk], in_ref[2 * chunk + 1])
        recv_ref[0:8, chunk * BLOCK : (chunk + 1) * BLOCK] = first
        recv_ref[8:9, chunk * BLOCK : (chunk + 1) * BLOCK] = ninth


def parcels(owners):
    return [
        pltpu.VMEM((owners, PACKED, BLOCK), jnp.float32),
        pltpu.VMEM((owners, PACKED, BLOCK), jnp.float32),
        pltpu.SemaphoreType.DMA((owners,)),
        pltpu.SemaphoreType.DMA((owners,)),
    ]


def return_part(owners, pulled_ref, in_ref, out_ref, send_sem, recv_sem):
    chunks = pulled_ref.shape[1] // BLOCK
    for chunk in range(chunks):
        lanes = slice(chunk * BLOCK, (chunk + 1) * BLOCK)
        one, two = pack_two(pulled_ref[0:8, lanes], pulled_ref[8:9, lanes])
        out_ref[2 * chunk] = one
        out_ref[2 * chunk + 1] = two
    post(owners, out_ref, in_ref, send_sem, recv_sem)
    take_in(owners, out_ref, in_ref, send_sem, recv_sem)


def train_kernel(owners, columns, counts, *refs):
    parts = []
    for count in counts:
        parts.append(refs[:count])
        refs = refs[count:]
    sources, (landed_ref, slope_ref, home_ref, shown_ref), local, shared, draw_refs = parts[:5]
    pull_refs, early, border, late, deliver_refs, return_refs = parts[5:]
    tile_ref, last_ref, splats_ref, sh_ref, send_ref, target_ref, slots_ref, load_sem = local
    recv_ref, aim_ref, order_ref, rec_ref, coef_ref, saved_ref, grad_ref, pulled_ref = shared
    loads = [
        pltpu.make_async_copy(source, into, load_sem.at[at])
        for at, (source, into) in enumerate(
            zip(sources, (splats_ref, sh_ref, send_ref, target_ref, slots_ref, tile_ref))
        )
    ]
    deliver_part(
        owners, columns, loads, early[1:3] + late[1:3], recv_ref, home_ref, aim_ref, order_ref,
        slope_ref, *local[:-1], *border, *early, *deliver_refs,
    )
    forward_part(
        tile_ref, last_ref, recv_ref, order_ref, shown_ref, rec_ref, coef_ref, saved_ref,
        *draw_refs,
    )
    contrast_part(owners, columns, shown_ref, aim_ref, grad_ref, *late)
    backward_part(
        tile_ref, rec_ref, coef_ref, saved_ref, grad_ref, order_ref, pulled_ref, *pull_refs
    )
    return_part(owners, pulled_ref, landed_ref, *return_refs)


def train(splats, sh_coeffs, send_list, target, slots, tile_ids):
    own = splats.shape[1]
    chunks = own // BLOCK
    owners = lax.axis_size("gauss")
    rows, cols = target.shape[1:]
    ways = len(WAYS)
    slots_total = slots.shape[0]
    side = TILE_SIDE * TILE_SIDE

    def f32(*shape):
        return pltpu.VMEM(shape, jnp.float32)

    def bf16(*shape):
        return pltpu.VMEM(shape, jnp.bfloat16)

    def i32(*shape):
        return pltpu.VMEM(shape, jnp.int32)

    sems = pltpu.SemaphoreType.DMA
    args = (splats, sh_coeffs, send_list.reshape(chunks, BLOCK), target, slots, tile_ids)
    outs = (
        jax.ShapeDtypeStruct((owners, PACKED, BLOCK), jnp.float32),
        jax.ShapeDtypeStruct((64, own), jnp.float32),
        jax.ShapeDtypeStruct((chunks, BLOCK), jnp.int32),
        jax.ShapeDtypeStruct(target.shape, jnp.float32),
    )
    local = [
        pltpu.SMEM(tile_ids.shape, jnp.int32),
        pltpu.SMEM((TILES_DEV,), jnp.int32),
        f32(*splats.shape),
        f32(*sh_coeffs.shape),
        i32(chunks, BLOCK),
        f32(*target.shape),
        i32(*slots.shape),
        sems((len(args),)),
    ]
    shared = [
        f32(FIELDS, own),
        f32(3, EXT_ROWS, 2 * cols),
        i32(*slots.shape),
        f32(6, slots_total, BLOCK),
        bf16(slots_total, COEF_ROWS, BLOCK),
        f32(slots_total, 5, SEGMENTS, side),
        f32(TILES_DEV, 8, side),
        f32(FIELDS, own),
    ]
    draw_refs = [f32(slots_total * COEF_ROWS, BLOCK), f32(slots_total, 8, side), bf16(COEF_ROWS, side)]
    pull_refs = [
        bf16(TILES_DEV, COEF_ROWS, 2 * side),
        f32(slots_total + 1, 16, BLOCK),
        f32(slots_total, GRAD_ROWS, BLOCK),
        i32(2, slots_total, BLOCK),
        f32(2 * FIELDS * chunks, BLOCK),
        f32(2 * WIDTH, BLOCK, side),
        f32(2 * WIDTH, BLOCK, side),
        f32(2 * WIDTH, BLOCK, side),
        bf16(2 * WIDTH, 2 * BLOCK, side),
        bf16(2 * WIDTH, 2 * BLOCK, side),
        f32(2 * WIDTH, SEGMENTS, side),
    ]
    border = [f32(8, own), f32(chunks, BLOCK)]
    early = border_scratch(rows, cols) + [sems((ways,)), sems((ways,))]
    late = (
        border_scratch(rows, cols)
        + [bf16(12 * cols, 2 * cols), bf16(12 * cols, cols)]
        + [sems((ways,)), sems((ways,))]
    )
    landing, into, *pair = parcels(owners)
    groups = [local, shared, draw_refs, pull_refs, early, border, late]
    groups += [[landing, into] + pair, [landing] + pair]
    counts = (len(args), len(outs)) + tuple(len(group) for group in groups)
    return pl.pallas_call(
        functools.partial(train_kernel, owners, lax.axis_size("tile"), counts),
        out_shape=outs,
        in_specs=[hbm()] * len(args),
        out_specs=(vmem(),) * len(outs),
        scratch_shapes=sum(groups, []),
        compiler_params=pltpu.CompilerParams(
            collective_id=1, has_side_effects=True, vmem_limit_bytes=24 * 1024 * 1024
        ),
        name="train",
    )(*[pltpu.with_memory_space_constraint(value, pltpu.HBM) for value in args])


def settle_kernel(
    in_ref, slope_ref, home_ref, sh_ref, shown_ref, rendered_ref, splat_grad_ref, sh_grad_ref,
    table_ref, ninth_ref,
):
    rendered_ref[...] = shown_ref[...]
    chunks = sh_ref.shape[1] // BLOCK
    for chunk in range(chunks):
        first, ninth = unpack_two(in_ref[2 * chunk], in_ref[2 * chunk + 1])
        table_ref[:, chunk * BLOCK : (chunk + 1) * BLOCK] = first
        ninth_ref[chunk : chunk + 1, :] = ninth
    for chunk in range(chunks):
        lanes = slice(chunk * BLOCK, (chunk + 1) * BLOCK)
        first, last = gather_rows(table_ref, ninth_ref, chunks, home_ref[chunk : chunk + 1, :])
        splat_grad_ref[0:6, lanes] = first[0:6]
        tints = (first[6:7], first[7:8], last)
        basis = slope_ref[0:16, lanes]
        mixed = jnp.zeros((16, BLOCK), jnp.float32)
        for c in range(3):
            tint = jnp.broadcast_to(tints[c], (16, BLOCK))
            sh_grad_ref[16 * c : 16 * (c + 1), lanes] = tint * basis
            mixed = mixed + tint * sh_ref[16 * c : 16 * (c + 1), lanes]
        splat_grad_ref[6:9, lanes] = jnp.concatenate(
            [
                jnp.sum(mixed * slope_ref[16 * d : 16 * (d + 1), lanes], axis=0, keepdims=True)
                for d in (1, 2, 3)
            ],
            axis=0,
        )


def settle(landed, slopes, home, splats, sh_coeffs, shown):
    own = splats.shape[1]
    return pl.pallas_call(
        settle_kernel,
        out_shape=(
            jax.ShapeDtypeStruct(shown.shape, jnp.float32),
            jax.ShapeDtypeStruct(splats.shape, jnp.float32),
            jax.ShapeDtypeStruct(sh_coeffs.shape, jnp.float32),
        ),
        in_specs=[vmem()] * 5,
        out_specs=(vmem(), vmem(), vmem()),
        scratch_shapes=[
            pltpu.VMEM((8, own), jnp.float32),
            pltpu.VMEM((own // BLOCK, BLOCK), jnp.float32),
        ],
        compiler_params=pltpu.CompilerParams(vmem_limit_bytes=VMEM_ROOM),
        name="settle",
    )(landed, slopes, home, sh_coeffs, shown)


def body(splats, sh_coeffs, send_list, block_slots, block_tiles, target):
    landed, slopes, home, shown = train(
        splats, sh_coeffs, send_list, target, block_slots[0], block_tiles
    )
    return settle(landed, slopes, home, splats, sh_coeffs, shown)


def solution(mesh):
    in_specs = (
        P(None, ("gauss", "tile")),
        P(None, ("gauss", "tile")),
        P(("gauss", "tile")),
        P("gauss", "tile", None),
        P("gauss", "tile"),
        P(None, "gauss", "tile"),
    )
    out_specs = (P(None, "gauss", "tile"), P(None, ("gauss", "tile")), P(None, ("gauss", "tile")))
    return jax.shard_map(body, mesh=mesh, in_specs=in_specs, out_specs=out_specs, check_vma=False)
```

```python
import functools
import math

import jax
import jax.numpy as jnp
from jax import lax
from jax.experimental import pallas as pl
from jax.experimental.pallas import tpu as pltpu
from jax.sharding import PartitionSpec as P

TILE_SIDE = 16
TILES_DEV = 8


BASE_ZERO = 0.28209479177387814
BASE_ONE = 0.4886025119029199
BASE_TWO = (
    1.0925484305920792,
    -1.0925484305920792,
    0.31539156525252005,
    -1.0925484305920792,
    0.5462742152960396,
)
BASE_THREE = (
    -0.5900435899266435,
    2.890611442640554,
    -0.4570457994644658,
    0.3731763325901154,
    -0.4570457994644658,
    1.445305721320277,
    -0.5900435899266435,
)
CONST_ONE = 0.0001
CONST_TWO = 0.0009


SEGMENTS = 8
STEPS = 16
BLOCK = SEGMENTS * STEPS
HALF = 128
CENTRE = 7.5
MESH = pl.DeviceIdType.MESH
VMEM_ROOM = 16 * 1024 * 1024


LOG2E = 1.4426950408889634
FIELDS = 9
COEF_ROWS = 48
GROUP = 24
WIDTH = 2
TURN = 6
PACKED = 8
GRAD_ROWS = 24
ACROSS = (((1,), (1,)), ((), ()))
DOWN = (((0,), (0,)), ((), ()))


def pick(table, index):
    return jnp.take_along_axis(table, index, axis=1, mode="promise_in_bounds")


def coarse(value):
    return value.astype(jnp.bfloat16).astype(jnp.float32)


def halves(value):
    high = value.astype(jnp.bfloat16)
    low = (value - high.astype(jnp.float32)).astype(jnp.bfloat16)
    return high, low


def halve(target_ref, at, step, lanes, pair):
    high, low = halves(jnp.concatenate(pair, axis=0))
    rows = 2 * SEGMENTS * step
    target_ref[at, rows : rows + 2 * SEGMENTS, lanes] = high
    target_ref[at, BLOCK + rows : BLOCK + rows + 2 * SEGMENTS, lanes] = low


def pixel_basis():
    rows = lax.broadcasted_iota(jnp.int32, (8, 2 * HALF), 0)
    pixels = lax.broadcasted_iota(jnp.int32, (8, 2 * HALF), 1)
    along = (pixels % TILE_SIDE).astype(jnp.float32) - CENTRE
    down = (pixels // TILE_SIDE).astype(jnp.float32) - CENTRE
    basis = jnp.zeros((8, 2 * HALF), jnp.float32)
    terms = (along * along, along * down, down * down, along, down, jnp.ones_like(along))
    for at, term in enumerate(terms):
        basis = jnp.where(rows == at, term, basis)
    return basis


def spread_order(slots):
    lanes = lax.broadcasted_iota(jnp.int32, slots.shape, 1)
    return pick(slots, (lanes % SEGMENTS) * STEPS + lanes // SEGMENTS)


def tiles_of(tile_ref, first):
    at = lax.broadcasted_iota(jnp.int32, (SEGMENTS, BLOCK), 0)
    tiles = jnp.zeros((SEGMENTS, BLOCK), jnp.int32)
    for k in range(SEGMENTS):
        tiles = jnp.where(at == k, tile_ref[0, first + k], tiles)
    return tiles


def forward_part(
    tile_ref, last_ref, recv_ref, slots_ref, picture_ref, rec_ref, coef_ref, saved_ref,
    alpha_ref, share_ref, work_ref, image_ref, basis_ref,
):
    slots_total = slots_ref.shape[0]
    chunks = recv_ref.shape[1] // BLOCK
    origin_x = (lax.axis_index("tile") * (TILE_SIDE * TILES_DEV)).astype(jnp.float32) + CENTRE
    origin_y = (lax.axis_index("gauss") * TILE_SIDE).astype(jnp.float32) + CENTRE
    work_ref[...] = jnp.zeros_like(work_ref)
    basis = pixel_basis()
    basis_ref[...] = jnp.concatenate([basis] * 3 + [jnp.zeros_like(basis)] * 3, axis=0).astype(
        jnp.bfloat16
    )

    def collect(group, carry):
        first = group * SEGMENTS
        slots = slots_ref[pl.ds(pl.multiple_of(first, SEGMENTS), SEGMENTS), :]
        fine = slots % BLOCK
        chunk_at = slots // BLOCK
        found = [None] * FIELDS
        for chunk in range(chunks):
            hit = chunk_at == chunk
            for f in range(FIELDS):
                row = recv_ref[f : f + 1, chunk * BLOCK : (chunk + 1) * BLOCK]
                got = pick(jnp.broadcast_to(row, (SEGMENTS, BLOCK)), fine)
                found[f] = got if chunk == 0 else jnp.where(hit, got, found[f])
        tiles = tiles_of(tile_ref, first)
        base_x = (TILE_SIDE * jnp.minimum(tiles, TILES_DEV - 1)).astype(jnp.float32) + origin_x
        at_x = found[0] - base_x
        at_y = found[1] - origin_y
        con_a = -0.5 * found[2]
        con_b = -found[3]
        con_c = -0.5 * found[4]
        shut = 1.0 + jnp.exp(-found[5])
        for k, value in enumerate((at_x, at_y, con_a, con_b, con_c, 1.0 - 1.0 / shut)):
            rec_ref[k, pl.ds(pl.multiple_of(first, SEGMENTS), SEGMENTS), :] = value
        part_x = con_a * at_x
        part_y = con_c * at_y
        cross = con_b * at_y
        level = at_x * (part_x + cross) + at_y * part_y
        terms = (
            LOG2E * con_a,
            LOG2E * con_b,
            LOG2E * con_c,
            -LOG2E * (2.0 * part_x + cross),
            -LOG2E * (2.0 * part_y + con_b * at_x),
            LOG2E * (level - jnp.log(shut)),
        )

        def put(row, value):
            work_ref[pl.ds(first * COEF_ROWS + row, SEGMENTS, stride=COEF_ROWS), :] = value

        for k, term in enumerate(terms):
            high = coarse(term)
            rest = term - high
            middle = coarse(rest)
            put(k, high)
            put(8 + k, middle)
            put(16 + k, rest - middle)
        for c in range(3):
            high = coarse(found[6 + c])
            put(24 + c, high)
            put(32 + c, found[6 + c] - high)
            put(40 + c, high)
        return carry

    lax.fori_loop(0, slots_total // SEGMENTS, collect, 0)
    seg_at = lax.broadcasted_iota(jnp.int32, (SEGMENTS, HALF), 0)
    own_seg = seg_at == lax.broadcasted_iota(jnp.int32, (SEGMENTS, HALF), 1) % SEGMENTS

    def draw_local(slot):
        coefs = work_ref[pl.ds(pl.multiple_of(slot * COEF_ROWS, COEF_ROWS), COEF_ROWS), :].astype(
            jnp.bfloat16
        )
        coef_ref[slot] = coefs
        power = lax.dot_general(coefs, basis_ref[...], DOWN, preferred_element_type=jnp.float32)
        through = [jnp.ones((SEGMENTS, HALF), jnp.float32) for side in range(2)]
        weights = [[], []]
        for step in range(STEPS):
            for side in range(2):
                rows = slice(step * SEGMENTS, (step + 1) * SEGMENTS)
                lanes = slice(side * HALF, (side + 1) * HALF)
                alpha = jnp.exp2(power[rows, lanes])
                weight = alpha * through[side]
                alpha_ref[slot, rows, lanes] = alpha
                share_ref[slot, rows, lanes] = weight
                through[side] = through[side] - weight
                weights[side].append(weight)
        weight = jnp.concatenate([jnp.concatenate(w, axis=0) for w in weights], axis=1)
        tints = []
        for part in (24, 32):
            for c in range(3):
                row = work_ref[pl.ds(slot * COEF_ROWS + part + c, 1), :]
                tints.append(jnp.where(own_seg, jnp.broadcast_to(row, (SEGMENTS, HALF)), 0.0))
        tint = jnp.concatenate(tints, axis=0).astype(jnp.bfloat16)
        sums = jnp.dot(
            jnp.concatenate([tint, tint], axis=1),
            jnp.concatenate(halves(weight), axis=0),
            preferred_element_type=jnp.float32,
        )
        return through, sums[0:24] + sums[24:48]

    def draw_join(slot, carry, through, sums):
        tile = tile_ref[0, slot]
        fresh = (slot == 0) | (tile != tile_ref[0, jnp.maximum(slot - 1, 0)])
        after = []
        for side in range(2):
            start = jnp.where(fresh, 1.0, carry[side][0])
            running = through[side]
            for shift in (1, 2, 4):
                running = jnp.where(
                    seg_at >= shift, running * pltpu.roll(running, shift, 0), running
                )
            before = jnp.where(seg_at == 0, 1.0, pltpu.roll(running, 1, 0)) * start
            kept = [start * running[SEGMENTS - 1 : SEGMENTS]]
            lanes = slice(side * HALF, (side + 1) * HALF)
            saved_ref[slot, 0, :, lanes] = before
            saved_ref[slot, 1, :, lanes] = through[side]
            for c in range(3):
                part = sums[c * SEGMENTS : (c + 1) * SEGMENTS, lanes]
                saved_ref[slot, 2 + c, :, lanes] = part
                shade_sum = jnp.sum(before * part, axis=0, keepdims=True)
                shade_sum = jnp.where(fresh, 0.0, carry[side][1 + c]) + shade_sum
                image_ref[slot, c : c + 1, lanes] = shade_sum
                kept.append(shade_sum)
            after.append(tuple(kept))
        return tuple(after)

    def draw(pair, carry):
        locals_two = [draw_local(GROUP * pair + k) for k in range(GROUP)]
        for k in range(GROUP):
            carry = draw_join(GROUP * pair + k, carry, *locals_two[k])
        return carry

    start = (jnp.ones((1, HALF), jnp.float32),) + (jnp.zeros((1, HALF), jnp.float32),) * 3
    lax.fori_loop(0, slots_total // GROUP, draw, (start, start))
    lane_tile = lax.broadcasted_iota(jnp.int32, (SEGMENTS, HALF), 1) // TILE_SIDE
    for side in range(2):
        lanes = slice(side * HALF, (side + 1) * HALF)
        for c in range(3):
            shown = jnp.zeros((SEGMENTS, HALF), jnp.float32)
            for tile in range(TILES_DEV):
                row = image_ref[last_ref[tile], c : c + 1, lanes]
                row = jnp.broadcast_to(row, (SEGMENTS, HALF))
                moved = pltpu.roll(row, TILE_SIDE * tile, 1) if tile else row
                for bit in (1, 2, 4):
                    moved = jnp.where(
                        (seg_at & bit) > 0, pltpu.roll(moved, HALF - TILE_SIDE * bit, 1), moved
                    )
                shown = jnp.where(lane_tile == tile, moved, shown)
            picture_ref[c, side * SEGMENTS : (side + 1) * SEGMENTS, :] = shown


def backward_part(
    tile_ref, rec_ref, coef_ref, saved_ref, alpha_ref, share_ref, heavy_ref, grad_ref,
    slots_ref, out_ref,
    rhs_ref, mom_ref, back_ref, where_ref, acc_ref, lit_ref, force_ref, behind_ref,
):
    chunks = out_ref.shape[1] // BLOCK
    slots_total = coef_ref.shape[0]
    acc_ref[...] = jnp.zeros_like(acc_ref)
    basis = pixel_basis()
    blank = jnp.zeros_like(basis)
    basis16 = jnp.concatenate([basis, blank], axis=0).astype(jnp.bfloat16)
    for tile in range(TILES_DEV):
        grads = grad_ref[tile]
        high = coarse(grads)
        rhs_ref[tile] = jnp.concatenate([blank, high, high, grads - high], axis=0).astype(
            jnp.bfloat16
        )
    seg_at = lax.broadcasted_iota(jnp.int32, (SEGMENTS, HALF), 0)

    def prepare(slot, carry, buf):
        tile = tile_ref[0, slot]
        later = tile_ref[0, jnp.minimum(slot + 1, slots_total - 1)]
        final = (slot == slots_total - 1) | (tile != later)
        shown = jnp.minimum(tile, TILES_DEV - 1)
        grads = grad_ref[shown]
        after = []
        for side in range(2):
            lanes = slice(side * HALF, (side + 1) * HALF)
            start = jnp.where(final, 0.0, carry[side])
            total = grads[0:1, lanes] * saved_ref[slot, 2, :, lanes]
            for c in (1, 2):
                total = total + grads[c : c + 1, lanes] * saved_ref[slot, 2 + c, :, lanes]
            factor = saved_ref[slot, 1, :, lanes]
            for shift in (1, 2, 4):
                inside = seg_at < SEGMENTS - shift
                total = jnp.where(
                    inside, total + factor * pltpu.roll(total, SEGMENTS - shift, 0), total
                )
                factor = jnp.where(
                    inside, factor * pltpu.roll(factor, SEGMENTS - shift, 0), factor
                )
            entering = total + factor * start
            after.append(entering[0:1])
            behind_ref[buf, :, lanes] = jnp.where(
                seg_at < SEGMENTS - 1, pltpu.roll(entering, SEGMENTS - 1, 0), start
            )
        lit_ref[buf] = lax.dot_general(
            coef_ref[slot, 16:COEF_ROWS, :], rhs_ref[shown], DOWN, preferred_element_type=jnp.float32
        )
        return tuple(after)

    def trace(slots, bufs):
        chains = [(k, side) for k in range(len(slots)) for side in range(2)]
        lanes = [slice(side * HALF, (side + 1) * HALF) for side in range(2)]
        later = {(k, side): behind_ref[bufs[k], :, lanes[side]] for k, side in chains}
        for step in reversed(range(STEPS // 2)):
            for k, side in chains:
                pair = []
                for at in (2 * step + 1, 2 * step):
                    rows = slice(at * SEGMENTS, (at + 1) * SEGMENTS)
                    gap = lit_ref[bufs[k], rows, lanes[side]] - later[k, side]
                    alpha = alpha_ref[slots[k], rows, lanes[side]]
                    later[k, side] = later[k, side] + alpha * gap
                    pair.append(share_ref[slots[k], rows, lanes[side]] * gap)
                halve(force_ref, bufs[k], step, lanes[side], pair[::-1])

    def reduce(slot, buf):
        shown = jnp.minimum(tile_ref[0, slot], TILES_DEV - 1)
        found = lax.dot_general(
            basis16, force_ref[buf], ACROSS, preferred_element_type=jnp.float32
        )
        painted = lax.dot_general(
            jnp.concatenate(halves(grad_ref[shown]), axis=0),
            heavy_ref[slot],
            ACROSS,
            preferred_element_type=jnp.float32,
        )
        painted = painted[0:8] + painted[8:16]
        mom_ref[slot, 0:8, :] = found[0:8, :BLOCK] + found[0:8, BLOCK:]
        mom_ref[slot, 8:16, :] = painted[:, :BLOCK] + painted[:, BLOCK:]

    runs = slots_total // WIDTH

    def slot_of(run, k):
        return (runs - 1 - run) * WIDTH + k

    def ready(run, carry, half):
        for k in reversed(range(WIDTH)):
            carry = prepare(slot_of(run, k), carry, half * WIDTH + k)
        return carry

    def gather_in(run, half):
        for k in range(WIDTH):
            reduce(slot_of(run, k), half * WIDTH + k)

    def follow(run, half):
        trace(
            [slot_of(run, k) for k in range(WIDTH)], [half * WIDTH + k for k in range(WIDTH)]
        )

    def pull(turn, carry):
        for part in range(TURN):
            run = TURN * turn + part + 1
            half = (part + 1) % 2
            gather_in(run - 1, 1 - half)
            carry = ready(run + 1, carry, 1 - half)
            follow(run, half)
        return carry

    zeros = jnp.zeros((1, HALF), jnp.float32)
    carry = ready(0, (zeros, zeros), 0)
    carry = ready(1, carry, 1)
    follow(0, 0)
    carry = lax.fori_loop(0, (runs - 2) // TURN, pull, carry)
    for run in range((runs - 2) // TURN * TURN + 1, runs):
        half = run % 2
        gather_in(run - 1, 1 - half)
        if run + 1 < runs:
            carry = ready(run + 1, carry, 1 - half)
        follow(run, half)
    gather_in(runs - 1, (runs - 1) % 2)
    lane_rows = lax.broadcasted_iota(jnp.int32, (BLOCK, 4 * BLOCK), 0)
    chunk_rows = lax.broadcasted_iota(jnp.int32, (chunks, BLOCK), 0)

    def settle(group, carry):
        first = pl.multiple_of(group * SEGMENTS, SEGMENTS)
        tiles = tiles_of(tile_ref, first)
        used = tiles < TILES_DEV
        rows = pl.ds(first, SEGMENTS)

        m_xx, m_xy, m_yy, m_x, m_y, m_0 = [
            mom_ref[rows, k, :] for k in range(6)
        ]
        at_x, at_y, con_a, con_b, con_c, shut_s = [rec_ref[k, rows, :] for k in range(6)]
        h_x = m_x - at_x * m_0
        h_y = m_y - at_y * m_0
        h_xx = m_xx - 2.0 * at_x * m_x + at_x * at_x * m_0
        h_xy = m_xy - at_x * m_y - at_y * m_x + at_x * at_y * m_0
        h_yy = m_yy - 2.0 * at_y * m_y + at_y * at_y * m_0
        results = [
            -2.0 * con_a * h_x - con_b * h_y,
            -2.0 * con_c * h_y - con_b * h_x,
            -0.5 * h_xx,
            -h_xy,
            -0.5 * h_yy,
            shut_s * m_0,
        ] + [mom_ref[rows, 8 + c, :] for c in range(3)]
        for f, value in enumerate(results):
            kept = jnp.where(used, value, 0.0)
            high = coarse(kept)
            back_ref[rows, f, :] = high
            back_ref[rows, 12 + f, :] = kept - high
        slots = slots_ref[rows, :]
        where_ref[0, rows, :] = slots % BLOCK
        where_ref[1, rows, :] = slots // BLOCK
        for quad in range(0, SEGMENTS, 4):
            stacked = []
            for k in range(quad, quad + 4):
                hit = chunk_rows == where_ref[1, pl.ds(first + k, 1), :]
                stacked.append(
                    jnp.concatenate(
                        [
                            jnp.where(hit, back_ref[first + k, part + f : part + f + 1, :], 0.0)
                            for part in (0, 12)
                            for f in range(FIELDS)
                        ],
                        axis=0,
                    ).astype(jnp.bfloat16)
                )
            fine = jnp.concatenate(
                [where_ref[0, pl.ds(first + k, 1), :] for k in range(quad, quad + 4)], axis=1
            )
            select = jnp.where(lane_rows == fine, 1.0, 0.0).astype(jnp.bfloat16)
            acc_ref[...] += lax.dot_general(
                jnp.concatenate(stacked, axis=1), select, ACROSS, preferred_element_type=jnp.float32
            )
        return carry

    lax.fori_loop(0, slots_total // SEGMENTS, settle, 0, unroll=2)
    total = FIELDS * chunks
    for chunk in range(chunks):
        lanes = slice(chunk * BLOCK, (chunk + 1) * BLOCK)
        out_ref[0:8, lanes] = (
            acc_ref[pl.ds(chunk, 8, stride=chunks), :]
            + acc_ref[pl.ds(total + chunk, 8, stride=chunks), :]
        )
        at = 8 * chunks + chunk
        out_ref[8:9, lanes] = acc_ref[at : at + 1, :] + acc_ref[total + at : total + at + 1, :]


def hbm():
    return pl.BlockSpec(memory_space=pltpu.HBM)


def smem():
    return pl.BlockSpec(memory_space=pltpu.SMEM)


def vmem():
    return pl.BlockSpec(memory_space=pltpu.VMEM)


WAYS = [(down, right) for down in (-1, 0, 1) for right in (-1, 0, 1) if (down, right) != (0, 0)]
NORM = sum(math.exp(-m * m / 4.5) for m in range(-5, 6))
EXT_ROWS = 40
MID_ROWS = 32


def neighbour(bands, columns, way):
    there_band = lax.axis_index("gauss") + way[0]
    there_col = lax.axis_index("tile") + way[1]
    exists = (there_band >= 0) & (there_band < bands) & (there_col >= 0) & (there_col < columns)
    return exists, (there_band, there_col)


def greet_round(barrier, bands, columns):
    peers = jnp.int32(0)
    for way in WAYS:
        if way[1] == 0:
            continue
        exists, there = neighbour(bands, columns, way)
        peers = peers + exists.astype(jnp.int32)

        @pl.when(exists)
        def _(there=there):
            pl.semaphore_signal(barrier, inc=1, device_id=there, device_id_type=MESH)

    return peers


def border_copies(bands, columns, plane_ref, edge_ref, tall_ref, side_ref, send_sem, recv_sem):
    found = []
    for at, way in enumerate(WAYS):
        exists, there = neighbour(bands, columns, way)
        landing = len(WAYS) - 1 - at
        source = plane_ref if way[1] == 0 else edge_ref
        target = tall_ref.at[landing] if way[1] == 0 else side_ref.at[landing]
        found.append(
            (
                exists,
                pltpu.make_async_remote_copy(
                    src_ref=source,
                    dst_ref=target,
                    send_sem=send_sem.at[at],
                    recv_sem=recv_sem.at[landing],
                    device_id=there,
                    device_id_type=MESH,
                ),
                pltpu.make_async_remote_copy(
                    src_ref=source,
                    dst_ref=tall_ref.at[at] if way[1] == 0 else side_ref.at[at],
                    send_sem=send_sem.at[at],
                    recv_sem=recv_sem.at[at],
                    device_id=there,
                    device_id_type=MESH,
                ),
            )
        )
    return found


def border_start(copies):
    for exists, out, back in copies:

        @pl.when(exists)
        def _(out=out):
            out.start()


def border_wait(copies):
    for exists, out, back in copies:

        @pl.when(exists)
        def _(out=out, back=back):
            out.wait_send()
            back.wait_recv()


def pack_edges(plane_ref, edge_ref):
    lanes = lax.broadcasted_iota(jnp.int32, edge_ref.shape, 1)
    packed = jnp.zeros(edge_ref.shape, jnp.float32)
    for c in range(3):
        plane = plane_ref[c]
        near = pltpu.roll(plane, 32 * c, 1) if c else plane
        far = pltpu.roll(plane, 32 * c + 32, 1)
        packed = jnp.where(
            lanes // 32 == c, jnp.where(lanes % 32 < 16, near, far), packed
        )
    edge_ref[...] = packed


def stretch(above, own, below):
    turn = lax.broadcasted_iota(jnp.int32, (8, own.shape[1]), 0) >= 6
    mixed = jnp.where(turn, above[0:8], below[8:16])
    return jnp.concatenate([own, above[8:16], below[0:8], mixed], axis=0)


def extend(plane_ref, tall_ref, side_ref):
    east = lax.broadcasted_iota(jnp.int32, side_ref.shape[1:], 1) % 32 < 16
    borders = [
        jnp.where(east, side_ref[WAYS.index((down, 1))], side_ref[WAYS.index((down, -1))])
        for down in (-1, 0, 1)
    ]
    border = stretch(*borders)
    planes = []
    for c in range(3):
        main = stretch(
            tall_ref[WAYS.index((-1, 0)), c], plane_ref[c], tall_ref[WAYS.index((1, 0)), c]
        )
        turned = pltpu.roll(border, HALF - 32 * c, 1) if c else border
        planes.append(jnp.concatenate([main, turned], axis=1))
    return planes


def window_weight(gap):
    gap = gap.astype(jnp.float32)
    return jnp.where(jnp.abs(gap) < 5.5, jnp.exp(gap * gap / -4.5) * (1.0 / NORM), 0.0)


def split_rows(value):
    first = coarse(value)
    rest = value - first
    second = coarse(rest)
    return first, second, rest - second


def six_data(value, axis):
    first, second, third = split_rows(value)
    return jnp.concatenate([first, second, third, first, second, first], axis=axis).astype(
        jnp.bfloat16
    )


def six_weights(value, axis):
    first, second, third = split_rows(value)
    return jnp.concatenate([first, first, first, second, second, third], axis=axis).astype(
        jnp.bfloat16
    )


def ext_row(at):
    return jnp.where(at < 16, at, jnp.where(at < 24, at - 24, jnp.where(at < 38, at - 8, at - 48)))


def ext_col(at):
    return jnp.where(at < 144, at, jnp.where(at < 160, at - 160, 10000))


def mid_col(at):
    return jnp.where(at < 192, at, at - 256)


def iota(shape, axis):
    return lax.broadcasted_iota(jnp.int32, shape, axis)


def fdot(left, right):
    return jnp.dot(left, right, preferred_element_type=jnp.float32)


def weigh_part(saved_ref, share_ref, heavy_ref):
    def weigh(group, carry):
        for step in range(STEPS // 2):
            for k in range(4):
                slot = 4 * group + k
                for side in range(2):
                    lanes = slice(side * HALF, (side + 1) * HALF)
                    before = saved_ref[slot, 0, :, lanes]
                    pair = []
                    for at in (2 * step, 2 * step + 1):
                        rows = slice(at * SEGMENTS, (at + 1) * SEGMENTS)
                        weight = share_ref[slot, rows, lanes] * before
                        share_ref[slot, rows, lanes] = weight
                        pair.append(weight)
                    halve(heavy_ref, slot, step, lanes, pair)
        return carry

    lax.fori_loop(0, share_ref.shape[0] // 4, weigh, 0)


def contrast_part(
    bands, columns, meanwhile, shown_ref, aim_ref, out_ref,
    edge_ref, tall_ref, side_ref, wide_ref, back_ref, send_sem, recv_sem,
):
    band = lax.axis_index("gauss")
    column = lax.axis_index("tile")
    rows, cols = shown_ref.shape[1:]
    pack_edges(shown_ref, edge_ref)
    copies = border_copies(
        bands, columns, shown_ref, edge_ref, tall_ref, side_ref, send_sem, recv_sem
    )
    border_start(copies)
    wide = 2 * cols
    for half in range(2):
        lanes = slice(half * cols, (half + 1) * cols)
        shape = (wide, cols)
        across = window_weight(mid_col(iota(shape, 1) + half * cols) - ext_col(iota(shape, 0)))
        wide_ref[:, lanes] = six_weights(across, 0)
    back = window_weight(mid_col(iota((wide, cols), 0)) - iota((wide, cols), 1))
    back_ref[...] = six_weights(back, 0)
    shape = (MID_ROWS, EXT_ROWS)
    down = window_weight(iota(shape, 0) - 5 - ext_row(iota(shape, 1)))
    down = six_weights(down, 1)
    shape = (rows, MID_ROWS)
    up = six_weights(window_weight(iota(shape, 0) - iota(shape, 1) + 5), 1)
    meanwhile()
    border_wait(copies)
    pics = extend(shown_ref, tall_ref, side_ref)
    strips = []
    for kind in range(4):
        for c in range(3):
            pic, aim = pics[c], aim_ref[c]
            plane = (pic, aim, pic * pic + aim * aim, pic * aim)[kind] if kind > 1 else (
                pic if kind == 0 else aim
            )
            strips.append(fdot(down, six_data(plane, 0)))
    moments = fdot(six_data(jnp.concatenate(strips, axis=0), 1), wide_ref[...])
    shape = (MID_ROWS, wide)
    row_at = band * rows + iota(shape, 0) - 5
    col_at = column * cols + mid_col(iota(shape, 1))
    inside = (row_at >= 0) & (row_at < bands * rows) & (col_at >= 0) & (col_at < columns * cols)
    strips = [None] * 9
    for c in range(3):
        mu_x, mu_y, squares, cross = [
            moments[(3 * kind + c) * MID_ROWS : (3 * kind + c + 1) * MID_ROWS] for kind in range(4)
        ]
        mean_xy = mu_x * mu_y
        mean_sq = mu_x * mu_x + mu_y * mu_y
        top_1 = 2.0 * mean_xy + CONST_ONE
        top_2 = 2.0 * (cross - mean_xy) + CONST_TWO
        low_1 = mean_sq + CONST_ONE
        low_2 = squares - mean_sq + CONST_TWO
        inverse = -0.2 / (low_1 * low_2)
        value = top_1 * top_2 * inverse
        value_1 = value * low_2 * inverse * -5.0
        value_2 = value * low_1 * inverse * -5.0
        slope_mean = 2.0 * mu_y * (top_2 - top_1) * inverse - 2.0 * mu_x * (value_1 - value_2)
        for kind, slope in enumerate((slope_mean, -value_2, 2.0 * top_1 * inverse)):
            strips[3 * kind + c] = fdot(up, six_data(jnp.where(inside, slope, 0.0), 0))
    spread = fdot(six_data(jnp.concatenate(strips, axis=0), 1), back_ref[...])
    lane_row = iota((SEGMENTS, HALF), 1) // TILE_SIDE
    seg_at = iota((SEGMENTS, HALF), 0)
    out_ref[...] = jnp.zeros_like(out_ref)
    for c in range(3):
        pic = shown_ref[c]
        aim = aim_ref[c, 0:rows, 0:cols]
        parts = [spread[(3 * kind + c) * rows : (3 * kind + c + 1) * rows] for kind in range(3)]
        total = parts[0] + 2.0 * pic * parts[1] + aim * parts[2] + 1.6 * (pic - aim)
        for side in range(2):
            part = total[side * SEGMENTS : (side + 1) * SEGMENTS]
            skewed = pltpu.roll(part, 0, 1, stride=TILE_SIDE, stride_axis=0)
            for tile in range(TILES_DEV):
                moved = pltpu.roll(skewed, HALF - TILE_SIDE * tile, 1) if tile else skewed
                kept = jnp.where(lane_row == seg_at, moved, 0.0)
                out_ref[tile, c : c + 1, side * HALF : (side + 1) * HALF] = jnp.sum(
                    kept, axis=0, keepdims=True
                )


def border_scratch(rows, cols):
    ways = len(WAYS)
    return [
        pltpu.VMEM((rows, cols), jnp.float32),
        pltpu.VMEM((ways, 3, rows, cols), jnp.float32),
        pltpu.VMEM((ways, rows, cols), jnp.float32),
    ]


def basis_rows(x, y, z):
    xx, yy, zz = x * x, y * y, z * z
    return [
        jnp.full_like(x, BASE_ZERO),
        -BASE_ONE * y,
        BASE_ONE * z,
        -BASE_ONE * x,
        BASE_TWO[0] * x * y,
        BASE_TWO[1] * y * z,
        BASE_TWO[2] * (2.0 * zz - xx - yy),
        BASE_TWO[3] * x * z,
        BASE_TWO[4] * (xx - yy),
        BASE_THREE[0] * y * (3.0 * xx - yy),
        BASE_THREE[1] * x * y * z,
        BASE_THREE[2] * y * (4.0 * zz - xx - yy),
        BASE_THREE[3] * z * (2.0 * zz - 3.0 * xx - 3.0 * yy),
        BASE_THREE[4] * x * (4.0 * zz - xx - yy),
        BASE_THREE[5] * z * (xx - yy),
        BASE_THREE[6] * x * (xx - 3.0 * yy),
    ]


def slope_rows(x, y, z):
    xx, yy, zz = x * x, y * y, z * z
    xy, yz, xz = x * y, y * z, x * z
    none = jnp.zeros_like(x)
    one = jnp.ones_like(x)
    two, three = BASE_TWO, BASE_THREE
    along_x = [
        none, none, none, -BASE_ONE * one,
        two[0] * y, none, -2.0 * two[2] * x, two[3] * z, 2.0 * two[4] * x,
        6.0 * three[0] * xy, three[1] * yz, -2.0 * three[2] * xy, -6.0 * three[3] * xz,
        three[4] * (4.0 * zz - 3.0 * xx - yy), 2.0 * three[5] * xz, three[6] * (3.0 * xx - 3.0 * yy),
    ]
    along_y = [
        none, -BASE_ONE * one, none, none,
        two[0] * x, two[1] * z, -2.0 * two[2] * y, none, -2.0 * two[4] * y,
        three[0] * (3.0 * xx - 3.0 * yy), three[1] * xz, three[2] * (4.0 * zz - xx - 3.0 * yy),
        -6.0 * three[3] * yz, -2.0 * three[4] * xy, -2.0 * three[5] * yz, -6.0 * three[6] * xy,
    ]
    along_z = [
        none, none, BASE_ONE * one, none,
        none, two[1] * y, 4.0 * two[2] * z, two[3] * x, none,
        none, three[1] * xy, 8.0 * three[2] * yz, three[3] * (6.0 * zz - 3.0 * xx - 3.0 * yy),
        8.0 * three[4] * xz, three[5] * (xx - yy), none,
    ]
    return along_x, along_y, along_z


def lane_of():
    return lax.broadcasted_iota(jnp.int32, (8, BLOCK), 1)


def row_of():
    return lax.broadcasted_iota(jnp.int32, (8, BLOCK), 0)


def gather_rows(table_ref, ninth_ref, chunks, index):
    index = jnp.broadcast_to(index, (8, BLOCK))
    fine = index % BLOCK
    chunk_at = index // BLOCK
    first = None
    ninth = jnp.zeros((8, BLOCK), jnp.float32)
    for chunk in range(chunks):
        got = pick(table_ref[0:8, chunk * BLOCK : (chunk + 1) * BLOCK], fine)
        first = got if chunk == 0 else jnp.where(chunk_at == chunk, got, first)
    for base in range(0, chunks, 8):
        got = pick(ninth_ref[base : base + 8, :], fine)
        ninth = ninth + jnp.where(chunk_at == row_of() + base, got, 0.0)
    return first, jnp.sum(ninth, axis=0, keepdims=True)


def pack_two(first, last):
    left = lane_of() < BLOCK // 2
    swapped = pltpu.roll(first, BLOCK // 2, 1)
    one = jnp.where(left, first, pltpu.roll(swapped, 4, 0))
    two = jnp.where(left, swapped, pltpu.roll(first, 4, 0))
    tail = row_of() >= 4
    ninth = jnp.broadcast_to(last, (8, BLOCK))
    return jnp.where(tail, ninth, one), jnp.where(tail, pltpu.roll(ninth, BLOCK // 2, 1), two)


def unpack_two(one, two):
    left = lane_of() < BLOCK // 2
    upper = jnp.where(left, one, pltpu.roll(two, BLOCK // 2, 1))
    lower = jnp.where(left, pltpu.roll(one, BLOCK // 2, 1), two)
    return jnp.where(row_of() < 4, upper, pltpu.roll(lower, 4, 0)), upper[4:5]


def ring(gap, owners):
    there = lax.axis_index("gauss") + gap
    return jnp.where(there >= owners, there - owners, there)


def far_first(owners):
    return sorted(range(1, owners), key=lambda gap: (abs(2 * gap - owners), gap))


def greet(owners):
    barrier = pltpu.get_barrier_semaphore()
    column = lax.axis_index("tile")
    for gap in far_first(owners):
        pl.semaphore_signal(
            barrier, inc=1, device_id=(ring(gap, owners), column), device_id_type=MESH
        )
    return barrier


def parcel(owners, gap, out_ref, in_ref, send_sem, recv_sem):
    band = lax.axis_index("gauss")
    there = ring(gap, owners)
    return pltpu.make_async_remote_copy(
        src_ref=out_ref.at[there],
        dst_ref=in_ref.at[band],
        send_sem=send_sem.at[gap],
        recv_sem=recv_sem.at[gap],
        device_id=(there, lax.axis_index("tile")),
        device_id_type=MESH,
    )


def post(owners, out_ref, in_ref, send_sem, recv_sem):
    band = lax.axis_index("gauss")
    for gap in far_first(owners):
        parcel(owners, gap, out_ref, in_ref, send_sem, recv_sem).start()
    in_ref[band] = out_ref[band]


def take_in(owners, out_ref, in_ref, send_sem, recv_sem):
    for gap in range(1, owners):
        parcel(owners, gap, out_ref, in_ref, send_sem, recv_sem).wait()


def count_tiles(tile_ref, last_ref):
    for tile in range(TILES_DEV):
        last = jnp.int32(-1)
        for slot in range(tile_ref.shape[1]):
            last = last + (tile_ref[0, slot] <= tile).astype(jnp.int32)
        last_ref[tile] = last


def deliver_part(
    owners, columns, loads, clear, recv_ref, home_ref, aim_ref, order_ref, slope_ref,
    tile_ref, last_ref, splats_ref, sh_ref, send_ref, target_ref, slots_ref,
    table_ref, ninth_ref, edge_ref, tall_ref, side_ref, border_send, border_recv,
    out_ref, in_ref, send_sem, recv_sem,
):
    for load in loads:
        load.start()
    for ref in clear:
        ref[...] = jnp.zeros_like(ref)
    barrier = greet(owners)
    peers = greet_round(barrier, owners, columns)
    for load in loads:
        load.wait()
    own = splats_ref.shape[1]
    chunks = own // BLOCK
    basis = jnp.concatenate(
        basis_rows(splats_ref[6:7, :], splats_ref[7:8, :], splats_ref[8:9, :]), axis=0
    )
    colours = [
        0.5 + jnp.sum(sh_ref[16 * c : 16 * (c + 1), :] * basis, axis=0, keepdims=True)
        for c in range(3)
    ]
    table_ref[0:6, :] = splats_ref[0:6, :]
    table_ref[6:8, :] = jnp.concatenate(colours[0:2], axis=0)
    for chunk in range(chunks):
        ninth_ref[chunk : chunk + 1, :] = colours[2][:, chunk * BLOCK : (chunk + 1) * BLOCK]
    for chunk in range(chunks):
        one, two = pack_two(
            *gather_rows(table_ref, ninth_ref, chunks, send_ref[chunk : chunk + 1, :])
        )
        out_ref[2 * chunk] = one
        out_ref[2 * chunk + 1] = two
    pack_edges(target_ref, edge_ref)
    pl.semaphore_wait(barrier, owners - 1 + peers)
    post(owners, out_ref, in_ref, send_sem, recv_sem)
    copies = border_copies(
        owners, columns, target_ref, edge_ref, tall_ref, side_ref, border_send, border_recv
    )
    border_start(copies)
    chunk_rows = lax.broadcasted_iota(jnp.int32, (chunks, BLOCK), 0)
    lanes = lax.broadcasted_iota(jnp.int32, (chunks, BLOCK), 1).astype(jnp.float32)
    lane_rows = lax.broadcasted_iota(jnp.int32, (BLOCK, BLOCK), 0)
    home = jnp.zeros((2 * chunks, BLOCK), jnp.float32)
    for chunk in range(chunks):
        index = send_ref[chunk : chunk + 1, :]
        hit = chunk_rows == index // BLOCK
        source = jnp.concatenate(
            [jnp.where(hit, float(chunk), 0.0), jnp.where(hit, lanes, 0.0)], axis=0
        ).astype(jnp.bfloat16)
        select = jnp.where(lane_rows == index % BLOCK, 1.0, 0.0).astype(jnp.bfloat16)
        home = home + lax.dot_general(source, select, ACROSS, preferred_element_type=jnp.float32)
    home_ref[...] = (home[:chunks] * float(BLOCK) + home[chunks:]).astype(jnp.int32)
    count_tiles(tile_ref, last_ref)
    facing = [splats_ref[6 + d : 7 + d, :] for d in range(3)]
    slope_ref[0:16, :] = basis
    for d, rows in enumerate(slope_rows(*facing)):
        slope_ref[16 * (d + 1) : 16 * (d + 2), :] = jnp.concatenate(rows, axis=0)
    for first in range(0, slots_ref.shape[0], SEGMENTS):
        rows = slice(first, first + SEGMENTS)
        order_ref[rows, :] = spread_order(slots_ref[rows, :])
    border_wait(copies)
    for c, plane in enumerate(extend(target_ref, tall_ref, side_ref)):
        aim_ref[c] = plane
    take_in(owners, out_ref, in_ref, send_sem, recv_sem)
    for chunk in range(chunks):
        first, ninth = unpack_two(in_ref[2 * chunk], in_ref[2 * chunk + 1])
        recv_ref[0:8, chunk * BLOCK : (chunk + 1) * BLOCK] = first
        recv_ref[8:9, chunk * BLOCK : (chunk + 1) * BLOCK] = ninth


def parcels(owners):
    return [
        pltpu.VMEM((owners, PACKED, BLOCK), jnp.float32),
        pltpu.VMEM((owners, PACKED, BLOCK), jnp.float32),
        pltpu.SemaphoreType.DMA((owners,)),
        pltpu.SemaphoreType.DMA((owners,)),
    ]


def return_part(owners, pulled_ref, in_ref, out_ref, send_sem, recv_sem):
    chunks = pulled_ref.shape[1] // BLOCK
    for chunk in range(chunks):
        lanes = slice(chunk * BLOCK, (chunk + 1) * BLOCK)
        one, two = pack_two(pulled_ref[0:8, lanes], pulled_ref[8:9, lanes])
        out_ref[2 * chunk] = one
        out_ref[2 * chunk + 1] = two
    post(owners, out_ref, in_ref, send_sem, recv_sem)
    take_in(owners, out_ref, in_ref, send_sem, recv_sem)


def train_kernel(owners, columns, counts, *refs):
    parts = []
    for count in counts:
        parts.append(refs[:count])
        refs = refs[count:]
    sources, (landed_ref, slope_ref, home_ref, shown_ref), local, shared, draw_refs = parts[:5]
    pull_refs, early, border, late, deliver_refs, return_refs = parts[5:]
    tile_ref, last_ref, splats_ref, sh_ref, send_ref, target_ref, slots_ref, load_sem = local
    recv_ref, aim_ref, order_ref, rec_ref, coef_ref, saved_ref, *shared = shared
    alpha_ref, share_ref, heavy_ref, grad_ref, pulled_ref = shared
    loads = [
        pltpu.make_async_copy(source, into, load_sem.at[at])
        for at, (source, into) in enumerate(
            zip(sources, (splats_ref, sh_ref, send_ref, target_ref, slots_ref, tile_ref))
        )
    ]
    deliver_part(
        owners, columns, loads, early[1:3] + late[1:3], recv_ref, home_ref, aim_ref, order_ref,
        slope_ref, *local[:-1], *border, *early, *deliver_refs,
    )
    forward_part(
        tile_ref, last_ref, recv_ref, order_ref, shown_ref, rec_ref, coef_ref, saved_ref,
        alpha_ref, share_ref, *draw_refs,
    )
    contrast_part(
        owners, columns, functools.partial(weigh_part, saved_ref, share_ref, heavy_ref),
        shown_ref, aim_ref, grad_ref, *late,
    )
    backward_part(
        tile_ref, rec_ref, coef_ref, saved_ref, alpha_ref, share_ref, heavy_ref, grad_ref,
        order_ref, pulled_ref, *pull_refs,
    )
    return_part(owners, pulled_ref, landed_ref, *return_refs)


def train(splats, sh_coeffs, send_list, target, slots, tile_ids):
    own = splats.shape[1]
    chunks = own // BLOCK
    owners = lax.axis_size("gauss")
    rows, cols = target.shape[1:]
    ways = len(WAYS)
    slots_total = slots.shape[0]
    side = TILE_SIDE * TILE_SIDE

    def f32(*shape):
        return pltpu.VMEM(shape, jnp.float32)

    def bf16(*shape):
        return pltpu.VMEM(shape, jnp.bfloat16)

    def i32(*shape):
        return pltpu.VMEM(shape, jnp.int32)

    sems = pltpu.SemaphoreType.DMA
    args = (splats, sh_coeffs, send_list.reshape(chunks, BLOCK), target, slots, tile_ids)
    outs = (
        jax.ShapeDtypeStruct((owners, PACKED, BLOCK), jnp.float32),
        jax.ShapeDtypeStruct((64, own), jnp.float32),
        jax.ShapeDtypeStruct((chunks, BLOCK), jnp.int32),
        jax.ShapeDtypeStruct(target.shape, jnp.float32),
    )
    local = [
        pltpu.SMEM(tile_ids.shape, jnp.int32),
        pltpu.SMEM((TILES_DEV,), jnp.int32),
        f32(*splats.shape),
        f32(*sh_coeffs.shape),
        i32(chunks, BLOCK),
        f32(*target.shape),
        i32(*slots.shape),
        sems((len(args),)),
    ]
    shared = [
        f32(FIELDS, own),
        f32(3, EXT_ROWS, 2 * cols),
        i32(*slots.shape),
        f32(6, slots_total, BLOCK),
        bf16(slots_total, COEF_ROWS, BLOCK),
        f32(slots_total, 5, SEGMENTS, side),
        f32(slots_total, BLOCK, side),
        f32(slots_total, BLOCK, side),
        bf16(slots_total, 2 * BLOCK, side),
        f32(TILES_DEV, 8, side),
        f32(FIELDS, own),
    ]
    draw_refs = [f32(slots_total * COEF_ROWS, BLOCK), f32(slots_total, 8, side), bf16(COEF_ROWS, side)]
    pull_refs = [
        bf16(TILES_DEV, COEF_ROWS - 16, side),
        f32(slots_total, 16, BLOCK),
        f32(slots_total, GRAD_ROWS, BLOCK),
        i32(2, slots_total, BLOCK),
        f32(2 * FIELDS * chunks, BLOCK),
        f32(2 * WIDTH, BLOCK, side),
        bf16(2 * WIDTH, 2 * BLOCK, side),
        f32(2 * WIDTH, SEGMENTS, side),
    ]
    border = [f32(8, own), f32(chunks, BLOCK)]
    early = border_scratch(rows, cols) + [sems((ways,)), sems((ways,))]
    late = (
        border_scratch(rows, cols)
        + [bf16(12 * cols, 2 * cols), bf16(12 * cols, cols)]
        + [sems((ways,)), sems((ways,))]
    )
    landing, into, *pair = parcels(owners)
    groups = [local, shared, draw_refs, pull_refs, early, border, late]
    groups += [[landing, into] + pair, [landing] + pair]
    counts = (len(args), len(outs)) + tuple(len(group) for group in groups)
    return pl.pallas_call(
        functools.partial(train_kernel, owners, lax.axis_size("tile"), counts),
        out_shape=outs,
        in_specs=[hbm()] * len(args),
        out_specs=(vmem(),) * len(outs),
        scratch_shapes=sum(groups, []),
        compiler_params=pltpu.CompilerParams(
            collective_id=1, has_side_effects=True, vmem_limit_bytes=40 * 1024 * 1024
        ),
        name="train",
    )(*[pltpu.with_memory_space_constraint(value, pltpu.HBM) for value in args])


def settle_kernel(
    in_ref, slope_ref, home_ref, sh_ref, shown_ref, rendered_ref, splat_grad_ref, sh_grad_ref,
    table_ref, ninth_ref,
):
    rendered_ref[...] = shown_ref[...]
    chunks = sh_ref.shape[1] // BLOCK
    for chunk in range(chunks):
        first, ninth = unpack_two(in_ref[2 * chunk], in_ref[2 * chunk + 1])
        table_ref[:, chunk * BLOCK : (chunk + 1) * BLOCK] = first
        ninth_ref[chunk : chunk + 1, :] = ninth
    for chunk in range(chunks):
        lanes = slice(chunk * BLOCK, (chunk + 1) * BLOCK)
        first, last = gather_rows(table_ref, ninth_ref, chunks, home_ref[chunk : chunk + 1, :])
        splat_grad_ref[0:6, lanes] = first[0:6]
        tints = (first[6:7], first[7:8], last)
        basis = slope_ref[0:16, lanes]
        mixed = jnp.zeros((16, BLOCK), jnp.float32)
        for c in range(3):
            tint = jnp.broadcast_to(tints[c], (16, BLOCK))
            sh_grad_ref[16 * c : 16 * (c + 1), lanes] = tint * basis
            mixed = mixed + tint * sh_ref[16 * c : 16 * (c + 1), lanes]
        splat_grad_ref[6:9, lanes] = jnp.concatenate(
            [
                jnp.sum(mixed * slope_ref[16 * d : 16 * (d + 1), lanes], axis=0, keepdims=True)
                for d in (1, 2, 3)
            ],
            axis=0,
        )


def settle(landed, slopes, home, splats, sh_coeffs, shown):
    own = splats.shape[1]
    return pl.pallas_call(
        settle_kernel,
        out_shape=(
            jax.ShapeDtypeStruct(shown.shape, jnp.float32),
            jax.ShapeDtypeStruct(splats.shape, jnp.float32),
            jax.ShapeDtypeStruct(sh_coeffs.shape, jnp.float32),
        ),
        in_specs=[vmem()] * 5,
        out_specs=(vmem(), vmem(), vmem()),
        scratch_shapes=[
            pltpu.VMEM((8, own), jnp.float32),
            pltpu.VMEM((own // BLOCK, BLOCK), jnp.float32),
        ],
        compiler_params=pltpu.CompilerParams(vmem_limit_bytes=VMEM_ROOM),
        name="settle",
    )(landed, slopes, home, sh_coeffs, shown)


def body(splats, sh_coeffs, send_list, block_slots, block_tiles, target):
    landed, slopes, home, shown = train(
        splats, sh_coeffs, send_list, target, block_slots[0], block_tiles
    )
    return settle(landed, slopes, home, splats, sh_coeffs, shown)


def solution(mesh):
    in_specs = (
        P(None, ("gauss", "tile")),
        P(None, ("gauss", "tile")),
        P(("gauss", "tile")),
        P("gauss", "tile", None),
        P("gauss", "tile"),
        P(None, "gauss", "tile"),
    )
    out_specs = (P(None, "gauss", "tile"), P(None, ("gauss", "tile")), P(None, ("gauss", "tile")))
    return jax.shard_map(body, mesh=mesh, in_specs=in_specs, out_specs=out_specs, check_vma=False)
```

```python
import functools
import math

import jax
import jax.numpy as jnp
from jax import lax
from jax.experimental import pallas as pl
from jax.experimental.pallas import tpu as pltpu
from jax.sharding import PartitionSpec as P

TILE_SIDE = 16
TILES_DEV = 8


BASE_ZERO = 0.28209479177387814
BASE_ONE = 0.4886025119029199
BASE_TWO = (
    1.0925484305920792,
    -1.0925484305920792,
    0.31539156525252005,
    -1.0925484305920792,
    0.5462742152960396,
)
BASE_THREE = (
    -0.5900435899266435,
    2.890611442640554,
    -0.4570457994644658,
    0.3731763325901154,
    -0.4570457994644658,
    1.445305721320277,
    -0.5900435899266435,
)
CONST_ONE = 0.0001
CONST_TWO = 0.0009


SEGMENTS = 8
STEPS = 16
BLOCK = SEGMENTS * STEPS
HALF = 128
CENTRE = 7.5
MESH = pl.DeviceIdType.MESH
VMEM_ROOM = 16 * 1024 * 1024


LOG2E = 1.4426950408889634
FIELDS = 9
COEF_ROWS = 48
GROUP = 24
WIDTH = 2
TURN = 6
PACKED = 8
GRAD_ROWS = 24
ACROSS = (((1,), (1,)), ((), ()))
DOWN = (((0,), (0,)), ((), ()))


def pick(table, index):
    return jnp.take_along_axis(table, index, axis=1, mode="promise_in_bounds")


def coarse(value):
    return value.astype(jnp.bfloat16).astype(jnp.float32)


def halves(value):
    high = value.astype(jnp.bfloat16)
    low = (value - high.astype(jnp.float32)).astype(jnp.bfloat16)
    return high, low


def swap_blocks(value):
    rows = lax.broadcasted_iota(jnp.int32, value.shape, 0)
    blocks = lax.broadcasted_iota(jnp.int32, value.shape, 1) // TILE_SIDE
    for bit in (1, 2, 4):
        up = pltpu.roll(pltpu.roll(value, SEGMENTS - bit, 0), TILE_SIDE * bit, 1)
        down = pltpu.roll(pltpu.roll(value, bit, 0), HALF - TILE_SIDE * bit, 1)
        low, left = (rows & bit) == 0, (blocks & bit) == 0
        value = jnp.where(low == left, value, jnp.where(low, up, down))
    return value


def halve(target_ref, at, step, lanes, pair):
    high, low = halves(jnp.concatenate(pair, axis=0))
    rows = 2 * SEGMENTS * step
    target_ref[at, rows : rows + 2 * SEGMENTS, lanes] = high
    target_ref[at, BLOCK + rows : BLOCK + rows + 2 * SEGMENTS, lanes] = low


def pixel_basis():
    rows = lax.broadcasted_iota(jnp.int32, (8, 2 * HALF), 0)
    pixels = lax.broadcasted_iota(jnp.int32, (8, 2 * HALF), 1)
    along = (pixels % TILE_SIDE).astype(jnp.float32) - CENTRE
    down = (pixels // TILE_SIDE).astype(jnp.float32) - CENTRE
    basis = jnp.zeros((8, 2 * HALF), jnp.float32)
    terms = (along * along, along * down, down * down, along, down, jnp.ones_like(along))
    for at, term in enumerate(terms):
        basis = jnp.where(rows == at, term, basis)
    return basis


def spread_order(slots):
    lanes = lax.broadcasted_iota(jnp.int32, slots.shape, 1)
    return pick(slots, (lanes % SEGMENTS) * STEPS + lanes // SEGMENTS)


def tiles_of(tile_ref, first):
    at = lax.broadcasted_iota(jnp.int32, (SEGMENTS, BLOCK), 0)
    tiles = jnp.zeros((SEGMENTS, BLOCK), jnp.int32)
    for k in range(SEGMENTS):
        tiles = jnp.where(at == k, tile_ref[0, first + k], tiles)
    return tiles


def forward_part(
    tile_ref, last_ref, recv_ref, slots_ref, picture_ref, rec_ref, coef_ref, saved_ref,
    alpha_ref, share_ref, work_ref, image_ref, basis_ref,
):
    slots_total = slots_ref.shape[0]
    chunks = recv_ref.shape[1] // BLOCK
    origin_x = (lax.axis_index("tile") * (TILE_SIDE * TILES_DEV)).astype(jnp.float32) + CENTRE
    origin_y = (lax.axis_index("gauss") * TILE_SIDE).astype(jnp.float32) + CENTRE

    def collect(group, carry):
        first = group * SEGMENTS
        slots = slots_ref[pl.ds(pl.multiple_of(first, SEGMENTS), SEGMENTS), :]
        fine = slots % BLOCK
        chunk_at = slots // BLOCK
        found = [None] * FIELDS
        for chunk in range(chunks):
            hit = chunk_at == chunk
            for f in range(FIELDS):
                row = recv_ref[f : f + 1, chunk * BLOCK : (chunk + 1) * BLOCK]
                got = pick(jnp.broadcast_to(row, (SEGMENTS, BLOCK)), fine)
                found[f] = got if chunk == 0 else jnp.where(hit, got, found[f])
        tiles = tiles_of(tile_ref, first)
        base_x = (TILE_SIDE * jnp.minimum(tiles, TILES_DEV - 1)).astype(jnp.float32) + origin_x
        at_x = found[0] - base_x
        at_y = found[1] - origin_y
        con_a = -0.5 * found[2]
        con_b = -found[3]
        con_c = -0.5 * found[4]
        shut = 1.0 + jnp.exp(-found[5])
        for k, value in enumerate((at_x, at_y, con_a, con_b, con_c, 1.0 - 1.0 / shut)):
            rec_ref[k, pl.ds(pl.multiple_of(first, SEGMENTS), SEGMENTS), :] = value
        part_x = con_a * at_x
        part_y = con_c * at_y
        cross = con_b * at_y
        level = at_x * (part_x + cross) + at_y * part_y
        terms = (
            LOG2E * con_a,
            LOG2E * con_b,
            LOG2E * con_c,
            -LOG2E * (2.0 * part_x + cross),
            -LOG2E * (2.0 * part_y + con_b * at_x),
            LOG2E * (level - jnp.log(shut)),
        )

        def put(row, value):
            work_ref[pl.ds(first * COEF_ROWS + row, SEGMENTS, stride=COEF_ROWS), :] = value

        for k, term in enumerate(terms):
            high = coarse(term)
            rest = term - high
            middle = coarse(rest)
            put(k, high)
            put(8 + k, middle)
            put(16 + k, rest - middle)
        for c in range(3):
            high = coarse(found[6 + c])
            put(24 + c, high)
            put(32 + c, found[6 + c] - high)
            put(40 + c, high)
        return carry

    lax.fori_loop(0, slots_total // SEGMENTS, collect, 0)
    seg_at = lax.broadcasted_iota(jnp.int32, (SEGMENTS, HALF), 0)
    own_seg = seg_at == lax.broadcasted_iota(jnp.int32, (SEGMENTS, HALF), 1) % SEGMENTS

    def draw_local(slot):
        coefs = work_ref[pl.ds(pl.multiple_of(slot * COEF_ROWS, COEF_ROWS), COEF_ROWS), :].astype(
            jnp.bfloat16
        )
        coef_ref[slot] = coefs
        power = lax.dot_general(coefs, basis_ref[...], DOWN, preferred_element_type=jnp.float32)
        through = [jnp.ones((SEGMENTS, HALF), jnp.float32) for side in range(2)]
        weights = [[], []]
        for step in range(STEPS):
            for side in range(2):
                rows = slice(step * SEGMENTS, (step + 1) * SEGMENTS)
                lanes = slice(side * HALF, (side + 1) * HALF)
                alpha = jnp.exp2(power[rows, lanes])
                weight = alpha * through[side]
                alpha_ref[slot, rows, lanes] = alpha
                share_ref[slot, rows, lanes] = weight
                through[side] = through[side] - weight
                weights[side].append(weight)
        weight = jnp.concatenate([jnp.concatenate(w, axis=0) for w in weights], axis=1)
        tints = []
        for part in (24, 32):
            for c in range(3):
                row = work_ref[pl.ds(slot * COEF_ROWS + part + c, 1), :]
                tints.append(jnp.where(own_seg, jnp.broadcast_to(row, (SEGMENTS, HALF)), 0.0))
        tint = jnp.concatenate(tints, axis=0).astype(jnp.bfloat16)
        sums = jnp.dot(
            jnp.concatenate([tint, tint], axis=1),
            jnp.concatenate(halves(weight), axis=0),
            preferred_element_type=jnp.float32,
        )
        return through, sums[0:24] + sums[24:48]

    def draw_join(slot, carry, through, sums):
        tile = tile_ref[0, slot]
        fresh = (slot == 0) | (tile != tile_ref[0, jnp.maximum(slot - 1, 0)])
        after = []
        for side in range(2):
            start = jnp.where(fresh, 1.0, carry[side][0])
            running = through[side]
            for shift in (1, 2, 4):
                running = jnp.where(
                    seg_at >= shift, running * pltpu.roll(running, shift, 0), running
                )
            before = jnp.where(seg_at == 0, 1.0, pltpu.roll(running, 1, 0)) * start
            kept = [start * running[SEGMENTS - 1 : SEGMENTS]]
            lanes = slice(side * HALF, (side + 1) * HALF)
            saved_ref[slot, 0, :, lanes] = before
            saved_ref[slot, 1, :, lanes] = through[side]
            for c in range(3):
                part = sums[c * SEGMENTS : (c + 1) * SEGMENTS, lanes]
                saved_ref[slot, 2 + c, :, lanes] = part
                shade_sum = jnp.sum(before * part, axis=0, keepdims=True)
                shade_sum = jnp.where(fresh, 0.0, carry[side][1 + c]) + shade_sum
                image_ref[slot, c : c + 1, lanes] = shade_sum
                kept.append(shade_sum)
            after.append(tuple(kept))
        return tuple(after)

    def draw(pair, carry):
        locals_two = [draw_local(GROUP * pair + k) for k in range(GROUP)]
        for k in range(GROUP):
            carry = draw_join(GROUP * pair + k, carry, *locals_two[k])
        return carry

    start = (jnp.ones((1, HALF), jnp.float32),) + (jnp.zeros((1, HALF), jnp.float32),) * 3
    lax.fori_loop(0, slots_total // GROUP, draw, (start, start))
    for side in range(2):
        lanes = slice(side * HALF, (side + 1) * HALF)
        for c in range(3):
            rows = [image_ref[last_ref[tile], c : c + 1, lanes] for tile in range(TILES_DEV)]
            picture_ref[c, side * SEGMENTS : (side + 1) * SEGMENTS, :] = swap_blocks(
                jnp.concatenate(rows, axis=0)
            )


def backward_part(
    tile_ref, rec_ref, coef_ref, saved_ref, alpha_ref, share_ref, heavy_ref, grad_ref,
    slots_ref, select_ref, out_ref,
    rhs_ref, mom_ref, back_ref, where_ref, acc_ref, lit_ref, force_ref, behind_ref,
):
    chunks = out_ref.shape[1] // BLOCK
    slots_total = coef_ref.shape[0]
    acc_ref[...] = jnp.zeros_like(acc_ref)
    basis = pixel_basis()
    blank = jnp.zeros_like(basis)
    basis16 = jnp.concatenate([basis, blank], axis=0).astype(jnp.bfloat16)
    for tile in range(TILES_DEV):
        grads = grad_ref[tile]
        high = coarse(grads)
        rhs_ref[tile] = jnp.concatenate([blank, high, high, grads - high], axis=0).astype(
            jnp.bfloat16
        )
    seg_at = lax.broadcasted_iota(jnp.int32, (SEGMENTS, HALF), 0)

    def prepare(slot, carry, buf):
        tile = tile_ref[0, slot]
        later = tile_ref[0, jnp.minimum(slot + 1, slots_total - 1)]
        final = (slot == slots_total - 1) | (tile != later)
        shown = jnp.minimum(tile, TILES_DEV - 1)
        grads = grad_ref[shown]
        after = []
        for side in range(2):
            lanes = slice(side * HALF, (side + 1) * HALF)
            start = jnp.where(final, 0.0, carry[side])
            total = grads[0:1, lanes] * saved_ref[slot, 2, :, lanes]
            for c in (1, 2):
                total = total + grads[c : c + 1, lanes] * saved_ref[slot, 2 + c, :, lanes]
            factor = saved_ref[slot, 1, :, lanes]
            for shift in (1, 2, 4):
                inside = seg_at < SEGMENTS - shift
                total = jnp.where(
                    inside, total + factor * pltpu.roll(total, SEGMENTS - shift, 0), total
                )
                factor = jnp.where(
                    inside, factor * pltpu.roll(factor, SEGMENTS - shift, 0), factor
                )
            entering = total + factor * start
            after.append(entering[0:1])
            behind_ref[buf, :, lanes] = jnp.where(
                seg_at < SEGMENTS - 1, pltpu.roll(entering, SEGMENTS - 1, 0), start
            )
        lit_ref[buf] = lax.dot_general(
            coef_ref[slot, 16:COEF_ROWS, :], rhs_ref[shown], DOWN, preferred_element_type=jnp.float32
        )
        return tuple(after)

    def trace(slots, bufs):
        chains = [(k, side) for k in range(len(slots)) for side in range(2)]
        lanes = [slice(side * HALF, (side + 1) * HALF) for side in range(2)]
        later = {(k, side): behind_ref[bufs[k], :, lanes[side]] for k, side in chains}
        for step in reversed(range(STEPS // 2)):
            for k, side in chains:
                pair = []
                for at in (2 * step + 1, 2 * step):
                    rows = slice(at * SEGMENTS, (at + 1) * SEGMENTS)
                    gap = lit_ref[bufs[k], rows, lanes[side]] - later[k, side]
                    alpha = alpha_ref[slots[k], rows, lanes[side]]
                    later[k, side] = later[k, side] + alpha * gap
                    pair.append(share_ref[slots[k], rows, lanes[side]] * gap)
                halve(force_ref, bufs[k], step, lanes[side], pair[::-1])

    def reduce(slot, buf):
        shown = jnp.minimum(tile_ref[0, slot], TILES_DEV - 1)
        found = lax.dot_general(
            basis16, force_ref[buf], ACROSS, preferred_element_type=jnp.float32
        )
        painted = lax.dot_general(
            jnp.concatenate(halves(grad_ref[shown]), axis=0),
            heavy_ref[slot],
            ACROSS,
            preferred_element_type=jnp.float32,
        )
        painted = painted[0:8] + painted[8:16]
        mom_ref[slot, 0:8, :] = found[0:8, :BLOCK] + found[0:8, BLOCK:]
        mom_ref[slot, 8:16, :] = painted[:, :BLOCK] + painted[:, BLOCK:]

    runs = slots_total // WIDTH

    def slot_of(run, k):
        return (runs - 1 - run) * WIDTH + k

    def ready(run, carry, half):
        for k in reversed(range(WIDTH)):
            carry = prepare(slot_of(run, k), carry, half * WIDTH + k)
        return carry

    def gather_in(run, half):
        for k in range(WIDTH):
            reduce(slot_of(run, k), half * WIDTH + k)

    def follow(run, half):
        trace(
            [slot_of(run, k) for k in range(WIDTH)], [half * WIDTH + k for k in range(WIDTH)]
        )

    def pull(turn, carry):
        for part in range(TURN):
            run = TURN * turn + part + 1
            half = (part + 1) % 2
            gather_in(run - 1, 1 - half)
            carry = ready(run + 1, carry, 1 - half)
            follow(run, half)
        return carry

    zeros = jnp.zeros((1, HALF), jnp.float32)
    carry = ready(0, (zeros, zeros), 0)
    carry = ready(1, carry, 1)
    follow(0, 0)
    carry = lax.fori_loop(0, (runs - 2) // TURN, pull, carry)
    for run in range((runs - 2) // TURN * TURN + 1, runs):
        half = run % 2
        gather_in(run - 1, 1 - half)
        if run + 1 < runs:
            carry = ready(run + 1, carry, 1 - half)
        follow(run, half)
    gather_in(runs - 1, (runs - 1) % 2)
    chunk_rows = lax.broadcasted_iota(jnp.int32, (chunks, BLOCK), 0)

    def settle(group, carry):
        first = pl.multiple_of(group * SEGMENTS, SEGMENTS)
        tiles = tiles_of(tile_ref, first)
        used = tiles < TILES_DEV
        rows = pl.ds(first, SEGMENTS)

        m_xx, m_xy, m_yy, m_x, m_y, m_0 = [
            mom_ref[rows, k, :] for k in range(6)
        ]
        at_x, at_y, con_a, con_b, con_c, shut_s = [rec_ref[k, rows, :] for k in range(6)]
        h_x = m_x - at_x * m_0
        h_y = m_y - at_y * m_0
        h_xx = m_xx - 2.0 * at_x * m_x + at_x * at_x * m_0
        h_xy = m_xy - at_x * m_y - at_y * m_x + at_x * at_y * m_0
        h_yy = m_yy - 2.0 * at_y * m_y + at_y * at_y * m_0
        results = [
            -2.0 * con_a * h_x - con_b * h_y,
            -2.0 * con_c * h_y - con_b * h_x,
            -0.5 * h_xx,
            -h_xy,
            -0.5 * h_yy,
            shut_s * m_0,
        ] + [mom_ref[rows, 8 + c, :] for c in range(3)]
        for f, value in enumerate(results):
            kept = jnp.where(used, value, 0.0)
            high = coarse(kept)
            back_ref[rows, f, :] = high
            back_ref[rows, 12 + f, :] = kept - high
        slots = slots_ref[rows, :]
        where_ref[rows, :] = slots // BLOCK
        for quad in range(0, SEGMENTS, 4):
            stacked = []
            for k in range(quad, quad + 4):
                hit = chunk_rows == where_ref[pl.ds(first + k, 1), :]
                stacked.append(
                    jnp.concatenate(
                        [
                            jnp.where(hit, back_ref[first + k, part + f : part + f + 1, :], 0.0)
                            for part in (0, 12)
                            for f in range(FIELDS)
                        ],
                        axis=0,
                    ).astype(jnp.bfloat16)
                )
            acc_ref[...] += lax.dot_general(
                jnp.concatenate(stacked, axis=1),
                select_ref[2 * group + quad // 4],
                ACROSS,
                preferred_element_type=jnp.float32,
            )
        return carry

    lax.fori_loop(0, slots_total // SEGMENTS, settle, 0, unroll=2)
    total = FIELDS * chunks
    for chunk in range(chunks):
        lanes = slice(chunk * BLOCK, (chunk + 1) * BLOCK)
        out_ref[0:8, lanes] = (
            acc_ref[pl.ds(chunk, 8, stride=chunks), :]
            + acc_ref[pl.ds(total + chunk, 8, stride=chunks), :]
        )
        at = 8 * chunks + chunk
        out_ref[8:9, lanes] = acc_ref[at : at + 1, :] + acc_ref[total + at : total + at + 1, :]


def hbm():
    return pl.BlockSpec(memory_space=pltpu.HBM)


def smem():
    return pl.BlockSpec(memory_space=pltpu.SMEM)


def vmem():
    return pl.BlockSpec(memory_space=pltpu.VMEM)


WAYS = [(down, right) for down in (-1, 0, 1) for right in (-1, 0, 1) if (down, right) != (0, 0)]
NORM = sum(math.exp(-m * m / 4.5) for m in range(-5, 6))
EXT_ROWS = 40
MID_ROWS = 32


def neighbour(bands, columns, way):
    there_band = lax.axis_index("gauss") + way[0]
    there_col = lax.axis_index("tile") + way[1]
    exists = (there_band >= 0) & (there_band < bands) & (there_col >= 0) & (there_col < columns)
    return exists, (there_band, there_col)


def greet_round(barrier, bands, columns):
    peers = jnp.int32(0)
    for way in WAYS:
        if way[1] == 0:
            continue
        exists, there = neighbour(bands, columns, way)
        peers = peers + exists.astype(jnp.int32)

        @pl.when(exists)
        def _(there=there):
            pl.semaphore_signal(barrier, inc=1, device_id=there, device_id_type=MESH)

    return peers


def border_copies(bands, columns, plane_ref, edge_ref, tall_ref, side_ref, send_sem, recv_sem):
    found = []
    for at, way in enumerate(WAYS):
        exists, there = neighbour(bands, columns, way)
        landing = len(WAYS) - 1 - at
        source = plane_ref if way[1] == 0 else edge_ref
        target = tall_ref.at[landing] if way[1] == 0 else side_ref.at[landing]
        found.append(
            (
                exists,
                pltpu.make_async_remote_copy(
                    src_ref=source,
                    dst_ref=target,
                    send_sem=send_sem.at[at],
                    recv_sem=recv_sem.at[landing],
                    device_id=there,
                    device_id_type=MESH,
                ),
                pltpu.make_async_remote_copy(
                    src_ref=source,
                    dst_ref=tall_ref.at[at] if way[1] == 0 else side_ref.at[at],
                    send_sem=send_sem.at[at],
                    recv_sem=recv_sem.at[at],
                    device_id=there,
                    device_id_type=MESH,
                ),
            )
        )
    return found


def border_start(copies):
    for exists, out, back in copies:

        @pl.when(exists)
        def _(out=out):
            out.start()


def border_wait(copies):
    for exists, out, back in copies:

        @pl.when(exists)
        def _(out=out, back=back):
            out.wait_send()
            back.wait_recv()


def pack_edges(plane_ref, edge_ref):
    lanes = lax.broadcasted_iota(jnp.int32, edge_ref.shape, 1)
    packed = jnp.zeros(edge_ref.shape, jnp.float32)
    for c in range(3):
        plane = plane_ref[c]
        near = pltpu.roll(plane, 32 * c, 1) if c else plane
        far = pltpu.roll(plane, 32 * c + 32, 1)
        packed = jnp.where(
            lanes // 32 == c, jnp.where(lanes % 32 < 16, near, far), packed
        )
    edge_ref[...] = packed


def stretch(above, own, below):
    turn = lax.broadcasted_iota(jnp.int32, (8, own.shape[1]), 0) >= 6
    mixed = jnp.where(turn, above[0:8], below[8:16])
    return jnp.concatenate([own, above[8:16], below[0:8], mixed], axis=0)


def extend(plane_ref, tall_ref, side_ref):
    east = lax.broadcasted_iota(jnp.int32, side_ref.shape[1:], 1) % 32 < 16
    borders = [
        jnp.where(east, side_ref[WAYS.index((down, 1))], side_ref[WAYS.index((down, -1))])
        for down in (-1, 0, 1)
    ]
    border = stretch(*borders)
    planes = []
    for c in range(3):
        main = stretch(
            tall_ref[WAYS.index((-1, 0)), c], plane_ref[c], tall_ref[WAYS.index((1, 0)), c]
        )
        turned = pltpu.roll(border, HALF - 32 * c, 1) if c else border
        planes.append(jnp.concatenate([main, turned], axis=1))
    return planes


def window_weight(gap):
    gap = gap.astype(jnp.float32)
    return jnp.where(jnp.abs(gap) < 5.5, jnp.exp(gap * gap / -4.5) * (1.0 / NORM), 0.0)


def split_rows(value):
    first = coarse(value)
    rest = value - first
    second = coarse(rest)
    return first, second, rest - second


def six_data(value, axis):
    first, second, third = split_rows(value)
    return jnp.concatenate([first, second, third, first, second, first], axis=axis).astype(
        jnp.bfloat16
    )


def six_weights(value, axis):
    first, second, third = split_rows(value)
    return jnp.concatenate([first, first, first, second, second, third], axis=axis).astype(
        jnp.bfloat16
    )


def ext_row(at):
    return jnp.where(at < 16, at, jnp.where(at < 24, at - 24, jnp.where(at < 38, at - 8, at - 48)))


def ext_col(at):
    return jnp.where(at < 144, at, jnp.where(at < 160, at - 160, 10000))


def mid_col(at):
    return jnp.where(at < 192, at, at - 256)


def iota(shape, axis):
    return lax.broadcasted_iota(jnp.int32, shape, axis)


def fdot(left, right):
    return jnp.dot(left, right, preferred_element_type=jnp.float32)


def weigh_part(saved_ref, share_ref, heavy_ref):
    def weigh(group, carry):
        for step in range(STEPS // 2):
            for k in range(4):
                slot = 4 * group + k
                for side in range(2):
                    lanes = slice(side * HALF, (side + 1) * HALF)
                    before = saved_ref[slot, 0, :, lanes]
                    pair = []
                    for at in (2 * step, 2 * step + 1):
                        rows = slice(at * SEGMENTS, (at + 1) * SEGMENTS)
                        weight = share_ref[slot, rows, lanes] * before
                        share_ref[slot, rows, lanes] = weight
                        pair.append(weight)
                    halve(heavy_ref, slot, step, lanes, pair)
        return carry

    lax.fori_loop(0, share_ref.shape[0] // 4, weigh, 0)


def contrast_part(
    bands, columns, meanwhile, shown_ref, aim_ref, out_ref,
    edge_ref, tall_ref, side_ref, wide_ref, back_ref, send_sem, recv_sem,
):
    band = lax.axis_index("gauss")
    column = lax.axis_index("tile")
    rows, cols = shown_ref.shape[1:]
    pack_edges(shown_ref, edge_ref)
    copies = border_copies(
        bands, columns, shown_ref, edge_ref, tall_ref, side_ref, send_sem, recv_sem
    )
    border_start(copies)
    wide = 2 * cols
    for half in range(2):
        lanes = slice(half * cols, (half + 1) * cols)
        shape = (wide, cols)
        across = window_weight(mid_col(iota(shape, 1) + half * cols) - ext_col(iota(shape, 0)))
        wide_ref[:, lanes] = six_weights(across, 0)
    back = window_weight(mid_col(iota((wide, cols), 0)) - iota((wide, cols), 1))
    back_ref[...] = six_weights(back, 0)
    shape = (MID_ROWS, EXT_ROWS)
    down = window_weight(iota(shape, 0) - 5 - ext_row(iota(shape, 1)))
    down = six_weights(down, 1)
    shape = (rows, MID_ROWS)
    up = six_weights(window_weight(iota(shape, 0) - iota(shape, 1) + 5), 1)
    meanwhile()
    border_wait(copies)
    pics = extend(shown_ref, tall_ref, side_ref)
    strips = []
    for kind in range(4):
        for c in range(3):
            pic, aim = pics[c], aim_ref[c]
            plane = (pic, aim, pic * pic + aim * aim, pic * aim)[kind] if kind > 1 else (
                pic if kind == 0 else aim
            )
            strips.append(fdot(down, six_data(plane, 0)))
    moments = fdot(six_data(jnp.concatenate(strips, axis=0), 1), wide_ref[...])
    shape = (MID_ROWS, wide)
    row_at = band * rows + iota(shape, 0) - 5
    col_at = column * cols + mid_col(iota(shape, 1))
    inside = (row_at >= 0) & (row_at < bands * rows) & (col_at >= 0) & (col_at < columns * cols)
    strips = [None] * 9
    for c in range(3):
        mu_x, mu_y, squares, cross = [
            moments[(3 * kind + c) * MID_ROWS : (3 * kind + c + 1) * MID_ROWS] for kind in range(4)
        ]
        mean_xy = mu_x * mu_y
        mean_sq = mu_x * mu_x + mu_y * mu_y
        top_1 = 2.0 * mean_xy + CONST_ONE
        top_2 = 2.0 * (cross - mean_xy) + CONST_TWO
        low_1 = mean_sq + CONST_ONE
        low_2 = squares - mean_sq + CONST_TWO
        inverse = -0.2 / (low_1 * low_2)
        value = top_1 * top_2 * inverse
        value_1 = value * low_2 * inverse * -5.0
        value_2 = value * low_1 * inverse * -5.0
        slope_mean = 2.0 * mu_y * (top_2 - top_1) * inverse - 2.0 * mu_x * (value_1 - value_2)
        for kind, slope in enumerate((slope_mean, -value_2, 2.0 * top_1 * inverse)):
            strips[3 * kind + c] = fdot(up, six_data(jnp.where(inside, slope, 0.0), 0))
    spread = fdot(six_data(jnp.concatenate(strips, axis=0), 1), back_ref[...])
    out_ref[...] = jnp.zeros_like(out_ref)
    for c in range(3):
        pic = shown_ref[c]
        aim = aim_ref[c, 0:rows, 0:cols]
        parts = [spread[(3 * kind + c) * rows : (3 * kind + c + 1) * rows] for kind in range(3)]
        total = parts[0] + 2.0 * pic * parts[1] + aim * parts[2] + 1.6 * (pic - aim)
        for side in range(2):
            moved = swap_blocks(total[side * SEGMENTS : (side + 1) * SEGMENTS])
            for tile in range(TILES_DEV):
                out_ref[tile, c : c + 1, side * HALF : (side + 1) * HALF] = moved[tile : tile + 1]


def border_scratch(rows, cols):
    ways = len(WAYS)
    return [
        pltpu.VMEM((rows, cols), jnp.float32),
        pltpu.VMEM((ways, 3, rows, cols), jnp.float32),
        pltpu.VMEM((ways, rows, cols), jnp.float32),
    ]


def basis_rows(x, y, z):
    xx, yy, zz = x * x, y * y, z * z
    return [
        jnp.full_like(x, BASE_ZERO),
        -BASE_ONE * y,
        BASE_ONE * z,
        -BASE_ONE * x,
        BASE_TWO[0] * x * y,
        BASE_TWO[1] * y * z,
        BASE_TWO[2] * (2.0 * zz - xx - yy),
        BASE_TWO[3] * x * z,
        BASE_TWO[4] * (xx - yy),
        BASE_THREE[0] * y * (3.0 * xx - yy),
        BASE_THREE[1] * x * y * z,
        BASE_THREE[2] * y * (4.0 * zz - xx - yy),
        BASE_THREE[3] * z * (2.0 * zz - 3.0 * xx - 3.0 * yy),
        BASE_THREE[4] * x * (4.0 * zz - xx - yy),
        BASE_THREE[5] * z * (xx - yy),
        BASE_THREE[6] * x * (xx - 3.0 * yy),
    ]


def slope_rows(x, y, z):
    xx, yy, zz = x * x, y * y, z * z
    xy, yz, xz = x * y, y * z, x * z
    none = jnp.zeros_like(x)
    one = jnp.ones_like(x)
    two, three = BASE_TWO, BASE_THREE
    along_x = [
        none, none, none, -BASE_ONE * one,
        two[0] * y, none, -2.0 * two[2] * x, two[3] * z, 2.0 * two[4] * x,
        6.0 * three[0] * xy, three[1] * yz, -2.0 * three[2] * xy, -6.0 * three[3] * xz,
        three[4] * (4.0 * zz - 3.0 * xx - yy), 2.0 * three[5] * xz, three[6] * (3.0 * xx - 3.0 * yy),
    ]
    along_y = [
        none, -BASE_ONE * one, none, none,
        two[0] * x, two[1] * z, -2.0 * two[2] * y, none, -2.0 * two[4] * y,
        three[0] * (3.0 * xx - 3.0 * yy), three[1] * xz, three[2] * (4.0 * zz - xx - 3.0 * yy),
        -6.0 * three[3] * yz, -2.0 * three[4] * xy, -2.0 * three[5] * yz, -6.0 * three[6] * xy,
    ]
    along_z = [
        none, none, BASE_ONE * one, none,
        none, two[1] * y, 4.0 * two[2] * z, two[3] * x, none,
        none, three[1] * xy, 8.0 * three[2] * yz, three[3] * (6.0 * zz - 3.0 * xx - 3.0 * yy),
        8.0 * three[4] * xz, three[5] * (xx - yy), none,
    ]
    return along_x, along_y, along_z


def lane_of():
    return lax.broadcasted_iota(jnp.int32, (8, BLOCK), 1)


def row_of():
    return lax.broadcasted_iota(jnp.int32, (8, BLOCK), 0)


def gather_rows(table_ref, ninth_ref, chunks, index):
    index = jnp.broadcast_to(index, (8, BLOCK))
    fine = index % BLOCK
    chunk_at = index // BLOCK
    first = None
    ninth = jnp.zeros((8, BLOCK), jnp.float32)
    for chunk in range(chunks):
        got = pick(table_ref[0:8, chunk * BLOCK : (chunk + 1) * BLOCK], fine)
        first = got if chunk == 0 else jnp.where(chunk_at == chunk, got, first)
    for base in range(0, chunks, 8):
        got = pick(ninth_ref[base : base + 8, :], fine)
        ninth = ninth + jnp.where(chunk_at == row_of() + base, got, 0.0)
    return first, jnp.sum(ninth, axis=0, keepdims=True)


def pack_two(first, last):
    left = lane_of() < BLOCK // 2
    swapped = pltpu.roll(first, BLOCK // 2, 1)
    one = jnp.where(left, first, pltpu.roll(swapped, 4, 0))
    two = jnp.where(left, swapped, pltpu.roll(first, 4, 0))
    tail = row_of() >= 4
    ninth = jnp.broadcast_to(last, (8, BLOCK))
    return jnp.where(tail, ninth, one), jnp.where(tail, pltpu.roll(ninth, BLOCK // 2, 1), two)


def unpack_two(one, two):
    left = lane_of() < BLOCK // 2
    upper = jnp.where(left, one, pltpu.roll(two, BLOCK // 2, 1))
    lower = jnp.where(left, pltpu.roll(one, BLOCK // 2, 1), two)
    return jnp.where(row_of() < 4, upper, pltpu.roll(lower, 4, 0)), upper[4:5]


def ring(gap, owners):
    there = lax.axis_index("gauss") + gap
    return jnp.where(there >= owners, there - owners, there)


def far_first(owners):
    return sorted(range(1, owners), key=lambda gap: (-abs(2 * gap - owners), gap))


def greet(owners):
    barrier = pltpu.get_barrier_semaphore()
    column = lax.axis_index("tile")
    for gap in far_first(owners):
        pl.semaphore_signal(
            barrier, inc=1, device_id=(ring(gap, owners), column), device_id_type=MESH
        )
    return barrier


def parcel(owners, gap, out_ref, in_ref, send_sem, recv_sem):
    band = lax.axis_index("gauss")
    there = ring(gap, owners)
    return pltpu.make_async_remote_copy(
        src_ref=out_ref.at[there, 0:5],
        dst_ref=in_ref.at[band, 0:5],
        send_sem=send_sem.at[gap],
        recv_sem=recv_sem.at[gap],
        device_id=(there, lax.axis_index("tile")),
        device_id_type=MESH,
    )


def post(owners, out_ref, in_ref, send_sem, recv_sem):
    band = lax.axis_index("gauss")
    for gap in far_first(owners):
        parcel(owners, gap, out_ref, in_ref, send_sem, recv_sem).start()
    in_ref[band] = out_ref[band]


def take_in(owners, out_ref, in_ref, send_sem, recv_sem):
    for gap in range(1, owners):
        parcel(owners, gap, out_ref, in_ref, send_sem, recv_sem).wait()


def count_tiles(tile_ref, last_ref):
    for tile in range(TILES_DEV):
        last = jnp.int32(-1)
        for slot in range(tile_ref.shape[1]):
            last = last + (tile_ref[0, slot] <= tile).astype(jnp.int32)
        last_ref[tile] = last


def prepare_part(order_ref, select_ref, work_ref, basis_ref):
    work_ref[...] = jnp.zeros_like(work_ref)
    basis = pixel_basis()
    basis_ref[...] = jnp.concatenate([basis] * 3 + [jnp.zeros_like(basis)] * 3, axis=0).astype(
        jnp.bfloat16
    )
    lane_rows = lax.broadcasted_iota(jnp.int32, (BLOCK, 4 * BLOCK), 0)
    for first in range(0, order_ref.shape[0], 4):
        fine = [order_ref[first + k : first + k + 1, :] % BLOCK for k in range(4)]
        select_ref[first // 4] = jnp.where(
            lane_rows == jnp.concatenate(fine, axis=1), 1.0, 0.0
        ).astype(jnp.bfloat16)


def deliver_part(
    owners, columns, loads, clear, meanwhile, recv_ref, home_ref, aim_ref, order_ref, slope_ref,
    tile_ref, last_ref, splats_ref, sh_ref, send_ref, target_ref, slots_ref,
    table_ref, ninth_ref, edge_ref, tall_ref, side_ref, border_send, border_recv,
    out_ref, in_ref, send_sem, recv_sem,
):
    for load in loads:
        load.start()
    for ref in clear:
        ref[...] = jnp.zeros_like(ref)
    barrier = greet(owners)
    peers = greet_round(barrier, owners, columns)
    for load in loads:
        load.wait()
    own = splats_ref.shape[1]
    chunks = own // BLOCK
    basis = jnp.concatenate(
        basis_rows(splats_ref[6:7, :], splats_ref[7:8, :], splats_ref[8:9, :]), axis=0
    )
    colours = [
        0.5 + jnp.sum(sh_ref[16 * c : 16 * (c + 1), :] * basis, axis=0, keepdims=True)
        for c in range(3)
    ]
    table_ref[0:6, :] = splats_ref[0:6, :]
    table_ref[6:8, :] = jnp.concatenate(colours[0:2], axis=0)
    for chunk in range(chunks):
        ninth_ref[chunk : chunk + 1, :] = colours[2][:, chunk * BLOCK : (chunk + 1) * BLOCK]
    for chunk in range(chunks):
        one, two = pack_two(
            *gather_rows(table_ref, ninth_ref, chunks, send_ref[chunk : chunk + 1, :])
        )
        out_ref[2 * chunk] = one
        out_ref[2 * chunk + 1] = two
    pack_edges(target_ref, edge_ref)
    pl.semaphore_wait(barrier, owners - 1 + peers)
    post(owners, out_ref, in_ref, send_sem, recv_sem)
    copies = border_copies(
        owners, columns, target_ref, edge_ref, tall_ref, side_ref, border_send, border_recv
    )
    border_start(copies)
    chunk_rows = lax.broadcasted_iota(jnp.int32, (chunks, BLOCK), 0)
    lanes = lax.broadcasted_iota(jnp.int32, (chunks, BLOCK), 1).astype(jnp.float32)
    lane_rows = lax.broadcasted_iota(jnp.int32, (BLOCK, BLOCK), 0)
    home = jnp.zeros((2 * chunks, BLOCK), jnp.float32)
    for chunk in range(chunks):
        index = send_ref[chunk : chunk + 1, :]
        hit = chunk_rows == index // BLOCK
        source = jnp.concatenate(
            [jnp.where(hit, float(chunk), 0.0), jnp.where(hit, lanes, 0.0)], axis=0
        ).astype(jnp.bfloat16)
        select = jnp.where(lane_rows == index % BLOCK, 1.0, 0.0).astype(jnp.bfloat16)
        home = home + lax.dot_general(source, select, ACROSS, preferred_element_type=jnp.float32)
    home_ref[...] = (home[:chunks] * float(BLOCK) + home[chunks:]).astype(jnp.int32)
    count_tiles(tile_ref, last_ref)
    facing = [splats_ref[6 + d : 7 + d, :] for d in range(3)]
    slope_ref[0:16, :] = basis
    for d, rows in enumerate(slope_rows(*facing)):
        slope_ref[16 * (d + 1) : 16 * (d + 2), :] = jnp.concatenate(rows, axis=0)
    for first in range(0, slots_ref.shape[0], SEGMENTS):
        rows = slice(first, first + SEGMENTS)
        order_ref[rows, :] = spread_order(slots_ref[rows, :])
    meanwhile()
    border_wait(copies)
    for c, plane in enumerate(extend(target_ref, tall_ref, side_ref)):
        aim_ref[c] = plane
    take_in(owners, out_ref, in_ref, send_sem, recv_sem)
    for chunk in range(chunks):
        first, ninth = unpack_two(in_ref[2 * chunk], in_ref[2 * chunk + 1])
        recv_ref[0:8, chunk * BLOCK : (chunk + 1) * BLOCK] = first
        recv_ref[8:9, chunk * BLOCK : (chunk + 1) * BLOCK] = ninth


def parcels(owners):
    return [
        pltpu.VMEM((owners, PACKED, BLOCK), jnp.float32),
        pltpu.VMEM((owners, PACKED, BLOCK), jnp.float32),
        pltpu.SemaphoreType.DMA((owners,)),
        pltpu.SemaphoreType.DMA((owners,)),
    ]


def return_part(owners, pulled_ref, in_ref, out_ref, send_sem, recv_sem):
    chunks = pulled_ref.shape[1] // BLOCK
    for chunk in range(chunks):
        lanes = slice(chunk * BLOCK, (chunk + 1) * BLOCK)
        one, two = pack_two(pulled_ref[0:8, lanes], pulled_ref[8:9, lanes])
        out_ref[2 * chunk] = one
        out_ref[2 * chunk + 1] = two
    post(owners, out_ref, in_ref, send_sem, recv_sem)
    take_in(owners, out_ref, in_ref, send_sem, recv_sem)


def train_kernel(owners, columns, counts, *refs):
    parts = []
    for count in counts:
        parts.append(refs[:count])
        refs = refs[count:]
    sources, (landed_ref, slope_ref, home_ref, shown_ref), local, shared, draw_refs = parts[:5]
    pull_refs, early, border, late, deliver_refs, return_refs = parts[5:]
    tile_ref, last_ref, splats_ref, sh_ref, send_ref, target_ref, slots_ref, load_sem = local
    recv_ref, aim_ref, order_ref, rec_ref, coef_ref, saved_ref, *shared = shared
    alpha_ref, share_ref, heavy_ref, grad_ref, pulled_ref, select_ref = shared
    loads = [
        pltpu.make_async_copy(source, into, load_sem.at[at])
        for at, (source, into) in enumerate(
            zip(sources, (splats_ref, sh_ref, send_ref, target_ref, slots_ref, tile_ref))
        )
    ]
    deliver_part(
        owners, columns, loads, early[1:3] + late[1:3],
        functools.partial(prepare_part, order_ref, select_ref, draw_refs[0], draw_refs[2]), recv_ref, home_ref, aim_ref, order_ref,
        slope_ref, *local[:-1], *border, *early, *deliver_refs,
    )
    forward_part(
        tile_ref, last_ref, recv_ref, order_ref, shown_ref, rec_ref, coef_ref, saved_ref,
        alpha_ref, share_ref, *draw_refs,
    )
    contrast_part(
        owners, columns, functools.partial(weigh_part, saved_ref, share_ref, heavy_ref),
        shown_ref, aim_ref, grad_ref, *late,
    )
    backward_part(
        tile_ref, rec_ref, coef_ref, saved_ref, alpha_ref, share_ref, heavy_ref, grad_ref,
        order_ref, select_ref, pulled_ref, *pull_refs,
    )
    return_part(owners, pulled_ref, landed_ref, *return_refs)


def train(splats, sh_coeffs, send_list, target, slots, tile_ids):
    own = splats.shape[1]
    chunks = own // BLOCK
    owners = lax.axis_size("gauss")
    rows, cols = target.shape[1:]
    ways = len(WAYS)
    slots_total = slots.shape[0]
    side = TILE_SIDE * TILE_SIDE

    def f32(*shape):
        return pltpu.VMEM(shape, jnp.float32)

    def bf16(*shape):
        return pltpu.VMEM(shape, jnp.bfloat16)

    def i32(*shape):
        return pltpu.VMEM(shape, jnp.int32)

    sems = pltpu.SemaphoreType.DMA
    args = (splats, sh_coeffs, send_list.reshape(chunks, BLOCK), target, slots, tile_ids)
    outs = (
        jax.ShapeDtypeStruct((owners, PACKED, BLOCK), jnp.float32),
        jax.ShapeDtypeStruct((64, own), jnp.float32),
        jax.ShapeDtypeStruct((chunks, BLOCK), jnp.int32),
        jax.ShapeDtypeStruct(target.shape, jnp.float32),
    )
    local = [
        pltpu.SMEM(tile_ids.shape, jnp.int32),
        pltpu.SMEM((TILES_DEV,), jnp.int32),
        f32(*splats.shape),
        f32(*sh_coeffs.shape),
        i32(chunks, BLOCK),
        f32(*target.shape),
        i32(*slots.shape),
        sems((len(args),)),
    ]
    shared = [
        f32(FIELDS, own),
        f32(3, EXT_ROWS, 2 * cols),
        i32(*slots.shape),
        f32(6, slots_total, BLOCK),
        bf16(slots_total, COEF_ROWS, BLOCK),
        f32(slots_total, 5, SEGMENTS, side),
        f32(slots_total, BLOCK, side),
        f32(slots_total, BLOCK, side),
        bf16(slots_total, 2 * BLOCK, side),
        f32(TILES_DEV, 8, side),
        f32(FIELDS, own),
        bf16(slots_total // 4, BLOCK, 4 * BLOCK),
    ]
    draw_refs = [f32(slots_total * COEF_ROWS, BLOCK), f32(slots_total, 8, side), bf16(COEF_ROWS, side)]
    pull_refs = [
        bf16(TILES_DEV, COEF_ROWS - 16, side),
        f32(slots_total, 16, BLOCK),
        f32(slots_total, GRAD_ROWS, BLOCK),
        i32(slots_total, BLOCK),
        f32(2 * FIELDS * chunks, BLOCK),
        f32(2 * WIDTH, BLOCK, side),
        bf16(2 * WIDTH, 2 * BLOCK, side),
        f32(2 * WIDTH, SEGMENTS, side),
    ]
    border = [f32(8, own), f32(chunks, BLOCK)]
    early = border_scratch(rows, cols) + [sems((ways,)), sems((ways,))]
    late = (
        border_scratch(rows, cols)
        + [bf16(12 * cols, 2 * cols), bf16(12 * cols, cols)]
        + [sems((ways,)), sems((ways,))]
    )
    landing, into, *pair = parcels(owners)
    groups = [local, shared, draw_refs, pull_refs, early, border, late]
    groups += [[landing, into] + pair, [landing] + pair]
    counts = (len(args), len(outs)) + tuple(len(group) for group in groups)
    return pl.pallas_call(
        functools.partial(train_kernel, owners, lax.axis_size("tile"), counts),
        out_shape=outs,
        in_specs=[hbm()] * len(args),
        out_specs=(vmem(),) * len(outs),
        scratch_shapes=sum(groups, []),
        compiler_params=pltpu.CompilerParams(
            collective_id=1, has_side_effects=True, vmem_limit_bytes=40 * 1024 * 1024
        ),
        name="train",
    )(*[pltpu.with_memory_space_constraint(value, pltpu.HBM) for value in args])


def settle_kernel(
    in_ref, slope_ref, home_ref, sh_ref, shown_ref, rendered_ref, splat_grad_ref, sh_grad_ref,
    table_ref, ninth_ref,
):
    rendered_ref[...] = shown_ref[...]
    chunks = sh_ref.shape[1] // BLOCK
    for chunk in range(chunks):
        first, ninth = unpack_two(in_ref[2 * chunk], in_ref[2 * chunk + 1])
        table_ref[:, chunk * BLOCK : (chunk + 1) * BLOCK] = first
        ninth_ref[chunk : chunk + 1, :] = ninth
    for chunk in range(chunks):
        lanes = slice(chunk * BLOCK, (chunk + 1) * BLOCK)
        first, last = gather_rows(table_ref, ninth_ref, chunks, home_ref[chunk : chunk + 1, :])
        splat_grad_ref[0:6, lanes] = first[0:6]
        tints = (first[6:7], first[7:8], last)
        basis = slope_ref[0:16, lanes]
        mixed = jnp.zeros((16, BLOCK), jnp.float32)
        for c in range(3):
            tint = jnp.broadcast_to(tints[c], (16, BLOCK))
            sh_grad_ref[16 * c : 16 * (c + 1), lanes] = tint * basis
            mixed = mixed + tint * sh_ref[16 * c : 16 * (c + 1), lanes]
        splat_grad_ref[6:9, lanes] = jnp.concatenate(
            [
                jnp.sum(mixed * slope_ref[16 * d : 16 * (d + 1), lanes], axis=0, keepdims=True)
                for d in (1, 2, 3)
            ],
            axis=0,
        )


def settle(landed, slopes, home, splats, sh_coeffs, shown):
    own = splats.shape[1]
    return pl.pallas_call(
        settle_kernel,
        out_shape=(
            jax.ShapeDtypeStruct(shown.shape, jnp.float32),
            jax.ShapeDtypeStruct(splats.shape, jnp.float32),
            jax.ShapeDtypeStruct(sh_coeffs.shape, jnp.float32),
        ),
        in_specs=[vmem()] * 5,
        out_specs=(vmem(), vmem(), vmem()),
        scratch_shapes=[
            pltpu.VMEM((8, own), jnp.float32),
            pltpu.VMEM((own // BLOCK, BLOCK), jnp.float32),
        ],
        compiler_params=pltpu.CompilerParams(vmem_limit_bytes=VMEM_ROOM),
        name="settle",
    )(landed, slopes, home, sh_coeffs, shown)


def body(splats, sh_coeffs, send_list, block_slots, block_tiles, target):
    landed, slopes, home, shown = train(
        splats, sh_coeffs, send_list, target, block_slots[0], block_tiles
    )
    return settle(landed, slopes, home, splats, sh_coeffs, shown)


def solution(mesh):
    in_specs = (
        P(None, ("gauss", "tile")),
        P(None, ("gauss", "tile")),
        P(("gauss", "tile")),
        P("gauss", "tile", None),
        P("gauss", "tile"),
        P(None, "gauss", "tile"),
    )
    out_specs = (P(None, "gauss", "tile"), P(None, ("gauss", "tile")), P(None, ("gauss", "tile")))
    return jax.shard_map(body, mesh=mesh, in_specs=in_specs, out_specs=out_specs, check_vma=False)
```

```python
import functools
import math

import jax
import jax.numpy as jnp
from jax import lax
from jax.experimental import pallas as pl
from jax.experimental.pallas import tpu as pltpu
from jax.sharding import PartitionSpec as P

TILE_SIDE = 16
TILES_DEV = 8


BASE_ZERO = 0.28209479177387814
BASE_ONE = 0.4886025119029199
BASE_TWO = (
    1.0925484305920792,
    -1.0925484305920792,
    0.31539156525252005,
    -1.0925484305920792,
    0.5462742152960396,
)
BASE_THREE = (
    -0.5900435899266435,
    2.890611442640554,
    -0.4570457994644658,
    0.3731763325901154,
    -0.4570457994644658,
    1.445305721320277,
    -0.5900435899266435,
)
CONST_ONE = 0.0001
CONST_TWO = 0.0009


SEGMENTS = 8
STEPS = 16
BLOCK = SEGMENTS * STEPS
HALF = 128
CENTRE = 7.5
MESH = pl.DeviceIdType.MESH
VMEM_ROOM = 16 * 1024 * 1024


LOG2E = 1.4426950408889634
FIELDS = 9
COEF_ROWS = 48
GROUP = 24
WIDTH = 2
TURN = 22
PACKED = 8
GRAD_ROWS = 24
ACROSS = (((1,), (1,)), ((), ()))
DOWN = (((0,), (0,)), ((), ()))


def pick(table, index):
    return jnp.take_along_axis(table, index, axis=1, mode="promise_in_bounds")


def coarse(value):
    return value.astype(jnp.bfloat16).astype(jnp.float32)


def halves(value):
    high = value.astype(jnp.bfloat16)
    low = (value - high.astype(jnp.float32)).astype(jnp.bfloat16)
    return high, low


def swap_blocks(value):
    rows = lax.broadcasted_iota(jnp.int32, value.shape, 0)
    blocks = lax.broadcasted_iota(jnp.int32, value.shape, 1) // TILE_SIDE
    for bit in (1, 2, 4):
        up = pltpu.roll(pltpu.roll(value, SEGMENTS - bit, 0), TILE_SIDE * bit, 1)
        down = pltpu.roll(pltpu.roll(value, bit, 0), HALF - TILE_SIDE * bit, 1)
        low, left = (rows & bit) == 0, (blocks & bit) == 0
        value = jnp.where(low == left, value, jnp.where(low, up, down))
    return value


def halve(target_ref, at, step, lanes, pair):
    high, low = halves(jnp.concatenate(pair, axis=0))
    rows = 2 * SEGMENTS * step
    target_ref[at, rows : rows + 2 * SEGMENTS, lanes] = high
    target_ref[at, BLOCK + rows : BLOCK + rows + 2 * SEGMENTS, lanes] = low


def pixel_basis():
    rows = lax.broadcasted_iota(jnp.int32, (8, 2 * HALF), 0)
    pixels = lax.broadcasted_iota(jnp.int32, (8, 2 * HALF), 1)
    along = (pixels % TILE_SIDE).astype(jnp.float32) - CENTRE
    down = (pixels // TILE_SIDE).astype(jnp.float32) - CENTRE
    basis = jnp.zeros((8, 2 * HALF), jnp.float32)
    terms = (along * along, along * down, down * down, along, down, jnp.ones_like(along))
    for at, term in enumerate(terms):
        basis = jnp.where(rows == at, term, basis)
    return basis


def spread_order(slots):
    lanes = lax.broadcasted_iota(jnp.int32, slots.shape, 1)
    return pick(slots, (lanes % SEGMENTS) * STEPS + lanes // SEGMENTS)


def tiles_of(tile_ref, first):
    at = lax.broadcasted_iota(jnp.int32, (SEGMENTS, BLOCK), 0)
    tiles = jnp.zeros((SEGMENTS, BLOCK), jnp.int32)
    for k in range(SEGMENTS):
        tiles = jnp.where(at == k, tile_ref[0, first + k], tiles)
    return tiles


def forward_part(
    tile_ref, last_ref, recv_ref, slots_ref, picture_ref, rec_ref, coef_ref, saved_ref,
    alpha_ref, share_ref, work_ref, image_ref, basis_ref,
):
    slots_total = slots_ref.shape[0]
    chunks = recv_ref.shape[1] // BLOCK
    origin_x = (lax.axis_index("tile") * (TILE_SIDE * TILES_DEV)).astype(jnp.float32) + CENTRE
    origin_y = (lax.axis_index("gauss") * TILE_SIDE).astype(jnp.float32) + CENTRE

    def collect(group, carry):
        first = group * SEGMENTS
        slots = slots_ref[pl.ds(pl.multiple_of(first, SEGMENTS), SEGMENTS), :]
        fine = slots % BLOCK
        chunk_at = slots // BLOCK
        found = [None] * FIELDS
        for chunk in range(chunks):
            hit = chunk_at == chunk
            for f in range(FIELDS):
                row = recv_ref[f : f + 1, chunk * BLOCK : (chunk + 1) * BLOCK]
                got = pick(jnp.broadcast_to(row, (SEGMENTS, BLOCK)), fine)
                found[f] = got if chunk == 0 else jnp.where(hit, got, found[f])
        tiles = tiles_of(tile_ref, first)
        base_x = (TILE_SIDE * jnp.minimum(tiles, TILES_DEV - 1)).astype(jnp.float32) + origin_x
        at_x = found[0] - base_x
        at_y = found[1] - origin_y
        con_a = -0.5 * found[2]
        con_b = -found[3]
        con_c = -0.5 * found[4]
        shut = 1.0 + jnp.exp(-found[5])
        for k, value in enumerate((at_x, at_y, con_a, con_b, con_c, 1.0 - 1.0 / shut)):
            rec_ref[k, pl.ds(pl.multiple_of(first, SEGMENTS), SEGMENTS), :] = value
        part_x = con_a * at_x
        part_y = con_c * at_y
        cross = con_b * at_y
        level = at_x * (part_x + cross) + at_y * part_y
        terms = (
            LOG2E * con_a,
            LOG2E * con_b,
            LOG2E * con_c,
            -LOG2E * (2.0 * part_x + cross),
            -LOG2E * (2.0 * part_y + con_b * at_x),
            LOG2E * (level - jnp.log(shut)),
        )

        def put(row, value):
            work_ref[pl.ds(first * COEF_ROWS + row, SEGMENTS, stride=COEF_ROWS), :] = value

        for k, term in enumerate(terms):
            high = coarse(term)
            rest = term - high
            middle = coarse(rest)
            put(k, high)
            put(8 + k, middle)
            put(16 + k, rest - middle)
        for c in range(3):
            high = coarse(found[6 + c])
            put(24 + c, high)
            put(32 + c, found[6 + c] - high)
            put(40 + c, high)
        return carry

    lax.fori_loop(0, slots_total // SEGMENTS, collect, 0, unroll=2)
    seg_at = lax.broadcasted_iota(jnp.int32, (SEGMENTS, HALF), 0)
    own_seg = seg_at == lax.broadcasted_iota(jnp.int32, (SEGMENTS, HALF), 1) % SEGMENTS

    def draw_local(slot):
        coefs = work_ref[pl.ds(pl.multiple_of(slot * COEF_ROWS, COEF_ROWS), COEF_ROWS), :].astype(
            jnp.bfloat16
        )
        coef_ref[slot] = coefs
        power = lax.dot_general(coefs, basis_ref[...], DOWN, preferred_element_type=jnp.float32)
        through = [jnp.ones((SEGMENTS, HALF), jnp.float32) for side in range(2)]
        weights = [[], []]
        for step in range(STEPS):
            for side in range(2):
                rows = slice(step * SEGMENTS, (step + 1) * SEGMENTS)
                lanes = slice(side * HALF, (side + 1) * HALF)
                alpha = jnp.exp2(power[rows, lanes])
                weight = alpha * through[side]
                alpha_ref[slot, rows, lanes] = alpha
                share_ref[slot, rows, lanes] = weight
                through[side] = through[side] - weight
                weights[side].append(weight)
        weight = jnp.concatenate([jnp.concatenate(w, axis=0) for w in weights], axis=1)
        tints = []
        for part in (24, 32):
            for c in range(3):
                row = work_ref[pl.ds(slot * COEF_ROWS + part + c, 1), :]
                tints.append(jnp.where(own_seg, jnp.broadcast_to(row, (SEGMENTS, HALF)), 0.0))
        tint = jnp.concatenate(tints, axis=0).astype(jnp.bfloat16)
        sums = jnp.dot(
            jnp.concatenate([tint, tint], axis=1),
            jnp.concatenate(halves(weight), axis=0),
            preferred_element_type=jnp.float32,
        )
        return through, sums[0:24] + sums[24:48]

    def draw_join(slot, carry, through, sums):
        tile = tile_ref[0, slot]
        fresh = (slot == 0) | (tile != tile_ref[0, jnp.maximum(slot - 1, 0)])
        after = []
        for side in range(2):
            start = jnp.where(fresh, 1.0, carry[side][0])
            running = through[side]
            for shift in (1, 2, 4):
                running = jnp.where(
                    seg_at >= shift, running * pltpu.roll(running, shift, 0), running
                )
            before = jnp.where(seg_at == 0, 1.0, pltpu.roll(running, 1, 0)) * start
            kept = [start * running[SEGMENTS - 1 : SEGMENTS]]
            lanes = slice(side * HALF, (side + 1) * HALF)
            saved_ref[slot, 0, :, lanes] = before
            saved_ref[slot, 1, :, lanes] = through[side]
            for c in range(3):
                part = sums[c * SEGMENTS : (c + 1) * SEGMENTS, lanes]
                saved_ref[slot, 2 + c, :, lanes] = part
                shade_sum = jnp.sum(before * part, axis=0, keepdims=True)
                shade_sum = jnp.where(fresh, 0.0, carry[side][1 + c]) + shade_sum
                image_ref[slot, c : c + 1, lanes] = shade_sum
                kept.append(shade_sum)
            after.append(tuple(kept))
        return tuple(after)

    def draw(pair, carry):
        locals_two = [draw_local(GROUP * pair + k) for k in range(GROUP)]
        for k in range(GROUP):
            carry = draw_join(GROUP * pair + k, carry, *locals_two[k])
        return carry

    start = (jnp.ones((1, HALF), jnp.float32),) + (jnp.zeros((1, HALF), jnp.float32),) * 3
    lax.fori_loop(0, slots_total // GROUP, draw, (start, start))
    for side in range(2):
        lanes = slice(side * HALF, (side + 1) * HALF)
        for c in range(3):
            rows = [image_ref[last_ref[tile], c : c + 1, lanes] for tile in range(TILES_DEV)]
            picture_ref[c, side * SEGMENTS : (side + 1) * SEGMENTS, :] = swap_blocks(
                jnp.concatenate(rows, axis=0)
            )


def backward_part(
    tile_ref, rec_ref, coef_ref, saved_ref, alpha_ref, share_ref, heavy_ref, grad_ref,
    slots_ref, select_ref, out_ref,
    rhs_ref, mom_ref, back_ref, where_ref, acc_ref, lit_ref, force_ref, behind_ref,
):
    chunks = out_ref.shape[1] // BLOCK
    slots_total = coef_ref.shape[0]
    acc_ref[...] = jnp.zeros_like(acc_ref)
    basis = pixel_basis()
    blank = jnp.zeros_like(basis)
    basis16 = jnp.concatenate([basis, blank], axis=0).astype(jnp.bfloat16)
    for tile in range(TILES_DEV):
        grads = grad_ref[tile]
        high = coarse(grads)
        rhs_ref[tile] = jnp.concatenate([blank, high, high, grads - high], axis=0).astype(
            jnp.bfloat16
        )
    seg_at = lax.broadcasted_iota(jnp.int32, (SEGMENTS, HALF), 0)

    def prepare(slot, carry, buf):
        tile = tile_ref[0, slot]
        later = tile_ref[0, jnp.minimum(slot + 1, slots_total - 1)]
        final = (slot == slots_total - 1) | (tile != later)
        shown = jnp.minimum(tile, TILES_DEV - 1)
        grads = grad_ref[shown]
        after = []
        for side in range(2):
            lanes = slice(side * HALF, (side + 1) * HALF)
            start = jnp.where(final, 0.0, carry[side])
            total = grads[0:1, lanes] * saved_ref[slot, 2, :, lanes]
            for c in (1, 2):
                total = total + grads[c : c + 1, lanes] * saved_ref[slot, 2 + c, :, lanes]
            factor = saved_ref[slot, 1, :, lanes]
            for shift in (1, 2, 4):
                inside = seg_at < SEGMENTS - shift
                total = jnp.where(
                    inside, total + factor * pltpu.roll(total, SEGMENTS - shift, 0), total
                )
                factor = jnp.where(
                    inside, factor * pltpu.roll(factor, SEGMENTS - shift, 0), factor
                )
            entering = total + factor * start
            after.append(entering[0:1])
            behind_ref[buf, :, lanes] = jnp.where(
                seg_at < SEGMENTS - 1, pltpu.roll(entering, SEGMENTS - 1, 0), start
            )
        lit_ref[buf] = lax.dot_general(
            coef_ref[slot, 16:COEF_ROWS, :], rhs_ref[shown], DOWN, preferred_element_type=jnp.float32
        )
        return tuple(after)

    def trace(slots, bufs):
        chains = [(k, side) for k in range(len(slots)) for side in range(2)]
        lanes = [slice(side * HALF, (side + 1) * HALF) for side in range(2)]
        later = {(k, side): behind_ref[bufs[k], :, lanes[side]] for k, side in chains}
        for step in reversed(range(STEPS // 2)):
            for k, side in chains:
                pair = []
                for at in (2 * step + 1, 2 * step):
                    rows = slice(at * SEGMENTS, (at + 1) * SEGMENTS)
                    gap = lit_ref[bufs[k], rows, lanes[side]] - later[k, side]
                    alpha = alpha_ref[slots[k], rows, lanes[side]]
                    later[k, side] = later[k, side] + alpha * gap
                    pair.append(share_ref[slots[k], rows, lanes[side]] * gap)
                halve(force_ref, bufs[k], step, lanes[side], pair[::-1])

    def reduce(slot, buf):
        shown = jnp.minimum(tile_ref[0, slot], TILES_DEV - 1)
        found = lax.dot_general(
            basis16, force_ref[buf], ACROSS, preferred_element_type=jnp.float32
        )
        painted = lax.dot_general(
            jnp.concatenate(halves(grad_ref[shown]), axis=0),
            heavy_ref[slot],
            ACROSS,
            preferred_element_type=jnp.float32,
        )
        painted = painted[0:8] + painted[8:16]
        mom_ref[slot, 0:8, :] = found[0:8, :BLOCK] + found[0:8, BLOCK:]
        mom_ref[slot, 8:16, :] = painted[:, :BLOCK] + painted[:, BLOCK:]

    runs = slots_total // WIDTH

    def slot_of(run, k):
        return (runs - 1 - run) * WIDTH + k

    def ready(run, carry, half):
        for k in reversed(range(WIDTH)):
            carry = prepare(slot_of(run, k), carry, half * WIDTH + k)
        return carry

    def gather_in(run, half):
        for k in range(WIDTH):
            reduce(slot_of(run, k), half * WIDTH + k)

    def follow(run, half):
        trace(
            [slot_of(run, k) for k in range(WIDTH)], [half * WIDTH + k for k in range(WIDTH)]
        )

    def pull(turn, carry):
        for part in range(TURN):
            run = TURN * turn + part + 1
            half = (part + 1) % 2
            gather_in(run - 1, 1 - half)
            carry = ready(run + 1, carry, 1 - half)
            follow(run, half)
        return carry

    zeros = jnp.zeros((1, HALF), jnp.float32)
    carry = ready(0, (zeros, zeros), 0)
    carry = ready(1, carry, 1)
    follow(0, 0)
    carry = lax.fori_loop(0, (runs - 2) // TURN, pull, carry)
    for run in range((runs - 2) // TURN * TURN + 1, runs):
        half = run % 2
        gather_in(run - 1, 1 - half)
        if run + 1 < runs:
            carry = ready(run + 1, carry, 1 - half)
        follow(run, half)
    gather_in(runs - 1, (runs - 1) % 2)
    chunk_rows = lax.broadcasted_iota(jnp.int32, (chunks, BLOCK), 0)

    def settle(group, carry):
        first = pl.multiple_of(group * SEGMENTS, SEGMENTS)
        tiles = tiles_of(tile_ref, first)
        used = tiles < TILES_DEV
        rows = pl.ds(first, SEGMENTS)

        m_xx, m_xy, m_yy, m_x, m_y, m_0 = [
            mom_ref[rows, k, :] for k in range(6)
        ]
        at_x, at_y, con_a, con_b, con_c, shut_s = [rec_ref[k, rows, :] for k in range(6)]
        h_x = m_x - at_x * m_0
        h_y = m_y - at_y * m_0
        h_xx = m_xx - 2.0 * at_x * m_x + at_x * at_x * m_0
        h_xy = m_xy - at_x * m_y - at_y * m_x + at_x * at_y * m_0
        h_yy = m_yy - 2.0 * at_y * m_y + at_y * at_y * m_0
        results = [
            -2.0 * con_a * h_x - con_b * h_y,
            -2.0 * con_c * h_y - con_b * h_x,
            -0.5 * h_xx,
            -h_xy,
            -0.5 * h_yy,
            shut_s * m_0,
        ] + [mom_ref[rows, 8 + c, :] for c in range(3)]
        for f, value in enumerate(results):
            kept = jnp.where(used, value, 0.0)
            high = coarse(kept)
            back_ref[rows, f, :] = high
            back_ref[rows, 12 + f, :] = kept - high
        slots = slots_ref[rows, :]
        where_ref[rows, :] = slots // BLOCK
        for quad in range(0, SEGMENTS, 4):
            stacked = []
            for k in range(quad, quad + 4):
                hit = chunk_rows == where_ref[pl.ds(first + k, 1), :]
                stacked.append(
                    jnp.concatenate(
                        [
                            jnp.where(hit, back_ref[first + k, part + f : part + f + 1, :], 0.0)
                            for part in (0, 12)
                            for f in range(FIELDS)
                        ],
                        axis=0,
                    ).astype(jnp.bfloat16)
                )
            acc_ref[...] += lax.dot_general(
                jnp.concatenate(stacked, axis=1),
                select_ref[2 * group + quad // 4],
                ACROSS,
                preferred_element_type=jnp.float32,
            )
        return carry

    lax.fori_loop(0, slots_total // SEGMENTS, settle, 0, unroll=2)
    total = FIELDS * chunks
    for chunk in range(chunks):
        lanes = slice(chunk * BLOCK, (chunk + 1) * BLOCK)
        out_ref[0:8, lanes] = (
            acc_ref[pl.ds(chunk, 8, stride=chunks), :]
            + acc_ref[pl.ds(total + chunk, 8, stride=chunks), :]
        )
        at = 8 * chunks + chunk
        out_ref[8:9, lanes] = acc_ref[at : at + 1, :] + acc_ref[total + at : total + at + 1, :]


def hbm():
    return pl.BlockSpec(memory_space=pltpu.HBM)


def smem():
    return pl.BlockSpec(memory_space=pltpu.SMEM)


def vmem():
    return pl.BlockSpec(memory_space=pltpu.VMEM)


WAYS = [(down, right) for down in (-1, 0, 1) for right in (-1, 0, 1) if (down, right) != (0, 0)]
NORM = sum(math.exp(-m * m / 4.5) for m in range(-5, 6))
EXT_ROWS = 40
MID_ROWS = 32


def neighbour(bands, columns, way):
    there_band = lax.axis_index("gauss") + way[0]
    there_col = lax.axis_index("tile") + way[1]
    exists = (there_band >= 0) & (there_band < bands) & (there_col >= 0) & (there_col < columns)
    return exists, (there_band, there_col)


def greet_round(barrier, bands, columns):
    peers = jnp.int32(0)
    for way in WAYS:
        if way[1] == 0:
            continue
        exists, there = neighbour(bands, columns, way)
        peers = peers + exists.astype(jnp.int32)

        @pl.when(exists)
        def _(there=there):
            pl.semaphore_signal(barrier, inc=1, device_id=there, device_id_type=MESH)

    return peers


def border_copies(bands, columns, plane_ref, edge_ref, tall_ref, side_ref, send_sem, recv_sem):
    found = []
    for at, way in enumerate(WAYS):
        exists, there = neighbour(bands, columns, way)
        landing = len(WAYS) - 1 - at
        source = plane_ref if way[1] == 0 else edge_ref
        target = tall_ref.at[landing] if way[1] == 0 else side_ref.at[landing]
        found.append(
            (
                exists,
                pltpu.make_async_remote_copy(
                    src_ref=source,
                    dst_ref=target,
                    send_sem=send_sem.at[at],
                    recv_sem=recv_sem.at[landing],
                    device_id=there,
                    device_id_type=MESH,
                ),
                pltpu.make_async_remote_copy(
                    src_ref=source,
                    dst_ref=tall_ref.at[at] if way[1] == 0 else side_ref.at[at],
                    send_sem=send_sem.at[at],
                    recv_sem=recv_sem.at[at],
                    device_id=there,
                    device_id_type=MESH,
                ),
            )
        )
    return found


def border_start(copies):
    for exists, out, back in copies:

        @pl.when(exists)
        def _(out=out):
            out.start()


def border_wait(copies):
    for exists, out, back in copies:

        @pl.when(exists)
        def _(out=out, back=back):
            out.wait_send()
            back.wait_recv()


def pack_edges(plane_ref, edge_ref):
    lanes = lax.broadcasted_iota(jnp.int32, edge_ref.shape, 1)
    packed = jnp.zeros(edge_ref.shape, jnp.float32)
    for c in range(3):
        plane = plane_ref[c]
        near = pltpu.roll(plane, 32 * c, 1) if c else plane
        far = pltpu.roll(plane, 32 * c + 32, 1)
        packed = jnp.where(
            lanes // 32 == c, jnp.where(lanes % 32 < 16, near, far), packed
        )
    edge_ref[...] = packed


def stretch(above, own, below):
    turn = lax.broadcasted_iota(jnp.int32, (8, own.shape[1]), 0) >= 6
    mixed = jnp.where(turn, above[0:8], below[8:16])
    return jnp.concatenate([own, above[8:16], below[0:8], mixed], axis=0)


def extend(plane_ref, tall_ref, side_ref):
    east = lax.broadcasted_iota(jnp.int32, side_ref.shape[1:], 1) % 32 < 16
    borders = [
        jnp.where(east, side_ref[WAYS.index((down, 1))], side_ref[WAYS.index((down, -1))])
        for down in (-1, 0, 1)
    ]
    border = stretch(*borders)
    planes = []
    for c in range(3):
        main = stretch(
            tall_ref[WAYS.index((-1, 0)), c], plane_ref[c], tall_ref[WAYS.index((1, 0)), c]
        )
        turned = pltpu.roll(border, HALF - 32 * c, 1) if c else border
        planes.append(jnp.concatenate([main, turned], axis=1))
    return planes


def window_weight(gap):
    gap = gap.astype(jnp.float32)
    return jnp.where(jnp.abs(gap) < 5.5, jnp.exp(gap * gap / -4.5) * (1.0 / NORM), 0.0)


def split_rows(value):
    first = coarse(value)
    rest = value - first
    second = coarse(rest)
    return first, second, rest - second


def six_data(value, axis):
    first, second, third = split_rows(value)
    return jnp.concatenate([first, second, third, first, second, first], axis=axis).astype(
        jnp.bfloat16
    )


def six_weights(value, axis):
    first, second, third = split_rows(value)
    return jnp.concatenate([first, first, first, second, second, third], axis=axis).astype(
        jnp.bfloat16
    )


def ext_row(at):
    return jnp.where(at < 16, at, jnp.where(at < 24, at - 24, jnp.where(at < 38, at - 8, at - 48)))


def ext_col(at):
    return jnp.where(at < 144, at, jnp.where(at < 160, at - 160, 10000))


def mid_col(at):
    return jnp.where(at < 192, at, at - 256)


def iota(shape, axis):
    return lax.broadcasted_iota(jnp.int32, shape, axis)


def fdot(left, right):
    return jnp.dot(left, right, preferred_element_type=jnp.float32)


def band_part(rows, cols, wide_ref, back_ref):
    wide = 2 * cols
    for half in range(2):
        lanes = slice(half * cols, (half + 1) * cols)
        shape = (wide, cols)
        across = window_weight(mid_col(iota(shape, 1) + half * cols) - ext_col(iota(shape, 0)))
        wide_ref[:, lanes] = six_weights(across, 0)
    back = window_weight(mid_col(iota((wide, cols), 0)) - iota((wide, cols), 1))
    back_ref[...] = six_weights(back, 0)


def down_band():
    shape = (MID_ROWS, EXT_ROWS)
    return six_weights(window_weight(iota(shape, 0) - 5 - ext_row(iota(shape, 1))), 1)


def blur_planes(planes, wide_ref):
    down = down_band()
    strips = [fdot(down, six_data(plane, 0)) for plane in planes]
    return fdot(six_data(jnp.concatenate(strips, axis=0), 1), wide_ref[...])


def weigh_part(saved_ref, share_ref, heavy_ref):
    def weigh(group, carry):
        for step in range(STEPS // 2):
            for k in range(4):
                slot = 4 * group + k
                for side in range(2):
                    lanes = slice(side * HALF, (side + 1) * HALF)
                    before = saved_ref[slot, 0, :, lanes]
                    pair = []
                    for at in (2 * step, 2 * step + 1):
                        rows = slice(at * SEGMENTS, (at + 1) * SEGMENTS)
                        weight = share_ref[slot, rows, lanes] * before
                        share_ref[slot, rows, lanes] = weight
                        pair.append(weight)
                    halve(heavy_ref, slot, step, lanes, pair)
        return carry

    lax.fori_loop(0, share_ref.shape[0] // 4, weigh, 0)


def contrast_part(
    bands, columns, meanwhile, shown_ref, aim_ref, still_ref, out_ref,
    edge_ref, tall_ref, side_ref, wide_ref, back_ref, send_sem, recv_sem,
):
    band = lax.axis_index("gauss")
    column = lax.axis_index("tile")
    rows, cols = shown_ref.shape[1:]
    pack_edges(shown_ref, edge_ref)
    copies = border_copies(
        bands, columns, shown_ref, edge_ref, tall_ref, side_ref, send_sem, recv_sem
    )
    border_start(copies)
    meanwhile()
    border_wait(copies)
    pics = extend(shown_ref, tall_ref, side_ref)
    aims = [aim_ref[c] for c in range(3)]
    moments = blur_planes(
        pics
        + [pic * pic for pic in pics]
        + [pic * aim for pic, aim in zip(pics, aims)],
        wide_ref,
    )
    up = (rows, MID_ROWS)
    up = six_weights(window_weight(iota(up, 0) - iota(up, 1) + 5), 1)
    wide = 2 * cols
    shape = (MID_ROWS, wide)
    row_at = band * rows + iota(shape, 0) - 5
    col_at = column * cols + mid_col(iota(shape, 1))
    inside = (row_at >= 0) & (row_at < bands * rows) & (col_at >= 0) & (col_at < columns * cols)
    strips = [None] * 9
    for c in range(3):
        mu_x, squares, cross = [
            moments[(3 * kind + c) * MID_ROWS : (3 * kind + c + 1) * MID_ROWS] for kind in range(3)
        ]
        mu_y, more = [
            still_ref[(3 * kind + c) * MID_ROWS : (3 * kind + c + 1) * MID_ROWS] for kind in range(2)
        ]
        squares = squares + more
        mean_xy = mu_x * mu_y
        mean_sq = mu_x * mu_x + mu_y * mu_y
        top_1 = 2.0 * mean_xy + CONST_ONE
        top_2 = 2.0 * (cross - mean_xy) + CONST_TWO
        low_1 = mean_sq + CONST_ONE
        low_2 = squares - mean_sq + CONST_TWO
        inverse = -0.2 / (low_1 * low_2)
        value = top_1 * top_2 * inverse
        value_1 = value * low_2 * inverse * -5.0
        value_2 = value * low_1 * inverse * -5.0
        slope_mean = 2.0 * mu_y * (top_2 - top_1) * inverse - 2.0 * mu_x * (value_1 - value_2)
        for kind, slope in enumerate((slope_mean, -value_2, 2.0 * top_1 * inverse)):
            strips[3 * kind + c] = fdot(up, six_data(jnp.where(inside, slope, 0.0), 0))
    spread = fdot(six_data(jnp.concatenate(strips, axis=0), 1), back_ref[...])
    out_ref[...] = jnp.zeros_like(out_ref)
    for c in range(3):
        pic = shown_ref[c]
        aim = aim_ref[c, 0:rows, 0:cols]
        parts = [spread[(3 * kind + c) * rows : (3 * kind + c + 1) * rows] for kind in range(3)]
        total = parts[0] + 2.0 * pic * parts[1] + aim * parts[2] + 1.6 * (pic - aim)
        for side in range(2):
            moved = swap_blocks(total[side * SEGMENTS : (side + 1) * SEGMENTS])
            for tile in range(TILES_DEV):
                out_ref[tile, c : c + 1, side * HALF : (side + 1) * HALF] = moved[tile : tile + 1]


def border_scratch(rows, cols):
    ways = len(WAYS)
    return [
        pltpu.VMEM((rows, cols), jnp.float32),
        pltpu.VMEM((ways, 3, rows, cols), jnp.float32),
        pltpu.VMEM((ways, rows, cols), jnp.float32),
    ]


def basis_rows(x, y, z):
    xx, yy, zz = x * x, y * y, z * z
    return [
        jnp.full_like(x, BASE_ZERO),
        -BASE_ONE * y,
        BASE_ONE * z,
        -BASE_ONE * x,
        BASE_TWO[0] * x * y,
        BASE_TWO[1] * y * z,
        BASE_TWO[2] * (2.0 * zz - xx - yy),
        BASE_TWO[3] * x * z,
        BASE_TWO[4] * (xx - yy),
        BASE_THREE[0] * y * (3.0 * xx - yy),
        BASE_THREE[1] * x * y * z,
        BASE_THREE[2] * y * (4.0 * zz - xx - yy),
        BASE_THREE[3] * z * (2.0 * zz - 3.0 * xx - 3.0 * yy),
        BASE_THREE[4] * x * (4.0 * zz - xx - yy),
        BASE_THREE[5] * z * (xx - yy),
        BASE_THREE[6] * x * (xx - 3.0 * yy),
    ]


def slope_rows(x, y, z):
    xx, yy, zz = x * x, y * y, z * z
    xy, yz, xz = x * y, y * z, x * z
    none = jnp.zeros_like(x)
    one = jnp.ones_like(x)
    two, three = BASE_TWO, BASE_THREE
    along_x = [
        none, none, none, -BASE_ONE * one,
        two[0] * y, none, -2.0 * two[2] * x, two[3] * z, 2.0 * two[4] * x,
        6.0 * three[0] * xy, three[1] * yz, -2.0 * three[2] * xy, -6.0 * three[3] * xz,
        three[4] * (4.0 * zz - 3.0 * xx - yy), 2.0 * three[5] * xz, three[6] * (3.0 * xx - 3.0 * yy),
    ]
    along_y = [
        none, -BASE_ONE * one, none, none,
        two[0] * x, two[1] * z, -2.0 * two[2] * y, none, -2.0 * two[4] * y,
        three[0] * (3.0 * xx - 3.0 * yy), three[1] * xz, three[2] * (4.0 * zz - xx - 3.0 * yy),
        -6.0 * three[3] * yz, -2.0 * three[4] * xy, -2.0 * three[5] * yz, -6.0 * three[6] * xy,
    ]
    along_z = [
        none, none, BASE_ONE * one, none,
        none, two[1] * y, 4.0 * two[2] * z, two[3] * x, none,
        none, three[1] * xy, 8.0 * three[2] * yz, three[3] * (6.0 * zz - 3.0 * xx - 3.0 * yy),
        8.0 * three[4] * xz, three[5] * (xx - yy), none,
    ]
    return along_x, along_y, along_z


def lane_of():
    return lax.broadcasted_iota(jnp.int32, (8, BLOCK), 1)


def row_of():
    return lax.broadcasted_iota(jnp.int32, (8, BLOCK), 0)


def gather_rows(table_ref, ninth_ref, chunks, index):
    index = jnp.broadcast_to(index, (8, BLOCK))
    fine = index % BLOCK
    chunk_at = index // BLOCK
    first = None
    ninth = jnp.zeros((8, BLOCK), jnp.float32)
    for chunk in range(chunks):
        got = pick(table_ref[0:8, chunk * BLOCK : (chunk + 1) * BLOCK], fine)
        first = got if chunk == 0 else jnp.where(chunk_at == chunk, got, first)
    for base in range(0, chunks, 8):
        got = pick(ninth_ref[base : base + 8, :], fine)
        ninth = ninth + jnp.where(chunk_at == row_of() + base, got, 0.0)
    return first, jnp.sum(ninth, axis=0, keepdims=True)


def pack_two(first, last):
    left = lane_of() < BLOCK // 2
    swapped = pltpu.roll(first, BLOCK // 2, 1)
    one = jnp.where(left, first, pltpu.roll(swapped, 4, 0))
    two = jnp.where(left, swapped, pltpu.roll(first, 4, 0))
    tail = row_of() >= 4
    ninth = jnp.broadcast_to(last, (8, BLOCK))
    return jnp.where(tail, ninth, one), jnp.where(tail, pltpu.roll(ninth, BLOCK // 2, 1), two)


def unpack_two(one, two):
    left = lane_of() < BLOCK // 2
    upper = jnp.where(left, one, pltpu.roll(two, BLOCK // 2, 1))
    lower = jnp.where(left, pltpu.roll(one, BLOCK // 2, 1), two)
    return jnp.where(row_of() < 4, upper, pltpu.roll(lower, 4, 0)), upper[4:5]


def ring(gap, owners):
    there = lax.axis_index("gauss") + gap
    return jnp.where(there >= owners, there - owners, there)


def far_first(owners):
    return sorted(range(1, owners), key=lambda gap: (-abs(2 * gap - owners), gap))


def greet(owners):
    barrier = pltpu.get_barrier_semaphore()
    column = lax.axis_index("tile")
    for gap in far_first(owners):
        pl.semaphore_signal(
            barrier, inc=1, device_id=(ring(gap, owners), column), device_id_type=MESH
        )
    return barrier


def parcel(owners, gap, out_ref, in_ref, send_sem, recv_sem):
    band = lax.axis_index("gauss")
    there = ring(gap, owners)
    return pltpu.make_async_remote_copy(
        src_ref=out_ref.at[there, 0:5],
        dst_ref=in_ref.at[band, 0:5],
        send_sem=send_sem.at[gap],
        recv_sem=recv_sem.at[gap],
        device_id=(there, lax.axis_index("tile")),
        device_id_type=MESH,
    )


def post(owners, out_ref, in_ref, send_sem, recv_sem):
    band = lax.axis_index("gauss")
    for gap in far_first(owners):
        parcel(owners, gap, out_ref, in_ref, send_sem, recv_sem).start()
    in_ref[band] = out_ref[band]


def take_in(owners, out_ref, in_ref, send_sem, recv_sem):
    for gap in range(1, owners):
        parcel(owners, gap, out_ref, in_ref, send_sem, recv_sem).wait()


def count_tiles(tile_ref, last_ref):
    for tile in range(TILES_DEV):
        last = jnp.int32(-1)
        for slot in range(tile_ref.shape[1]):
            last = last + (tile_ref[0, slot] <= tile).astype(jnp.int32)
        last_ref[tile] = last


def prepare_part(work_ref, basis_ref):
    work_ref[...] = jnp.zeros_like(work_ref)
    basis = pixel_basis()
    basis_ref[...] = jnp.concatenate([basis] * 3 + [jnp.zeros_like(basis)] * 3, axis=0).astype(
        jnp.bfloat16
    )


def choose_part(order_ref, select_ref):
    lane_rows = lax.broadcasted_iota(jnp.int32, (BLOCK, 4 * BLOCK), 0)
    for first in range(0, order_ref.shape[0], 4):
        fine = [order_ref[first + k : first + k + 1, :] % BLOCK for k in range(4)]
        select_ref[first // 4] = jnp.where(
            lane_rows == jnp.concatenate(fine, axis=1), 1.0, 0.0
        ).astype(jnp.bfloat16)


def deliver_part(
    owners, columns, loads, clear, meanwhile, still_ref, wide_ref, back_ref, recv_ref, home_ref, aim_ref, order_ref, slope_ref,
    tile_ref, last_ref, splats_ref, sh_ref, send_ref, target_ref, slots_ref,
    table_ref, ninth_ref, edge_ref, tall_ref, side_ref, border_send, border_recv,
    out_ref, in_ref, send_sem, recv_sem,
):
    for load in loads:
        load.start()
    for ref in clear:
        ref[...] = jnp.zeros_like(ref)
    barrier = greet(owners)
    peers = greet_round(barrier, owners, columns)
    for load in loads:
        load.wait()
    own = splats_ref.shape[1]
    chunks = own // BLOCK
    basis = jnp.concatenate(
        basis_rows(splats_ref[6:7, :], splats_ref[7:8, :], splats_ref[8:9, :]), axis=0
    )
    colours = [
        0.5 + jnp.sum(sh_ref[16 * c : 16 * (c + 1), :] * basis, axis=0, keepdims=True)
        for c in range(3)
    ]
    table_ref[0:6, :] = splats_ref[0:6, :]
    table_ref[6:8, :] = jnp.concatenate(colours[0:2], axis=0)
    for chunk in range(chunks):
        ninth_ref[chunk : chunk + 1, :] = colours[2][:, chunk * BLOCK : (chunk + 1) * BLOCK]
    for chunk in range(chunks):
        one, two = pack_two(
            *gather_rows(table_ref, ninth_ref, chunks, send_ref[chunk : chunk + 1, :])
        )
        out_ref[2 * chunk] = one
        out_ref[2 * chunk + 1] = two
    pack_edges(target_ref, edge_ref)
    pl.semaphore_wait(barrier, owners - 1 + peers)
    post(owners, out_ref, in_ref, send_sem, recv_sem)
    copies = border_copies(
        owners, columns, target_ref, edge_ref, tall_ref, side_ref, border_send, border_recv
    )
    border_start(copies)
    chunk_rows = lax.broadcasted_iota(jnp.int32, (chunks, BLOCK), 0)
    lanes = lax.broadcasted_iota(jnp.int32, (chunks, BLOCK), 1).astype(jnp.float32)
    lane_rows = lax.broadcasted_iota(jnp.int32, (BLOCK, BLOCK), 0)
    home = jnp.zeros((2 * chunks, BLOCK), jnp.float32)
    for chunk in range(chunks):
        index = send_ref[chunk : chunk + 1, :]
        hit = chunk_rows == index // BLOCK
        source = jnp.concatenate(
            [jnp.where(hit, float(chunk), 0.0), jnp.where(hit, lanes, 0.0)], axis=0
        ).astype(jnp.bfloat16)
        select = jnp.where(lane_rows == index % BLOCK, 1.0, 0.0).astype(jnp.bfloat16)
        home = home + lax.dot_general(source, select, ACROSS, preferred_element_type=jnp.float32)
    home_ref[...] = (home[:chunks] * float(BLOCK) + home[chunks:]).astype(jnp.int32)
    count_tiles(tile_ref, last_ref)
    facing = [splats_ref[6 + d : 7 + d, :] for d in range(3)]
    slope_ref[0:16, :] = basis
    for d, rows in enumerate(slope_rows(*facing)):
        slope_ref[16 * (d + 1) : 16 * (d + 2), :] = jnp.concatenate(rows, axis=0)
    for first in range(0, slots_ref.shape[0], SEGMENTS):
        rows = slice(first, first + SEGMENTS)
        order_ref[rows, :] = spread_order(slots_ref[rows, :])
    meanwhile()
    band_part(*target_ref.shape[1:], wide_ref, back_ref)
    border_wait(copies)
    aims = extend(target_ref, tall_ref, side_ref)
    for c, plane in enumerate(aims):
        aim_ref[c] = plane
    still_ref[...] = blur_planes(aims + [aim * aim for aim in aims], wide_ref)
    take_in(owners, out_ref, in_ref, send_sem, recv_sem)
    for chunk in range(chunks):
        first, ninth = unpack_two(in_ref[2 * chunk], in_ref[2 * chunk + 1])
        recv_ref[0:8, chunk * BLOCK : (chunk + 1) * BLOCK] = first
        recv_ref[8:9, chunk * BLOCK : (chunk + 1) * BLOCK] = ninth


def parcels(owners):
    return [
        pltpu.VMEM((owners, PACKED, BLOCK), jnp.float32),
        pltpu.VMEM((owners, PACKED, BLOCK), jnp.float32),
        pltpu.SemaphoreType.DMA((owners,)),
        pltpu.SemaphoreType.DMA((owners,)),
    ]


def return_part(owners, pulled_ref, in_ref, out_ref, send_sem, recv_sem):
    chunks = pulled_ref.shape[1] // BLOCK
    for chunk in range(chunks):
        lanes = slice(chunk * BLOCK, (chunk + 1) * BLOCK)
        one, two = pack_two(pulled_ref[0:8, lanes], pulled_ref[8:9, lanes])
        out_ref[2 * chunk] = one
        out_ref[2 * chunk + 1] = two
    post(owners, out_ref, in_ref, send_sem, recv_sem)
    take_in(owners, out_ref, in_ref, send_sem, recv_sem)


def train_kernel(owners, columns, counts, *refs):
    parts = []
    for count in counts:
        parts.append(refs[:count])
        refs = refs[count:]
    sources, (landed_ref, slope_ref, home_ref, shown_ref), local, shared, draw_refs = parts[:5]
    pull_refs, early, border, late, deliver_refs, return_refs = parts[5:]
    tile_ref, last_ref, splats_ref, sh_ref, send_ref, target_ref, slots_ref, load_sem = local
    recv_ref, aim_ref, order_ref, rec_ref, coef_ref, saved_ref, *shared = shared
    alpha_ref, share_ref, heavy_ref, grad_ref, pulled_ref, select_ref, still_ref = shared
    loads = [
        pltpu.make_async_copy(source, into, load_sem.at[at])
        for at, (source, into) in enumerate(
            zip(sources, (splats_ref, sh_ref, send_ref, target_ref, slots_ref, tile_ref))
        )
    ]
    deliver_part(
        owners, columns, loads, early[1:3] + late[1:3],
        functools.partial(prepare_part, draw_refs[0], draw_refs[2]),
        still_ref, late[3], late[4], recv_ref, home_ref, aim_ref, order_ref,
        slope_ref, *local[:-1], *border, *early, *deliver_refs,
    )
    forward_part(
        tile_ref, last_ref, recv_ref, order_ref, shown_ref, rec_ref, coef_ref, saved_ref,
        alpha_ref, share_ref, *draw_refs,
    )

    def meanwhile():
        weigh_part(saved_ref, share_ref, heavy_ref)
        choose_part(order_ref, select_ref)

    contrast_part(
        owners, columns, meanwhile,
        shown_ref, aim_ref, still_ref, grad_ref, *late,
    )
    backward_part(
        tile_ref, rec_ref, coef_ref, saved_ref, alpha_ref, share_ref, heavy_ref, grad_ref,
        order_ref, select_ref, pulled_ref, *pull_refs,
    )
    return_part(owners, pulled_ref, landed_ref, *return_refs)


def train(splats, sh_coeffs, send_list, target, slots, tile_ids):
    own = splats.shape[1]
    chunks = own // BLOCK
    owners = lax.axis_size("gauss")
    rows, cols = target.shape[1:]
    ways = len(WAYS)
    slots_total = slots.shape[0]
    side = TILE_SIDE * TILE_SIDE

    def f32(*shape):
        return pltpu.VMEM(shape, jnp.float32)

    def bf16(*shape):
        return pltpu.VMEM(shape, jnp.bfloat16)

    def i32(*shape):
        return pltpu.VMEM(shape, jnp.int32)

    sems = pltpu.SemaphoreType.DMA
    args = (splats, sh_coeffs, send_list.reshape(chunks, BLOCK), target, slots, tile_ids)
    outs = (
        jax.ShapeDtypeStruct((owners, PACKED, BLOCK), jnp.float32),
        jax.ShapeDtypeStruct((64, own), jnp.float32),
        jax.ShapeDtypeStruct((chunks, BLOCK), jnp.int32),
        jax.ShapeDtypeStruct(target.shape, jnp.float32),
    )
    local = [
        pltpu.SMEM(tile_ids.shape, jnp.int32),
        pltpu.SMEM((TILES_DEV,), jnp.int32),
        f32(*splats.shape),
        f32(*sh_coeffs.shape),
        i32(chunks, BLOCK),
        f32(*target.shape),
        i32(*slots.shape),
        sems((len(args),)),
    ]
    shared = [
        f32(FIELDS, own),
        f32(3, EXT_ROWS, 2 * cols),
        i32(*slots.shape),
        f32(6, slots_total, BLOCK),
        bf16(slots_total, COEF_ROWS, BLOCK),
        f32(slots_total, 5, SEGMENTS, side),
        f32(slots_total, BLOCK, side),
        f32(slots_total, BLOCK, side),
        bf16(slots_total, 2 * BLOCK, side),
        f32(TILES_DEV, 8, side),
        f32(FIELDS, own),
        bf16(slots_total // 4, BLOCK, 4 * BLOCK),
        f32(6 * MID_ROWS, 2 * cols),
    ]
    draw_refs = [f32(slots_total * COEF_ROWS, BLOCK), f32(slots_total, 8, side), bf16(COEF_ROWS, side)]
    pull_refs = [
        bf16(TILES_DEV, COEF_ROWS - 16, side),
        f32(slots_total, 16, BLOCK),
        f32(slots_total, GRAD_ROWS, BLOCK),
        i32(slots_total, BLOCK),
        f32(2 * FIELDS * chunks, BLOCK),
        f32(2 * WIDTH, BLOCK, side),
        bf16(2 * WIDTH, 2 * BLOCK, side),
        f32(2 * WIDTH, SEGMENTS, side),
    ]
    border = [f32(8, own), f32(chunks, BLOCK)]
    early = border_scratch(rows, cols) + [sems((ways,)), sems((ways,))]
    late = (
        border_scratch(rows, cols)
        + [bf16(12 * cols, 2 * cols), bf16(12 * cols, cols)]
        + [sems((ways,)), sems((ways,))]
    )
    landing, into, *pair = parcels(owners)
    groups = [local, shared, draw_refs, pull_refs, early, border, late]
    groups += [[landing, into] + pair, [landing] + pair]
    counts = (len(args), len(outs)) + tuple(len(group) for group in groups)
    return pl.pallas_call(
        functools.partial(train_kernel, owners, lax.axis_size("tile"), counts),
        out_shape=outs,
        in_specs=[hbm()] * len(args),
        out_specs=(vmem(),) * len(outs),
        scratch_shapes=sum(groups, []),
        compiler_params=pltpu.CompilerParams(
            collective_id=1, has_side_effects=True, vmem_limit_bytes=40 * 1024 * 1024
        ),
        name="train",
    )(*[pltpu.with_memory_space_constraint(value, pltpu.HBM) for value in args])


def settle_kernel(
    in_ref, slope_ref, home_ref, sh_ref, shown_ref, rendered_ref, splat_grad_ref, sh_grad_ref,
    table_ref, ninth_ref,
):
    rendered_ref[...] = shown_ref[...]
    chunks = sh_ref.shape[1] // BLOCK
    for chunk in range(chunks):
        first, ninth = unpack_two(in_ref[2 * chunk], in_ref[2 * chunk + 1])
        table_ref[:, chunk * BLOCK : (chunk + 1) * BLOCK] = first
        ninth_ref[chunk : chunk + 1, :] = ninth
    for chunk in range(chunks):
        lanes = slice(chunk * BLOCK, (chunk + 1) * BLOCK)
        first, last = gather_rows(table_ref, ninth_ref, chunks, home_ref[chunk : chunk + 1, :])
        splat_grad_ref[0:6, lanes] = first[0:6]
        tints = (first[6:7], first[7:8], last)
        basis = slope_ref[0:16, lanes]
        mixed = jnp.zeros((16, BLOCK), jnp.float32)
        for c in range(3):
            tint = jnp.broadcast_to(tints[c], (16, BLOCK))
            sh_grad_ref[16 * c : 16 * (c + 1), lanes] = tint * basis
            mixed = mixed + tint * sh_ref[16 * c : 16 * (c + 1), lanes]
        splat_grad_ref[6:9, lanes] = jnp.concatenate(
            [
                jnp.sum(mixed * slope_ref[16 * d : 16 * (d + 1), lanes], axis=0, keepdims=True)
                for d in (1, 2, 3)
            ],
            axis=0,
        )


def settle(landed, slopes, home, splats, sh_coeffs, shown):
    own = splats.shape[1]
    return pl.pallas_call(
        settle_kernel,
        out_shape=(
            jax.ShapeDtypeStruct(shown.shape, jnp.float32),
            jax.ShapeDtypeStruct(splats.shape, jnp.float32),
            jax.ShapeDtypeStruct(sh_coeffs.shape, jnp.float32),
        ),
        in_specs=[vmem()] * 5,
        out_specs=(vmem(), vmem(), vmem()),
        scratch_shapes=[
            pltpu.VMEM((8, own), jnp.float32),
            pltpu.VMEM((own // BLOCK, BLOCK), jnp.float32),
        ],
        compiler_params=pltpu.CompilerParams(vmem_limit_bytes=VMEM_ROOM),
        name="settle",
    )(landed, slopes, home, sh_coeffs, shown)


def body(splats, sh_coeffs, send_list, block_slots, block_tiles, target):
    landed, slopes, home, shown = train(
        splats, sh_coeffs, send_list, target, block_slots[0], block_tiles
    )
    return settle(landed, slopes, home, splats, sh_coeffs, shown)


def solution(mesh):
    in_specs = (
        P(None, ("gauss", "tile")),
        P(None, ("gauss", "tile")),
        P(("gauss", "tile")),
        P("gauss", "tile", None),
        P("gauss", "tile"),
        P(None, "gauss", "tile"),
    )
    out_specs = (P(None, "gauss", "tile"), P(None, ("gauss", "tile")), P(None, ("gauss", "tile")))
    return jax.shard_map(body, mesh=mesh, in_specs=in_specs, out_specs=out_specs, check_vma=False)
```
